32 devices in a mesh: blk: 8 (over z, x), grp: 4 (over y, core).
Axes of the slice: x: 2, y: 2, z: 4, core: 2. Of those that a mesh axis runs over, the one named last changes fastest.
Arguments:
- tokens: bfloat16 [4, 2048, 1024], P(None, ('blk', 'grp')), may hold values from -6 to 6
- segments: int32 [4, 2048], P(None, 'blk'), may hold values from 1 to 11, as said below
- cotangent: bfloat16 [4, 2048, 1024], P(None, ('blk', 'grp')), may hold values from -6 to 6
- norm_gain: bfloat16 [1024], P(('blk', 'grp')), may hold values from 0.5 to 1.5
- entry_weight: bfloat16 [1024, 4096], P(('blk', 'grp')), may hold values from -0.1875 to 0.1875
- kernel_weight: bfloat16 [4, 2048], P(None, ('blk', 'grp')), may hold values from -3 to 3
- kernel_offset: bfloat16 [2048], P(('blk', 'grp')), may hold values from -0.5 to 0.5
- select_weight: bfloat16 [2048, 96], P(('blk', 'grp')), may hold values from -0.125 to 0.125
- delta_weight: bfloat16 [64, 2048], P(None, ('blk', 'grp')), may hold values from -0.75 to 0.75
- timestep_bias: bfloat16 [2048], P(('blk', 'grp')), may hold values from -9 to -2
- decay_log: bfloat16 [16, 2048], P(None, ('blk', 'grp')), may hold values from -1.5 to 1.5
- skip_gain: bfloat16 [2048], P(('blk', 'grp')), may hold values from 0.5 to 1.5
- exit_weight: bfloat16 [2048, 1024], P(('blk', 'grp')), may hold values from -0.375 to 0.375
Outputs:
- block_out: bfloat16 [4, 2048, 1024], P(None, ('blk', 'grp'))
- input_grad: bfloat16 [4, 2048, 1024], P(None, ('blk', 'grp'))
- gain_grad: float32 [1024], P(('blk', 'grp'))
- entry_grad: float32 [1024, 4096], P(('blk', 'grp'))
- kernel_grad: float32 [4, 2048], P(None, ('blk', 'grp'))
- offset_grad: float32 [2048], P(('blk', 'grp'))
- select_grad: float32 [2048, 96], P(('blk', 'grp'))
- delta_grad: float32 [64, 2048], P(None, ('blk', 'grp'))
- timestep_grad: float32 [2048], P(('blk', 'grp'))
- decay_grad: float32 [16, 2048], P(None, ('blk', 'grp'))
- skip_grad: float32 [2048], P(('blk', 'grp'))
- exit_grad: float32 [2048, 1024], P(('blk', 'grp'))
The draws below stay inside these ranges and needn't reach their ends.
Inputs may be any that keep to these rules, and one draw needn't show every extreme that they name: `segments`: along each sequence the numbers never fall; a run of equal numbers is one document of 200 to 2000 tokens, save the last of a sequence, which may be shorter; the first document of a sequence has number 1 and, where there are two or more, the last has 11; in one sequence, drawn from the seed, all tokens form one document.
All inputs are finite; a program needn't handle non-finite values.
Results may differ from the reference program's by a relative error of at most 0.012.
Values may be sent and summed in bfloat16 or wider, within the bound.
No kernel may reach another device: no remote copies, remote signals or barrier semaphores. Data moves between devices by JAX's collectives and lax.ppermute only.
A program may use at most 192 MiB of HBM per device.

```python
import jax
import jax.numpy as jnp
from jax import lax

D = 1024
DI = 2048
NSTATE = 16
RANK = 64
CONV = 4
SEL = 96
SEQS = 4
LEN = 2048
DOC_MIN = 200
DOC_MAX = 2000


def draw_segments(key, part):
    doc_count = LEN // DOC_MIN + 1
    length_key, chosen_key = jax.random.split(jax.random.fold_in(key, 17))
    doc_lengths = jax.random.randint(length_key, (SEQS, doc_count), DOC_MIN, DOC_MAX + 1).astype(jnp.int32)
    doc_ends = jnp.cumsum(doc_lengths, axis=1).astype(jnp.int32)
    positions = jnp.arange(LEN, dtype=jnp.int32)

    def number_row(ends_row):
        return jnp.searchsorted(ends_row, positions, side='right').astype(jnp.int32)
    doc_index = jax.vmap(number_row)(doc_ends)
    final_index = doc_index[:, LEN - 1:LEN]
    numbered = jnp.where(doc_index == final_index, LEN // DOC_MIN, doc_index) + 1
    chosen_row = jax.random.randint(chosen_key, (), 0, SEQS)
    row_ids = jnp.arange(SEQS, dtype=jnp.int32)[:, None]
    return jnp.where(row_ids == chosen_row, 1, numbered).astype(jnp.int32)


def steps_of(key, dims, shards, low, top_value):
    def one(axis_at, parts):
        steps = jax.random.uniform(jax.random.fold_in(jax.random.fold_in(key, 6), axis_at), (parts,), jnp.float32, low / len(shards), top_value / len(shards))
        return jnp.repeat(jnp.exp(steps), dims[axis_at] // parts).reshape((-1,) + (1,) * (len(dims) - axis_at - 1))

    loudness = one(*shards[0])
    for cut in shards[1:]:
        loudness = loudness * one(*cut)
    return loudness


def normal_values(own_key, dims, width, reach, pieces=(), held_as=jnp.bfloat16):
    factor_of = steps_of(own_key, dims, pieces, -0.22, 0.18) if pieces else 1.0
    values = jax.random.normal(own_key, dims, jnp.float32) * width * factor_of
    return jnp.minimum(jnp.maximum(values, -reach), reach).astype(held_as)


def setup_inputs(seed: int = 0) -> dict:
    key_list = jax.random.split(jax.random.key(seed), 14)
    return {
        "tokens": normal_values(key_list[0], (SEQS, LEN, D), 1.0, 6.0, ((1, 32),)),
        "segments": draw_segments(jax.random.fold_in(key_list[13], 71), 0),
        "cotangent": normal_values(key_list[2], (SEQS, LEN, D), 1.0, 6.0, ((1, 32),)),
        "norm_gain": jnp.clip(1.0 + 0.1 * jax.random.normal(key_list[3], (D,), jnp.float32), 0.5, 1.5).astype(jnp.bfloat16),
        "entry_weight": normal_values(key_list[4], (D, 2 * DI), D ** -0.5, 0.1875, ((0, 32),)),
        "kernel_weight": normal_values(key_list[5], (CONV, DI), CONV ** -0.5, 3.0, ((1, 32),)),
        "kernel_offset": jnp.clip(jax.random.uniform(key_list[6], (DI,), jnp.float32, -0.5, 0.5) * steps_of(key_list[6], (DI,), ((0, 32),), -0.4, 0.0), -0.5, 0.5).astype(jnp.bfloat16),
        "select_weight": normal_values(key_list[7], (DI, SEL), DI ** -0.5, 0.125, ((0, 32),)),
        "delta_weight": normal_values(key_list[8], (RANK, DI), RANK ** -0.5, 0.75, ((1, 32),)),
        "timestep_bias": jnp.clip(-9.0 + 7.0 * jax.random.uniform(key_list[9], (DI,), jnp.float32) ** steps_of(key_list[9], (DI,), ((0, 32),), -0.2, 0.2), -9.0, -2.0).astype(jnp.bfloat16),
        "decay_log": jnp.clip(jax.random.uniform(key_list[10], (NSTATE, DI), jnp.float32, -1.5, 1.5) * steps_of(key_list[10], (NSTATE, DI), ((1, 32),), -0.4, 0.0), -1.5, 1.5).astype(jnp.bfloat16),
        "skip_gain": jnp.clip(0.5 + 1.0 * jax.random.uniform(key_list[11], (DI,), jnp.float32) ** steps_of(key_list[11], (DI,), ((0, 32),), -0.2, 0.2), 0.5, 1.5).astype(jnp.bfloat16),
        "exit_weight": normal_values(key_list[12], (DI, D), (DI // 8) ** -0.5, 0.375, ((0, 32),)),
    }


epsilon = 1e-05
highest = lax.Precision.HIGHEST

@jax.custom_vjp
def low(v):
    return lax.optimization_barrier(v.astype(jnp.bfloat16)).astype(jnp.float32)

@jax.custom_vjp
def low_back(v):
    return v

def low_keep(v):
    return (low(v), None)

def low_pass(kept, grad):
    return (grad,)

def back_keep(v):
    return (v, None)

def back_low(kept, grad):
    return (low(grad),)
low.defvjp(low_keep, low_pass)
low_back.defvjp(back_keep, back_low)

def silu_value(values):
    return values * jax.nn.sigmoid(values)

def matmul(left, right):
    return jnp.dot(left, right, precision=highest)

def scan_block(carry_state, block_inputs):
    hidden, rate_matrix = carry_state

    def one_step(hidden_now, step_inputs):
        step_row, filter_row, write_row, read_row, reset_row = step_inputs
        decays = jnp.exp(step_row[None, :] * rate_matrix) * (1.0 - reset_row)
        hidden_now = decays * hidden_now + (step_row * filter_row)[None, :] * write_row[:, None]
        return (hidden_now, lax.optimization_barrier(jnp.sum(hidden_now * read_row[:, None], axis=0)))
    hidden, emitted = lax.scan(one_step, hidden, block_inputs)
    return ((hidden, rate_matrix), emitted)

def block_forward(params, inputs, labels):
    norm_gain, entry_weight, kernel_weight, kernel_offset, select_weight, delta_weight, timestep_bias, decay_log, skip_gain, exit_weight = params
    total_tokens = inputs.shape[0]
    root_scale = lax.rsqrt(lax.optimization_barrier(jnp.mean(inputs * inputs, axis=1, keepdims=True)) + epsilon)
    normed = low(inputs * root_scale * norm_gain)
    projected = low_back(matmul(normed, entry_weight))
    inner_part = low(projected[:, :DI])
    gating = projected[:, DI:]
    rim_rows = CONV - 1
    padded = jnp.concatenate([jnp.zeros((rim_rows, DI), jnp.float32), inner_part], axis=0)
    padded_labels = jnp.concatenate([jnp.full((rim_rows,), -1, jnp.int32), labels.astype(jnp.int32)], axis=0)
    kernel_sum = kernel_offset + jnp.zeros_like(inner_part)
    for k in range(CONV):
        same_document = (padded_labels[k:k + total_tokens] == labels).astype(jnp.float32)[:, None]
        kernel_sum = kernel_sum + kernel_weight[k] * padded[k:k + total_tokens] * same_document
    filtered = low(silu_value(kernel_sum))
    selected = low_back(matmul(filtered, select_weight))
    low_rank = selected[:, :RANK]
    write_gate = selected[:, RANK:RANK + NSTATE]
    read_gate = selected[:, RANK + NSTATE:]
    steps_dt = jax.nn.softplus(matmul(low_rank, delta_weight) + timestep_bias)
    rate_matrix = -jnp.exp(decay_log)
    previous_labels = jnp.concatenate([labels[:1], labels[:-1]], axis=0)
    resets = (labels != previous_labels).astype(jnp.float32)
    block_tokens = 128
    block_count = total_tokens // block_tokens

    def split_blocks(values):
        return values.reshape((block_count, block_tokens) + values.shape[1:])
    block_inputs = (split_blocks(steps_dt), split_blocks(filtered), split_blocks(write_gate), split_blocks(read_gate), split_blocks(resets))
    start_state = (jnp.zeros((NSTATE, DI), jnp.float32), rate_matrix)
    final_state, emitted = lax.scan(jax.checkpoint(scan_block), start_state, block_inputs)
    scan_sum = emitted.reshape(total_tokens, DI)
    scan_out = low(low_back(scan_sum + skip_gain * filtered))
    gated = low(scan_out * silu_value(gating))
    return inputs + matmul(gated, exit_weight)

def reference(tokens, segments, cotangent, norm_gain, entry_weight, kernel_weight, kernel_offset, select_weight, delta_weight, timestep_bias, decay_log, skip_gain, exit_weight):
    params = tuple((p.astype(jnp.float32) for p in (norm_gain, entry_weight, kernel_weight, kernel_offset, select_weight, delta_weight, timestep_bias, decay_log, skip_gain, exit_weight)))

    def one_sequence(totals, items):
        inputs, labels, cotan_rows = items

        def closed(weights, rows):
            return block_forward(weights, rows, labels)
        outputs, pullback = jax.vjp(closed, params, inputs.astype(jnp.float32))
        weight_grads, input_grads = pullback(cotan_rows.astype(jnp.float32))
        totals = jax.tree.map(lambda left, right: left + right, totals, weight_grads)
        return (totals, (outputs.astype(jnp.bfloat16), input_grads.astype(jnp.bfloat16)))
    zero_grads = tuple((jnp.zeros_like(p) for p in params))
    totals, results = lax.scan(one_sequence, zero_grads, (tokens, segments, cotangent))
    block_out, input_grad = results
    return (block_out, input_grad, totals[0], totals[1], totals[2], totals[3], totals[4], totals[5], totals[6], totals[7], totals[8], totals[9])
```

```python
import jax
import jax.numpy as jnp
from jax import lax
from jax.experimental import pallas as pl
from jax.experimental.pallas import tpu as pltpu
from jax.sharding import PartitionSpec as P

epsilon = 1e-05
log2_e = 1.4426950408889634
log_2 = 0.6931471805599453
reset_push = 1e6
f32 = jnp.float32
bf16 = jnp.bfloat16
small_rows = 192
both = ("blk", "grp")


def dot(left, right, dims=((1,), (0,))):
    return lax.dot_general(left, right, (dims, ((), ())), preferred_element_type=f32)


def sigmoid(values):
    return 1.0 / (1.0 + jnp.exp(-values))


def spread(block, axis):
    count = lax.axis_size(axis)
    copies = jnp.broadcast_to(block[None], (count,) + block.shape)
    return lax.all_to_all(copies, axis, split_axis=0, concat_axis=0, tiled=True)


def ordering(rows, chunks):
    steps = rows // chunks
    out_row = lax.broadcasted_iota(jnp.int32, (rows, rows), 0)
    in_row = lax.broadcasted_iota(jnp.int32, (rows, rows), 1)
    wanted = (out_row % chunks) * steps + out_row // chunks
    return jnp.where(in_row == wanted, 1.0, 0.0).astype(bf16)


def kernel_call(body, outs, scratch, limit, *operands):
    places = [
        pl.BlockSpec(memory_space=pltpu.SMEM)
        if value.dtype == jnp.int32
        else pl.BlockSpec(memory_space=pltpu.VMEM)
        for value in operands
    ]
    flops = 2_000_000_000
    return pl.pallas_call(
        body,
        out_shape=[jax.ShapeDtypeStruct(shape, kind) for shape, kind in outs],
        in_specs=places,
        out_specs=[pl.BlockSpec(memory_space=pltpu.VMEM) for _ in outs],
        scratch_shapes=scratch,
        compiler_params=pltpu.CompilerParams(vmem_limit_bytes=limit << 20),
        cost_estimate=pl.CostEstimate(flops=flops, bytes_accessed=8_000_000, transcendentals=0),
    )(*operands)


def read_rows(tokens_ref, order, me, block):
    groups, sequences, _, width = tokens_ref.shape
    parts = [
        tokens_ref[k ^ me, :, pl.ds(pl.multiple_of(block * 8, 8), 8), :].astype(f32)
        for k in range(groups)
    ]
    rows = jnp.concatenate(parts, axis=0).reshape(groups * sequences * 8, width)
    return rows


def small_row(small_ref, index):
    tail = small_ref[176:192, :].astype(f32)
    return tail[index : index + 1, :]


def entry_kernel(
    place_ref, tokens_ref, rim_ref, gain_ref, mask_ref, weight_ref, small_ref,
    normed_ref, inner_ref, filter_ref, chosen_ref,
):
    me = place_ref[1]
    groups, sequences, steps, width = tokens_ref.shape
    chunks = groups * sequences
    block_rows = chunks * 8
    rim_rows = 3 * chunks
    order = ordering(block_rows, chunks)

    def scaled(rows):
        root = lax.rsqrt(jnp.mean(rows * rows, axis=1, keepdims=True) + epsilon)
        return (rows * root * gain_ref[...]).astype(bf16)

    rim = scaled(rim_ref[...].astype(f32))
    inner_ref[0:rim_rows, :] = dot(rim, weight_ref[...]).astype(bf16)
    taps = [small_row(small_ref, k) for k in range(4)]
    offset = small_row(small_ref, 4)

    def lap(block, carry):
        base = pl.multiple_of(block * block_rows, block_rows)
        rows = scaled(read_rows(tokens_ref, order, me, block))
        normed = dot(order, rows).astype(bf16)
        normed_ref[pl.ds(base, block_rows), :] = normed
        inner = dot(normed, weight_ref[...]).astype(bf16)
        inner_ref[pl.ds(pl.multiple_of(base + rim_rows, 16), block_rows), :] = inner
        total = offset
        for k in range(3):
            same = mask_ref[pl.ds(base, block_rows), k : k + 1]
            part = inner_ref[pl.ds(pl.multiple_of(base + k * chunks, 16), block_rows), :]
            total = total + taps[k] * part.astype(f32) * same
        total = total + taps[3] * inner.astype(f32)
        filtered = (total * sigmoid(total)).astype(bf16)
        filter_ref[pl.ds(base, block_rows), :] = filtered.astype(f32)
        chosen = dot(small_ref[64:160, :], filtered, ((1,), (1,)))
        chosen_ref[:, pl.ds(base, block_rows)] = chosen.astype(bf16)
        return carry

    lax.fori_loop(0, steps // 8, lap, 0)


def gate_kernel(
    place_ref, cotangent_ref, normed_ref, weight_ref, exit_ref, rows_ref, value_ref, slope_ref, grad_ref
):
    me = place_ref[1]
    groups, sequences, steps, width = cotangent_ref.shape
    chunks = groups * sequences
    block_rows = chunks * 8
    order = ordering(block_rows, chunks)

    def lap(block, carry):
        at = pl.ds(pl.multiple_of(block * block_rows, block_rows), block_rows)
        rows = read_rows(cotangent_ref, order, me, block).astype(bf16)
        ordered = dot(order, rows).astype(bf16)
        rows_ref[at, :] = ordered
        gating = dot(normed_ref[at, :], weight_ref[...])
        grad_gated = dot(ordered, exit_ref[...], ((1,), (1,)))
        gate = sigmoid(gating)
        value = gating * gate
        value_ref[at, :] = value
        slope_ref[at, :] = grad_gated * (gate * (1.0 + gating * (1.0 - gate)))
        grad_ref[at, :] = (grad_gated * value).astype(bf16).astype(f32)
        return carry

    lax.fori_loop(0, steps // 8, lap, 0)


def fill_rates(small_ref, rates_ref):
    states = rates_ref.shape[0]
    rates = -jnp.exp(small_ref[160 : 160 + states, :].astype(f32)) * log2_e
    for n in range(states):
        rates_ref[n] = jnp.broadcast_to(rates[n : n + 1, :], rates_ref.shape[1:])


def fill_gates(gates_ref, write_ref, read_ref, half):
    steps, states = write_ref.shape[:2]
    at = pl.ds(pl.multiple_of(half * 8, 8), 8)

    def lap(t, carry):
        values = gates_ref[t, at, :]
        for n in range(states):
            write_ref[t, n] = jnp.broadcast_to(values[:, 64 + n : 65 + n], (8, 128))
            read_ref[t, n] = jnp.broadcast_to(values[:, 80 + n : 81 + n], (8, 128))
        return carry

    lax.fori_loop(0, steps, lap, 0)


def piece_kernel(
    chosen_ref, mask_ref, small_ref, filter_ref, grad_ref,
    gates_ref, step_ref, slope_ref, end_ref, keep_ref, give_ref, sum_ref, ahead_ref, back_ref,
    rates_ref, write_ref, read_ref,
):
    steps, chunks, width = step_ref.shape
    states = end_ref.shape[0]
    chosen = jnp.sum(chosen_ref[...].astype(f32), axis=0)
    padded = jnp.concatenate([chosen, jnp.zeros((32, chosen.shape[1]), f32)], axis=0)
    gates_ref[...] = padded.T.reshape(steps, chunks, 128)
    fill_rates(small_ref, rates_ref)
    bias = small_row(small_ref, 5)
    delta = small_ref[0:64, :]

    def delta_lap(block, carry):
        at = pl.ds(pl.multiple_of(block * 8, 8), 8)
        low = gates_ref[at, :, :].reshape(8 * chunks, 128)[:, 0:64]
        high = low.astype(bf16)
        rest = (low - high.astype(f32)).astype(bf16)
        pre = dot(high, delta) + dot(rest, delta) + bias
        grown = jnp.exp(-jnp.abs(pre))
        step = jnp.maximum(pre, 0.0) + jnp.log1p(grown)
        step_ref[at, :, :] = step.reshape(8, chunks, width)
        slope_ref[at, :, :] = (jnp.where(pre >= 0, 1.0, grown) / (1.0 + grown)).reshape(8, chunks, width)
        return carry

    lax.fori_loop(0, steps // 8, delta_lap, 0)

    end_ref[...] = jnp.zeros_like(end_ref)
    give_ref[...] = jnp.zeros_like(give_ref)
    keep_ref[...] = jnp.ones_like(keep_ref)
    sum_ref[...] = jnp.zeros_like(sum_ref)

    def half_lap(half, carry):
        fill_gates(gates_ref, write_ref, read_ref, half)
        at = pl.ds(pl.multiple_of(half * 8, 8), 8)

        def lane_lap(lane, inner_carry):
            lanes = pl.ds(pl.multiple_of(lane * 128, 128), 128)

            def lap(block, total):
                pushed, drives, grads = [], [], []
                for j in range(8):
                    t = block * 8 + j
                    step = step_ref[t, at, lanes]
                    push = step + gates_ref[t, at, 96:97]
                    total = total + push
                    pushed.append(push)
                    drives.append(step * filter_ref[t, at, lanes])
                    grads.append(grad_ref[t, at, lanes])
                for n in range(states):
                    rate = rates_ref[n, :, lanes]
                    end = end_ref[n, at, lanes]
                    keep = keep_ref[n, at, lanes]
                    give = give_ref[n, at, lanes]
                    for j in range(8):
                        t = block * 8 + j
                        decay = jnp.exp2(pushed[j] * rate)
                        end = decay * end + drives[j] * write_ref[t, n]
                        keep = keep * decay
                        give = give + keep * (read_ref[t, n] * grads[j])
                    end_ref[n, at, lanes] = end
                    keep_ref[n, at, lanes] = keep
                    give_ref[n, at, lanes] = give
                return total

            total = lax.fori_loop(0, steps // 8, lap, jnp.zeros((8, 128), f32))
            sum_ref[at, lanes] = total
            return inner_carry

        return lax.fori_loop(0, width // 128, lane_lap, carry)

    push = mask_ref[:, 3:4] * reset_push
    gates_ref[:, :, 96:97] = push.reshape(steps, chunks, 1)
    lax.fori_loop(0, chunks // 8, half_lap, 0)

    sequences = ahead_ref.shape[0] // states
    groups = chunks // sequences
    for n in range(states):
        rows = slice(n * sequences, (n + 1) * sequences)
        ahead = jnp.zeros((sequences, width), f32)
        back = jnp.zeros((sequences, width), f32)
        for k in range(groups):
            part = slice(k * sequences, (k + 1) * sequences)
            ahead = keep_ref[n, part, :] * ahead + end_ref[n, part, :]
            other = slice((groups - 1 - k) * sequences, (groups - k) * sequences)
            back = give_ref[n, other, :] + keep_ref[n, other, :] * back
        ahead_ref[rows, :] = ahead
        back_ref[rows, :] = back


def scan_kernel(
    place_ref, came_ref, sums_ref, gates_ref, small_ref, step_ref, slope_ref, filter_ref, grad_ref,
    end_ref, keep_ref, give_ref,
    out_ref, delta_ref, direct_ref, rank_ref, chosen_ref, decay_ref, skip_ref, bias_ref,
    rates_ref, write_ref, read_ref, state_ref, product_ref, pick_ref, enter_ref, arrive_ref, sums_acc_ref,
):
    me = place_ref[0]
    steps, chunks, width = step_ref.shape
    states = end_ref.shape[0]
    pieces = came_ref.shape[0]
    sequences = sums_ref.shape[1]
    groups = chunks // sequences
    fill_rates(small_ref, rates_ref)

    def state_of(piece, n):
        return came_ref[piece, n * sequences : (n + 1) * sequences, :].astype(f32)

    for n in range(states):
        rate = rates_ref[n, 0:sequences, :]

        def step_in(piece, state):
            return jnp.exp2(sums_ref[piece] * rate) * state + state_of(piece, n)

        def step_back(k, state):
            return step_in(pieces - 1 - k, state)

        zero = jnp.zeros((sequences, width), f32)
        ahead = lax.fori_loop(0, me, step_in, zero)
        back = lax.fori_loop(0, pieces - 1 - me, step_back, zero)
        for k in range(groups):
            part = slice(k * sequences, (k + 1) * sequences)
            enter_ref[n, part, :] = ahead
            ahead = keep_ref[n, part, :] * ahead + end_ref[n, part, :]
            other = slice((groups - 1 - k) * sequences, (groups - k) * sequences)
            arrive_ref[n, other, :] = back
            back = give_ref[n, other, :] + keep_ref[n, other, :] * back

    spot = lax.broadcasted_iota(jnp.int32, (2 * states * 128, 128), 0) // 128
    column = lax.broadcasted_iota(jnp.int32, (2 * states * 128, 128), 1)
    pick_ref[...] = jnp.where(column == spot + 64, 1.0, 0.0).astype(bf16)
    sums_acc_ref[...] = jnp.zeros_like(sums_acc_ref)
    decay_ref[...] = jnp.zeros_like(decay_ref)
    skip_ref[...] = jnp.zeros_like(skip_ref)
    skip_gain = small_row(small_ref, 6)
    skip_spread = jnp.broadcast_to(skip_gain, (8, width))
    rates_ref[states] = skip_spread
    span = 4

    def half_lap(half, carry):
        fill_gates(gates_ref, write_ref, read_ref, half)
        at = pl.ds(pl.multiple_of(half * 8, 8), 8)

        def lane_lap(lane, inner_carry):
            lanes = pl.ds(pl.multiple_of(lane * 128, 128), 128)

            def forward(block, states_now):
                pushed, drives, grads, outs, feeds = [], [], [], [], []
                for j in range(span):
                    t = block * span + j
                    step = step_ref[t, at, lanes]
                    feed = filter_ref[t, at, lanes]
                    pushed.append(step + gates_ref[t, at, 96:97])
                    drives.append(step * feed)
                    grads.append(grad_ref[t, at, lanes])
                    feeds.append(feed)
                    outs.append(feed * rates_ref[states, :, lanes])
                nexts = []
                for n in range(states):
                    rate = rates_ref[n, :, lanes]
                    hidden = states_now[n]
                    seen = []
                    for j in range(span):
                        t = block * span + j
                        hidden = jnp.exp2(pushed[j] * rate) * hidden + drives[j] * write_ref[t, n]
                        state_ref[t, n] = hidden
                        outs[j] = outs[j] + hidden * read_ref[t, n]
                        seen.append(grads[j] * hidden)
                    spot = slice((states + n) * 128, (states + n + 1) * 128)
                    rows = pl.ds(pl.multiple_of(block * span * 8, span * 8), span * 8)
                    product_ref[rows, spot] = jnp.concatenate(seen, axis=0).astype(bf16)
                    nexts.append(hidden)
                for j in range(span):
                    out_ref[block * span + j, at, lanes] = outs[j]
                return tuple(nexts)

            first = tuple(enter_ref[n, at, lanes] for n in range(states))
            lax.fori_loop(0, steps // span, forward, first)

            def backward(k, held):
                block = steps // span - 1 - k
                passed, totals, skip_total = held
                pushed, raw, drives, grads, weighted, slopes, feeds = [], [], [], [], [], [], []
                for j in range(span):
                    t = block * span + j
                    step = step_ref[t, at, lanes]
                    feed = filter_ref[t, at, lanes]
                    grad = grad_ref[t, at, lanes]
                    raw.append(step)
                    feeds.append(feed)
                    pushed.append(step + gates_ref[t, at, 96:97])
                    drives.append(step * feed)
                    grads.append(grad)
                    weighted.append(jnp.zeros((8, 128), f32))
                    slopes.append(jnp.zeros((8, 128), f32))
                    skip_total = skip_total + grad * feed
                next_passed, next_totals = [], []
                before = jnp.maximum(block * span - 1, 0)
                for n in range(states):
                    rate = rates_ref[n, :, lanes]
                    gone = passed[n]
                    total = totals[n]
                    seen = [None] * span
                    for j in reversed(range(span)):
                        t = block * span + j
                        adjoint = read_ref[t, n] * grads[j] + gone
                        weighted[j] = weighted[j] + adjoint * write_ref[t, n]
                        seen[j] = adjoint * drives[j]
                        gone = adjoint * jnp.exp2(pushed[j] * rate)
                        if j > 0:
                            earlier = state_ref[t - 1, n]
                        else:
                            earlier = jnp.where(block > 0, state_ref[before, n], enter_ref[n, at, lanes])
                        turn = gone * earlier
                        slopes[j] = slopes[j] + turn * rate
                        total = total + turn * raw[j]
                    spot = slice(n * 128, (n + 1) * 128)
                    rows = pl.ds(pl.multiple_of(block * span * 8, span * 8), span * 8)
                    product_ref[rows, spot] = jnp.concatenate(seen, axis=0).astype(bf16)
                    next_passed.append(gone)
                    next_totals.append(total)
                skip_now = rates_ref[states, :, lanes]
                for j in range(span):
                    t = block * span + j
                    grown = slopes[j] * log_2 + weighted[j] * feeds[j]
                    delta_ref[t, at, lanes] = grown * slope_ref[t, at, lanes]
                    direct_ref[t, at, lanes] = weighted[j] * raw[j] + grads[j] * skip_now
                return (tuple(next_passed), tuple(next_totals), skip_total)

            last = tuple(arrive_ref[n, at, lanes] for n in range(states))
            empty = tuple(jnp.zeros((8, 128), f32) for _ in range(states))
            ended = lax.fori_loop(
                0, steps // span, backward, (last, empty, jnp.zeros((8, 128), f32))
            )
            for n in range(states):
                part = jnp.sum(ended[1][n], axis=0, keepdims=True)
                decay_ref[n : n + 1, lanes] += part * rates_ref[n, 0:1, lanes] * log_2
            skip_ref[0:1, lanes] += jnp.sum(ended[2], axis=0, keepdims=True)
            summed = dot(product_ref[...], pick_ref[...])
            sums_acc_ref[:, at, :] += summed.reshape(steps, 8, 128)
            return inner_carry

        return lax.fori_loop(0, width // 128, lane_lap, carry)

    lax.fori_loop(0, chunks // 8, half_lap, 0)

    rows = steps * chunks
    grads = delta_ref[...].reshape(rows, width)
    bias_ref[...] = jnp.sum(grads, axis=0, keepdims=True)
    grads = grads.astype(bf16)
    low = gates_ref[...].reshape(rows, 128)[:, 0:64].astype(bf16)
    rank_ref[...] = dot(low, grads, ((0,), (0,)))
    back = dot(small_ref[0:64, :], grads, ((1,), (1,)))
    sums = sums_acc_ref[...].reshape(rows, 128).T
    chosen_ref[0:64, :] = back.astype(bf16)
    chosen_ref[64:96, :] = sums[64:96, :].astype(bf16)


def store_rows(out_ref, order, values, block):
    groups, sequences, _, width = out_ref.shape
    back = dot(order, values.astype(bf16), ((0,), (0,)))
    shaped = back.reshape(groups, sequences, 8, width).astype(bf16)
    out_ref[:, :, pl.ds(pl.multiple_of(block * 8, 8), 8), :] = shaped


def leave_kernel(
    scan_ref, value_ref, slope_ref, rows_ref, normed_ref, exit_ref,
    gating_ref, out_ref, exit_grad_ref, entry_grad_ref, gated_ref,
):
    groups, sequences, steps, width = out_ref.shape
    chunks = groups * sequences
    block_rows = chunks * 8
    order = ordering(block_rows, chunks)

    def lap(block, carry):
        at = pl.ds(pl.multiple_of(block * block_rows, block_rows), block_rows)
        scan_out = scan_ref[at, :].astype(bf16).astype(f32)
        gated = (scan_out * value_ref[at, :]).astype(bf16)
        gated_ref[at, :] = gated
        gating_ref[at, :] = (scan_out * slope_ref[at, :]).astype(bf16)
        store_rows(out_ref, order, dot(gated, exit_ref[...]), block)
        return carry

    lax.fori_loop(0, steps // 8, lap, 0)
    exit_grad_ref[...] = dot(gated_ref[...], rows_ref[...], ((0,), (0,))).astype(bf16)
    entry_grad_ref[...] = dot(normed_ref[...], gating_ref[...], ((0,), (0,))).astype(bf16)


def filter_kernel(
    chosen_ref, direct_ref, inner_ref, filter_ref, mask_ref, small_ref,
    grads_ref, spill_ref, select_ref, taps_ref, offset_ref, picked_ref,
):
    rows, width = grads_ref.shape
    chunks = spill_ref.shape[0] // 3
    block_rows = chunks * 8
    chosen = jnp.sum(chosen_ref[...].astype(f32), axis=0).astype(bf16)
    select_ref[...] = dot(chosen, filter_ref[...].astype(bf16))
    picked_ref[...] = chosen.astype(f32).T.astype(bf16)
    taps = [small_row(small_ref, k) for k in range(4)]
    offset = small_row(small_ref, 4)
    offset_ref[...] = jnp.zeros_like(offset_ref)
    taps_ref[...] = jnp.zeros_like(taps_ref)

    def lap(block, carry):
        base = pl.multiple_of(block * block_rows, block_rows)
        at = pl.ds(base, block_rows)
        total = offset
        shifted = []
        for k in range(4):
            part = inner_ref[pl.ds(pl.multiple_of(base + k * chunks, 16), block_rows), :].astype(f32)
            if k < 3:
                part = part * mask_ref[at, k : k + 1]
            shifted.append(part)
            total = total + taps[k] * part
        gate = sigmoid(total)
        grad = direct_ref[at, :] + dot(picked_ref[at, :], small_ref[64:160, :])
        grad = grad * (gate * (1.0 + total * (1.0 - gate)))
        grads_ref[at, :] = grad
        offset_ref[...] += jnp.sum(grad, axis=0, keepdims=True)
        for k in range(4):
            taps_ref[k : k + 1, :] += jnp.sum(grad * shifted[k], axis=0, keepdims=True)
        return carry

    lax.fori_loop(0, rows // block_rows, lap, 0)
    for u in range(3):
        total = jnp.zeros((chunks, width), f32)
        for t in range(u + 1):
            part = slice(t * chunks, (t + 1) * chunks)
            total = total + grads_ref[part, :] * taps[u - t] * mask_ref[part, u - t : u - t + 1]
        spill_ref[u * chunks : (u + 1) * chunks, :] = total


def inner_kernel(
    grads_ref, spill_ref, mask_ref, small_ref, normed_ref, gating_ref, weight_ref, gate_weight_ref,
    out_ref, entry_grad_ref, gain_ref, inner_ref, past_ref,
):
    groups, sequences, steps, width = out_ref.shape
    rows, inner_width = grads_ref.shape
    chunks = groups * sequences
    block_rows = chunks * 8
    order = ordering(block_rows, chunks)
    taps = [small_row(small_ref, k) for k in range(4)]
    gain_ref[...] = jnp.zeros_like(gain_ref)
    past_ref[0] = jnp.zeros_like(past_ref[0])
    past_ref[1] = jnp.zeros_like(past_ref[1])
    past_ref[2] = jnp.zeros_like(past_ref[2])
    rim_rows = 3 * chunks
    for k in range(3):
        past_ref[k, rows : rows + rim_rows, :] = jnp.zeros((rim_rows, inner_width), f32)

    def mask_lap(block, carry):
        at = pl.ds(pl.multiple_of(block * block_rows, block_rows), block_rows)
        grad = grads_ref[at, :]
        for k in range(3):
            past_ref[k, at, :] = grad * taps[k] * mask_ref[at, k : k + 1]
        return carry

    lax.fori_loop(0, steps // 8, mask_lap, 0)

    def lap(block, carry):
        base = pl.multiple_of(block * block_rows, block_rows)
        at = pl.ds(base, block_rows)
        total = grads_ref[at, :] * taps[3]
        for k in range(3):
            later = pl.ds(pl.multiple_of(base + (3 - k) * chunks, 16), block_rows)
            total = total + past_ref[k, later, :]
        inner_ref[at, :] = total.astype(bf16)

        @pl.when(block == steps // 8 - 1)
        def _():
            tail = total[block_rows - rim_rows :, :] + spill_ref[...]
            inner_ref[rows - rim_rows : rows, :] = tail.astype(bf16)

        grad = dot(inner_ref[at, :], weight_ref[...], ((1,), (1,)))
        grad = grad + dot(gating_ref[at, :], gate_weight_ref[...], ((1,), (1,)))
        gain_ref[...] += jnp.sum(grad * normed_ref[at, :].astype(f32), axis=0, keepdims=True)
        store_rows(out_ref, order, grad, block)
        return carry

    lax.fori_loop(0, steps // 8, lap, 0)
    entry_grad_ref[...] = dot(normed_ref[...], inner_ref[...], ((0,), (0,))).astype(bf16)


def local(
    tokens,
    segments,
    cotangent,
    norm_gain,
    entry_weight,
    kernel_weight,
    kernel_offset,
    select_weight,
    delta_weight,
    timestep_bias,
    decay_log,
    skip_gain,
    exit_weight,
):
    sequences, steps, width = tokens.shape
    pieces, groups = lax.axis_size("blk"), lax.axis_size("grp")
    piece, group = lax.axis_index("blk"), lax.axis_index("grp")
    place = jnp.stack([piece, group]).astype(jnp.int32)
    chunks = groups * sequences
    rows = steps * chunks
    slice_rows, entry_width = entry_weight.shape
    own = kernel_offset.shape[0]
    inner_width = entry_width // 2
    group_width = inner_width // groups
    states = decay_log.shape[0]
    rank = delta_weight.shape[0]

    packed = jnp.concatenate(
        [
            delta_weight,
            select_weight.T,
            decay_log,
            kernel_weight,
            kernel_offset[None],
            timestep_bias[None],
            skip_gain[None],
            jnp.zeros((small_rows - 183, own), bf16),
        ],
        axis=0,
    )
    small_came = spread(jnp.concatenate([packed.reshape(-1), norm_gain]), "blk")
    small = small_came[:, : packed.size].reshape(pieces, small_rows, own)
    small = small.transpose(1, 0, 2).reshape(small_rows, group_width)

    def meet(values):
        pair = lax.ppermute(values, "grp", [(i, i ^ 2) for i in range(groups)])
        near = lax.ppermute(values, "grp", [(i, i ^ 1) for i in range(groups)])
        far = lax.ppermute(pair, "grp", [(i, i ^ 1) for i in range(groups)])
        return jnp.stack([values, near, pair, far])

    tokens_all = meet(tokens)
    cotangent_all = meet(cotangent)

    ahead = [(i, i + 1) for i in range(pieces - 1)]
    behind = [(i + 1, i) for i in range(pieces - 1)]
    tail = tokens[:, steps - 3 :]
    tail_before = lax.ppermute(tail, "blk", ahead)
    slice_rows = norm_gain.shape[0]
    gain_part = small_came[:, packed.size :].reshape(pieces * slice_rows)
    tail_values = jnp.stack([tail, tail_before]).reshape(-1)
    tails = lax.all_gather(jnp.concatenate([tail_values, gain_part]), "grp")
    gain_all = tails[:, tail_values.size :].reshape(groups, pieces, slice_rows)
    gain_all = gain_all.transpose(1, 0, 2).reshape(1, width).astype(f32)
    tails = tails[:, : tail_values.size].reshape((groups, 2) + tail.shape)
    rim = jnp.concatenate([tails[groups - 1 :, 1], tails[: groups - 1, 0]], axis=0)
    rim = rim.transpose(2, 0, 1, 3).reshape(3 * chunks, width)
    label_tail = lax.ppermute(segments[:, -3:], "blk", ahead)
    labels = jnp.concatenate([label_tail, segments], axis=1)
    length = segments.shape[1]
    shifted = jnp.stack([labels[:, k : k + length] for k in range(3)], axis=-1)
    same = (shifted == segments[:, :, None]).astype(f32)
    columns = jnp.concatenate([same, 1.0 - same[:, :, 2:3]], axis=2)
    mask = columns.reshape(sequences, groups, steps, 4).transpose(2, 1, 0, 3).reshape(rows, 4)

    halves = entry_weight.reshape(slice_rows, 2, pieces, groups, own).transpose(1, 3, 0, 2, 4)

    def columns_of(half):
        block = halves[half].reshape(1, groups, slice_rows, group_width)
        copies = jnp.broadcast_to(block, (pieces,) + block.shape[1:])
        copies = copies.reshape(pieces * groups, slice_rows, group_width)
        parts = lax.all_to_all(copies, both, split_axis=0, concat_axis=0, tiled=True)
        return parts.reshape(width, group_width)

    inner_weight = columns_of(0)
    gate_weight = columns_of(1)
    exit_rows = spread(exit_weight, "blk").reshape(group_width, width)

    normed, inner, filtered, chosen = kernel_call(
        entry_kernel,
        [
            ((rows, width), bf16),
            ((rows + 3 * chunks, group_width), bf16),
            ((rows, group_width), f32),
            ((96, rows), bf16),
        ],
        [],
        40,
        place, tokens_all, rim, gain_all, mask, inner_weight, small,
    )
    chosen_all = lax.all_gather(chosen, "grp")
    cotangent_rows, gate_value, gate_slope, grad_scan = kernel_call(
        gate_kernel,
        [
            ((rows, width), bf16),
            ((rows, group_width), f32),
            ((rows, group_width), f32),
            ((rows, group_width), f32),
        ],
        [],
        40,
        place, cotangent_all, normed, gate_weight, exit_rows,
    )
    cube = (steps, chunks, group_width)
    bank = (states, chunks, group_width)
    gates, step_sizes, step_slopes, ends, keeps, gives, sums, ahead_state, back_state = kernel_call(
        piece_kernel,
        [
            ((steps, chunks, 128), f32),
            (cube, f32),
            (cube, f32),
            (bank, f32),
            (bank, f32),
            (bank, f32),
            ((chunks, group_width), f32),
            ((states * sequences, group_width), f32),
            ((states * sequences, group_width), f32),
        ],
        [
            pltpu.VMEM((states, 8, group_width), f32),
            pltpu.VMEM((steps, states, 8, 128), f32),
            pltpu.VMEM((steps, states, 8, 128), f32),
        ],
        48,
        chosen_all, mask, small, filtered.reshape(cube), grad_scan.reshape(cube),
    )
    piece_sum = jnp.sum(sums.reshape(groups, sequences, group_width), axis=0)
    first = lax.reduce_precision(piece_sum, 8, 7)
    second = lax.reduce_precision(piece_sum - first, 8, 7)
    third = piece_sum - first - second
    extra = jnp.concatenate([first, second, third, jnp.zeros_like(first)], axis=0)
    forward_load = jnp.concatenate([ahead_state, extra], axis=0).astype(bf16)
    back_load = jnp.concatenate([back_state, extra], axis=0).astype(bf16)
    later = (jnp.arange(pieces) > piece)[:, None, None]
    loads = jnp.where(later, forward_load[None], back_load[None])
    came = lax.all_to_all(loads, "blk", split_axis=0, concat_axis=0, tiled=True)
    at = states * sequences
    came_sums = came[:, at : at + 3 * sequences].astype(f32)
    came_sums = came_sums.reshape(pieces, 3, sequences, group_width).sum(axis=1)

    scan_out, grad_delta, grad_direct, rank_grad, chosen_grad, decay_grad, skip_grad, bias_grad = kernel_call(
        scan_kernel,
        [
            (cube, f32),
            (cube, f32),
            (cube, f32),
            ((rank, group_width), f32),
            ((96, rows), bf16),
            ((states, group_width), f32),
            ((1, group_width), f32),
            ((1, group_width), f32),
        ],
        [
            pltpu.VMEM((states + 1, 8, group_width), f32),
            pltpu.VMEM((steps, states, 8, 128), f32),
            pltpu.VMEM((steps, states, 8, 128), f32),
            pltpu.VMEM((steps, states, 8, 128), f32),
            pltpu.VMEM((steps * 8, 2 * states * 128), bf16),
            pltpu.VMEM((2 * states * 128, 128), bf16),
            pltpu.VMEM(bank, f32),
            pltpu.VMEM(bank, f32),
            pltpu.VMEM((steps, chunks, 128), f32),
        ],
        56,
        place, came, came_sums, gates, small, step_sizes, step_slopes, filtered.reshape(cube),
        grad_scan.reshape(cube), ends, keeps, gives,
    )
    chosen_grads = lax.all_gather(chosen_grad, "grp")
    shape4 = (groups, sequences, steps, width)
    grad_gating, out_parts, exit_grad, gate_entry_grad = kernel_call(
        leave_kernel,
        [
            ((rows, group_width), bf16),
            (shape4, bf16),
            ((group_width, width), bf16),
            ((width, group_width), bf16),
        ],
        [pltpu.VMEM((rows, group_width), bf16)],
        48,
        scan_out.reshape(rows, group_width), gate_value, gate_slope, cotangent_rows, normed, exit_rows,
    )
    grad_sums, spill, select_grad, taps_grad, offset_grad = kernel_call(
        filter_kernel,
        [
            ((rows, group_width), f32),
            ((3 * chunks, group_width), f32),
            ((96, group_width), f32),
            ((4, group_width), f32),
            ((1, group_width), f32),
        ],
        [pltpu.VMEM((rows, 96), bf16)],
        48,
        chosen_grads, grad_direct.reshape(rows, group_width), inner, filtered, mask, small,
    )
    spill = spill.reshape(3, groups, sequences, group_width)
    spill_after = lax.ppermute(spill[:, 0], "blk", behind)
    spill = jnp.concatenate([spill[:, 1:], spill_after[:, None]], axis=1).reshape(3 * chunks, group_width)
    grad_parts, inner_entry_grad, gain_sum = kernel_call(
        inner_kernel,
        [
            (shape4, bf16),
            ((width, group_width), bf16),
            ((1, width), f32),
        ],
        [
            pltpu.VMEM((rows, group_width), bf16),
            pltpu.VMEM((3, rows + 3 * chunks, group_width), f32),
        ],
        48,
        grad_sums, spill, mask, small, normed, grad_gating, inner_weight, gate_weight,
    )

    def gathered_sum(parts):
        came = lax.all_to_all(parts, "grp", split_axis=0, concat_axis=0, tiled=True)
        return jnp.sum(came.astype(f32), axis=0)

    residual = tokens.astype(f32)
    block_out = (residual + gathered_sum(out_parts)).astype(bf16)

    exit_parts = lax.all_to_all(
        exit_grad.reshape(pieces, own, width), "blk", split_axis=0, concat_axis=0, tiled=True
    )
    exit_out = jnp.sum(exit_parts.astype(f32), axis=0)

    def entry_half(grads):
        parts = grads.reshape(pieces * groups, slice_rows, group_width)
        came = lax.all_to_all(parts, both, split_axis=0, concat_axis=0, tiled=True)
        came = came.reshape(pieces, groups, slice_rows, pieces, own)
        summed = jnp.sum(came.astype(f32), axis=0)
        return summed.transpose(1, 2, 0, 3).reshape(slice_rows, inner_width)

    entry_out = jnp.concatenate([entry_half(inner_entry_grad), entry_half(gate_entry_grad)], axis=1)

    small_grads = jnp.concatenate(
        [rank_grad, select_grad, decay_grad, taps_grad, offset_grad, bias_grad, skip_grad], axis=0
    )
    count = small_grads.shape[0]
    split = small_grads.reshape(count, pieces, own).transpose(1, 0, 2).reshape(pieces, count * own)
    gain_split = gain_sum.reshape(pieces, groups * slice_rows)
    sent = jnp.concatenate([split, gain_split], axis=1)
    came_small = jnp.sum(
        lax.all_to_all(sent, "blk", split_axis=0, concat_axis=0, tiled=True), axis=0
    )
    gain_sums = jnp.sum(lax.all_gather(came_small[count * own :], "grp"), axis=0)
    gain_out = lax.dynamic_slice_in_dim(gain_sums, group * slice_rows, slice_rows)
    gain_out = gain_out / norm_gain.astype(f32)
    mine = came_small[: count * own].reshape(count, own)

    grad_hat = gathered_sum(grad_parts) * gain_all[0]
    root = lax.rsqrt(jnp.mean(residual * residual, axis=2, keepdims=True) + epsilon)
    hat_own = residual * root
    grad_input = root * (grad_hat - hat_own * jnp.mean(grad_hat * hat_own, axis=2, keepdims=True))
    input_grad = (cotangent.astype(f32) + grad_input).astype(bf16)
    return (
        block_out,
        input_grad,
        gain_out,
        entry_out,
        mine[176:180],
        mine[180],
        mine[64:160].T,
        mine[0:64],
        mine[181],
        mine[160:176],
        mine[182],
        exit_out,
    )


def solution(mesh):
    placed = (
        P(None, both, None),
        P(None, "blk"),
        P(None, both, None),
        P(both),
        P(both, None),
        P(None, both),
        P(both),
        P(both, None),
        P(None, both),
        P(both),
        P(None, both),
        P(both),
        P(both, None),
    )
    return jax.shard_map(
        local,
        mesh=mesh,
        in_specs=placed,
        out_specs=(
            P(None, both, None),
            P(None, both, None),
            P(both),
            P(both, None),
            P(None, both),
            P(both),
            P(both, None),
            P(None, both),
            P(both),
            P(None, both),
            P(both),
            P(both, None),
        ),
        check_vma=False,
    )
```

```python
import jax
import jax.numpy as jnp
from jax import lax
from jax.experimental import pallas as pl
from jax.experimental.pallas import tpu as pltpu
from jax.sharding import PartitionSpec as P

epsilon = 1e-05
log2_e = 1.4426950408889634
log_2 = 0.6931471805599453
reset_push = 1e6
f32 = jnp.float32
bf16 = jnp.bfloat16
small_rows = 192
both = ("blk", "grp")


def dot(left, right, dims=((1,), (0,))):
    return lax.dot_general(left, right, (dims, ((), ())), preferred_element_type=f32)


def sigmoid(values):
    return 1.0 / (1.0 + jnp.exp(-values))


def spread(block, axis):
    count = lax.axis_size(axis)
    copies = jnp.broadcast_to(block[None], (count,) + block.shape)
    return lax.all_to_all(copies, axis, split_axis=0, concat_axis=0, tiled=True)


def ordering(groups, sequences, me):
    chunks = groups * sequences
    rows = chunks * 8
    out_row = lax.broadcasted_iota(jnp.int32, (rows, rows), 0)
    in_row = lax.broadcasted_iota(jnp.int32, (rows, rows), 1)
    chunk = out_row % chunks
    wanted = (((chunk // sequences) ^ me) * sequences + chunk % sequences) * 8 + out_row // chunks
    return jnp.where(in_row == wanted, 1.0, 0.0).astype(bf16)


def kernel_call(body, micros, outs, scratch, limit, *operands):
    places = [
        pl.BlockSpec(memory_space=pltpu.SMEM)
        if value.dtype == jnp.int32
        else pl.BlockSpec(memory_space=pltpu.VMEM)
        for value in operands
    ]
    flops = micros * 1_150_000_000
    return pl.pallas_call(
        body,
        out_shape=[jax.ShapeDtypeStruct(shape, kind) for shape, kind in outs],
        in_specs=places,
        out_specs=[pl.BlockSpec(memory_space=pltpu.VMEM) for _ in outs],
        scratch_shapes=scratch,
        compiler_params=pltpu.CompilerParams(vmem_limit_bytes=limit << 20),
        cost_estimate=pl.CostEstimate(flops=flops, bytes_accessed=8_000_000, transcendentals=0),
    )(*operands)


def read_rows(slab_refs, block):
    sequences, _, width = slab_refs[0].shape
    at = pl.ds(pl.multiple_of(block * 8, 8), 8)
    parts = [slab[:, at, :].astype(f32) for slab in slab_refs]
    return jnp.concatenate(parts, axis=0).reshape(len(slab_refs) * sequences * 8, width)


def small_row(small_ref, index):
    tail = small_ref[176:192, :].astype(f32)
    return tail[index : index + 1, :]


def assemble(whole_ref, stacks, me):
    for side, stack_ref in enumerate(stacks):
        count = stack_ref.shape[0]
        rows = whole_ref.shape[0] // (2 * count)
        for k in range(count):
            target = pl.ds(pl.multiple_of((me ^ (2 * k + side)) * rows, 8), rows)
            whole_ref[target, :] = stack_ref[k, 0:rows, :]


def entry_kernel(
    place_ref, slab0_ref, slab1_ref, slab2_ref, slab3_ref, rim_ref, gain_ref, mask_ref, near_ref, far_ref, small_ref,
    normed_ref, inner_ref, filter_ref, chosen_ref, weight_ref,
):
    slabs = (slab0_ref, slab1_ref, slab2_ref, slab3_ref)
    groups = len(slabs)
    sequences, steps, width = slab0_ref.shape
    chunks = groups * sequences
    block_rows = chunks * 8
    inner_width = inner_ref.shape[1]
    order = ordering(groups, sequences, place_ref[1])
    assemble(weight_ref, (near_ref, far_ref), place_ref[0])

    def scaled(rows):
        root = lax.rsqrt(jnp.mean(rows * rows, axis=1, keepdims=True) + epsilon)
        return (rows * root * gain_ref[...]).astype(bf16)

    last = dot(order, scaled(read_rows(slabs, steps // 8 - 1))).astype(bf16)
    last = dot(last[block_rows - 3 * chunks :, :], weight_ref[...]).reshape(3, chunks, inner_width)
    rim = dot(scaled(rim_ref[...].astype(f32)), weight_ref[...]).reshape(3, sequences, inner_width)
    rim = jnp.concatenate([rim, last[:, : chunks - sequences, :]], axis=1)
    inner_ref[0 : 3 * chunks, :] = rim.reshape(3 * chunks, inner_width).astype(bf16)
    taps = [small_row(small_ref, k) for k in range(4)]
    offset = small_row(small_ref, 4)

    def lap(block, carry):
        base = pl.multiple_of(block * block_rows, block_rows)
        normed = dot(order, scaled(read_rows(slabs, block))).astype(bf16)
        normed_ref[pl.ds(base, block_rows), :] = normed
        inner = dot(normed, weight_ref[...]).astype(bf16)
        inner_ref[pl.ds(pl.multiple_of(base + 3 * chunks, 16), block_rows), :] = inner
        total = offset
        for k in range(3):
            same = mask_ref[pl.ds(base, block_rows), k : k + 1]
            part = inner_ref[pl.ds(pl.multiple_of(base + k * chunks, 16), block_rows), :]
            total = total + taps[k] * part.astype(f32) * same
        total = total + taps[3] * inner.astype(f32)
        filtered = (total * sigmoid(total)).astype(bf16)
        filter_ref[pl.ds(base, block_rows), :] = filtered.astype(f32)
        chosen = dot(small_ref[64:160, :], filtered, ((1,), (1,)))
        chosen_ref[:, pl.ds(base, block_rows)] = chosen.astype(bf16)
        return carry

    lax.fori_loop(0, steps // 8, lap, 0)


def gate_kernel(
    place_ref, slab0_ref, slab1_ref, slab2_ref, slab3_ref, normed_ref, near_ref, far_ref, exit_near_ref, exit_far_ref,
    rows_ref, value_ref, slope_ref, grad_ref, weight_ref, exit_ref,
):
    slabs = (slab0_ref, slab1_ref, slab2_ref, slab3_ref)
    sequences, steps, width = slab0_ref.shape
    block_rows = len(slabs) * sequences * 8
    order = ordering(len(slabs), sequences, place_ref[1])
    assemble(weight_ref, (near_ref, far_ref), place_ref[0])
    assemble(exit_ref, (exit_near_ref, exit_far_ref), place_ref[0])

    def lap(block, carry):
        at = pl.ds(pl.multiple_of(block * block_rows, block_rows), block_rows)
        ordered = dot(order, read_rows(slabs, block).astype(bf16)).astype(bf16)
        rows_ref[at, :] = ordered
        gating = dot(normed_ref[at, :], weight_ref[...])
        grad_gated = dot(ordered, exit_ref[...], ((1,), (1,)))
        gate = sigmoid(gating)
        value = gating * gate
        value_ref[at, :] = value
        slope_ref[at, :] = grad_gated * (gate * (1.0 + gating * (1.0 - gate)))
        grad_ref[at, :] = (grad_gated * value).astype(bf16).astype(f32)
        return carry

    lax.fori_loop(0, steps // 8, lap, 0)


def fill_rates(small_ref, rates_ref):
    states = rates_ref.shape[0]
    rates = -jnp.exp(small_ref[160 : 160 + states, :].astype(f32)) * log2_e
    for n in range(states):
        rates_ref[n] = jnp.broadcast_to(rates[n : n + 1, :], rates_ref.shape[1:])


def fill_picks(pick_ref):
    depth, width = pick_ref.shape
    source = lax.broadcasted_iota(jnp.int32, (depth, width), 0) % (depth // 2)
    target = lax.broadcasted_iota(jnp.int32, (depth, width), 1) // 128
    pick_ref[...] = jnp.where(source == target, 1.0, 0.0).astype(bf16)


def fill_gates(gates_ref, pick_ref, spread_ref, half):
    steps = gates_ref.shape[0]
    values = gates_ref[:, pl.ds(pl.multiple_of(half * 8, 8), 8), :].reshape(steps * 8, 128)[:, 64:96]
    high = values.astype(bf16)
    rest = (values - high.astype(f32)).astype(bf16)
    pair = jnp.concatenate([high, rest], axis=1)
    span = 2048

    def lap(k, carry):
        columns = pl.ds(pl.multiple_of(k * span, span), span)
        spread_ref[:, columns] = dot(pair, pick_ref[:, columns])
        return carry

    lax.fori_loop(0, spread_ref.shape[1] // span, lap, 0)


def gate_of(spread_ref, t, n):
    return spread_ref[pl.ds(pl.multiple_of(t * 8, 8), 8), n * 128 : (n + 1) * 128]


def lane_slices(width):
    return [slice(k * 128, (k + 1) * 128) for k in range(width // 128)]


def piece_kernel(
    place_ref, chosen_ref, other_ref, mask_ref, small_ref, filter_ref, grad_ref,
    gates_ref, step_ref, slope_ref, end_ref, keep_ref, give_ref, load_ref,
    rates_ref, spread_ref, pick_ref, sum_ref, ahead_ref, back_ref,
):
    me = place_ref[0]
    steps, chunks, width = step_ref.shape
    states = end_ref.shape[0]
    chosen = chosen_ref[...].astype(f32) + other_ref[...].astype(f32)
    padded = jnp.concatenate([chosen, jnp.zeros((32, chosen.shape[1]), f32)], axis=0)
    gates_ref[...] = padded.T.reshape(steps, chunks, 128)
    fill_rates(small_ref, rates_ref)
    fill_picks(pick_ref)
    bias = small_row(small_ref, 5)
    delta = small_ref[0:64, :]

    def delta_lap(block, carry):
        at = pl.ds(pl.multiple_of(block * 8, 8), 8)
        low = gates_ref[at, :, :].reshape(8 * chunks, 128)[:, 0:64]
        high = low.astype(bf16)
        rest = (low - high.astype(f32)).astype(bf16)
        pre = dot(high, delta) + dot(rest, delta) + bias
        grown = jnp.exp(-jnp.abs(pre))
        step = jnp.maximum(pre, 0.0) + jnp.log1p(grown)
        step_ref[at, :, :] = step.reshape(8, chunks, width)
        slope_ref[at, :, :] = (jnp.where(pre >= 0, 1.0, grown) / (1.0 + grown)).reshape(8, chunks, width)
        return carry

    lax.fori_loop(0, steps // 8, delta_lap, 0)

    push = mask_ref[:, 3:4] * reset_push
    gates_ref[:, :, 96:97] = push.reshape(steps, chunks, 1)
    end_ref[...] = jnp.zeros_like(end_ref)
    give_ref[...] = jnp.zeros_like(give_ref)
    keep_ref[...] = jnp.ones_like(keep_ref)
    span = 4
    lanes = lane_slices(width)
    spots = [(j, i) for j in range(span) for i in range(len(lanes))]

    def half_lap(half, carry):
        fill_gates(gates_ref, pick_ref, spread_ref, half)
        at = pl.ds(pl.multiple_of(half * 8, 8), 8)

        def lap(block, totals):
            totals = list(totals)
            pushed, drives, grads = {}, {}, {}
            for j, i in spots:
                t = block * span + j
                step = step_ref[t, at, lanes[i]]
                push = step + gates_ref[t, at, 96:97]
                totals[i] = totals[i] + push
                pushed[j, i] = push
                drives[j, i] = step * filter_ref[t, at, lanes[i]]
                grads[j, i] = grad_ref[t, at, lanes[i]]
            for n in range(states):
                rate = [rates_ref[n, :, one] for one in lanes]
                end = [end_ref[n, at, one] for one in lanes]
                keep = [keep_ref[n, at, one] for one in lanes]
                give = [give_ref[n, at, one] for one in lanes]
                for j in range(span):
                    write = gate_of(spread_ref, block * span + j, n)
                    read = gate_of(spread_ref, block * span + j, states + n)
                    for i in range(len(lanes)):
                        decay = jnp.exp2(pushed[j, i] * rate[i])
                        end[i] = decay * end[i] + drives[j, i] * write
                        keep[i] = keep[i] * decay
                        give[i] = give[i] + keep[i] * (read * grads[j, i])
                for i, one in enumerate(lanes):
                    end_ref[n, at, one] = end[i]
                    keep_ref[n, at, one] = keep[i]
                    give_ref[n, at, one] = give[i]
            return tuple(totals)

        start = tuple(jnp.zeros((8, 128), f32) for _ in lanes)
        totals = lax.fori_loop(0, steps // span, lap, start)
        for i, one in enumerate(lanes):
            sum_ref[at, one] = totals[i]
        return carry

    lax.fori_loop(0, chunks // 8, half_lap, 0)

    sequences = ahead_ref.shape[0] // (states + 4)
    groups = chunks // sequences
    for n in range(states):
        rows = slice(n * sequences, (n + 1) * sequences)
        ahead = jnp.zeros((sequences, width), f32)
        back = jnp.zeros((sequences, width), f32)
        for k in range(groups):
            part = slice(k * sequences, (k + 1) * sequences)
            ahead = keep_ref[n, part, :] * ahead + end_ref[n, part, :]
            other = slice((groups - 1 - k) * sequences, (groups - k) * sequences)
            back = give_ref[n, other, :] + keep_ref[n, other, :] * back
        ahead_ref[rows, :] = ahead
        back_ref[rows, :] = back
    total = jnp.zeros((sequences, width), f32)
    for k in range(groups):
        total = total + sum_ref[k * sequences : (k + 1) * sequences, :]
    held = states * sequences
    for k in range(3):
        term = total.astype(bf16).astype(f32)
        ahead_ref[held + k * sequences : held + (k + 1) * sequences, :] = term
        total = total - term
    ahead_ref[held + 3 * sequences :, :] = jnp.zeros((sequences, width), f32)
    back_ref[held:, :] = ahead_ref[held:, :]

    def load_lap(piece, carry):
        load = jnp.where(piece > me, ahead_ref[...], back_ref[...])
        load_ref[piece] = load.astype(bf16)
        return carry

    lax.fori_loop(0, load_ref.shape[0], load_lap, 0)


def fill_unpicks(unpick_ref, first):
    spot = lax.broadcasted_iota(jnp.int32, unpick_ref.shape, 0) // 128
    column = lax.broadcasted_iota(jnp.int32, unpick_ref.shape, 1)
    unpick_ref[...] = jnp.where(column == spot + first, 1.0, 0.0).astype(bf16)


def forward_kernel(
    place_ref, came_ref, gates_ref, small_ref, step_ref, filter_ref, grad_ref, end_ref, keep_ref, give_ref,
    out_ref, read_sum_ref, enter_ref, arrive_ref,
    rates_ref, spread_ref, pick_ref, product_ref, unpick_ref, passed_ref, whole_ref,
):
    me = place_ref[0]
    steps, chunks, width = step_ref.shape
    states = end_ref.shape[0]
    pieces = came_ref.shape[0]
    sequences = came_ref.shape[1] // (states + 4)
    groups = chunks // sequences
    fill_rates(small_ref, rates_ref)
    fill_picks(pick_ref)
    fill_unpicks(unpick_ref, 64 + states)

    held = states * sequences
    rates = [jnp.broadcast_to(rates_ref[n, 0:1, :], (sequences, width)) for n in range(states)]
    rates = jnp.concatenate(rates, axis=0)

    def step_in(piece, state):
        values = came_ref[piece].astype(f32)
        total = values[held : held + sequences, :]
        for k in range(1, 3):
            total = total + values[held + k * sequences : held + (k + 1) * sequences, :]
        total = jnp.concatenate([total] * states, axis=0)
        return jnp.exp2(total * rates) * state + values[:held, :]

    def step_back(k, state):
        return step_in(pieces - 1 - k, state)

    zero = jnp.zeros((held, width), f32)
    whole_ref[0] = lax.fori_loop(0, me, step_in, zero)
    whole_ref[1] = lax.fori_loop(0, pieces - 1 - me, step_back, zero)
    for n in range(states):
        ahead = whole_ref[0, n * sequences : (n + 1) * sequences, :]
        back = whole_ref[1, n * sequences : (n + 1) * sequences, :]
        for k in range(groups):
            part = slice(k * sequences, (k + 1) * sequences)
            enter_ref[n, part, :] = ahead
            ahead = keep_ref[n, part, :] * ahead + end_ref[n, part, :]
            other = slice((groups - 1 - k) * sequences, (groups - k) * sequences)
            arrive_ref[n, other, :] = back
            back = give_ref[n, other, :] + keep_ref[n, other, :] * back

    rates_ref[states] = jnp.broadcast_to(small_row(small_ref, 6), (8, width))
    span = 4
    lanes = lane_slices(width)
    spots = [(j, i) for j in range(span) for i in range(len(lanes))]

    def half_lap(half, carry):
        fill_gates(gates_ref, pick_ref, spread_ref, half)
        at = pl.ds(pl.multiple_of(half * 8, 8), 8)
        for n in range(states):
            for i, one in enumerate(lanes):
                passed_ref[n, i] = enter_ref[n, at, one]

        def forward(block, inner_carry):
            pushed, drives, grads, outs = {}, {}, {}, {}
            for j, i in spots:
                t = block * span + j
                step = step_ref[t, at, lanes[i]]
                feed = filter_ref[t, at, lanes[i]]
                pushed[j, i] = step + gates_ref[t, at, 96:97]
                drives[j, i] = step * feed
                grads[j, i] = grad_ref[t, at, lanes[i]]
                outs[j, i] = feed * rates_ref[states, :, lanes[i]]
            rows = pl.ds(pl.multiple_of(block * span * 8, span * 8), span * 8)
            for n in range(states):
                rate = [rates_ref[n, :, one] for one in lanes]
                hidden = [passed_ref[n, i] for i in range(len(lanes))]
                seen = []
                for j in range(span):
                    t = block * span + j
                    write = gate_of(spread_ref, t, n)
                    read = gate_of(spread_ref, t, states + n)
                    total = None
                    for i in range(len(lanes)):
                        hidden[i] = jnp.exp2(pushed[j, i] * rate[i]) * hidden[i] + drives[j, i] * write
                        outs[j, i] = outs[j, i] + hidden[i] * read
                        one = grads[j, i] * hidden[i]
                        total = one if total is None else total + one
                    seen.append(total)
                product_ref[rows, n * 128 : (n + 1) * 128] = jnp.concatenate(seen, axis=0).astype(bf16)
                for i in range(len(lanes)):
                    passed_ref[n, i] = hidden[i]
            for j, i in spots:
                out_ref[block * span + j, at, lanes[i]] = outs[j, i]
            return inner_carry

        lax.fori_loop(0, steps // span, forward, 0)
        summed = dot(product_ref[...], unpick_ref[...])
        read_sum_ref[:, at, :] = summed.reshape(steps, 8, 128)
        return carry

    lax.fori_loop(0, chunks // 8, half_lap, 0)


def backward_kernel(
    gates_ref, small_ref, step_ref, slope_ref, filter_ref, grad_ref, read_sum_ref, enter_ref, arrive_ref,
    direct_ref, rank_ref, chosen_ref, decay_ref, skip_ref, bias_ref,
    rates_ref, spread_ref, pick_ref, state_ref, product_ref, unpick_ref, delta_ref, sums_acc_ref,
    passed_ref, total_ref,
):
    steps, chunks, width = step_ref.shape
    states = enter_ref.shape[0]
    fill_rates(small_ref, rates_ref)
    fill_picks(pick_ref)
    fill_unpicks(unpick_ref, 64)
    decay_ref[...] = jnp.zeros_like(decay_ref)
    skip_ref[...] = jnp.zeros_like(skip_ref)
    rates_ref[states] = jnp.broadcast_to(small_row(small_ref, 6), (8, width))
    span = 4
    lanes = lane_slices(width)
    spots = [(j, i) for j in range(span) for i in range(len(lanes))]
    blocks = steps // span

    def half_lap(half, carry):
        fill_gates(gates_ref, pick_ref, spread_ref, half)
        at = pl.ds(pl.multiple_of(half * 8, 8), 8)
        for n in range(states):
            for i, one in enumerate(lanes):
                first = enter_ref[n, at, one]
                state_ref[0, n, i] = first
                passed_ref[n, i] = first

        def forward(block, inner_carry):
            pushed, drives = {}, {}
            for j, i in spots:
                t = block * span + j
                step = step_ref[t, at, lanes[i]]
                pushed[j, i] = step + gates_ref[t, at, 96:97]
                drives[j, i] = step * filter_ref[t, at, lanes[i]]
            for n in range(states):
                rate = [rates_ref[n, :, one] for one in lanes]
                hidden = [passed_ref[n, i] for i in range(len(lanes))]
                for j in range(span):
                    t = block * span + j
                    write = gate_of(spread_ref, t, n)
                    for i in range(len(lanes)):
                        hidden[i] = jnp.exp2(pushed[j, i] * rate[i]) * hidden[i] + drives[j, i] * write
                        state_ref[t + 1, n, i] = hidden[i]
                for i in range(len(lanes)):
                    passed_ref[n, i] = hidden[i]
            return inner_carry

        lax.fori_loop(0, blocks, forward, 0)
        for n in range(states):
            for i, one in enumerate(lanes):
                passed_ref[n, i] = arrive_ref[n, at, one]
                total_ref[n, i] = jnp.zeros((8, 128), f32)

        def backward(k, skips):
            block = blocks - 1 - k
            skips = list(skips)
            raw, feeds, pushed, drives, grads, weighted, slopes = {}, {}, {}, {}, {}, {}, {}
            for j, i in spots:
                t = block * span + j
                step = step_ref[t, at, lanes[i]]
                feed = filter_ref[t, at, lanes[i]]
                grad = grad_ref[t, at, lanes[i]]
                raw[j, i] = step
                feeds[j, i] = feed
                pushed[j, i] = step + gates_ref[t, at, 96:97]
                drives[j, i] = step * feed
                grads[j, i] = grad
                weighted[j, i] = jnp.zeros((8, 128), f32)
                slopes[j, i] = jnp.zeros((8, 128), f32)
                skips[i] = skips[i] + grad * feed
            rows = pl.ds(pl.multiple_of(block * span * 8, span * 8), span * 8)
            for n in range(states):
                rate = [rates_ref[n, :, one] for one in lanes]
                gone = [passed_ref[n, i] for i in range(len(lanes))]
                turns = [total_ref[n, i] for i in range(len(lanes))]
                seen = [None] * span
                for j in reversed(range(span)):
                    t = block * span + j
                    write = gate_of(spread_ref, t, n)
                    read = gate_of(spread_ref, t, states + n)
                    for i in range(len(lanes)):
                        adjoint = read * grads[j, i] + gone[i]
                        weighted[j, i] = weighted[j, i] + adjoint * write
                        one = adjoint * drives[j, i]
                        seen[j] = one if seen[j] is None else seen[j] + one
                        gone[i] = adjoint * jnp.exp2(pushed[j, i] * rate[i])
                        turn = gone[i] * state_ref[t, n, i]
                        slopes[j, i] = slopes[j, i] + turn * rate[i]
                        turns[i] = turns[i] + turn * raw[j, i]
                product_ref[rows, n * 128 : (n + 1) * 128] = jnp.concatenate(seen, axis=0).astype(bf16)
                for i in range(len(lanes)):
                    passed_ref[n, i] = gone[i]
                    total_ref[n, i] = turns[i]
            for j, i in spots:
                t = block * span + j
                grown = slopes[j, i] * log_2 + weighted[j, i] * feeds[j, i]
                delta_ref[t, at, lanes[i]] = grown * slope_ref[t, at, lanes[i]]
                direct = weighted[j, i] * raw[j, i] + grads[j, i] * rates_ref[states, :, lanes[i]]
                direct_ref[t, at, lanes[i]] = direct
            return tuple(skips)

        start = tuple(jnp.zeros((8, 128), f32) for _ in lanes)
        skips = lax.fori_loop(0, blocks, backward, start)
        for i, one in enumerate(lanes):
            skip_ref[0:1, one] += jnp.sum(skips[i], axis=0, keepdims=True)
            for n in range(states):
                part = jnp.sum(total_ref[n, i], axis=0, keepdims=True)
                decay_ref[n : n + 1, one] += part * rates_ref[n, 0:1, one] * log_2
        summed = dot(product_ref[...], unpick_ref[...])
        sums_acc_ref[:, at, :] = summed.reshape(steps, 8, 128) + read_sum_ref[:, at, :]
        return carry

    lax.fori_loop(0, chunks // 8, half_lap, 0)

    rows = steps * chunks
    grads = delta_ref[...].reshape(rows, width)
    bias_ref[...] = jnp.sum(grads, axis=0, keepdims=True)
    grads = grads.astype(bf16)
    low = gates_ref[...].reshape(rows, 128)[:, 0:64].astype(bf16)
    rank_ref[...] = dot(low, grads, ((0,), (0,)))
    back = dot(small_ref[0:64, :], grads, ((1,), (1,)))
    sums = sums_acc_ref[...].reshape(rows, 128).T
    chosen_ref[0:64, :] = back.astype(bf16)
    chosen_ref[64:96, :] = sums[64:96, :].astype(bf16)


def store_rows(keep_ref, send_ref, order, values, block):
    _, sequences, _, width = keep_ref.shape
    back = dot(order, values.astype(bf16), ((0,), (0,)))
    shaped = back.reshape(4, sequences, 8, width).astype(bf16)
    at = pl.ds(pl.multiple_of(block * 8, 8), 8)
    for k in range(4):
        target = send_ref if k % 2 else keep_ref
        target[k // 2, :, at, :] = shaped[k]


def store_blocks(keep_ref, send_ref, me, *parts):
    count = keep_ref.shape[0]
    below = 0
    for values_ref in parts:
        rows = values_ref.shape[0] // (2 * count)
        for k in range(2 * count):
            source = pl.ds(pl.multiple_of((me ^ k) * rows, 8), rows)
            target = send_ref if k % 2 else keep_ref
            target[k // 2, below : below + rows, :] = values_ref[source, :].astype(bf16)
        below += rows


def leave_kernel(
    place_ref, scan_ref, value_ref, slope_ref, rows_ref, normed_ref, exit_near_ref, exit_far_ref,
    gating_ref, out_keep_ref, out_send_ref, exit_grad_ref, keep_ref, send_ref,
    gated_ref, entry_grad_ref, exit_ref,
):
    assemble(exit_ref, (exit_near_ref, exit_far_ref), place_ref[0])
    sequences, steps = out_keep_ref.shape[1:3]
    groups = 4
    block_rows = groups * sequences * 8
    order = ordering(groups, sequences, place_ref[1])

    def lap(block, carry):
        at = pl.ds(pl.multiple_of(block * block_rows, block_rows), block_rows)
        scan_out = scan_ref[at, :].astype(bf16).astype(f32)
        gated = (scan_out * value_ref[at, :]).astype(bf16)
        gated_ref[at, :] = gated
        gating_ref[at, :] = (scan_out * slope_ref[at, :]).astype(bf16)
        store_rows(out_keep_ref, out_send_ref, order, dot(gated, exit_ref[...]), block)
        return carry

    lax.fori_loop(0, steps // 8, lap, 0)
    exit_grad_ref[...] = dot(gated_ref[...], rows_ref[...], ((0,), (0,))).astype(bf16)
    entry_grad_ref[...] = dot(normed_ref[...], gating_ref[...], ((0,), (0,)))
    store_blocks(keep_ref, send_ref, place_ref[0], entry_grad_ref)


def filter_kernel(
    place_ref, chosen_ref, other_ref, direct_ref, inner_ref, filter_ref, mask_ref, small_ref,
    rank_ref, decay_ref, bias_ref, skip_ref,
    grads_ref, spill_ref, first_ref, *refs,
):
    block_refs, (packed_ref, picked_ref, taps_ref, offset_ref) = refs[:-4], refs[-4:]
    rows, width = grads_ref.shape
    chunks = spill_ref.shape[1]
    block_rows = chunks * 8
    chosen = (chosen_ref[...].astype(f32) + other_ref[...].astype(f32)).astype(bf16)
    packed_ref[0:64, :] = rank_ref[...]
    packed_ref[64:160, :] = dot(chosen, filter_ref[...].astype(bf16))
    packed_ref[160:176, :] = decay_ref[...]
    picked_ref[...] = chosen.astype(f32).T.astype(bf16)
    taps = [small_row(small_ref, k) for k in range(4)]
    offset = small_row(small_ref, 4)
    offset_ref[...] = jnp.zeros_like(offset_ref)
    taps_ref[...] = jnp.zeros_like(taps_ref)

    def lap(block, carry):
        base = pl.multiple_of(block * block_rows, block_rows)
        at = pl.ds(base, block_rows)
        total = offset
        shifted = []
        for k in range(4):
            part = inner_ref[pl.ds(pl.multiple_of(base + k * chunks, 16), block_rows), :].astype(f32)
            if k < 3:
                part = part * mask_ref[at, k : k + 1]
            shifted.append(part)
            total = total + taps[k] * part
        gate = sigmoid(total)
        grad = direct_ref[at, :] + dot(picked_ref[at, :], small_ref[64:160, :])
        grad = grad * (gate * (1.0 + total * (1.0 - gate)))
        grads_ref[at, :] = grad
        offset_ref[...] += jnp.sum(grad, axis=0, keepdims=True)
        for k in range(4):
            taps_ref[k : k + 1, :] += jnp.sum(grad * shifted[k], axis=0, keepdims=True)
        return carry

    lax.fori_loop(0, rows // block_rows, lap, 0)
    packed_ref[176:180, :] = taps_ref[...]
    packed_ref[180:181, :] = offset_ref[...]
    packed_ref[181:182, :] = bias_ref[...]
    packed_ref[182:183, :] = skip_ref[...]
    packed_ref[183:192, :] = jnp.zeros((9, width), f32)
    if len(block_refs) == 1:
        block_refs[0][...] = packed_ref[...]
    else:
        for k, block_ref in enumerate(block_refs):
            lanes = pl.ds(pl.multiple_of(((place_ref[0] >> 1) ^ k) * 128, 128), 128)
            block_ref[...] = packed_ref[:, lanes]
    for u in range(3):
        total = jnp.zeros((chunks, width), f32)
        for t in range(u + 1):
            part = slice(t * chunks, (t + 1) * chunks)
            total = total + grads_ref[part, :] * taps[u - t] * mask_ref[part, u - t : u - t + 1]
        spill_ref[u] = total
        first_ref[u] = total[0 : first_ref.shape[1], :]


def inner_kernel(
    grads_ref, spill_ref, after_ref, mask_ref, small_ref, normed_ref,
    inner_ref, entry_grad_ref,
    past_ref,
):
    rows, inner_width = grads_ref.shape
    chunks, sequences = spill_ref.shape[1], after_ref.shape[1]
    block_rows = chunks * 8
    blocks = rows // block_rows
    later_spill = jnp.concatenate([spill_ref[:, sequences:, :], after_ref[...]], axis=1)
    later_spill = later_spill.reshape(3 * chunks, inner_width)
    taps = [small_row(small_ref, k) for k in range(4)]
    rim_rows = 3 * chunks
    for k in range(3):
        past_ref[k, rows : rows + rim_rows, :] = jnp.zeros((rim_rows, inner_width), f32)

    def mask_lap(block, carry):
        at = pl.ds(pl.multiple_of(block * block_rows, block_rows), block_rows)
        grad = grads_ref[at, :]
        for k in range(3):
            past_ref[k, at, :] = grad * taps[k] * mask_ref[at, k : k + 1]
        return carry

    lax.fori_loop(0, blocks, mask_lap, 0)

    def lap(block, carry):
        base = pl.multiple_of(block * block_rows, block_rows)
        at = pl.ds(base, block_rows)
        total = grads_ref[at, :] * taps[3]
        for k in range(3):
            later = pl.ds(pl.multiple_of(base + (3 - k) * chunks, 16), block_rows)
            total = total + past_ref[k, later, :]
        inner_ref[at, :] = total.astype(bf16)

        @pl.when(block == blocks - 1)
        def _():
            tail = total[block_rows - rim_rows :, :] + later_spill
            inner_ref[rows - rim_rows : rows, :] = tail.astype(bf16)

        return carry

    lax.fori_loop(0, blocks, lap, 0)
    entry_grad_ref[...] = dot(normed_ref[...], inner_ref[...], ((0,), (0,))).astype(bf16)


def normed_kernel(
    place_ref, inner_ref, gating_ref, near_ref, far_ref, gate_near_ref, gate_far_ref,
    out_keep_ref, out_send_ref,
    weight_ref, gate_weight_ref,
):
    assemble(weight_ref, (near_ref, far_ref), place_ref[0])
    assemble(gate_weight_ref, (gate_near_ref, gate_far_ref), place_ref[0])
    sequences, steps = out_keep_ref.shape[1:3]
    groups = 4
    block_rows = groups * sequences * 8
    order = ordering(groups, sequences, place_ref[1])

    def lap(block, carry):
        at = pl.ds(pl.multiple_of(block * block_rows, block_rows), block_rows)
        grad = dot(inner_ref[at, :], weight_ref[...], ((1,), (1,)))
        grad = grad + dot(gating_ref[at, :], gate_weight_ref[...], ((1,), (1,)))
        store_rows(out_keep_ref, out_send_ref, order, grad, block)
        return carry

    lax.fori_loop(0, steps // 8, lap, 0)


def part_kernel(keep_ref, came_ref, total_ref, *part_refs):
    total_ref[...] = keep_ref[0].astype(f32) + came_ref[0].astype(f32)
    for k, part_ref in enumerate(part_refs):
        part_ref[...] = (keep_ref[k + 1].astype(f32) + came_ref[k + 1].astype(f32)).astype(bf16)


def side_sum_kernel(place_ref, total_ref, *refs):
    part_refs, out_refs = refs[:-4], refs[-4:]
    total = total_ref[...]
    for part_ref in part_refs:
        total = total + part_ref[...].astype(f32)
    rows = out_refs[0].shape[0]
    for k, out_ref in enumerate(out_refs):
        block = total[0:rows, :]
        for j in range(1, len(out_refs)):
            block = jnp.where((place_ref[1] ^ k) == j, total[j * rows : (j + 1) * rows, :], block)
        out_ref[...] = block.astype(bf16)


def small_sum_kernel(own_ref, *refs):
    part_refs, out_ref = refs[:-1], refs[-1]
    total = own_ref[...]
    for part_ref in part_refs:
        total = total + part_ref[...]
    out_ref[...] = total


def interleave_kernel(place_ref, weight_ref, inner_ref, gate0_ref, gate1_ref, gate2_ref, gate3_ref, out_ref, gain_ref):
    gate_refs = (gate0_ref, gate1_ref, gate2_ref, gate3_ref)
    pieces, groups, rows, width = inner_ref.shape
    for k in range(groups):
        inner = inner_ref[0, k].astype(f32)
        for piece in range(1, pieces):
            inner = inner + inner_ref[piece, k].astype(f32)
        gate = gate_refs[0][...].astype(f32)
        for m in range(1, groups):
            gate = jnp.where((place_ref[1] ^ m) == k, gate_refs[m][...].astype(f32), gate)
        for half, values in enumerate((inner, gate)):
            for j in range(width // 64):
                column = half * groups * width + (j * groups + k) * 64
                out_ref[:, column : column + 64] = values[:, j * 64 : (j + 1) * 64]
    total = jnp.sum(out_ref[...] * weight_ref[...].astype(f32), axis=1, keepdims=True)
    gain_ref[...] = jnp.broadcast_to(total, gain_ref.shape)


def local(
    tokens,
    segments,
    cotangent,
    norm_gain,
    entry_weight,
    kernel_weight,
    kernel_offset,
    select_weight,
    delta_weight,
    timestep_bias,
    decay_log,
    skip_gain,
    exit_weight,
):
    sequences, steps, width = tokens.shape
    pieces, groups = lax.axis_size("blk"), lax.axis_size("grp")
    piece, group = lax.axis_index("blk"), lax.axis_index("grp")
    place = jnp.stack([piece, group]).astype(jnp.int32)
    chunks = groups * sequences
    rows = steps * chunks
    slice_rows, entry_width = entry_weight.shape
    own = kernel_offset.shape[0]
    inner_width = entry_width // 2
    group_width = inner_width // groups
    states = decay_log.shape[0]
    rank = delta_weight.shape[0]

    def flipped(value, axis, bits):
        return lax.ppermute(value, axis, [(i, i ^ bits) for i in range(lax.axis_size(axis))])

    def after(value, *others):
        return lax.optimization_barrier((value,) + others)[0]

    def rounds(*values):
        return lax.optimization_barrier(values)

    packed = jnp.concatenate(
        [
            delta_weight,
            select_weight.T,
            decay_log,
            kernel_weight,
            kernel_offset[None],
            timestep_bias[None],
            skip_gain[None],
            jnp.zeros((small_rows - 183, own), bf16),
        ],
        axis=0,
    )
    def side_blocks(block):
        return [block] + [flipped(block, "blk", 2 * k) for k in range(1, pieces // 2)]

    place_of_gain = (piece * groups + group) * slice_rows
    gain_line = lax.dynamic_update_slice_in_dim(jnp.zeros((width,), bf16), norm_gain, place_of_gain, 0)
    gain_line = jnp.pad(gain_line.reshape(1, -1, group_width), ((0, 0), (0, 8 - width // group_width), (0, 0)))
    halves = entry_weight.reshape(slice_rows, 2, pieces, groups, own).transpose(3, 1, 0, 2, 4)
    halves = halves.reshape(groups, 2 * slice_rows, group_width)
    halves = jnp.concatenate([halves, jnp.broadcast_to(gain_line, (groups,) + gain_line.shape[1:])], axis=1)
    exit_block = jnp.concatenate([exit_weight, jnp.pad(packed.reshape(-1), (0, -packed.size % (16 * width))).reshape(-1, width)])
    halves, exit_block, tokens = rounds(halves, exit_block, tokens)
    halves = lax.all_to_all(halves, "grp", split_axis=0, concat_axis=0, tiled=True)
    exit_side = side_blocks(exit_block)
    token_pair = flipped(tokens, "grp", 2)
    halves, token_pair, tokens, *exit_side = rounds(halves, token_pair, tokens, *exit_side)

    gain_rows = jnp.sum(halves[:, 2 * slice_rows :].astype(f32), axis=0).astype(bf16)
    inner_block = halves[:, :slice_rows].reshape(groups * slice_rows, group_width)
    inner_block = jnp.concatenate([inner_block, gain_rows])
    gate_block = halves[:, slice_rows : 2 * slice_rows].reshape(groups * slice_rows, group_width)
    inner_side = side_blocks(inner_block)
    exit_near = jnp.stack(exit_side)
    exit_far = flipped(exit_near, "blk", 1)
    token_slabs = (tokens, flipped(tokens, "grp", 1), token_pair, flipped(token_pair, "grp", 1))
    exit_near, exit_far, gate_block, cotangent, *rest = rounds(
        exit_near, exit_far, gate_block, cotangent, *inner_side, *token_slabs
    )
    inner_side, token_slabs = rest[: pieces // 2], rest[pieces // 2 :]
    small = jnp.stack([exit_near[:, own:], exit_far[:, own:]], axis=1).reshape(pieces, -1)[:, : packed.size]
    bits = pieces.bit_length() - 1
    small = small.reshape((2,) * bits + (small_rows, own))
    for k in range(bits):
        small = jnp.where((piece >> (bits - 1 - k)) & 1, jnp.flip(small, k), small)
    small = small.reshape(pieces, small_rows, own).transpose(1, 0, 2).reshape(small_rows, group_width)

    inner_near = jnp.stack(inner_side)
    ahead = [(i, i + 1) for i in range(pieces - 1)]
    behind = [(i + 1, i) for i in range(pieces - 1)]
    tails = jnp.stack([slab[:, steps - 3 :] for slab in token_slabs])
    tail = lax.dynamic_index_in_dim(tails, group ^ (groups - 1), 0, keepdims=False)
    rim_source = tail.transpose(1, 0, 2).reshape(3 * sequences, width)
    rim = lax.ppermute(rim_source, "blk", ahead)
    inner_far = flipped(inner_near, "blk", 1)
    gate_block, cotangent = rounds(gate_block, cotangent, inner_near, rim_source)[:2]
    gate_side = side_blocks(gate_block)
    cotangent_pair = flipped(cotangent, "grp", 2)
    label_tail = lax.ppermute(segments[:, -3:], "blk", ahead)
    labels = jnp.concatenate([label_tail, segments], axis=1)
    length = segments.shape[1]
    shifted = jnp.stack([labels[:, k : k + length] for k in range(3)], axis=-1)
    same = (shifted == segments[:, :, None]).astype(f32)
    columns = jnp.concatenate([same, 1.0 - same[:, :, 2:3]], axis=2)
    mask = columns.reshape(sequences, groups, steps, 4).transpose(2, 1, 0, 3).reshape(rows, 4)
    inner_near, inner_far, rim, cotangent_pair, cotangent, *gate_side = rounds(
        inner_near, inner_far, rim, cotangent_pair, cotangent, *gate_side
    )
    gain_all = jnp.sum(inner_near[:, -8:].astype(f32), axis=0) + jnp.sum(inner_far[:, -8:].astype(f32), axis=0)
    gain_all = gain_all[: width // group_width].reshape(1, width)

    gate_near = jnp.stack(gate_side)
    gate_far = flipped(gate_near, "blk", 1)
    cotangent_slabs = (
        cotangent,
        flipped(cotangent, "grp", 1),
        cotangent_pair,
        flipped(cotangent_pair, "grp", 1),
    )

    def group_sum(value):
        half = value.astype(f32) + flipped(value, "grp", 1).astype(f32)
        half = half.astype(bf16)
        return half, flipped(half, "grp", 2)

    normed, inner, filtered, chosen = kernel_call(
        entry_kernel,
        9,
        [
            ((rows, width), bf16),
            ((rows + 3 * chunks, group_width), bf16),
            ((rows, group_width), f32),
            ((96, rows), bf16),
        ],
        [pltpu.VMEM((width, group_width), bf16)],
        40,
        place, *token_slabs, rim, gain_all, mask, inner_near, inner_far, small,
    )
    chosen_pair = group_sum(chosen)
    cotangent_rows, gate_value, gate_slope, grad_scan = kernel_call(
        gate_kernel,
        8,
        [
            ((rows, width), bf16),
            ((rows, group_width), f32),
            ((rows, group_width), f32),
            ((rows, group_width), f32),
        ],
        [pltpu.VMEM((width, group_width), bf16), pltpu.VMEM((group_width, width), bf16)],
        40,
        place, *cotangent_slabs, normed, gate_near, gate_far, exit_near, exit_far,
    )
    cube = (steps, chunks, group_width)
    bank = (states, chunks, group_width)
    load_rows = (states + 4) * sequences
    gates, step_sizes, step_slopes, ends, keeps, gives, loads = kernel_call(
        piece_kernel,
        23,
        [
            ((steps, chunks, 128), f32),
            (cube, f32),
            (cube, f32),
            (bank, f32),
            (bank, f32),
            (bank, f32),
            ((pieces, load_rows, group_width), bf16),
        ],
        [
            pltpu.VMEM((states, 8, group_width), f32),
            pltpu.VMEM((steps * 8, 2 * states * 128), f32),
            pltpu.VMEM((4 * states, 2 * states * 128), bf16),
            pltpu.VMEM((chunks, group_width), f32),
            pltpu.VMEM((load_rows, group_width), f32),
            pltpu.VMEM((load_rows, group_width), f32),
        ],
        48,
        place, *chosen_pair, mask, small, filtered.reshape(cube), grad_scan.reshape(cube),
    )
    came = lax.all_to_all(loads, "blk", split_axis=0, concat_axis=0, tiled=True)

    lanes = group_width // 128
    gate_scratch = [
        pltpu.VMEM((states + 1, 8, group_width), f32),
        pltpu.VMEM((steps * 8, 2 * states * 128), f32),
        pltpu.VMEM((4 * states, 2 * states * 128), bf16),
    ]
    product_scratch = [pltpu.VMEM((steps * 8, states * 128), bf16), pltpu.VMEM((states * 128, 128), bf16)]
    scan_out, read_sums, enter, arrive = kernel_call(
        forward_kernel,
        18,
        [(cube, f32), ((steps, chunks, 128), f32), (bank, f32), (bank, f32)],
        gate_scratch
        + product_scratch
        + [pltpu.VMEM((states, lanes, 8, 128), f32), pltpu.VMEM((2, states * sequences, group_width), f32)],
        48,
        place, came, gates, small, step_sizes, filtered.reshape(cube), grad_scan.reshape(cube), ends, keeps, gives,
    )
    half_slabs = ((2, sequences, steps, width), bf16)
    block_height = groups * slice_rows
    entry_half = ((pieces // 2, block_height, group_width), bf16)
    grad_gating, out_keep, out_send, exit_grad, gate_keep, gate_send = kernel_call(
        leave_kernel,
        12,
        [((rows, group_width), bf16), half_slabs, half_slabs, ((group_width, width), bf16), entry_half, entry_half],
        [
            pltpu.VMEM((rows, group_width), bf16),
            pltpu.VMEM((width, group_width), f32),
            pltpu.VMEM((group_width, width), bf16),
        ],
        48,
        place, scan_out.reshape(rows, group_width), gate_value, gate_slope, cotangent_rows, normed, exit_near, exit_far,
    )

    exit_parts = lax.all_to_all(
        exit_grad.reshape(pieces, own, width), "blk", split_axis=0, concat_axis=0, tiled=True
    )
    gate_came = flipped(gate_send, "blk", 1)
    out_came = flipped(out_send, "grp", 1)
    grad_direct, rank_grad, chosen_grad, decay_grad, skip_grad, bias_grad = kernel_call(
        backward_kernel,
        35,
        [
            (cube, f32),
            ((rank, group_width), f32),
            ((96, rows), bf16),
            ((states, group_width), f32),
            ((1, group_width), f32),
            ((1, group_width), f32),
        ],
        gate_scratch
        + [pltpu.VMEM((steps + 1, states, lanes, 8, 128), f32)]
        + product_scratch
        + [
            pltpu.VMEM(cube, f32),
            pltpu.VMEM((steps, chunks, 128), f32),
            pltpu.VMEM((states, lanes, 8, 128), f32),
            pltpu.VMEM((states, lanes, 8, 128), f32),
        ],
        56,
        gates, small, step_sizes, step_slopes, filtered.reshape(cube), after(grad_scan, out_send).reshape(cube),
        read_sums, enter, arrive,
    )
    chosen_grad, exit_parts, gate_came, out_came = rounds(chosen_grad, exit_parts, gate_came, out_came)
    chosen_grads = group_sum(chosen_grad)

    def slab_part(keep, came):
        return (keep[1].astype(f32) + came[1].astype(f32)).astype(bf16)

    gate_total, *gate_side_parts = kernel_call(
        part_kernel,
        2,
        [(entry_half[0][1:], f32)] + [(entry_half[0][1:], bf16)] * (pieces // 2 - 1),
        [],
        16,
        gate_keep, gate_came,
    )
    gate_side_parts = [flipped(part, "blk", 2 * k + 2) for k, part in enumerate(gate_side_parts)]
    out_other = flipped(after(slab_part(out_keep, out_came), chosen_grads[1]), "grp", 2)

    paired = 2 * own == 128
    small_block = (small_rows, 128 if paired else group_width)
    grad_sums, spill, first_spill, *small_grads = kernel_call(
        filter_kernel,
        6,
        [
            ((rows, group_width), f32),
            ((3, chunks, group_width), f32),
            ((3, sequences, group_width), f32),
        ]
        + [(small_block, f32)] * (pieces // 2 if paired else 1),
        [
            pltpu.VMEM((small_rows, group_width), f32),
            pltpu.VMEM((rows, 96), bf16),
            pltpu.VMEM((4, group_width), f32),
            pltpu.VMEM((1, group_width), f32),
        ],
        48,
        place, *chosen_grads, grad_direct.reshape(rows, group_width), inner, filtered, mask, small,
        rank_grad, decay_grad, bias_grad, skip_grad,
    )
    spill_after = lax.ppermute(first_spill, "blk", behind)
    gate_total, grad_sums, *gate_side_parts = rounds(gate_total, grad_sums, *gate_side_parts)
    gate_blocks = kernel_call(
        side_sum_kernel,
        2,
        [((slice_rows, group_width), bf16)] * groups,
        [],
        16,
        place, gate_total, *gate_side_parts,
    )
    gate_blocks = [gate_blocks[0]] + [flipped(gate_blocks[k], "grp", k) for k in range(1, groups)]
    grad_inner, inner_entry = kernel_call(
        inner_kernel,
        6,
        [((rows, group_width), bf16), ((width, group_width), bf16)],
        [pltpu.VMEM((3, rows + 3 * chunks, group_width), f32)],
        48,
        grad_sums, spill, spill_after, mask, small, normed,
    )
    if paired:
        came_small = [small_grads[0]] + [flipped(small_grads[k], "blk", 2 * k) for k in range(1, pieces // 2)]
    else:
        came_small = small_grads
    grad_inner, inner_entry, out_other, *rest = rounds(grad_inner, inner_entry, out_other, *gate_blocks, *came_small)
    gate_blocks, came_small = rest[:groups], rest[groups:]
    inner_parts = lax.all_to_all(
        inner_entry.reshape(pieces * groups, slice_rows, group_width), both, split_axis=0, concat_axis=0, tiled=True
    )
    grad_keep, grad_send = kernel_call(
        normed_kernel,
        10,
        [half_slabs, half_slabs],
        [pltpu.VMEM((width, group_width), bf16), pltpu.VMEM((width, group_width), bf16)],
        48,
        place, grad_inner, grad_gating, inner_near, inner_far, gate_near, gate_far,
    )
    grad_came = flipped(grad_send, "grp", 1)
    grad_other = flipped(slab_part(grad_keep, grad_came), "grp", 2)
    residual = tokens.astype(f32)
    block_out = residual + out_keep[0].astype(f32) + out_came[0].astype(f32) + out_other.astype(f32)
    block_out = block_out.astype(bf16)
    exit_out = jnp.sum(exit_parts.astype(f32), axis=0)
    inner_parts = inner_parts.reshape(pieces, groups, slice_rows, group_width)
    if own == 64:
        entry_out, gain_out = kernel_call(
            interleave_kernel,
            3,
            [((slice_rows, entry_width), f32), ((slice_rows, 128), f32)],
            [],
            16,
            place, entry_weight, inner_parts, *gate_blocks,
        )
        gain_out = gain_out[:, 0]
    else:
        inner_sum = jnp.sum(inner_parts.astype(f32), axis=0)
        gate_parts = jnp.stack(gate_blocks).astype(f32)
        for k in range(2):
            pairs = gate_parts.reshape(2, 2, slice_rows, group_width)
            gate_parts = jnp.where((group >> (1 - k)) & 1, jnp.flip(pairs, k), pairs)
        entry_parts = jnp.stack([inner_sum, gate_parts.reshape(inner_sum.shape)], axis=0)
        entry_parts = entry_parts.reshape(2, groups, slice_rows, pieces, own)
        entry_out = entry_parts.transpose(2, 0, 3, 1, 4).reshape(slice_rows, entry_width)
        gain_out = jnp.sum(entry_out * entry_weight.astype(f32), axis=1)
    gain_out = gain_out / norm_gain.astype(f32)

    if paired:
        small_sum = kernel_call(small_sum_kernel, 1, [(small_block, f32)], [], 16, *came_small)[0]
        small_sum = small_sum + flipped(small_sum, "blk", 1)
        mine = lax.dynamic_slice_in_dim(small_sum, (piece & 1) * own, own, 1)
    else:
        split = came_small[0].reshape(small_rows, pieces, own).transpose(1, 0, 2)
        came_small = lax.all_to_all(split, "blk", split_axis=0, concat_axis=0, tiled=True)
        mine = jnp.sum(came_small, axis=0)

    grad_hat = grad_keep[0].astype(f32) + grad_came[0].astype(f32) + grad_other.astype(f32)
    grad_hat = grad_hat * gain_all[0]
    root = lax.rsqrt(jnp.mean(residual * residual, axis=2, keepdims=True) + epsilon)
    hat_own = residual * root
    grad_input = root * (grad_hat - hat_own * jnp.mean(grad_hat * hat_own, axis=2, keepdims=True))
    input_grad = (cotangent.astype(f32) + grad_input).astype(bf16)
    return (
        block_out,
        input_grad,
        gain_out,
        entry_out,
        mine[176:180],
        mine[180],
        mine[64:160].T,
        mine[0:64],
        mine[181],
        mine[160:176],
        mine[182],
        exit_out,
    )


def solution(mesh):
    placed = (
        P(None, both, None),
        P(None, "blk"),
        P(None, both, None),
        P(both),
        P(both, None),
        P(None, both),
        P(both),
        P(both, None),
        P(None, both),
        P(both),
        P(None, both),
        P(both),
        P(both, None),
    )
    return jax.shard_map(
        local,
        mesh=mesh,
        in_specs=placed,
        out_specs=(
            P(None, both, None),
            P(None, both, None),
            P(both),
            P(both, None),
            P(None, both),
            P(both),
            P(both, None),
            P(None, both),
            P(both),
            P(None, both),
            P(both),
            P(both, None),
        ),
        check_vma=False,
    )
```

```python
import jax
import jax.numpy as jnp
from jax import lax
from jax.experimental import pallas as pl
from jax.experimental.pallas import tpu as pltpu
from jax.sharding import PartitionSpec as P

epsilon = 1e-05
log2_e = 1.4426950408889634
log_2 = 0.6931471805599453
reset_push = 1e6
f32 = jnp.float32
bf16 = jnp.bfloat16
small_rows = 192
both = ("blk", "grp")


def dot(left, right, dims=((1,), (0,))):
    return lax.dot_general(left, right, (dims, ((), ())), preferred_element_type=f32)


def sigmoid(values):
    return 1.0 / (1.0 + jnp.exp(-values))


def spread(block, axis):
    count = lax.axis_size(axis)
    copies = jnp.broadcast_to(block[None], (count,) + block.shape)
    return lax.all_to_all(copies, axis, split_axis=0, concat_axis=0, tiled=True)


def ordering(groups, sequences, me):
    chunks = groups * sequences
    rows = chunks * 8
    out_row = lax.broadcasted_iota(jnp.int32, (rows, rows), 0)
    in_row = lax.broadcasted_iota(jnp.int32, (rows, rows), 1)
    chunk = out_row % chunks
    wanted = (((chunk // sequences) ^ me) * sequences + chunk % sequences) * 8 + out_row // chunks
    return jnp.where(in_row == wanted, 1.0, 0.0).astype(bf16)


def kernel_call(body, micros, outs, scratch, limit, *operands, halves=None, free=False):
    whole = pl.BlockSpec(memory_space=pltpu.VMEM)
    kinds = [(value.shape, value.dtype) for value in operands] + list(outs)

    def place(index):
        shape, kind = kinds[index]
        if kind == jnp.int32:
            return pl.BlockSpec(memory_space=pltpu.SMEM)
        axis = halves[index] if halves else None
        if axis is None and free:
            return pl.BlockSpec(shape, lambda *_: (0,) * len(shape))
        if axis is None:
            return whole
        block = tuple(size // 2 if k == axis else size for k, size in enumerate(shape))
        return pl.BlockSpec(block, lambda half: tuple(half if k == axis else 0 for k in range(len(block))))

    places = [place(k) for k in range(len(kinds))]
    return pl.pallas_call(
        body,
        out_shape=[jax.ShapeDtypeStruct(shape, kind) for shape, kind in outs],
        grid=(2,) if halves else (),
        in_specs=places[: len(operands)],
        out_specs=places[len(operands) :],
        scratch_shapes=scratch,
        compiler_params=pltpu.CompilerParams(vmem_limit_bytes=limit << 20),
        cost_estimate=pl.CostEstimate(
            flops=micros * 1_150_000_000, bytes_accessed=8_000_000, transcendentals=0
        ),
    )(*operands)


def read_rows(slab_refs, block):
    sequences, _, width = slab_refs[0].shape
    at = pl.ds(pl.multiple_of(block * 8, 8), 8)
    parts = [slab[:, at, :].astype(f32) for slab in slab_refs]
    return jnp.concatenate(parts, axis=0).reshape(len(slab_refs) * sequences * 8, width)


def small_row(small_ref, index):
    tail = small_ref[176:192, :].astype(f32)
    return tail[index : index + 1, :]


def assemble(whole_ref, stacks, me):
    for side, stack_ref in enumerate(stacks):
        count = stack_ref.shape[0]
        rows = whole_ref.shape[0] // (2 * count)
        for k in range(count):
            target = pl.ds(pl.multiple_of((me ^ (2 * k + side)) * rows, 8), rows)
            whole_ref[target, :] = stack_ref[k, 0:rows, :]


def entry_kernel(
    place_ref, slab0_ref, slab1_ref, slab2_ref, slab3_ref, rim_ref, gain_ref, mask_ref, near_ref, far_ref, small_ref,
    normed_ref, inner_ref, filter_ref, chosen_ref, weight_ref,
):
    slabs = (slab0_ref, slab1_ref, slab2_ref, slab3_ref)
    groups = len(slabs)
    sequences, steps, width = slab0_ref.shape
    chunks = groups * sequences
    block_rows = chunks * 8
    inner_width = inner_ref.shape[1]
    order = ordering(groups, sequences, place_ref[1])
    assemble(weight_ref, (near_ref, far_ref), place_ref[0])

    def scaled(rows):
        root = lax.rsqrt(jnp.mean(rows * rows, axis=1, keepdims=True) + epsilon)
        return (rows * root * gain_ref[...]).astype(bf16)

    taps = [small_row(small_ref, k) for k in range(4)]
    offset = small_row(small_ref, 4)

    def norm_lap(block, carry):
        base = pl.multiple_of(block * block_rows, block_rows)
        normed = dot(order, scaled(read_rows(slabs, block))).astype(bf16)
        normed_ref[pl.ds(base, block_rows), :] = normed
        return carry

    lax.fori_loop(0, steps // 8, norm_lap, 0)
    inner_ref[3 * chunks :, :] = dot(normed_ref[...], weight_ref[...]).astype(bf16)
    last = inner_ref[steps * chunks :, :].astype(f32).reshape(3, chunks, inner_width)
    rim = dot(scaled(rim_ref[...].astype(f32)), weight_ref[...]).reshape(3, sequences, inner_width)
    rim = jnp.concatenate([rim, last[:, : chunks - sequences, :]], axis=1)
    inner_ref[0 : 3 * chunks, :] = rim.reshape(3 * chunks, inner_width).astype(bf16)

    def lap(block, carry):
        base = pl.multiple_of(block * block_rows, block_rows)
        total = offset
        for k in range(3):
            same = mask_ref[pl.ds(base, block_rows), k : k + 1]
            part = inner_ref[pl.ds(pl.multiple_of(base + k * chunks, 16), block_rows), :]
            total = total + taps[k] * part.astype(f32) * same
        inner = inner_ref[pl.ds(pl.multiple_of(base + 3 * chunks, 16), block_rows), :]
        total = total + taps[3] * inner.astype(f32)
        filtered = (total * sigmoid(total)).astype(bf16)
        filter_ref[pl.ds(base, block_rows), :] = filtered.astype(f32)
        chosen = dot(small_ref[64:160, :], filtered, ((1,), (1,)))
        chosen_ref[:, pl.ds(base, block_rows)] = chosen.astype(bf16)
        return carry

    lax.fori_loop(0, steps // 8, lap, 0)


def gate_kernel(
    place_ref, slab0_ref, slab1_ref, slab2_ref, slab3_ref, normed_ref, near_ref, far_ref, exit_near_ref, exit_far_ref,
    rows_ref, value_ref, slope_ref, grad_ref, weight_ref, exit_ref, gating_ref, gated_ref,
):
    slabs = (slab0_ref, slab1_ref, slab2_ref, slab3_ref)
    sequences, steps, width = slab0_ref.shape
    block_rows = len(slabs) * sequences * 8
    order = ordering(len(slabs), sequences, place_ref[1])
    assemble(weight_ref, (near_ref, far_ref), place_ref[0])
    assemble(exit_ref, (exit_near_ref, exit_far_ref), place_ref[0])

    def order_lap(block, carry):
        at = pl.ds(pl.multiple_of(block * block_rows, block_rows), block_rows)
        rows_ref[at, :] = dot(order, read_rows(slabs, block).astype(bf16)).astype(bf16)
        return carry

    lax.fori_loop(0, steps // 8, order_lap, 0)
    gating_ref[...] = dot(normed_ref[...], weight_ref[...])
    gated_ref[...] = dot(rows_ref[...], exit_ref[...], ((1,), (1,)))

    def lap(block, carry):
        at = pl.ds(pl.multiple_of(block * block_rows, block_rows), block_rows)
        gating = gating_ref[at, :]
        grad_gated = gated_ref[at, :]
        gate = sigmoid(gating)
        value = gating * gate
        value_ref[at, :] = value
        slope_ref[at, :] = grad_gated * (gate * (1.0 + gating * (1.0 - gate)))
        grad_ref[at, :] = (grad_gated * value).astype(bf16).astype(f32)
        return carry

    lax.fori_loop(0, steps // 8, lap, 0)


def fill_rates(small_ref, rates_ref):
    states = rates_ref.shape[0]
    rates = -jnp.exp(small_ref[160 : 160 + states, :].astype(f32)) * log2_e
    for n in range(states):
        rates_ref[n] = jnp.broadcast_to(rates[n : n + 1, :], rates_ref.shape[1:])


def fill_picks(pick_ref):
    depth, width = pick_ref.shape
    source = lax.broadcasted_iota(jnp.int32, (depth, width), 0) % (depth // 2)
    target = lax.broadcasted_iota(jnp.int32, (depth, width), 1) // 128
    pick_ref[...] = jnp.where(source == target, 1.0, 0.0).astype(bf16)


def fill_gates(gates_ref, pick_ref, spread_ref, at):
    steps = gates_ref.shape[0]
    values = gates_ref[:, at, :].reshape(steps * 8, 128)[:, 64:96]
    high = values.astype(bf16)
    rest = (values - high.astype(f32)).astype(bf16)
    pair = jnp.concatenate([high, rest], axis=1)
    span = 2048

    def lap(k, carry):
        columns = pl.ds(pl.multiple_of(k * span, span), span)
        spread_ref[:, columns] = dot(pair, pick_ref[:, columns])
        return carry

    lax.fori_loop(0, spread_ref.shape[1] // span, lap, 0)


def gate_of(spread_ref, t, n):
    return spread_ref[pl.ds(pl.multiple_of(t * 8, 8), 8), n * 128 : (n + 1) * 128]


def lane_slices(width):
    return [slice(k * 128, (k + 1) * 128) for k in range(width // 128)]


def piece_kernel(
    place_ref, chosen_ref, other_ref, mask_ref, small_ref, filter_ref, grad_ref,
    gates_ref, step_ref, slope_ref, end_ref, keep_ref, give_ref, load_ref,
    rates_ref, spread_ref, pick_ref, sum_ref, ahead_ref, back_ref,
):
    me = place_ref[0]
    steps, chunks, width = step_ref.shape
    states = end_ref.shape[0]
    chosen = chosen_ref[...].astype(f32) + other_ref[...].astype(f32)
    padded = jnp.concatenate([chosen, jnp.zeros((32, chosen.shape[1]), f32)], axis=0)
    gates_ref[...] = padded.T.reshape(steps, chunks, 128)
    fill_rates(small_ref, rates_ref)
    fill_picks(pick_ref)
    bias = small_row(small_ref, 5)
    delta = small_ref[0:64, :]

    def delta_lap(block, carry):
        at = pl.ds(pl.multiple_of(block * 8, 8), 8)
        low = gates_ref[at, :, :].reshape(8 * chunks, 128)[:, 0:64]
        high = low.astype(bf16)
        rest = (low - high.astype(f32)).astype(bf16)
        pre = dot(high, delta) + dot(rest, delta) + bias
        grown = jnp.exp(-jnp.abs(pre))
        step = jnp.maximum(pre, 0.0) + jnp.log1p(grown)
        step_ref[at, :, :] = step.reshape(8, chunks, width)
        slope_ref[at, :, :] = (jnp.where(pre >= 0, 1.0, grown) / (1.0 + grown)).reshape(8, chunks, width)
        return carry

    lax.fori_loop(0, steps // 8, delta_lap, 0)

    push = mask_ref[:, 3:4] * reset_push
    gates_ref[:, :, 96:97] = push.reshape(steps, chunks, 1)
    end_ref[...] = jnp.zeros_like(end_ref)
    give_ref[...] = jnp.zeros_like(give_ref)
    keep_ref[...] = jnp.ones_like(keep_ref)
    span = 4
    lanes = lane_slices(width)
    spots = [(j, i) for j in range(span) for i in range(len(lanes))]

    def half_lap(half, carry):
        at = pl.ds(pl.multiple_of(half * 8, 8), 8)
        fill_gates(gates_ref, pick_ref, spread_ref, at)

        def lap(block, totals):
            totals = list(totals)
            pushed, drives, grads = {}, {}, {}
            for j, i in spots:
                t = block * span + j
                step = step_ref[t, at, lanes[i]]
                push = step + gates_ref[t, at, 96:97]
                totals[i] = totals[i] + push
                pushed[j, i] = push
                drives[j, i] = step * filter_ref[t, at, lanes[i]]
                grads[j, i] = grad_ref[t, at, lanes[i]]
            for n in range(states):
                rate = [rates_ref[n, :, one] for one in lanes]
                end = [end_ref[n, at, one] for one in lanes]
                keep = [keep_ref[n, at, one] for one in lanes]
                give = [give_ref[n, at, one] for one in lanes]
                for j in range(span):
                    write = gate_of(spread_ref, block * span + j, n)
                    read = gate_of(spread_ref, block * span + j, states + n)
                    for i in range(len(lanes)):
                        decay = jnp.exp2(pushed[j, i] * rate[i])
                        end[i] = decay * end[i] + drives[j, i] * write
                        keep[i] = keep[i] * decay
                        give[i] = give[i] + keep[i] * (read * grads[j, i])
                for i, one in enumerate(lanes):
                    end_ref[n, at, one] = end[i]
                    keep_ref[n, at, one] = keep[i]
                    give_ref[n, at, one] = give[i]
            return tuple(totals)

        start = tuple(jnp.zeros((8, 128), f32) for _ in lanes)
        totals = lax.fori_loop(0, steps // span, lap, start)
        for i, one in enumerate(lanes):
            sum_ref[at, one] = totals[i]
        return carry

    lax.fori_loop(0, chunks // 8, half_lap, 0)

    sequences = ahead_ref.shape[0] // (states + 4)
    groups = chunks // sequences
    for n in range(states):
        rows = slice(n * sequences, (n + 1) * sequences)
        ahead = jnp.zeros((sequences, width), f32)
        back = jnp.zeros((sequences, width), f32)
        for k in range(groups):
            part = slice(k * sequences, (k + 1) * sequences)
            ahead = keep_ref[n, part, :] * ahead + end_ref[n, part, :]
            other = slice((groups - 1 - k) * sequences, (groups - k) * sequences)
            back = give_ref[n, other, :] + keep_ref[n, other, :] * back
        ahead_ref[rows, :] = ahead
        back_ref[rows, :] = back
    total = jnp.zeros((sequences, width), f32)
    for k in range(groups):
        total = total + sum_ref[k * sequences : (k + 1) * sequences, :]
    held = states * sequences
    for k in range(3):
        term = total.astype(bf16).astype(f32)
        ahead_ref[held + k * sequences : held + (k + 1) * sequences, :] = term
        total = total - term
    ahead_ref[held + 3 * sequences :, :] = jnp.zeros((sequences, width), f32)
    back_ref[held:, :] = ahead_ref[held:, :]

    def load_lap(piece, carry):
        load = jnp.where(piece > me, ahead_ref[...], back_ref[...])
        load_ref[piece] = load.astype(bf16)
        return carry

    lax.fori_loop(0, load_ref.shape[0], load_lap, 0)


def fill_unpicks(unpick_ref, first):
    spot = lax.broadcasted_iota(jnp.int32, unpick_ref.shape, 0) // 128
    column = lax.broadcasted_iota(jnp.int32, unpick_ref.shape, 1)
    unpick_ref[...] = jnp.where(column == spot + first, 1.0, 0.0).astype(bf16)


def forward_kernel(
    place_ref, came_ref, gates_ref, small_ref, step_ref, filter_ref, grad_ref, end_ref, keep_ref, give_ref,
    out_ref, read_sum_ref, start_ref, arrive_ref,
    rates_ref, spread_ref, pick_ref, product_ref, unpick_ref, passed_ref, whole_ref, enter_ref,
):
    me = place_ref[0]
    half = pl.program_id(0)
    steps, _, width = step_ref.shape
    states, chunks = end_ref.shape[:2]
    pieces = came_ref.shape[0]
    sequences = came_ref.shape[1] // (states + 4)
    groups = chunks // sequences
    @pl.when(half == 0)
    def _():
        fill_rates(small_ref, rates_ref)
        fill_picks(pick_ref)
        fill_unpicks(unpick_ref, 64 + states)
        rates_ref[states] = jnp.broadcast_to(small_row(small_ref, 6), (8, width))

        held = states * sequences
        rates = [jnp.broadcast_to(rates_ref[n, 0:1, :], (sequences, width)) for n in range(states)]
        rates = jnp.concatenate(rates, axis=0)

        def step_in(piece, state):
            values = came_ref[piece].astype(f32)
            total = values[held : held + sequences, :]
            for k in range(1, 3):
                total = total + values[held + k * sequences : held + (k + 1) * sequences, :]
            total = jnp.concatenate([total] * states, axis=0)
            return jnp.exp2(total * rates) * state + values[:held, :]

        def step_back(k, state):
            return step_in(pieces - 1 - k, state)

        zero = jnp.zeros((held, width), f32)
        whole_ref[0] = lax.fori_loop(0, me, step_in, zero)
        whole_ref[1] = lax.fori_loop(0, pieces - 1 - me, step_back, zero)
        for n in range(states):
            ahead = whole_ref[0, n * sequences : (n + 1) * sequences, :]
            back = whole_ref[1, n * sequences : (n + 1) * sequences, :]
            for k in range(groups):
                part = slice(k * sequences, (k + 1) * sequences)
                enter_ref[n, part, :] = ahead
                ahead = keep_ref[n, part, :] * ahead + end_ref[n, part, :]
                other = slice((groups - 1 - k) * sequences, (groups - k) * sequences)
                arrive_ref[n, other, :] = back
                back = give_ref[n, other, :] + keep_ref[n, other, :] * back

    span = 4
    lanes = lane_slices(width)
    spots = [(j, i) for j in range(span) for i in range(len(lanes))]

    fill_gates(gates_ref, pick_ref, spread_ref, slice(None))
    at = pl.ds(pl.multiple_of(half * 8, 8), 8)
    for n in range(states):
        for i, one in enumerate(lanes):
            passed_ref[n, i] = enter_ref[n, at, one]

    def forward(block, inner_carry):
        pushed, drives, grads, outs = {}, {}, {}, {}
        for j, i in spots:
            t = block * span + j
            step = step_ref[t, :, lanes[i]]
            feed = filter_ref[t, :, lanes[i]]
            pushed[j, i] = step + gates_ref[t, :, 96:97]
            drives[j, i] = step * feed
            grads[j, i] = grad_ref[t, :, lanes[i]]
            outs[j, i] = feed * rates_ref[states, :, lanes[i]]
        rows = pl.ds(pl.multiple_of(block * span * 8, span * 8), span * 8)
        for n in range(states):
            rate = [rates_ref[n, :, one] for one in lanes]
            hidden = [passed_ref[n, i] for i in range(len(lanes))]
            for i, one in enumerate(lanes):
                start_ref[block, n, :, one] = hidden[i]
            seen = []
            for j in range(span):
                t = block * span + j
                write = gate_of(spread_ref, t, n)
                read = gate_of(spread_ref, t, states + n)
                total = None
                for i in range(len(lanes)):
                    hidden[i] = jnp.exp2(pushed[j, i] * rate[i]) * hidden[i] + drives[j, i] * write
                    outs[j, i] = outs[j, i] + hidden[i] * read
                    one = grads[j, i] * hidden[i]
                    total = one if total is None else total + one
                seen.append(total)
            product_ref[rows, n * 128 : (n + 1) * 128] = jnp.concatenate(seen, axis=0).astype(bf16)
            for i in range(len(lanes)):
                passed_ref[n, i] = hidden[i]
        for j, i in spots:
            out_ref[block * span + j, :, lanes[i]] = outs[j, i]
        return inner_carry

    lax.fori_loop(0, steps // span, forward, 0)
    summed = dot(product_ref[...], unpick_ref[...])
    read_sum_ref[...] = summed.reshape(steps, 8, 128)


def backward_kernel(
    gates_ref, small_ref, step_ref, slope_ref, filter_ref, grad_ref, read_sum_ref, start_ref, arrive_ref,
    direct_ref, rank_ref, chosen_ref, decay_ref, skip_ref, bias_ref,
    rates_ref, spread_ref, pick_ref, product_ref, unpick_ref, delta_ref, sums_acc_ref,
    passed_ref, total_ref,
):
    half = pl.program_id(0)
    steps, _, width = step_ref.shape
    chunks = delta_ref.shape[1]
    blocks, states = start_ref.shape[:2]
    span = steps // blocks

    @pl.when(half == 0)
    def _():
        fill_rates(small_ref, rates_ref)
        fill_picks(pick_ref)
        fill_unpicks(unpick_ref, 64)
        decay_ref[...] = jnp.zeros_like(decay_ref)
        skip_ref[...] = jnp.zeros_like(skip_ref)
        rank_ref[...] = jnp.zeros_like(rank_ref)
        bias_ref[...] = jnp.zeros_like(bias_ref)
        rates_ref[states] = jnp.broadcast_to(small_row(small_ref, 6), (8, width))

    lanes = lane_slices(width)
    spots = [(j, i) for j in range(span) for i in range(len(lanes))]

    fill_gates(gates_ref, pick_ref, spread_ref, slice(None))
    at = pl.ds(pl.multiple_of(half * 8, 8), 8)
    for n in range(states):
        for i, one in enumerate(lanes):
            passed_ref[n, i] = arrive_ref[n, :, one]
            total_ref[n, i] = jnp.zeros((8, 128), f32)

    def backward(k, skips):
        block = blocks - 1 - k
        skips = list(skips)
        raw, feeds, pushed, drives, grads, weighted, slopes = {}, {}, {}, {}, {}, {}, {}
        for j, i in spots:
            t = block * span + j
            step = step_ref[t, :, lanes[i]]
            feed = filter_ref[t, :, lanes[i]]
            grad = grad_ref[t, :, lanes[i]]
            raw[j, i] = step
            feeds[j, i] = feed
            pushed[j, i] = step + gates_ref[t, :, 96:97]
            drives[j, i] = step * feed
            grads[j, i] = grad
            weighted[j, i] = jnp.zeros((8, 128), f32)
            slopes[j, i] = jnp.zeros((8, 128), f32)
            skips[i] = skips[i] + grad * feed
        rows = pl.ds(pl.multiple_of(block * span * 8, span * 8), span * 8)
        for n in range(states):
            rate = [rates_ref[n, :, one] for one in lanes]
            gone = [passed_ref[n, i] for i in range(len(lanes))]
            turns = [total_ref[n, i] for i in range(len(lanes))]
            hidden = [[start_ref[block, n, :, one] for one in lanes]]
            decays = []
            for j in range(span):
                decays.append([jnp.exp2(pushed[j, i] * rate[i]) for i in range(len(lanes))])
                if j < span - 1:
                    write = gate_of(spread_ref, block * span + j, n)
                    last = hidden[-1]
                    hidden.append(
                        [decays[j][i] * last[i] + drives[j, i] * write for i in range(len(lanes))]
                    )
            seen = [None] * span
            for j in reversed(range(span)):
                t = block * span + j
                write = gate_of(spread_ref, t, n)
                read = gate_of(spread_ref, t, states + n)
                for i in range(len(lanes)):
                    adjoint = read * grads[j, i] + gone[i]
                    weighted[j, i] = weighted[j, i] + adjoint * write
                    one = adjoint * drives[j, i]
                    seen[j] = one if seen[j] is None else seen[j] + one
                    gone[i] = adjoint * decays[j][i]
                    turn = gone[i] * hidden[j][i]
                    slopes[j, i] = slopes[j, i] + turn * rate[i]
                    turns[i] = turns[i] + turn * raw[j, i]
            product_ref[rows, n * 128 : (n + 1) * 128] = jnp.concatenate(seen, axis=0).astype(bf16)
            for i in range(len(lanes)):
                passed_ref[n, i] = gone[i]
                total_ref[n, i] = turns[i]
        for j, i in spots:
            t = block * span + j
            grown = slopes[j, i] * log_2 + weighted[j, i] * feeds[j, i]
            delta_ref[t, at, lanes[i]] = grown * slope_ref[t, :, lanes[i]]
            direct = weighted[j, i] * raw[j, i] + grads[j, i] * rates_ref[states, :, lanes[i]]
            direct_ref[t, :, lanes[i]] = direct
        return tuple(skips)

    start = tuple(jnp.zeros((8, 128), f32) for _ in lanes)
    skips = lax.fori_loop(0, blocks, backward, start)
    for i, one in enumerate(lanes):
        skip_ref[0:1, one] += jnp.sum(skips[i], axis=0, keepdims=True)
        for n in range(states):
            part = jnp.sum(total_ref[n, i], axis=0, keepdims=True)
            decay_ref[n : n + 1, one] += part * rates_ref[n, 0:1, one] * log_2
    summed = dot(product_ref[...], unpick_ref[...])
    sums_acc_ref[:, at, :] = summed.reshape(steps, 8, 128) + read_sum_ref[...]

    grads = delta_ref[:, at, :].reshape(steps * 8, width)
    bias_ref[...] += jnp.sum(grads, axis=0, keepdims=True)
    low = gates_ref[...].reshape(steps * 8, 128)[:, 0:64].astype(bf16)
    rank_ref[...] += dot(low, grads.astype(bf16), ((0,), (0,)))

    @pl.when(half == 1)
    def _():
        rows = steps * chunks
        whole = delta_ref[...].reshape(rows, width).astype(bf16)
        back = dot(small_ref[0:64, :], whole, ((1,), (1,)))
        sums = sums_acc_ref[...].reshape(rows, 128).T
        chosen_ref[0:64, :] = back.astype(bf16)
        chosen_ref[64:96, :] = sums[64:96, :].astype(bf16)


def store_rows(keep_ref, send_ref, order, values, block):
    _, sequences, _, width = keep_ref.shape
    back = dot(order, values.astype(bf16), ((0,), (0,)))
    shaped = back.reshape(4, sequences, 8, width).astype(bf16)
    at = pl.ds(pl.multiple_of(block * 8, 8), 8)
    for k in range(4):
        target = send_ref if k % 2 else keep_ref
        target[k // 2, :, at, :] = shaped[k]


def store_blocks(keep_ref, send_ref, me, *parts):
    count = keep_ref.shape[0]
    below = 0
    for values_ref in parts:
        rows = values_ref.shape[0] // (2 * count)
        for k in range(2 * count):
            source = pl.ds(pl.multiple_of((me ^ k) * rows, 8), rows)
            target = send_ref if k % 2 else keep_ref
            target[k // 2, below : below + rows, :] = values_ref[source, :].astype(bf16)
        below += rows


def leave_kernel(
    place_ref, scan_ref, value_ref, slope_ref, rows_ref, normed_ref, exit_near_ref, exit_far_ref,
    gating_ref, out_keep_ref, out_send_ref, exit_grad_ref, keep_ref, send_ref,
    gated_ref, entry_grad_ref, exit_ref, out_ref,
):
    assemble(exit_ref, (exit_near_ref, exit_far_ref), place_ref[0])
    sequences, steps = out_keep_ref.shape[1:3]
    groups = 4
    block_rows = groups * sequences * 8
    order = ordering(groups, sequences, place_ref[1])

    def lap(block, carry):
        at = pl.ds(pl.multiple_of(block * block_rows, block_rows), block_rows)
        scan_out = scan_ref[at, :].astype(bf16).astype(f32)
        gated = (scan_out * value_ref[at, :]).astype(bf16)
        gated_ref[at, :] = gated
        gating_ref[at, :] = (scan_out * slope_ref[at, :]).astype(bf16)
        return carry

    lax.fori_loop(0, steps // 8, lap, 0)
    span = 256

    def column_lap(block, carry):
        at = pl.ds(pl.multiple_of(block * span, span), span)
        out_ref[:, at] = dot(gated_ref[...], exit_ref[:, at]).astype(bf16)
        return carry

    lax.fori_loop(0, out_ref.shape[1] // span, column_lap, 0)

    def store_lap(block, carry):
        at = pl.ds(pl.multiple_of(block * block_rows, block_rows), block_rows)
        store_rows(out_keep_ref, out_send_ref, order, out_ref[at, :], block)
        return carry

    lax.fori_loop(0, steps // 8, store_lap, 0)
    exit_grad_ref[...] = dot(gated_ref[...], rows_ref[...], ((0,), (0,))).astype(bf16)
    entry_grad_ref[...] = dot(normed_ref[...], gating_ref[...], ((0,), (0,)))
    store_blocks(keep_ref, send_ref, place_ref[0], entry_grad_ref)


def filter_kernel(
    place_ref, chosen_ref, other_ref, direct_ref, inner_ref, filter_ref, mask_ref, small_ref,
    rank_ref, decay_ref, bias_ref, skip_ref, gate_keep_ref, gate_came_ref,
    grads_ref, spill_ref, first_ref, small_out_ref, total_ref, *refs,
):
    part_refs, (packed_ref, picked_ref, taps_ref, offset_ref) = refs[:-4], refs[-4:]
    rows, width = grads_ref.shape
    chunks = spill_ref.shape[1]
    block_rows = chunks * 8
    chosen = (chosen_ref[...].astype(f32) + other_ref[...].astype(f32)).astype(bf16)
    packed_ref[0:64, :] = rank_ref[...]
    packed_ref[64:160, :] = dot(chosen, filter_ref[...].astype(bf16))
    packed_ref[160:176, :] = decay_ref[...]
    picked_ref[...] = chosen.astype(f32).T.astype(bf16)
    taps = [small_row(small_ref, k) for k in range(4)]
    offset = small_row(small_ref, 4)
    offset_ref[...] = jnp.zeros_like(offset_ref)
    taps_ref[...] = jnp.zeros_like(taps_ref)

    def lap(block, carry):
        base = pl.multiple_of(block * block_rows, block_rows)
        at = pl.ds(base, block_rows)
        total = offset
        shifted = []
        for k in range(4):
            part = inner_ref[pl.ds(pl.multiple_of(base + k * chunks, 16), block_rows), :].astype(f32)
            if k < 3:
                part = part * mask_ref[at, k : k + 1]
            shifted.append(part)
            total = total + taps[k] * part
        gate = sigmoid(total)
        grad = direct_ref[at, :] + dot(picked_ref[at, :], small_ref[64:160, :])
        grad = grad * (gate * (1.0 + total * (1.0 - gate)))
        grads_ref[at, :] = grad
        offset_ref[...] += jnp.sum(grad, axis=0, keepdims=True)
        for k in range(4):
            taps_ref[k : k + 1, :] += jnp.sum(grad * shifted[k], axis=0, keepdims=True)
        return carry

    lax.fori_loop(0, rows // block_rows, lap, 0)
    packed_ref[176:180, :] = taps_ref[...]
    packed_ref[180:181, :] = offset_ref[...]
    packed_ref[181:182, :] = bias_ref[...]
    packed_ref[182:183, :] = skip_ref[...]
    packed_ref[183:192, :] = jnp.zeros((9, width), f32)
    small_out_ref[...] = packed_ref[...]
    height = gate_keep_ref.shape[1]
    below = (total_ref.shape[0] - height) * 4
    for k, target in enumerate((total_ref,) + part_refs):
        target[0:height, :] = (gate_keep_ref[k].astype(f32) + gate_came_ref[k].astype(f32)).astype(target.dtype)
        if below:
            lanes = pl.ds(pl.multiple_of(((place_ref[0] >> 1) ^ k) * 128, 128), 128)
            for q in range(4):
                values = packed_ref[q * below // 4 : (q + 1) * below // 4, lanes]
                target[height:, q * 128 : (q + 1) * 128] = values.astype(target.dtype)
    for u in range(3):
        total = jnp.zeros((chunks, width), f32)
        for t in range(u + 1):
            part = slice(t * chunks, (t + 1) * chunks)
            total = total + grads_ref[part, :] * taps[u - t] * mask_ref[part, u - t : u - t + 1]
        spill_ref[u] = total
        first_ref[u] = total[0 : first_ref.shape[1], :]


def inner_kernel(
    grads_ref, spill_ref, after_ref, mask_ref, small_ref, normed_ref,
    inner_ref, entry_grad_ref,
    past_ref,
):
    rows, inner_width = grads_ref.shape
    chunks, sequences = spill_ref.shape[1], after_ref.shape[1]
    block_rows = chunks * 8
    blocks = rows // block_rows
    later_spill = jnp.concatenate([spill_ref[:, sequences:, :], after_ref[...]], axis=1)
    later_spill = later_spill.reshape(3 * chunks, inner_width)
    taps = [small_row(small_ref, k) for k in range(4)]
    rim_rows = 3 * chunks
    for k in range(3):
        past_ref[k, rows : rows + rim_rows, :] = jnp.zeros((rim_rows, inner_width), f32)

    def mask_lap(block, carry):
        at = pl.ds(pl.multiple_of(block * block_rows, block_rows), block_rows)
        grad = grads_ref[at, :]
        for k in range(3):
            past_ref[k, at, :] = grad * taps[k] * mask_ref[at, k : k + 1]
        return carry

    lax.fori_loop(0, blocks, mask_lap, 0)

    def lap(block, carry):
        base = pl.multiple_of(block * block_rows, block_rows)
        at = pl.ds(base, block_rows)
        total = grads_ref[at, :] * taps[3]
        for k in range(3):
            later = pl.ds(pl.multiple_of(base + (3 - k) * chunks, 16), block_rows)
            total = total + past_ref[k, later, :]
        inner_ref[at, :] = total.astype(bf16)

        @pl.when(block == blocks - 1)
        def _():
            tail = total[block_rows - rim_rows :, :] + later_spill
            inner_ref[rows - rim_rows : rows, :] = tail.astype(bf16)

        return carry

    lax.fori_loop(0, blocks, lap, 0)
    entry_grad_ref[...] = dot(normed_ref[...], inner_ref[...], ((0,), (0,))).astype(bf16)


def normed_kernel(
    place_ref, inner_ref, gating_ref, near_ref, far_ref, gate_near_ref, gate_far_ref,
    out_keep_ref, out_send_ref,
    weight_ref, gate_weight_ref, grad_ref,
):
    assemble(weight_ref, (near_ref, far_ref), place_ref[0])
    assemble(gate_weight_ref, (gate_near_ref, gate_far_ref), place_ref[0])
    sequences, steps = out_keep_ref.shape[1:3]
    groups = 4
    block_rows = groups * sequences * 8
    order = ordering(groups, sequences, place_ref[1])

    span = 256

    def column_lap(block, carry):
        at = pl.ds(pl.multiple_of(block * span, span), span)
        grad = dot(inner_ref[...], weight_ref[at, :], ((1,), (1,)))
        grad = grad + dot(gating_ref[...], gate_weight_ref[at, :], ((1,), (1,)))
        grad_ref[:, at] = grad.astype(bf16)
        return carry

    lax.fori_loop(0, grad_ref.shape[1] // span, column_lap, 0)

    def lap(block, carry):
        at = pl.ds(pl.multiple_of(block * block_rows, block_rows), block_rows)
        store_rows(out_keep_ref, out_send_ref, order, grad_ref[at, :], block)
        return carry

    lax.fori_loop(0, steps // 8, lap, 0)


def side_sum_kernel(place_ref, total_ref, *refs):
    part_refs, out_refs, small_ref = refs[:-5], refs[-5:-1], refs[-1]
    total = total_ref[...]
    for part_ref in part_refs:
        total = total + part_ref[...].astype(f32)
    rows = out_refs[0].shape[0]
    for k, out_ref in enumerate(out_refs):
        block = total[0:rows, :]
        for j in range(1, len(out_refs)):
            block = jnp.where((place_ref[1] ^ k) == j, total[j * rows : (j + 1) * rows, :], block)
        out_ref[...] = block.astype(bf16)
    height = rows * len(out_refs)
    below = total.shape[0] - height
    if below:
        for q in range(4):
            small_ref[q * below : (q + 1) * below, :] = total[height:, q * 128 : (q + 1) * 128]
    else:
        small_ref[...] = jnp.zeros_like(small_ref)


def interleave_kernel(place_ref, weight_ref, inner_ref, gate0_ref, gate1_ref, gate2_ref, gate3_ref, out_ref, gain_ref):
    gate_refs = (gate0_ref, gate1_ref, gate2_ref, gate3_ref)
    pieces, groups, rows, width = inner_ref.shape
    for k in range(groups):
        inner = inner_ref[0, k].astype(f32)
        for piece in range(1, pieces):
            inner = inner + inner_ref[piece, k].astype(f32)
        gate = gate_refs[0][...].astype(f32)
        for m in range(1, groups):
            gate = jnp.where((place_ref[1] ^ m) == k, gate_refs[m][...].astype(f32), gate)
        for half, values in enumerate((inner, gate)):
            for j in range(width // 64):
                column = half * groups * width + (j * groups + k) * 64
                out_ref[:, column : column + 64] = values[:, j * 64 : (j + 1) * 64]
    total = jnp.sum(out_ref[...] * weight_ref[...].astype(f32), axis=1, keepdims=True)
    gain_ref[...] = jnp.broadcast_to(total, gain_ref.shape)


def local(
    tokens,
    segments,
    cotangent,
    norm_gain,
    entry_weight,
    kernel_weight,
    kernel_offset,
    select_weight,
    delta_weight,
    timestep_bias,
    decay_log,
    skip_gain,
    exit_weight,
):
    sequences, steps, width = tokens.shape
    pieces, groups = lax.axis_size("blk"), lax.axis_size("grp")
    piece, group = lax.axis_index("blk"), lax.axis_index("grp")
    place = jnp.stack([piece, group]).astype(jnp.int32)
    chunks = groups * sequences
    rows = steps * chunks
    slice_rows, entry_width = entry_weight.shape
    own = kernel_offset.shape[0]
    inner_width = entry_width // 2
    group_width = inner_width // groups
    states = decay_log.shape[0]
    rank = delta_weight.shape[0]

    def flipped(value, axis, bits):
        return lax.ppermute(value, axis, [(i, i ^ bits) for i in range(lax.axis_size(axis))])

    def after(value, *others):
        return lax.optimization_barrier((value,) + others)[0]

    def rounds(*values):
        return lax.optimization_barrier(values)

    packed = jnp.concatenate(
        [
            delta_weight,
            select_weight.T,
            decay_log,
            kernel_weight,
            kernel_offset[None],
            timestep_bias[None],
            skip_gain[None],
            jnp.zeros((small_rows - 183, own), bf16),
        ],
        axis=0,
    )
    def side_blocks(block):
        return [block] + [flipped(block, "blk", 2 * k) for k in range(1, pieces // 2)]

    place_of_gain = (piece * groups + group) * slice_rows
    gain_line = lax.dynamic_update_slice_in_dim(jnp.zeros((width,), bf16), norm_gain, place_of_gain, 0)
    gain_line = jnp.pad(gain_line.reshape(1, -1, group_width), ((0, 0), (0, 8 - width // group_width), (0, 0)))
    halves = entry_weight.reshape(slice_rows, 2, pieces, groups, own).transpose(3, 1, 0, 2, 4)
    halves = halves.reshape(groups, 2 * slice_rows, group_width)
    halves = jnp.concatenate([halves, jnp.broadcast_to(gain_line, (groups,) + gain_line.shape[1:])], axis=1)
    exit_block = jnp.concatenate([exit_weight, jnp.pad(packed.reshape(-1), (0, -packed.size % (16 * width))).reshape(-1, width)])
    halves, exit_block, tokens = rounds(halves, exit_block, tokens)
    halves = lax.all_to_all(halves, "grp", split_axis=0, concat_axis=0, tiled=True)
    exit_side = side_blocks(exit_block)
    token_pair = flipped(tokens, "grp", 2)
    halves, token_pair, tokens, *exit_side = rounds(halves, token_pair, tokens, *exit_side)

    gain_rows = jnp.sum(halves[:, 2 * slice_rows :].astype(f32), axis=0).astype(bf16)
    inner_block = halves[:, :slice_rows].reshape(groups * slice_rows, group_width)
    inner_block = jnp.concatenate([inner_block, gain_rows])
    gate_block = halves[:, slice_rows : 2 * slice_rows].reshape(groups * slice_rows, group_width)
    inner_side = side_blocks(inner_block)
    exit_near = jnp.stack(exit_side)
    exit_far = flipped(exit_near, "blk", 1)
    token_slabs = (tokens, flipped(tokens, "grp", 1), token_pair, flipped(token_pair, "grp", 1))
    exit_near, exit_far, gate_block, cotangent, *rest = rounds(
        exit_near, exit_far, gate_block, cotangent, *inner_side, *token_slabs
    )
    inner_side, token_slabs = rest[: pieces // 2], rest[pieces // 2 :]
    small = jnp.stack([exit_near[:, own:], exit_far[:, own:]], axis=1).reshape(pieces, -1)[:, : packed.size]
    bits = pieces.bit_length() - 1
    small = small.reshape((2,) * bits + (small_rows, own))
    for k in range(bits):
        small = jnp.where((piece >> (bits - 1 - k)) & 1, jnp.flip(small, k), small)
    small = small.reshape(pieces, small_rows, own).transpose(1, 0, 2).reshape(small_rows, group_width)

    inner_near = jnp.stack(inner_side)
    ahead = [(i, i + 1) for i in range(pieces - 1)]
    behind = [(i + 1, i) for i in range(pieces - 1)]
    tails = jnp.stack([slab[:, steps - 3 :] for slab in token_slabs])
    tail = lax.dynamic_index_in_dim(tails, group ^ (groups - 1), 0, keepdims=False)
    rim_source = tail.transpose(1, 0, 2).reshape(3 * sequences, width)
    rim = lax.ppermute(rim_source, "blk", ahead)
    inner_far = flipped(inner_near, "blk", 1)
    gate_block, cotangent = rounds(gate_block, cotangent, inner_near, rim_source)[:2]
    gate_side = side_blocks(gate_block)
    cotangent_pair = flipped(cotangent, "grp", 2)
    label_tail = lax.ppermute(segments[:, -3:], "blk", ahead)
    labels = jnp.concatenate([label_tail, segments], axis=1)
    length = segments.shape[1]
    shifted = jnp.stack([labels[:, k : k + length] for k in range(3)], axis=-1)
    same = (shifted == segments[:, :, None]).astype(f32)
    columns = jnp.concatenate([same, 1.0 - same[:, :, 2:3]], axis=2)
    mask = columns.reshape(sequences, groups, steps, 4).transpose(2, 1, 0, 3).reshape(rows, 4)
    inner_near, inner_far, rim, cotangent_pair, cotangent, *gate_side = rounds(
        inner_near, inner_far, rim, cotangent_pair, cotangent, *gate_side
    )
    gain_all = jnp.sum(inner_near[:, -8:].astype(f32), axis=0) + jnp.sum(inner_far[:, -8:].astype(f32), axis=0)
    gain_all = gain_all[: width // group_width].reshape(1, width)

    gate_near = jnp.stack(gate_side)
    gate_far = flipped(gate_near, "blk", 1)
    cotangent_slabs = (
        cotangent,
        flipped(cotangent, "grp", 1),
        cotangent_pair,
        flipped(cotangent_pair, "grp", 1),
    )

    def group_sum(value):
        half = value.astype(f32) + flipped(value, "grp", 1).astype(f32)
        half = half.astype(bf16)
        return half, flipped(half, "grp", 2)

    normed, inner, filtered, chosen = kernel_call(
        entry_kernel,
        9,
        [
            ((rows, width), bf16),
            ((rows + 3 * chunks, group_width), bf16),
            ((rows, group_width), f32),
            ((96, rows), bf16),
        ],
        [pltpu.VMEM((width, group_width), bf16)],
        12,
        place, *token_slabs, rim, gain_all, mask, inner_near, inner_far, small,
    )
    chosen_pair = group_sum(chosen)
    cotangent_rows, gate_value, gate_slope, grad_scan = kernel_call(
        gate_kernel,
        8,
        [
            ((rows, width), bf16),
            ((rows, group_width), f32),
            ((rows, group_width), f32),
            ((rows, group_width), f32),
        ],
        [
            pltpu.VMEM((width, group_width), bf16),
            pltpu.VMEM((group_width, width), bf16),
            pltpu.VMEM((rows, group_width), f32),
            pltpu.VMEM((rows, group_width), f32),
        ],
        16,
        place, *cotangent_slabs, normed, gate_near, gate_far, exit_near, exit_far,
    )
    cube = (steps, chunks, group_width)
    bank = (states, chunks, group_width)
    load_rows = (states + 4) * sequences
    gates, step_sizes, step_slopes, ends, keeps, gives, loads = kernel_call(
        piece_kernel,
        23,
        [
            ((steps, chunks, 128), f32),
            (cube, f32),
            (cube, f32),
            (bank, f32),
            (bank, f32),
            (bank, f32),
            ((pieces, load_rows, group_width), bf16),
        ],
        [
            pltpu.VMEM((states, 8, group_width), f32),
            pltpu.VMEM((steps * 8, 2 * states * 128), f32),
            pltpu.VMEM((4 * states, 2 * states * 128), bf16),
            pltpu.VMEM((chunks, group_width), f32),
            pltpu.VMEM((load_rows, group_width), f32),
            pltpu.VMEM((load_rows, group_width), f32),
        ],
        16,
        place, *chosen_pair, mask, small, filtered.reshape(cube), grad_scan.reshape(cube),
    )
    came = lax.all_to_all(loads, "blk", split_axis=0, concat_axis=0, tiled=True)

    lanes = group_width // 128
    gate_scratch = [
        pltpu.VMEM((states + 1, 8, group_width), f32),
        pltpu.VMEM((steps * 8, 2 * states * 128), f32),
        pltpu.VMEM((4 * states, 2 * states * 128), bf16),
    ]
    product_scratch = [pltpu.VMEM((steps * 8, states * 128), bf16), pltpu.VMEM((states * 128, 128), bf16)]
    starts = (steps // 4, states, chunks, group_width)
    scan_out, read_sums, block_starts, arrive = kernel_call(
        forward_kernel,
        18,
        [(cube, f32), ((steps, chunks, 128), f32), (starts, f32), (bank, f32)],
        gate_scratch
        + product_scratch
        + [pltpu.VMEM((states, lanes, 8, 128), f32), pltpu.VMEM((2, states * sequences, group_width), f32), pltpu.VMEM(bank, f32)],
        36,
        place, came, gates, small, step_sizes, filtered.reshape(cube), grad_scan.reshape(cube), ends, keeps, gives,
        halves=(None, None, 1, None, 1, 1, 1) + (None,) * 3 + (1, 1, 2, None),
    )
    half_slabs = ((2, sequences, steps, width), bf16)
    block_height = groups * slice_rows
    entry_half = ((pieces // 2, block_height, group_width), bf16)
    grad_gating, out_keep, out_send, exit_grad, gate_keep, gate_send = kernel_call(
        leave_kernel,
        12,
        [((rows, group_width), bf16), half_slabs, half_slabs, ((group_width, width), bf16), entry_half, entry_half],
        [
            pltpu.VMEM((rows, group_width), bf16),
            pltpu.VMEM((width, group_width), f32),
            pltpu.VMEM((group_width, width), bf16),
            pltpu.VMEM((rows, width), bf16),
        ],
        14,
        place, scan_out.reshape(rows, group_width), gate_value, gate_slope, cotangent_rows, normed, exit_near, exit_far,
    )

    exit_parts = lax.all_to_all(
        exit_grad.reshape(pieces, own, width), "blk", split_axis=0, concat_axis=0, tiled=True
    )
    gate_came = flipped(gate_send, "blk", 1)
    out_came = flipped(out_send, "grp", 1)
    grad_direct, rank_grad, chosen_grad, decay_grad, skip_grad, bias_grad = kernel_call(
        backward_kernel,
        35,
        [
            (cube, f32),
            ((rank, group_width), f32),
            ((96, rows), bf16),
            ((states, group_width), f32),
            ((1, group_width), f32),
            ((1, group_width), f32),
        ],
        gate_scratch
        + product_scratch
        + [
            pltpu.VMEM(cube, f32),
            pltpu.VMEM((steps, chunks, 128), f32),
            pltpu.VMEM((states, lanes, 8, 128), f32),
            pltpu.VMEM((states, lanes, 8, 128), f32),
        ],
        50,
        gates, small, step_sizes, step_slopes, filtered.reshape(cube), after(grad_scan, out_send).reshape(cube),
        read_sums, block_starts, arrive,
        halves=(1, None, 1, 1, 1, 1, 1, 2, 1, 1) + (None,) * 5,
    )
    chosen_grad, exit_parts, gate_came, out_came = rounds(chosen_grad, exit_parts, gate_came, out_came)
    chosen_grads = group_sum(chosen_grad)

    def slab_part(keep, came):
        return (keep[1].astype(f32) + came[1].astype(f32)).astype(bf16)

    exit_out = jnp.sum(exit_parts.astype(f32), axis=0)
    grad_direct, exit_out = rounds(grad_direct, exit_out)
    out_part = after(slab_part(out_keep, out_came), chosen_grads[0])
    out_other = flipped(out_part, "grp", 2)

    paired = 2 * own == 128
    side_block = (block_height + (small_rows // 4 if paired else 0), group_width)
    grad_sums, spill, first_spill, small_grads, side_total, *side_parts = kernel_call(
        filter_kernel,
        6,
        [
            ((rows, group_width), f32),
            ((3, chunks, group_width), f32),
            ((3, sequences, group_width), f32),
            ((small_rows, group_width), f32),
            (side_block, f32),
        ]
        + [(side_block, bf16)] * (pieces // 2 - 1),
        [
            pltpu.VMEM((small_rows, group_width), f32),
            pltpu.VMEM((rows, 96), bf16),
            pltpu.VMEM((4, group_width), f32),
            pltpu.VMEM((1, group_width), f32),
        ],
        62,
        place, *chosen_grads, grad_direct.reshape(rows, group_width), inner, filtered, mask, small,
        rank_grad, decay_grad, bias_grad, skip_grad, gate_keep, gate_came,
        free=True,
    )
    spill_after = lax.ppermute(first_spill, "blk", behind)
    side_parts = [flipped(part, "blk", 2 * k + 2) for k, part in enumerate(side_parts)]
    grad_inner, inner_entry = kernel_call(
        inner_kernel,
        6,
        [((rows, group_width), bf16), ((width, group_width), bf16)],
        [pltpu.VMEM((3, rows + 3 * chunks, group_width), f32)],
        14,
        grad_sums, spill, spill_after, mask, small, normed,
    )
    grad_inner, inner_entry, out_other = rounds(grad_inner, inner_entry, out_other)
    inner_parts = lax.all_to_all(
        inner_entry.reshape(pieces * groups, slice_rows, group_width), both, split_axis=0, concat_axis=0, tiled=True
    )
    grad_keep, grad_send = kernel_call(
        normed_kernel,
        10,
        [half_slabs, half_slabs],
        [
            pltpu.VMEM((width, group_width), bf16),
            pltpu.VMEM((width, group_width), bf16),
            pltpu.VMEM((rows, width), bf16),
        ],
        14,
        place, grad_inner, grad_gating, inner_near, inner_far, gate_near, gate_far,
    )
    grad_send, *side_parts = rounds(grad_send, *side_parts)
    grad_came = flipped(grad_send, "grp", 1)
    grad_part = slab_part(grad_keep, grad_came)
    grad_other = flipped(grad_part, "grp", 2)
    *gate_blocks, small_sum = kernel_call(
        side_sum_kernel,
        2,
        [((slice_rows, group_width), bf16)] * groups + [((small_rows, 128), f32)],
        [],
        16,
        place, after(side_total, grad_part), *side_parts,
    )
    gate_blocks = [gate_blocks[0]] + [flipped(gate_blocks[k], "grp", k) for k in range(1, groups)]
    residual = tokens.astype(f32)
    block_out = residual + out_keep[0].astype(f32) + out_came[0].astype(f32) + out_other.astype(f32)
    block_out = block_out.astype(bf16)
    inner_parts = inner_parts.reshape(pieces, groups, slice_rows, group_width)
    if own == 64:
        entry_out, gain_out = kernel_call(
            interleave_kernel,
            3,
            [((slice_rows, entry_width), f32), ((slice_rows, 128), f32)],
            [],
            16,
            place, entry_weight, inner_parts, *gate_blocks,
        )
        gain_out = gain_out[:, 0]
    else:
        inner_sum = jnp.sum(inner_parts.astype(f32), axis=0)
        gate_parts = jnp.stack(gate_blocks).astype(f32)
        for k in range(2):
            pairs = gate_parts.reshape(2, 2, slice_rows, group_width)
            gate_parts = jnp.where((group >> (1 - k)) & 1, jnp.flip(pairs, k), pairs)
        entry_parts = jnp.stack([inner_sum, gate_parts.reshape(inner_sum.shape)], axis=0)
        entry_parts = entry_parts.reshape(2, groups, slice_rows, pieces, own)
        entry_out = entry_parts.transpose(2, 0, 3, 1, 4).reshape(slice_rows, entry_width)
        gain_out = jnp.sum(entry_out * entry_weight.astype(f32), axis=1)
    gain_out = gain_out / norm_gain.astype(f32)

    if paired:
        small_sum = small_sum + flipped(small_sum, "blk", 1)
        mine = lax.dynamic_slice_in_dim(small_sum, (piece & 1) * own, own, 1)
    else:
        split = small_grads.reshape(small_rows, pieces, own).transpose(1, 0, 2)
        came_small = lax.all_to_all(split, "blk", split_axis=0, concat_axis=0, tiled=True)
        mine = jnp.sum(came_small, axis=0)

    grad_hat = grad_keep[0].astype(f32) + grad_came[0].astype(f32) + grad_other.astype(f32)
    grad_hat = grad_hat * gain_all[0]
    root = lax.rsqrt(jnp.mean(residual * residual, axis=2, keepdims=True) + epsilon)
    hat_own = residual * root
    grad_input = root * (grad_hat - hat_own * jnp.mean(grad_hat * hat_own, axis=2, keepdims=True))
    input_grad = (cotangent.astype(f32) + grad_input).astype(bf16)
    return (
        block_out,
        input_grad,
        gain_out,
        entry_out,
        mine[176:180],
        mine[180],
        mine[64:160].T,
        mine[0:64],
        mine[181],
        mine[160:176],
        mine[182],
        exit_out,
    )


def solution(mesh):
    placed = (
        P(None, both, None),
        P(None, "blk"),
        P(None, both, None),
        P(both),
        P(both, None),
        P(None, both),
        P(both),
        P(both, None),
        P(None, both),
        P(both),
        P(None, both),
        P(both),
        P(both, None),
    )
    return jax.shard_map(
        local,
        mesh=mesh,
        in_specs=placed,
        out_specs=(
            P(None, both, None),
            P(None, both, None),
            P(both),
            P(both, None),
            P(None, both),
            P(both),
            P(both, None),
            P(None, both),
            P(both),
            P(None, both),
            P(both),
            P(both, None),
        ),
        check_vma=False,
    )
```

```python
import jax
import jax.numpy as jnp
from jax import lax
from jax.experimental import pallas as pl
from jax.experimental.pallas import tpu as pltpu
from jax.sharding import PartitionSpec as P

epsilon = 1e-05
log2_e = 1.4426950408889634
log_2 = 0.6931471805599453
reset_push = 1e6
f32 = jnp.float32
bf16 = jnp.bfloat16
small_rows = 192
both = ("blk", "grp")


def dot(left, right, dims=((1,), (0,))):
    return lax.dot_general(left, right, (dims, ((), ())), preferred_element_type=f32)


def sigmoid(values):
    return 1.0 / (1.0 + jnp.exp(-values))


def spread(block, axis):
    count = lax.axis_size(axis)
    copies = jnp.broadcast_to(block[None], (count,) + block.shape)
    return lax.all_to_all(copies, axis, split_axis=0, concat_axis=0, tiled=True)


def ordering(groups, sequences, me):
    chunks = groups * sequences
    rows = chunks * 8
    out_row = lax.broadcasted_iota(jnp.int32, (rows, rows), 0)
    in_row = lax.broadcasted_iota(jnp.int32, (rows, rows), 1)
    chunk = out_row % chunks
    wanted = (((chunk // sequences) ^ me) * sequences + chunk % sequences) * 8 + out_row // chunks
    return jnp.where(in_row == wanted, 1.0, 0.0).astype(bf16)


def kernel_call(body, micros, outs, scratch, limit, *operands, halves=None, free=False):
    whole = pl.BlockSpec(memory_space=pltpu.VMEM)
    kinds = [(value.shape, value.dtype) for value in operands] + list(outs)

    def place(index):
        shape, kind = kinds[index]
        if kind == jnp.int32:
            return pl.BlockSpec(memory_space=pltpu.SMEM)
        axis = halves[index] if halves else None
        if axis is None and free:
            return pl.BlockSpec(shape, lambda *_: (0,) * len(shape))
        if axis is None:
            return whole
        block = tuple(size // 2 if k == axis else size for k, size in enumerate(shape))
        return pl.BlockSpec(block, lambda half: tuple(half if k == axis else 0 for k in range(len(block))))

    places = [place(k) for k in range(len(kinds))]
    return pl.pallas_call(
        body,
        out_shape=[jax.ShapeDtypeStruct(shape, kind) for shape, kind in outs],
        grid=(2,) if halves else (),
        in_specs=places[: len(operands)],
        out_specs=places[len(operands) :],
        scratch_shapes=scratch,
        compiler_params=pltpu.CompilerParams(vmem_limit_bytes=limit << 20),
        cost_estimate=pl.CostEstimate(
            flops=micros * 1_150_000_000, bytes_accessed=8_000_000, transcendentals=0
        ),
    )(*operands)


def read_rows(slab_refs, block):
    sequences, _, width = slab_refs[0].shape
    at = pl.ds(pl.multiple_of(block * 8, 8), 8)
    parts = [slab[:, at, :].astype(f32) for slab in slab_refs]
    return jnp.concatenate(parts, axis=0).reshape(len(slab_refs) * sequences * 8, width)


def small_row(small_ref, index):
    tail = small_ref[176:192, :].astype(f32)
    return tail[index : index + 1, :]


def assemble(whole_ref, stacks, me):
    for side, stack_ref in enumerate(stacks):
        count = stack_ref.shape[0]
        rows = whole_ref.shape[0] // (2 * count)
        for k in range(count):
            target = pl.ds(pl.multiple_of((me ^ (2 * k + side)) * rows, 8), rows)
            whole_ref[target, :] = stack_ref[k, 0:rows, :]


def entry_kernel(
    place_ref, slab0_ref, slab1_ref, slab2_ref, slab3_ref, rim_ref, gain_ref, mask_ref, near_ref, far_ref, small_ref,
    normed_ref, inner_ref, filter_ref, chosen_ref, weight_ref,
):
    slabs = (slab0_ref, slab1_ref, slab2_ref, slab3_ref)
    groups = len(slabs)
    sequences, steps, width = slab0_ref.shape
    chunks = groups * sequences
    block_rows = chunks * 8
    inner_width = inner_ref.shape[1]
    order = ordering(groups, sequences, place_ref[1])
    assemble(weight_ref, (near_ref, far_ref), place_ref[0])

    def scaled(rows):
        root = lax.rsqrt(jnp.mean(rows * rows, axis=1, keepdims=True) + epsilon)
        return (rows * root * gain_ref[...]).astype(bf16)

    taps = [small_row(small_ref, k) for k in range(4)]
    offset = small_row(small_ref, 4)

    def norm_lap(block, carry):
        base = pl.multiple_of(block * block_rows, block_rows)
        normed = dot(order, scaled(read_rows(slabs, block))).astype(bf16)
        normed_ref[pl.ds(base, block_rows), :] = normed
        return carry

    lax.fori_loop(0, steps // 8, norm_lap, 0)
    inner_ref[3 * chunks :, :] = dot(normed_ref[...], weight_ref[...]).astype(bf16)
    last = inner_ref[steps * chunks :, :].astype(f32).reshape(3, chunks, inner_width)
    rim = dot(scaled(rim_ref[...].astype(f32)), weight_ref[...]).reshape(3, sequences, inner_width)
    rim = jnp.concatenate([rim, last[:, : chunks - sequences, :]], axis=1)
    inner_ref[0 : 3 * chunks, :] = rim.reshape(3 * chunks, inner_width).astype(bf16)

    def lap(block, carry):
        base = pl.multiple_of(block * block_rows, block_rows)
        total = offset
        for k in range(3):
            same = mask_ref[pl.ds(base, block_rows), k : k + 1]
            part = inner_ref[pl.ds(pl.multiple_of(base + k * chunks, 16), block_rows), :]
            total = total + taps[k] * part.astype(f32) * same
        inner = inner_ref[pl.ds(pl.multiple_of(base + 3 * chunks, 16), block_rows), :]
        total = total + taps[3] * inner.astype(f32)
        filtered = (total * sigmoid(total)).astype(bf16)
        filter_ref[pl.ds(base, block_rows), :] = filtered.astype(f32)
        chosen = dot(small_ref[64:160, :], filtered, ((1,), (1,)))
        chosen_ref[:, pl.ds(base, block_rows)] = chosen.astype(bf16)
        return carry

    lax.fori_loop(0, steps // 8, lap, 0)


def gate_kernel(
    place_ref, slab0_ref, slab1_ref, slab2_ref, slab3_ref, normed_ref, near_ref, far_ref, exit_near_ref, exit_far_ref,
    rows_ref, value_ref, slope_ref, grad_ref, weight_ref, exit_ref, gating_ref, gated_ref,
):
    slabs = (slab0_ref, slab1_ref, slab2_ref, slab3_ref)
    sequences, steps, width = slab0_ref.shape
    block_rows = len(slabs) * sequences * 8
    order = ordering(len(slabs), sequences, place_ref[1])
    assemble(weight_ref, (near_ref, far_ref), place_ref[0])
    assemble(exit_ref, (exit_near_ref, exit_far_ref), place_ref[0])

    def order_lap(block, carry):
        at = pl.ds(pl.multiple_of(block * block_rows, block_rows), block_rows)
        rows_ref[at, :] = dot(order, read_rows(slabs, block).astype(bf16)).astype(bf16)
        return carry

    lax.fori_loop(0, steps // 8, order_lap, 0)
    gating_ref[...] = dot(normed_ref[...], weight_ref[...])
    gated_ref[...] = dot(rows_ref[...], exit_ref[...], ((1,), (1,)))

    def lap(block, carry):
        at = pl.ds(pl.multiple_of(block * block_rows, block_rows), block_rows)
        gating = gating_ref[at, :]
        grad_gated = gated_ref[at, :]
        gate = sigmoid(gating)
        value = gating * gate
        value_ref[at, :] = value
        slope_ref[at, :] = grad_gated * (gate * (1.0 + gating * (1.0 - gate)))
        grad_ref[at, :] = (grad_gated * value).astype(bf16).astype(f32)
        return carry

    lax.fori_loop(0, steps // 8, lap, 0)


def fill_rates(small_ref, rates_ref):
    states = rates_ref.shape[0]
    rates = -jnp.exp(small_ref[160 : 160 + states, :].astype(f32)) * log2_e
    for n in range(states):
        rates_ref[n] = jnp.broadcast_to(rates[n : n + 1, :], rates_ref.shape[1:])


def fill_picks(pick_ref):
    depth, width = pick_ref.shape
    source = lax.broadcasted_iota(jnp.int32, (depth, width), 0) % (depth // 2)
    target = lax.broadcasted_iota(jnp.int32, (depth, width), 1) // 128
    pick_ref[...] = jnp.where(source == target, 1.0, 0.0).astype(bf16)


def fill_gates(gates_ref, pick_ref, spread_ref, at):
    steps = gates_ref.shape[0]
    values = gates_ref[:, at, :].reshape(steps * 8, 128)[:, 64:96]
    high = values.astype(bf16)
    rest = (values - high.astype(f32)).astype(bf16)
    pair = jnp.concatenate([high, rest], axis=1)
    span = 2048

    def lap(k, carry):
        columns = pl.ds(pl.multiple_of(k * span, span), span)
        spread_ref[:, columns] = dot(pair, pick_ref[:, columns])
        return carry

    lax.fori_loop(0, spread_ref.shape[1] // span, lap, 0)


def gate_of(spread_ref, t, n):
    return spread_ref[pl.ds(pl.multiple_of(t * 8, 8), 8), n * 128 : (n + 1) * 128]


def lane_slices(width):
    return [slice(k * 128, (k + 1) * 128) for k in range(width // 128)]


def piece_kernel(
    place_ref, chosen_ref, other_ref, mask_ref, small_ref, filter_ref, grad_ref,
    gates_ref, step_ref, slope_ref, end_ref, keep_ref, give_ref, load_ref,
    rates_ref, spread_ref, pick_ref, sum_ref, ahead_ref, back_ref,
):
    me = place_ref[0]
    steps, chunks, width = step_ref.shape
    states = end_ref.shape[0]
    chosen = chosen_ref[...].astype(f32) + other_ref[...].astype(f32)
    padded = jnp.concatenate([chosen, jnp.zeros((32, chosen.shape[1]), f32)], axis=0)
    gates_ref[...] = padded.T.reshape(steps, chunks, 128)
    fill_rates(small_ref, rates_ref)
    fill_picks(pick_ref)
    bias = small_row(small_ref, 5)
    delta = small_ref[0:64, :]

    def delta_lap(block, carry):
        at = pl.ds(pl.multiple_of(block * 8, 8), 8)
        low = gates_ref[at, :, :].reshape(8 * chunks, 128)[:, 0:64]
        high = low.astype(bf16)
        rest = (low - high.astype(f32)).astype(bf16)
        pre = dot(high, delta) + dot(rest, delta) + bias
        grown = jnp.exp(-jnp.abs(pre))
        step = jnp.maximum(pre, 0.0) + jnp.log1p(grown)
        step_ref[at, :, :] = step.reshape(8, chunks, width)
        slope_ref[at, :, :] = (jnp.where(pre >= 0, 1.0, grown) / (1.0 + grown)).reshape(8, chunks, width)
        return carry

    lax.fori_loop(0, steps // 8, delta_lap, 0)

    push = mask_ref[:, 3:4] * reset_push
    gates_ref[:, :, 96:97] = push.reshape(steps, chunks, 1)
    end_ref[...] = jnp.zeros_like(end_ref)
    give_ref[...] = jnp.zeros_like(give_ref)
    keep_ref[...] = jnp.ones_like(keep_ref)
    span = 4
    lanes = lane_slices(width)
    spots = [(j, i) for j in range(span) for i in range(len(lanes))]

    def half_lap(half, carry):
        at = pl.ds(pl.multiple_of(half * 8, 8), 8)
        fill_gates(gates_ref, pick_ref, spread_ref, at)

        def lap(block, totals):
            totals = list(totals)
            pushed, drives, grads = {}, {}, {}
            for j, i in spots:
                t = block * span + j
                step = step_ref[t, at, lanes[i]]
                push = step + gates_ref[t, at, 96:97]
                totals[i] = totals[i] + push
                pushed[j, i] = push
                drives[j, i] = step * filter_ref[t, at, lanes[i]]
                grads[j, i] = grad_ref[t, at, lanes[i]]
            for n in range(states):
                rate = [rates_ref[n, :, one] for one in lanes]
                end = [end_ref[n, at, one] for one in lanes]
                keep = [keep_ref[n, at, one] for one in lanes]
                give = [give_ref[n, at, one] for one in lanes]
                for j in range(span):
                    write = gate_of(spread_ref, block * span + j, n)
                    read = gate_of(spread_ref, block * span + j, states + n)
                    for i in range(len(lanes)):
                        decay = jnp.exp2(pushed[j, i] * rate[i])
                        end[i] = decay * end[i] + drives[j, i] * write
                        keep[i] = keep[i] * decay
                        give[i] = give[i] + keep[i] * (read * grads[j, i])
                for i, one in enumerate(lanes):
                    end_ref[n, at, one] = end[i]
                    keep_ref[n, at, one] = keep[i]
                    give_ref[n, at, one] = give[i]
            return tuple(totals)

        start = tuple(jnp.zeros((8, 128), f32) for _ in lanes)
        totals = lax.fori_loop(0, steps // span, lap, start)
        for i, one in enumerate(lanes):
            sum_ref[at, one] = totals[i]
        return carry

    lax.fori_loop(0, chunks // 8, half_lap, 0)

    sequences = ahead_ref.shape[0] // (states + 2)
    groups = chunks // sequences
    for n in range(states):
        rows = slice(n * sequences, (n + 1) * sequences)
        ahead = jnp.zeros((sequences, width), f32)
        back = jnp.zeros((sequences, width), f32)
        for k in range(groups):
            part = slice(k * sequences, (k + 1) * sequences)
            ahead = keep_ref[n, part, :] * ahead + end_ref[n, part, :]
            other = slice((groups - 1 - k) * sequences, (groups - k) * sequences)
            back = give_ref[n, other, :] + keep_ref[n, other, :] * back
        ahead_ref[rows, :] = ahead
        back_ref[rows, :] = back
    total = jnp.zeros((sequences, width), f32)
    for k in range(groups):
        total = total + sum_ref[k * sequences : (k + 1) * sequences, :]
    held = states * sequences
    for k in range(2):
        term = total.astype(bf16).astype(f32)
        ahead_ref[held + k * sequences : held + (k + 1) * sequences, :] = term
        total = total - term
    back_ref[held:, :] = ahead_ref[held:, :]

    def load_lap(piece, carry):
        load = jnp.where(piece > me, ahead_ref[...], back_ref[...])
        load_ref[piece] = load.astype(bf16)
        return carry

    lax.fori_loop(0, load_ref.shape[0], load_lap, 0)


def fill_unpicks(unpick_ref, first):
    spot = lax.broadcasted_iota(jnp.int32, unpick_ref.shape, 0) // 128
    column = lax.broadcasted_iota(jnp.int32, unpick_ref.shape, 1)
    unpick_ref[...] = jnp.where(column == spot + first, 1.0, 0.0).astype(bf16)


def forward_kernel(
    place_ref, came_ref, gates_ref, small_ref, step_ref, filter_ref, grad_ref, end_ref, keep_ref, give_ref,
    out_ref, read_sum_ref, start_ref, arrive_ref,
    rates_ref, spread_ref, pick_ref, product_ref, unpick_ref, passed_ref, whole_ref, enter_ref,
):
    me = place_ref[0]
    half = pl.program_id(0)
    steps, _, width = step_ref.shape
    states, chunks = end_ref.shape[:2]
    pieces = came_ref.shape[0]
    sequences = came_ref.shape[1] // (states + 2)
    groups = chunks // sequences
    @pl.when(half == 0)
    def _():
        fill_rates(small_ref, rates_ref)
        fill_picks(pick_ref)
        fill_unpicks(unpick_ref, 64 + states)
        rates_ref[states] = jnp.broadcast_to(small_row(small_ref, 6), (8, width))

        held = states * sequences
        rates = [jnp.broadcast_to(rates_ref[n, 0:1, :], (sequences, width)) for n in range(states)]
        rates = jnp.concatenate(rates, axis=0)

        def step_in(piece, state):
            values = came_ref[piece].astype(f32)
            total = values[held : held + sequences, :]
            total = total + values[held + sequences :, :]
            total = jnp.concatenate([total] * states, axis=0)
            return jnp.exp2(total * rates) * state + values[:held, :]

        def step_back(k, state):
            return step_in(pieces - 1 - k, state)

        zero = jnp.zeros((held, width), f32)
        whole_ref[0] = lax.fori_loop(0, me, step_in, zero)
        whole_ref[1] = lax.fori_loop(0, pieces - 1 - me, step_back, zero)
        for n in range(states):
            ahead = whole_ref[0, n * sequences : (n + 1) * sequences, :]
            back = whole_ref[1, n * sequences : (n + 1) * sequences, :]
            for k in range(groups):
                part = slice(k * sequences, (k + 1) * sequences)
                enter_ref[n, part, :] = ahead
                ahead = keep_ref[n, part, :] * ahead + end_ref[n, part, :]
                other = slice((groups - 1 - k) * sequences, (groups - k) * sequences)
                arrive_ref[n, other, :] = back
                back = give_ref[n, other, :] + keep_ref[n, other, :] * back

    span = 4
    lanes = lane_slices(width)
    spots = [(j, i) for j in range(span) for i in range(len(lanes))]

    fill_gates(gates_ref, pick_ref, spread_ref, slice(None))
    at = pl.ds(pl.multiple_of(half * 8, 8), 8)
    for n in range(states):
        for i, one in enumerate(lanes):
            passed_ref[n, i] = enter_ref[n, at, one]

    def forward(block, inner_carry):
        pushed, drives, grads, outs = {}, {}, {}, {}
        for j, i in spots:
            t = block * span + j
            step = step_ref[t, :, lanes[i]]
            feed = filter_ref[t, :, lanes[i]]
            pushed[j, i] = step + gates_ref[t, :, 96:97]
            drives[j, i] = step * feed
            grads[j, i] = grad_ref[t, :, lanes[i]]
            outs[j, i] = feed * rates_ref[states, :, lanes[i]]
        rows = pl.ds(pl.multiple_of(block * span * 8, span * 8), span * 8)
        for n in range(states):
            rate = [rates_ref[n, :, one] for one in lanes]
            hidden = [passed_ref[n, i] for i in range(len(lanes))]
            for i, one in enumerate(lanes):
                start_ref[block, n, :, one] = hidden[i]
            seen = []
            for j in range(span):
                t = block * span + j
                write = gate_of(spread_ref, t, n)
                read = gate_of(spread_ref, t, states + n)
                total = None
                for i in range(len(lanes)):
                    hidden[i] = jnp.exp2(pushed[j, i] * rate[i]) * hidden[i] + drives[j, i] * write
                    outs[j, i] = outs[j, i] + hidden[i] * read
                    one = grads[j, i] * hidden[i]
                    total = one if total is None else total + one
                seen.append(total)
            product_ref[rows, n * 128 : (n + 1) * 128] = jnp.concatenate(seen, axis=0).astype(bf16)
            for i in range(len(lanes)):
                passed_ref[n, i] = hidden[i]
        for j, i in spots:
            out_ref[block * span + j, :, lanes[i]] = outs[j, i]
        return inner_carry

    lax.fori_loop(0, steps // span, forward, 0)
    summed = dot(product_ref[...], unpick_ref[...])
    read_sum_ref[...] = summed.reshape(steps, 8, 128)


def backward_kernel(
    gates_ref, small_ref, step_ref, slope_ref, filter_ref, grad_ref, read_sum_ref, start_ref, arrive_ref,
    direct_ref, rank_ref, chosen_ref, decay_ref, skip_ref, bias_ref,
    rates_ref, spread_ref, pick_ref, product_ref, unpick_ref, delta_ref, sums_acc_ref,
    passed_ref, total_ref,
):
    half = pl.program_id(0)
    steps, _, width = step_ref.shape
    chunks = delta_ref.shape[1]
    blocks, states = start_ref.shape[:2]
    span = steps // blocks

    @pl.when(half == 0)
    def _():
        fill_rates(small_ref, rates_ref)
        fill_picks(pick_ref)
        fill_unpicks(unpick_ref, 64)
        decay_ref[...] = jnp.zeros_like(decay_ref)
        skip_ref[...] = jnp.zeros_like(skip_ref)
        rank_ref[...] = jnp.zeros_like(rank_ref)
        bias_ref[...] = jnp.zeros_like(bias_ref)
        rates_ref[states] = jnp.broadcast_to(small_row(small_ref, 6), (8, width))

    lanes = lane_slices(width)
    spots = [(j, i) for j in range(span) for i in range(len(lanes))]

    fill_gates(gates_ref, pick_ref, spread_ref, slice(None))
    at = pl.ds(pl.multiple_of(half * 8, 8), 8)
    for n in range(states):
        for i, one in enumerate(lanes):
            passed_ref[n, i] = arrive_ref[n, :, one]
            total_ref[n, i] = jnp.zeros((8, 128), f32)

    def backward(k, skips):
        block = blocks - 1 - k
        skips = list(skips)
        raw, feeds, pushed, drives, grads, weighted, slopes = {}, {}, {}, {}, {}, {}, {}
        for j, i in spots:
            t = block * span + j
            step = step_ref[t, :, lanes[i]]
            feed = filter_ref[t, :, lanes[i]]
            grad = grad_ref[t, :, lanes[i]]
            raw[j, i] = step
            feeds[j, i] = feed
            pushed[j, i] = step + gates_ref[t, :, 96:97]
            drives[j, i] = step * feed
            grads[j, i] = grad
            weighted[j, i] = jnp.zeros((8, 128), f32)
            slopes[j, i] = jnp.zeros((8, 128), f32)
            skips[i] = skips[i] + grad * feed
        rows = pl.ds(pl.multiple_of(block * span * 8, span * 8), span * 8)
        for n in range(states):
            rate = [rates_ref[n, :, one] for one in lanes]
            gone = [passed_ref[n, i] for i in range(len(lanes))]
            turns = [total_ref[n, i] for i in range(len(lanes))]
            hidden = [[start_ref[block, n, :, one] for one in lanes]]
            decays = []
            for j in range(span):
                decays.append([jnp.exp2(pushed[j, i] * rate[i]) for i in range(len(lanes))])
                if j < span - 1:
                    write = gate_of(spread_ref, block * span + j, n)
                    last = hidden[-1]
                    hidden.append(
                        [decays[j][i] * last[i] + drives[j, i] * write for i in range(len(lanes))]
                    )
            seen = [None] * span
            for j in reversed(range(span)):
                t = block * span + j
                write = gate_of(spread_ref, t, n)
                read = gate_of(spread_ref, t, states + n)
                for i in range(len(lanes)):
                    adjoint = read * grads[j, i] + gone[i]
                    weighted[j, i] = weighted[j, i] + adjoint * write
                    one = adjoint * drives[j, i]
                    seen[j] = one if seen[j] is None else seen[j] + one
                    gone[i] = adjoint * decays[j][i]
                    turn = gone[i] * hidden[j][i]
                    slopes[j, i] = slopes[j, i] + turn * rate[i]
                    turns[i] = turns[i] + turn * raw[j, i]
            product_ref[rows, n * 128 : (n + 1) * 128] = jnp.concatenate(seen, axis=0).astype(bf16)
            for i in range(len(lanes)):
                passed_ref[n, i] = gone[i]
                total_ref[n, i] = turns[i]
        for j, i in spots:
            t = block * span + j
            grown = slopes[j, i] * log_2 + weighted[j, i] * feeds[j, i]
            delta_ref[t, at, lanes[i]] = grown * slope_ref[t, :, lanes[i]]
            direct = weighted[j, i] * raw[j, i] + grads[j, i] * rates_ref[states, :, lanes[i]]
            direct_ref[t, :, lanes[i]] = direct
        return tuple(skips)

    start = tuple(jnp.zeros((8, 128), f32) for _ in lanes)
    skips = lax.fori_loop(0, blocks, backward, start)
    for i, one in enumerate(lanes):
        skip_ref[0:1, one] += jnp.sum(skips[i], axis=0, keepdims=True)
        for n in range(states):
            part = jnp.sum(total_ref[n, i], axis=0, keepdims=True)
            decay_ref[n : n + 1, one] += part * rates_ref[n, 0:1, one] * log_2
    summed = dot(product_ref[...], unpick_ref[...])
    sums_acc_ref[:, at, :] = summed.reshape(steps, 8, 128) + read_sum_ref[...]

    grads = delta_ref[:, at, :].reshape(steps * 8, width)
    bias_ref[...] += jnp.sum(grads, axis=0, keepdims=True)
    low = gates_ref[...].reshape(steps * 8, 128)[:, 0:64].astype(bf16)
    rank_ref[...] += dot(low, grads.astype(bf16), ((0,), (0,)))

    @pl.when(half == 1)
    def _():
        rows = steps * chunks
        whole = delta_ref[...].reshape(rows, width).astype(bf16)
        back = dot(small_ref[0:64, :], whole, ((1,), (1,)))
        sums = sums_acc_ref[...].reshape(rows, 128).T
        chosen_ref[0:64, :] = back.astype(bf16)
        chosen_ref[64:96, :] = sums[64:96, :].astype(bf16)


def store_rows(keep_ref, send_ref, order, values, block):
    _, sequences, _, width = keep_ref.shape
    back = dot(order, values.astype(bf16), ((0,), (0,)))
    shaped = back.reshape(4, sequences, 8, width).astype(bf16)
    at = pl.ds(pl.multiple_of(block * 8, 8), 8)
    for k in range(4):
        target = send_ref if k % 2 else keep_ref
        target[k // 2, :, at, :] = shaped[k]


def store_blocks(keep_ref, send_ref, me, *parts):
    count = keep_ref.shape[0]
    below = 0
    for values_ref in parts:
        rows = values_ref.shape[0] // (2 * count)
        for k in range(2 * count):
            source = pl.ds(pl.multiple_of((me ^ k) * rows, 8), rows)
            target = send_ref if k % 2 else keep_ref
            target[k // 2, below : below + rows, :] = values_ref[source, :].astype(bf16)
        below += rows


def leave_kernel(
    place_ref, scan_ref, value_ref, slope_ref, rows_ref, normed_ref, exit_near_ref, exit_far_ref,
    gating_ref, out_keep_ref, out_send_ref, exit_grad_ref, keep_ref, send_ref,
    gated_ref, entry_grad_ref, exit_ref, out_ref,
):
    assemble(exit_ref, (exit_near_ref, exit_far_ref), place_ref[0])
    sequences, steps = out_keep_ref.shape[1:3]
    groups = 4
    block_rows = groups * sequences * 8
    order = ordering(groups, sequences, place_ref[1])

    def lap(block, carry):
        at = pl.ds(pl.multiple_of(block * block_rows, block_rows), block_rows)
        scan_out = scan_ref[at, :].astype(bf16).astype(f32)
        gated = (scan_out * value_ref[at, :]).astype(bf16)
        gated_ref[at, :] = gated
        gating_ref[at, :] = (scan_out * slope_ref[at, :]).astype(bf16)
        return carry

    lax.fori_loop(0, steps // 8, lap, 0)
    span = 256

    def column_lap(block, carry):
        at = pl.ds(pl.multiple_of(block * span, span), span)
        out_ref[:, at] = dot(gated_ref[...], exit_ref[:, at]).astype(bf16)
        return carry

    lax.fori_loop(0, out_ref.shape[1] // span, column_lap, 0)

    def store_lap(block, carry):
        at = pl.ds(pl.multiple_of(block * block_rows, block_rows), block_rows)
        store_rows(out_keep_ref, out_send_ref, order, out_ref[at, :], block)
        return carry

    lax.fori_loop(0, steps // 8, store_lap, 0)
    exit_grad_ref[...] = dot(gated_ref[...], rows_ref[...], ((0,), (0,))).astype(bf16)
    entry_grad_ref[...] = dot(normed_ref[...], gating_ref[...], ((0,), (0,)))
    store_blocks(keep_ref, send_ref, place_ref[0], entry_grad_ref)


def filter_kernel(
    place_ref, chosen_ref, other_ref, direct_ref, inner_ref, filter_ref, mask_ref, small_ref,
    rank_ref, decay_ref, bias_ref, skip_ref, gate_keep_ref, gate_came_ref,
    back_ref, tail_ref, first_ref, small_out_ref, total_ref, *refs,
):
    part_refs, (packed_ref, picked_ref, taps_ref, offset_ref, grads_ref, past_ref) = refs[:-6], refs[-6:]
    rows, width = grads_ref.shape
    chunks, sequences = tail_ref.shape[1], first_ref.shape[1]
    rim_rows = 3 * chunks
    for k in range(3):
        past_ref[k, rows : rows + rim_rows, :] = jnp.zeros((rim_rows, width), f32)
    block_rows = chunks * 8
    chosen = (chosen_ref[...].astype(f32) + other_ref[...].astype(f32)).astype(bf16)
    packed_ref[0:64, :] = rank_ref[...]
    packed_ref[64:160, :] = dot(chosen, filter_ref[...].astype(bf16))
    packed_ref[160:176, :] = decay_ref[...]
    picked_ref[...] = chosen.astype(f32).T.astype(bf16)
    taps = [small_row(small_ref, k) for k in range(4)]
    offset = small_row(small_ref, 4)
    offset_ref[...] = jnp.zeros_like(offset_ref)
    taps_ref[...] = jnp.zeros_like(taps_ref)

    def lap(block, carry):
        base = pl.multiple_of(block * block_rows, block_rows)
        at = pl.ds(base, block_rows)
        total = offset
        shifted = []
        for k in range(4):
            part = inner_ref[pl.ds(pl.multiple_of(base + k * chunks, 16), block_rows), :].astype(f32)
            if k < 3:
                part = part * mask_ref[at, k : k + 1]
            shifted.append(part)
            total = total + taps[k] * part
        gate = sigmoid(total)
        grad = direct_ref[at, :] + dot(picked_ref[at, :], small_ref[64:160, :])
        grad = grad * (gate * (1.0 + total * (1.0 - gate)))
        grads_ref[at, :] = grad
        for k in range(3):
            past_ref[k, at, :] = grad * taps[k] * mask_ref[at, k : k + 1]
        offset_ref[...] += jnp.sum(grad, axis=0, keepdims=True)
        for k in range(4):
            taps_ref[k : k + 1, :] += jnp.sum(grad * shifted[k], axis=0, keepdims=True)
        return carry

    lax.fori_loop(0, rows // block_rows, lap, 0)
    packed_ref[176:180, :] = taps_ref[...]
    packed_ref[180:181, :] = offset_ref[...]
    packed_ref[181:182, :] = bias_ref[...]
    packed_ref[182:183, :] = skip_ref[...]
    packed_ref[183:192, :] = jnp.zeros((9, width), f32)
    small_out_ref[...] = packed_ref[...]
    height = gate_keep_ref.shape[1]
    below = (total_ref.shape[0] - height) * 4
    for k, target in enumerate((total_ref,) + part_refs):
        target[0:height, :] = (gate_keep_ref[k].astype(f32) + gate_came_ref[k].astype(f32)).astype(target.dtype)
        if below:
            lanes = pl.ds(pl.multiple_of(((place_ref[0] >> 1) ^ k) * 128, 128), 128)
            for q in range(4):
                values = packed_ref[q * below // 4 : (q + 1) * below // 4, lanes]
                target[height:, q * 128 : (q + 1) * 128] = values.astype(target.dtype)
    spills = []
    for u in range(3):
        total = jnp.zeros((chunks, width), f32)
        for t in range(u + 1):
            total = total + past_ref[u - t, t * chunks : (t + 1) * chunks, :]
        first_ref[u] = total[0:sequences, :]
        spills.append(jnp.concatenate([total[sequences:, :], jnp.zeros((sequences, width), f32)], axis=0))

    def back_lap(block, carry):
        base = pl.multiple_of(block * block_rows, block_rows)
        at = pl.ds(base, block_rows)
        total = grads_ref[at, :] * taps[3]
        for k in range(3):
            later = pl.ds(pl.multiple_of(base + (3 - k) * chunks, 16), block_rows)
            total = total + past_ref[k, later, :]
        back_ref[at, :] = total.astype(bf16)

        @pl.when(block == rows // block_rows - 1)
        def _():
            for u in range(3):
                first = block_rows - rim_rows + u * chunks
                tail_ref[u] = total[first : first + chunks, :] + spills[u]

        return carry

    lax.fori_loop(0, rows // block_rows, back_lap, 0)


def inner_kernel(back_ref, tail_ref, after_ref, normed_ref, inner_ref, entry_grad_ref):
    rows, width = back_ref.shape
    chunks, sequences = tail_ref.shape[1], after_ref.shape[1]
    rim_rows = 3 * chunks
    inner_ref[0 : rows - rim_rows, :] = back_ref[0 : rows - rim_rows, :]
    later = jnp.concatenate([jnp.zeros((3, chunks - sequences, width), f32), after_ref[...]], axis=1)
    tail = (tail_ref[...] + later).reshape(rim_rows, width)
    inner_ref[rows - rim_rows :, :] = tail.astype(bf16)
    entry_grad_ref[...] = dot(normed_ref[...], inner_ref[...], ((0,), (0,))).astype(bf16)


def normed_kernel(
    place_ref, inner_ref, gating_ref, near_ref, far_ref, gate_near_ref, gate_far_ref,
    out_keep_ref, out_send_ref,
    weight_ref, gate_weight_ref, grad_ref,
):
    assemble(weight_ref, (near_ref, far_ref), place_ref[0])
    assemble(gate_weight_ref, (gate_near_ref, gate_far_ref), place_ref[0])
    sequences, steps = out_keep_ref.shape[1:3]
    groups = 4
    block_rows = groups * sequences * 8
    order = ordering(groups, sequences, place_ref[1])

    span = 256

    def column_lap(block, carry):
        at = pl.ds(pl.multiple_of(block * span, span), span)
        grad = dot(inner_ref[...], weight_ref[at, :], ((1,), (1,)))
        grad = grad + dot(gating_ref[...], gate_weight_ref[at, :], ((1,), (1,)))
        grad_ref[:, at] = grad.astype(bf16)
        return carry

    lax.fori_loop(0, grad_ref.shape[1] // span, column_lap, 0)

    def lap(block, carry):
        at = pl.ds(pl.multiple_of(block * block_rows, block_rows), block_rows)
        store_rows(out_keep_ref, out_send_ref, order, grad_ref[at, :], block)
        return carry

    lax.fori_loop(0, steps // 8, lap, 0)


def side_sum_kernel(place_ref, total_ref, *refs):
    part_refs, out_refs, small_ref = refs[:-5], refs[-5:-1], refs[-1]
    total = total_ref[...]
    for part_ref in part_refs:
        total = total + part_ref[...].astype(f32)
    rows = out_refs[0].shape[0]
    for k, out_ref in enumerate(out_refs):
        block = total[0:rows, :]
        for j in range(1, len(out_refs)):
            block = jnp.where((place_ref[1] ^ k) == j, total[j * rows : (j + 1) * rows, :], block)
        out_ref[...] = block.astype(bf16)
    height = rows * len(out_refs)
    below = total.shape[0] - height
    if below:
        for q in range(4):
            small_ref[q * below : (q + 1) * below, :] = total[height:, q * 128 : (q + 1) * 128]
    else:
        small_ref[...] = jnp.zeros_like(small_ref)


def interleave_kernel(place_ref, weight_ref, inner_ref, gate0_ref, gate1_ref, gate2_ref, gate3_ref, out_ref, gain_ref):
    gate_refs = (gate0_ref, gate1_ref, gate2_ref, gate3_ref)
    pieces, groups, rows, width = inner_ref.shape
    for k in range(groups):
        inner = inner_ref[0, k].astype(f32)
        for piece in range(1, pieces):
            inner = inner + inner_ref[piece, k].astype(f32)
        gate = gate_refs[0][...].astype(f32)
        for m in range(1, groups):
            gate = jnp.where((place_ref[1] ^ m) == k, gate_refs[m][...].astype(f32), gate)
        for half, values in enumerate((inner, gate)):
            for j in range(width // 64):
                column = half * groups * width + (j * groups + k) * 64
                out_ref[:, column : column + 64] = values[:, j * 64 : (j + 1) * 64]
    total = jnp.sum(out_ref[...] * weight_ref[...].astype(f32), axis=1, keepdims=True)
    gain_ref[...] = jnp.broadcast_to(total, gain_ref.shape)


def local(
    tokens,
    segments,
    cotangent,
    norm_gain,
    entry_weight,
    kernel_weight,
    kernel_offset,
    select_weight,
    delta_weight,
    timestep_bias,
    decay_log,
    skip_gain,
    exit_weight,
):
    sequences, steps, width = tokens.shape
    pieces, groups = lax.axis_size("blk"), lax.axis_size("grp")
    piece, group = lax.axis_index("blk"), lax.axis_index("grp")
    place = jnp.stack([piece, group]).astype(jnp.int32)
    chunks = groups * sequences
    rows = steps * chunks
    slice_rows, entry_width = entry_weight.shape
    own = kernel_offset.shape[0]
    inner_width = entry_width // 2
    group_width = inner_width // groups
    states = decay_log.shape[0]
    rank = delta_weight.shape[0]

    def flipped(value, axis, bits):
        return lax.ppermute(value, axis, [(i, i ^ bits) for i in range(lax.axis_size(axis))])

    def after(value, *others):
        return lax.optimization_barrier((value,) + others)[0]

    def rounds(*values):
        return lax.optimization_barrier(values)

    packed = jnp.concatenate(
        [
            delta_weight,
            select_weight.T,
            decay_log,
            kernel_weight,
            kernel_offset[None],
            timestep_bias[None],
            skip_gain[None],
            jnp.zeros((small_rows - 183, own), bf16),
        ],
        axis=0,
    )
    def side_blocks(block):
        return [block] + [flipped(block, "blk", 2 * k) for k in range(1, pieces // 2)]

    place_of_gain = (piece * groups + group) * slice_rows
    gain_line = lax.dynamic_update_slice_in_dim(jnp.zeros((width,), bf16), norm_gain, place_of_gain, 0)
    gain_line = jnp.pad(gain_line.reshape(1, -1, group_width), ((0, 0), (0, 8 - width // group_width), (0, 0)))
    halves = entry_weight.reshape(slice_rows, 2, pieces, groups, own).transpose(3, 1, 0, 2, 4)
    halves = halves.reshape(groups, 2 * slice_rows, group_width)
    halves = jnp.concatenate([halves, jnp.broadcast_to(gain_line, (groups,) + gain_line.shape[1:])], axis=1)
    exit_block = jnp.concatenate([exit_weight, jnp.pad(packed.reshape(-1), (0, -packed.size % (16 * width))).reshape(-1, width)])
    halves, exit_block, tokens = rounds(halves, exit_block, tokens)
    halves = lax.all_to_all(halves, "grp", split_axis=0, concat_axis=0, tiled=True)
    exit_side = side_blocks(exit_block)
    token_pair = flipped(tokens, "grp", 2)
    halves, token_pair, tokens, *exit_side = rounds(halves, token_pair, tokens, *exit_side)

    gain_rows = jnp.sum(halves[:, 2 * slice_rows :].astype(f32), axis=0).astype(bf16)
    inner_block = halves[:, :slice_rows].reshape(groups * slice_rows, group_width)
    inner_block = jnp.concatenate([inner_block, gain_rows])
    gate_block = halves[:, slice_rows : 2 * slice_rows].reshape(groups * slice_rows, group_width)
    inner_side = side_blocks(inner_block)
    exit_near = jnp.stack(exit_side)
    exit_far = flipped(exit_near, "blk", 1)
    token_slabs = (tokens, flipped(tokens, "grp", 1), token_pair, flipped(token_pair, "grp", 1))
    exit_near, exit_far, gate_block, cotangent, *rest = rounds(
        exit_near, exit_far, gate_block, cotangent, *inner_side, *token_slabs
    )
    inner_side, token_slabs = rest[: pieces // 2], rest[pieces // 2 :]
    small = jnp.stack([exit_near[:, own:], exit_far[:, own:]], axis=1).reshape(pieces, -1)[:, : packed.size]
    bits = pieces.bit_length() - 1
    small = small.reshape((2,) * bits + (small_rows, own))
    for k in range(bits):
        small = jnp.where((piece >> (bits - 1 - k)) & 1, jnp.flip(small, k), small)
    small = small.reshape(pieces, small_rows, own).transpose(1, 0, 2).reshape(small_rows, group_width)

    inner_near = jnp.stack(inner_side)
    ahead = [(i, i + 1) for i in range(pieces - 1)]
    behind = [(i + 1, i) for i in range(pieces - 1)]
    tails = jnp.stack([slab[:, steps - 3 :] for slab in token_slabs])
    tail = lax.dynamic_index_in_dim(tails, group ^ (groups - 1), 0, keepdims=False)
    rim_source = tail.transpose(1, 0, 2).reshape(3 * sequences, width)
    rim = lax.ppermute(rim_source, "blk", ahead)
    inner_far = flipped(inner_near, "blk", 1)
    gate_block, cotangent = rounds(gate_block, cotangent, inner_near, rim_source)[:2]
    gate_side = side_blocks(gate_block)
    cotangent_pair = flipped(cotangent, "grp", 2)
    label_tail = lax.ppermute(segments[:, -3:], "blk", ahead)
    labels = jnp.concatenate([label_tail, segments], axis=1)
    length = segments.shape[1]
    shifted = jnp.stack([labels[:, k : k + length] for k in range(3)], axis=-1)
    same = (shifted == segments[:, :, None]).astype(f32)
    columns = jnp.concatenate([same, 1.0 - same[:, :, 2:3]], axis=2)
    mask = columns.reshape(sequences, groups, steps, 4).transpose(2, 1, 0, 3).reshape(rows, 4)
    gain_all = jnp.sum(inner_near[:, -8:].astype(f32), axis=0) + jnp.sum(inner_far[:, -8:].astype(f32), axis=0)
    gain_all = gain_all[: width // group_width].reshape(1, width)

    gate_near = jnp.stack(gate_side)
    gate_far = flipped(gate_near, "blk", 1)
    cotangent_slabs = (
        cotangent,
        flipped(cotangent, "grp", 1),
        cotangent_pair,
        flipped(cotangent_pair, "grp", 1),
    )

    def group_sum(value):
        half = value.astype(f32) + flipped(value, "grp", 1).astype(f32)
        half = half.astype(bf16)
        return half, flipped(half, "grp", 2)

    normed, inner, filtered, chosen = kernel_call(
        entry_kernel,
        9,
        [
            ((rows, width), bf16),
            ((rows + 3 * chunks, group_width), bf16),
            ((rows, group_width), f32),
            ((96, rows), bf16),
        ],
        [pltpu.VMEM((width, group_width), bf16)],
        12,
        place, *token_slabs, rim, gain_all, mask, inner_near, inner_far, small,
    )
    chosen_pair = group_sum(chosen)
    cotangent_rows, gate_value, gate_slope, grad_scan = kernel_call(
        gate_kernel,
        8,
        [
            ((rows, width), bf16),
            ((rows, group_width), f32),
            ((rows, group_width), f32),
            ((rows, group_width), f32),
        ],
        [
            pltpu.VMEM((width, group_width), bf16),
            pltpu.VMEM((group_width, width), bf16),
            pltpu.VMEM((rows, group_width), f32),
            pltpu.VMEM((rows, group_width), f32),
        ],
        16,
        place, *cotangent_slabs, normed, gate_near, gate_far, exit_near, exit_far,
    )
    cube = (steps, chunks, group_width)
    bank = (states, chunks, group_width)
    load_rows = (states + 2) * sequences
    gates, step_sizes, step_slopes, ends, keeps, gives, loads = kernel_call(
        piece_kernel,
        23,
        [
            ((steps, chunks, 128), f32),
            (cube, f32),
            (cube, f32),
            (bank, f32),
            (bank, f32),
            (bank, f32),
            ((pieces, load_rows, group_width), bf16),
        ],
        [
            pltpu.VMEM((states, 8, group_width), f32),
            pltpu.VMEM((steps * 8, 2 * states * 128), f32),
            pltpu.VMEM((4 * states, 2 * states * 128), bf16),
            pltpu.VMEM((chunks, group_width), f32),
            pltpu.VMEM((load_rows, group_width), f32),
            pltpu.VMEM((load_rows, group_width), f32),
        ],
        16,
        place, *chosen_pair, mask, small, filtered.reshape(cube), grad_scan.reshape(cube),
    )
    came = lax.all_to_all(loads, "blk", split_axis=0, concat_axis=0, tiled=True)

    lanes = group_width // 128
    gate_scratch = [
        pltpu.VMEM((states + 1, 8, group_width), f32),
        pltpu.VMEM((steps * 8, 2 * states * 128), f32),
        pltpu.VMEM((4 * states, 2 * states * 128), bf16),
    ]
    product_scratch = [pltpu.VMEM((steps * 8, states * 128), bf16), pltpu.VMEM((states * 128, 128), bf16)]
    starts = (steps // 4, states, chunks, group_width)
    scan_out, read_sums, block_starts, arrive = kernel_call(
        forward_kernel,
        18,
        [(cube, f32), ((steps, chunks, 128), f32), (starts, f32), (bank, f32)],
        gate_scratch
        + product_scratch
        + [pltpu.VMEM((states, lanes, 8, 128), f32), pltpu.VMEM((2, states * sequences, group_width), f32), pltpu.VMEM(bank, f32)],
        36,
        place, came, gates, small, step_sizes, filtered.reshape(cube), grad_scan.reshape(cube), ends, keeps, gives,
        halves=(None, None, 1, None, 1, 1, 1) + (None,) * 3 + (1, 1, 2, None),
    )
    half_slabs = ((2, sequences, steps, width), bf16)
    block_height = groups * slice_rows
    entry_half = ((pieces // 2, block_height, group_width), bf16)
    grad_gating, out_keep, out_send, exit_grad, gate_keep, gate_send = kernel_call(
        leave_kernel,
        12,
        [((rows, group_width), bf16), half_slabs, half_slabs, ((group_width, width), bf16), entry_half, entry_half],
        [
            pltpu.VMEM((rows, group_width), bf16),
            pltpu.VMEM((width, group_width), f32),
            pltpu.VMEM((group_width, width), bf16),
            pltpu.VMEM((rows, width), bf16),
        ],
        14,
        place, scan_out.reshape(rows, group_width), gate_value, gate_slope, cotangent_rows, normed, exit_near, exit_far,
    )

    exit_parts = lax.all_to_all(
        exit_grad.reshape(pieces, own, width), "blk", split_axis=0, concat_axis=0, tiled=True
    )
    gate_came = flipped(gate_send, "blk", 1)
    out_came = flipped(out_send, "grp", 1)
    grad_direct, rank_grad, chosen_grad, decay_grad, skip_grad, bias_grad = kernel_call(
        backward_kernel,
        35,
        [
            (cube, f32),
            ((rank, group_width), f32),
            ((96, rows), bf16),
            ((states, group_width), f32),
            ((1, group_width), f32),
            ((1, group_width), f32),
        ],
        gate_scratch
        + product_scratch
        + [
            pltpu.VMEM(cube, f32),
            pltpu.VMEM((steps, chunks, 128), f32),
            pltpu.VMEM((states, lanes, 8, 128), f32),
            pltpu.VMEM((states, lanes, 8, 128), f32),
        ],
        50,
        gates, small, step_sizes, step_slopes, filtered.reshape(cube), after(grad_scan, out_send).reshape(cube),
        read_sums, block_starts, arrive,
        halves=(1, None, 1, 1, 1, 1, 1, 2, 1, 1) + (None,) * 5,
    )
    chosen_grad, exit_parts, gate_came, out_came = rounds(chosen_grad, exit_parts, gate_came, out_came)
    chosen_grads = group_sum(chosen_grad)

    def slab_part(keep, came):
        return (keep[1].astype(f32) + came[1].astype(f32)).astype(bf16)

    exit_out = jnp.sum(exit_parts.astype(f32), axis=0)
    grad_direct, exit_out = rounds(grad_direct, exit_out)
    out_part = after(slab_part(out_keep, out_came), chosen_grads[0])
    out_other = flipped(out_part, "grp", 2)

    paired = 2 * own == 128
    side_block = (block_height + (small_rows // 4 if paired else 0), group_width)
    grad_back, tail_back, first_spill, small_grads, side_total, *side_parts = kernel_call(
        filter_kernel,
        6,
        [
            ((rows, group_width), bf16),
            ((3, chunks, group_width), f32),
            ((3, sequences, group_width), f32),
            ((small_rows, group_width), f32),
            (side_block, f32),
        ]
        + [(side_block, bf16)] * (pieces // 2 - 1),
        [
            pltpu.VMEM((small_rows, group_width), f32),
            pltpu.VMEM((rows, 96), bf16),
            pltpu.VMEM((4, group_width), f32),
            pltpu.VMEM((1, group_width), f32),
            pltpu.VMEM((rows, group_width), f32),
            pltpu.VMEM((3, rows + 3 * chunks, group_width), f32),
        ],
        62,
        place, *chosen_grads, grad_direct.reshape(rows, group_width), inner, filtered, mask, small,
        rank_grad, decay_grad, bias_grad, skip_grad, gate_keep, gate_came,
        free=True,
    )
    spill_after = lax.ppermute(first_spill, "blk", behind)
    side_parts = [flipped(part, "blk", 2 * k + 2) for k, part in enumerate(side_parts)]
    grad_inner, inner_entry = kernel_call(
        inner_kernel,
        4,
        [((rows, group_width), bf16), ((width, group_width), bf16)],
        [],
        12,
        grad_back, tail_back, spill_after, normed,
    )
    grad_inner, inner_entry, out_other = rounds(grad_inner, inner_entry, out_other)
    inner_parts = lax.all_to_all(
        inner_entry.reshape(pieces * groups, slice_rows, group_width), both, split_axis=0, concat_axis=0, tiled=True
    )
    grad_keep, grad_send = kernel_call(
        normed_kernel,
        10,
        [half_slabs, half_slabs],
        [
            pltpu.VMEM((width, group_width), bf16),
            pltpu.VMEM((width, group_width), bf16),
            pltpu.VMEM((rows, width), bf16),
        ],
        14,
        place, grad_inner, grad_gating, inner_near, inner_far, gate_near, gate_far,
    )
    grad_send, *side_parts = rounds(grad_send, *side_parts)
    grad_came = flipped(grad_send, "grp", 1)
    grad_part = slab_part(grad_keep, grad_came)
    grad_other = flipped(grad_part, "grp", 2)
    *gate_blocks, small_sum = kernel_call(
        side_sum_kernel,
        2,
        [((slice_rows, group_width), bf16)] * groups + [((small_rows, 128), f32)],
        [],
        16,
        place, after(side_total, grad_part), *side_parts,
    )
    gate_blocks = [gate_blocks[0]] + [flipped(gate_blocks[k], "grp", k) for k in range(1, groups)]
    residual = tokens.astype(f32)
    block_out = residual + out_keep[0].astype(f32) + out_came[0].astype(f32) + out_other.astype(f32)
    block_out = block_out.astype(bf16)
    inner_parts = inner_parts.reshape(pieces, groups, slice_rows, group_width)
    if own == 64:
        entry_out, gain_out = kernel_call(
            interleave_kernel,
            3,
            [((slice_rows, entry_width), f32), ((slice_rows, 128), f32)],
            [],
            16,
            place, entry_weight, inner_parts, *gate_blocks,
        )
        gain_out = gain_out[:, 0]
    else:
        inner_sum = jnp.sum(inner_parts.astype(f32), axis=0)
        gate_parts = jnp.stack(gate_blocks).astype(f32)
        for k in range(2):
            pairs = gate_parts.reshape(2, 2, slice_rows, group_width)
            gate_parts = jnp.where((group >> (1 - k)) & 1, jnp.flip(pairs, k), pairs)
        entry_parts = jnp.stack([inner_sum, gate_parts.reshape(inner_sum.shape)], axis=0)
        entry_parts = entry_parts.reshape(2, groups, slice_rows, pieces, own)
        entry_out = entry_parts.transpose(2, 0, 3, 1, 4).reshape(slice_rows, entry_width)
        gain_out = jnp.sum(entry_out * entry_weight.astype(f32), axis=1)
    gain_out = gain_out / norm_gain.astype(f32)

    if paired:
        small_sum = small_sum + flipped(small_sum, "blk", 1)
        mine = lax.dynamic_slice_in_dim(small_sum, (piece & 1) * own, own, 1)
    else:
        split = small_grads.reshape(small_rows, pieces, own).transpose(1, 0, 2)
        came_small = lax.all_to_all(split, "blk", split_axis=0, concat_axis=0, tiled=True)
        mine = jnp.sum(came_small, axis=0)

    grad_hat = grad_keep[0].astype(f32) + grad_came[0].astype(f32) + grad_other.astype(f32)
    grad_hat = grad_hat * gain_all[0]
    root = lax.rsqrt(jnp.mean(residual * residual, axis=2, keepdims=True) + epsilon)
    hat_own = residual * root
    grad_input = root * (grad_hat - hat_own * jnp.mean(grad_hat * hat_own, axis=2, keepdims=True))
    input_grad = (cotangent.astype(f32) + grad_input).astype(bf16)
    return (
        block_out,
        input_grad,
        gain_out,
        entry_out,
        mine[176:180],
        mine[180],
        mine[64:160].T,
        mine[0:64],
        mine[181],
        mine[160:176],
        mine[182],
        exit_out,
    )


def solution(mesh):
    placed = (
        P(None, both, None),
        P(None, "blk"),
        P(None, both, None),
        P(both),
        P(both, None),
        P(None, both),
        P(both),
        P(both, None),
        P(None, both),
        P(both),
        P(None, both),
        P(both),
        P(both, None),
    )
    return jax.shard_map(
        local,
        mesh=mesh,
        in_specs=placed,
        out_specs=(
            P(None, both, None),
            P(None, both, None),
            P(both),
            P(both, None),
            P(None, both),
            P(both),
            P(both, None),
            P(None, both),
            P(both),
            P(None, both),
            P(both),
            P(both, None),
        ),
        check_vma=False,
    )
```

```python
import jax
import jax.numpy as jnp
from jax import lax
from jax.experimental import pallas as pl
from jax.experimental.pallas import tpu as pltpu
from jax.sharding import PartitionSpec as P

epsilon = 1e-05
log2_e = 1.4426950408889634
log_2 = 0.6931471805599453
reset_push = 1e6
f32 = jnp.float32
bf16 = jnp.bfloat16
small_rows = 192
both = ("blk", "grp")


def dot(left, right, dims=((1,), (0,))):
    return lax.dot_general(left, right, (dims, ((), ())), preferred_element_type=f32)


def sigmoid(values):
    return 1.0 / (1.0 + jnp.exp(-values))


def spread(block, axis):
    count = lax.axis_size(axis)
    copies = jnp.broadcast_to(block[None], (count,) + block.shape)
    return lax.all_to_all(copies, axis, split_axis=0, concat_axis=0, tiled=True)


def ordering(groups, sequences, me):
    chunks = groups * sequences
    rows = chunks * 8
    out_row = lax.broadcasted_iota(jnp.int32, (rows, rows), 0)
    in_row = lax.broadcasted_iota(jnp.int32, (rows, rows), 1)
    chunk = out_row % chunks
    wanted = (((chunk // sequences) ^ me) * sequences + chunk % sequences) * 8 + out_row // chunks
    return jnp.where(in_row == wanted, 1.0, 0.0).astype(bf16)


def kernel_call(body, micros, outs, scratch, limit, *operands, halves=None, free=False):
    whole = pl.BlockSpec(memory_space=pltpu.VMEM)
    kinds = [(value.shape, value.dtype) for value in operands] + list(outs)

    def place(index):
        shape, kind = kinds[index]
        if kind == jnp.int32:
            return pl.BlockSpec(memory_space=pltpu.SMEM)
        axis = halves[index] if halves else None
        if axis is None and free:
            return pl.BlockSpec(shape, lambda *_: (0,) * len(shape))
        if axis is None:
            return whole
        block = tuple(size // 2 if k == axis else size for k, size in enumerate(shape))
        return pl.BlockSpec(block, lambda half: tuple(half if k == axis else 0 for k in range(len(block))))

    places = [place(k) for k in range(len(kinds))]
    return pl.pallas_call(
        body,
        out_shape=[jax.ShapeDtypeStruct(shape, kind) for shape, kind in outs],
        grid=(2,) if halves else (),
        in_specs=places[: len(operands)],
        out_specs=places[len(operands) :],
        scratch_shapes=scratch,
        compiler_params=pltpu.CompilerParams(vmem_limit_bytes=limit << 20),
        cost_estimate=pl.CostEstimate(
            flops=micros * 1_150_000_000, bytes_accessed=8_000_000, transcendentals=0
        ),
    )(*operands)


def read_rows(slab_refs, block):
    sequences, _, width = slab_refs[0].shape
    at = pl.ds(pl.multiple_of(block * 8, 8), 8)
    parts = [slab[:, at, :].astype(f32) for slab in slab_refs]
    return jnp.concatenate(parts, axis=0).reshape(len(slab_refs) * sequences * 8, width)


def small_row(small_ref, index):
    tail = small_ref[176:192, :].astype(f32)
    return tail[index : index + 1, :]


def assemble(whole_ref, stacks, me):
    for side, stack_ref in enumerate(stacks):
        count = stack_ref.shape[0]
        rows = whole_ref.shape[0] // (2 * count)
        for k in range(count):
            target = pl.ds(pl.multiple_of((me ^ (2 * k + side)) * rows, 8), rows)
            whole_ref[target, :] = stack_ref[k, 0:rows, :]


def entry_kernel(
    place_ref, slab0_ref, slab1_ref, slab2_ref, slab3_ref, rim_ref, gain_ref, mask_ref, near_ref, far_ref, small_ref,
    normed_ref, inner_ref, filter_ref, chosen_ref, weight_ref,
):
    slabs = (slab0_ref, slab1_ref, slab2_ref, slab3_ref)
    groups = len(slabs)
    sequences, steps, width = slab0_ref.shape
    chunks = groups * sequences
    block_rows = chunks * 8
    inner_width = inner_ref.shape[1]
    order = ordering(groups, sequences, place_ref[1])
    assemble(weight_ref, (near_ref, far_ref), place_ref[0])

    def scaled(rows):
        root = lax.rsqrt(jnp.mean(rows * rows, axis=1, keepdims=True) + epsilon)
        return (rows * root * gain_ref[...]).astype(bf16)

    taps = [small_row(small_ref, k) for k in range(4)]
    offset = small_row(small_ref, 4)

    def norm_lap(block, carry):
        base = pl.multiple_of(block * block_rows, block_rows)
        normed = dot(order, scaled(read_rows(slabs, block))).astype(bf16)
        normed_ref[pl.ds(base, block_rows), :] = normed
        return carry

    lax.fori_loop(0, steps // 8, norm_lap, 0)
    inner_ref[3 * chunks :, :] = dot(normed_ref[...], weight_ref[...]).astype(bf16)
    last = inner_ref[steps * chunks :, :].astype(f32).reshape(3, chunks, inner_width)
    rim = dot(scaled(rim_ref[...].astype(f32)), weight_ref[...]).reshape(3, sequences, inner_width)
    rim = jnp.concatenate([rim, last[:, : chunks - sequences, :]], axis=1)
    inner_ref[0 : 3 * chunks, :] = rim.reshape(3 * chunks, inner_width).astype(bf16)

    def lap(block, carry):
        base = pl.multiple_of(block * block_rows, block_rows)
        total = offset
        for k in range(3):
            same = mask_ref[pl.ds(base, block_rows), k : k + 1]
            part = inner_ref[pl.ds(pl.multiple_of(base + k * chunks, 16), block_rows), :]
            total = total + taps[k] * part.astype(f32) * same
        inner = inner_ref[pl.ds(pl.multiple_of(base + 3 * chunks, 16), block_rows), :]
        total = total + taps[3] * inner.astype(f32)
        filtered = (total * sigmoid(total)).astype(bf16)
        filter_ref[pl.ds(base, block_rows), :] = filtered.astype(f32)
        chosen = dot(small_ref[64:160, :], filtered, ((1,), (1,)))
        chosen_ref[:, pl.ds(base, block_rows)] = chosen.astype(bf16)
        return carry

    lax.fori_loop(0, steps // 8, lap, 0)


def gate_kernel(
    place_ref, slab0_ref, slab1_ref, slab2_ref, slab3_ref, normed_ref, near_ref, far_ref, exit_near_ref, exit_far_ref,
    rows_ref, value_ref, slope_ref, grad_ref, weight_ref, exit_ref, gating_ref, gated_ref,
):
    slabs = (slab0_ref, slab1_ref, slab2_ref, slab3_ref)
    sequences, steps, width = slab0_ref.shape
    block_rows = len(slabs) * sequences * 8
    order = ordering(len(slabs), sequences, place_ref[1])
    assemble(weight_ref, (near_ref, far_ref), place_ref[0])
    assemble(exit_ref, (exit_near_ref, exit_far_ref), place_ref[0])

    def order_lap(block, carry):
        at = pl.ds(pl.multiple_of(block * block_rows, block_rows), block_rows)
        rows_ref[at, :] = dot(order, read_rows(slabs, block).astype(bf16)).astype(bf16)
        return carry

    lax.fori_loop(0, steps // 8, order_lap, 0)
    gating_ref[...] = dot(normed_ref[...], weight_ref[...])
    gated_ref[...] = dot(rows_ref[...], exit_ref[...], ((1,), (1,)))

    def lap(block, carry):
        at = pl.ds(pl.multiple_of(block * block_rows, block_rows), block_rows)
        gating = gating_ref[at, :]
        grad_gated = gated_ref[at, :]
        gate = sigmoid(gating)
        value = gating * gate
        value_ref[at, :] = value
        slope_ref[at, :] = grad_gated * (gate * (1.0 + gating * (1.0 - gate)))
        grad_ref[at, :] = (grad_gated * value).astype(bf16).astype(f32)
        return carry

    lax.fori_loop(0, steps // 8, lap, 0)


def fill_rates(small_ref, rates_ref):
    states = rates_ref.shape[0]
    rates = -jnp.exp(small_ref[160 : 160 + states, :].astype(f32)) * log2_e
    for n in range(states):
        rates_ref[n] = jnp.broadcast_to(rates[n : n + 1, :], rates_ref.shape[1:])


def fill_picks(pick_ref):
    depth, width = pick_ref.shape
    source = lax.broadcasted_iota(jnp.int32, (depth, width), 0) % (depth // 2)
    target = lax.broadcasted_iota(jnp.int32, (depth, width), 1) // 128
    pick_ref[...] = jnp.where(source == target, 1.0, 0.0).astype(bf16)


def fill_gates(gates_ref, pick_ref, spread_ref, at):
    steps = gates_ref.shape[0]
    values = gates_ref[:, at, :].reshape(steps * 8, 128)[:, 64:96]
    high = values.astype(bf16)
    rest = (values - high.astype(f32)).astype(bf16)
    pair = jnp.concatenate([high, rest], axis=1)
    span = 2048

    def lap(k, carry):
        columns = pl.ds(pl.multiple_of(k * span, span), span)
        spread_ref[:, columns] = dot(pair, pick_ref[:, columns])
        return carry

    lax.fori_loop(0, spread_ref.shape[1] // span, lap, 0)


def gate_of(spread_ref, t, n):
    return spread_ref[pl.ds(pl.multiple_of(t * 8, 8), 8), n * 128 : (n + 1) * 128]


def lane_slices(width):
    return [slice(k * 128, (k + 1) * 128) for k in range(width // 128)]


def piece_kernel(
    place_ref, chosen_ref, other_ref, mask_ref, small_ref, filter_ref, grad_ref,
    gates_ref, step_ref, slope_ref, end_ref, keep_ref, give_ref, load_ref,
    rates_ref, spread_ref, pick_ref, sum_ref, ahead_ref, back_ref,
):
    me = place_ref[0]
    steps, chunks, width = step_ref.shape
    states = end_ref.shape[0]
    chosen = chosen_ref[...].astype(f32) + other_ref[...].astype(f32)
    padded = jnp.concatenate([chosen, jnp.zeros((32, chosen.shape[1]), f32)], axis=0)
    gates_ref[...] = padded.T.reshape(steps, chunks, 128)
    fill_rates(small_ref, rates_ref)
    fill_picks(pick_ref)
    bias = small_row(small_ref, 5)
    delta = small_ref[0:64, :]

    def delta_lap(block, carry):
        at = pl.ds(pl.multiple_of(block * 8, 8), 8)
        low = gates_ref[at, :, :].reshape(8 * chunks, 128)[:, 0:64]
        high = low.astype(bf16)
        rest = (low - high.astype(f32)).astype(bf16)
        pre = dot(high, delta) + dot(rest, delta) + bias
        grown = jnp.exp(-jnp.abs(pre))
        step = jnp.maximum(pre, 0.0) + jnp.log1p(grown)
        step_ref[at, :, :] = step.reshape(8, chunks, width)
        slope_ref[at, :, :] = (jnp.where(pre >= 0, 1.0, grown) / (1.0 + grown)).reshape(8, chunks, width)
        return carry

    lax.fori_loop(0, steps // 8, delta_lap, 0)

    push = mask_ref[:, 3:4] * reset_push
    gates_ref[:, :, 96:97] = push.reshape(steps, chunks, 1)
    end_ref[...] = jnp.zeros_like(end_ref)
    give_ref[...] = jnp.zeros_like(give_ref)
    keep_ref[...] = jnp.ones_like(keep_ref)
    span = 4
    lanes = lane_slices(width)
    spots = [(j, i) for j in range(span) for i in range(len(lanes))]

    def half_lap(half, carry):
        at = pl.ds(pl.multiple_of(half * 8, 8), 8)
        fill_gates(gates_ref, pick_ref, spread_ref, at)

        def lap(block, totals):
            totals = list(totals)
            pushed, drives, grads = {}, {}, {}
            for j, i in spots:
                t = block * span + j
                step = step_ref[t, at, lanes[i]]
                push = step + gates_ref[t, at, 96:97]
                totals[i] = totals[i] + push
                pushed[j, i] = push
                drives[j, i] = step * filter_ref[t, at, lanes[i]]
                grads[j, i] = grad_ref[t, at, lanes[i]]
            for n in range(states):
                rate = [rates_ref[n, :, one] for one in lanes]
                end = [end_ref[n, at, one] for one in lanes]
                keep = [keep_ref[n, at, one] for one in lanes]
                give = [give_ref[n, at, one] for one in lanes]
                for j in range(span):
                    write = gate_of(spread_ref, block * span + j, n)
                    read = gate_of(spread_ref, block * span + j, states + n)
                    for i in range(len(lanes)):
                        decay = jnp.exp2(pushed[j, i] * rate[i])
                        end[i] = decay * end[i] + drives[j, i] * write
                        keep[i] = keep[i] * decay
                        give[i] = give[i] + keep[i] * (read * grads[j, i])
                for i, one in enumerate(lanes):
                    end_ref[n, at, one] = end[i]
                    keep_ref[n, at, one] = keep[i]
                    give_ref[n, at, one] = give[i]
            return tuple(totals)

        start = tuple(jnp.zeros((8, 128), f32) for _ in lanes)
        totals = lax.fori_loop(0, steps // span, lap, start)
        for i, one in enumerate(lanes):
            sum_ref[at, one] = totals[i]
        return carry

    lax.fori_loop(0, chunks // 8, half_lap, 0)

    sequences = ahead_ref.shape[0] // (states + 2)
    groups = chunks // sequences
    for n in range(states):
        rows = slice(n * sequences, (n + 1) * sequences)
        ahead = jnp.zeros((sequences, width), f32)
        back = jnp.zeros((sequences, width), f32)
        for k in range(groups):
            part = slice(k * sequences, (k + 1) * sequences)
            ahead = keep_ref[n, part, :] * ahead + end_ref[n, part, :]
            other = slice((groups - 1 - k) * sequences, (groups - k) * sequences)
            back = give_ref[n, other, :] + keep_ref[n, other, :] * back
        ahead_ref[rows, :] = ahead
        back_ref[rows, :] = back
    total = jnp.zeros((sequences, width), f32)
    for k in range(groups):
        total = total + sum_ref[k * sequences : (k + 1) * sequences, :]
    held = states * sequences
    for k in range(2):
        term = total.astype(bf16).astype(f32)
        ahead_ref[held + k * sequences : held + (k + 1) * sequences, :] = term
        total = total - term
    back_ref[held:, :] = ahead_ref[held:, :]

    def load_lap(piece, carry):
        load = jnp.where(piece > me, ahead_ref[...], back_ref[...])
        load_ref[piece] = load.astype(bf16)
        return carry

    lax.fori_loop(0, load_ref.shape[0], load_lap, 0)


def fill_unpicks(unpick_ref, first):
    spot = lax.broadcasted_iota(jnp.int32, unpick_ref.shape, 0) // 128
    column = lax.broadcasted_iota(jnp.int32, unpick_ref.shape, 1)
    unpick_ref[...] = jnp.where(column == spot + first, 1.0, 0.0).astype(bf16)


def forward_kernel(
    place_ref, came_ref, gates_ref, small_ref, step_ref, filter_ref, grad_ref, end_ref, keep_ref, give_ref,
    out_ref, read_sum_ref, start_ref, arrive_ref,
    rates_ref, spread_ref, pick_ref, product_ref, unpick_ref, passed_ref, whole_ref, enter_ref,
):
    me = place_ref[0]
    half = pl.program_id(0)
    steps, _, width = step_ref.shape
    states, chunks = end_ref.shape[:2]
    pieces = came_ref.shape[0]
    sequences = came_ref.shape[1] // (states + 2)
    groups = chunks // sequences
    @pl.when(half == 0)
    def _():
        fill_rates(small_ref, rates_ref)
        fill_picks(pick_ref)
        fill_unpicks(unpick_ref, 64 + states)
        rates_ref[states] = jnp.broadcast_to(small_row(small_ref, 6), (8, width))

        held = states * sequences
        rates = [jnp.broadcast_to(rates_ref[n, 0:1, :], (sequences, width)) for n in range(states)]
        rates = jnp.concatenate(rates, axis=0)

        def step_in(piece, state):
            values = came_ref[piece].astype(f32)
            total = values[held : held + sequences, :]
            total = total + values[held + sequences :, :]
            total = jnp.concatenate([total] * states, axis=0)
            return jnp.exp2(total * rates) * state + values[:held, :]

        def step_back(k, state):
            return step_in(pieces - 1 - k, state)

        zero = jnp.zeros((held, width), f32)
        whole_ref[0] = lax.fori_loop(0, me, step_in, zero)
        whole_ref[1] = lax.fori_loop(0, pieces - 1 - me, step_back, zero)
        for n in range(states):
            ahead = whole_ref[0, n * sequences : (n + 1) * sequences, :]
            back = whole_ref[1, n * sequences : (n + 1) * sequences, :]
            for k in range(groups):
                part = slice(k * sequences, (k + 1) * sequences)
                enter_ref[n, part, :] = ahead
                ahead = keep_ref[n, part, :] * ahead + end_ref[n, part, :]
                other = slice((groups - 1 - k) * sequences, (groups - k) * sequences)
                arrive_ref[n, other, :] = back
                back = give_ref[n, other, :] + keep_ref[n, other, :] * back

    span = 4
    lanes = lane_slices(width)
    spots = [(j, i) for j in range(span) for i in range(len(lanes))]

    fill_gates(gates_ref, pick_ref, spread_ref, slice(None))
    at = pl.ds(pl.multiple_of(half * 8, 8), 8)
    for n in range(states):
        for i, one in enumerate(lanes):
            passed_ref[n, i] = enter_ref[n, at, one]

    def forward(block, inner_carry):
        pushed, drives, grads, outs = {}, {}, {}, {}
        for j, i in spots:
            t = block * span + j
            step = step_ref[t, :, lanes[i]]
            feed = filter_ref[t, :, lanes[i]]
            pushed[j, i] = step + gates_ref[t, :, 96:97]
            drives[j, i] = step * feed
            grads[j, i] = grad_ref[t, :, lanes[i]]
            outs[j, i] = feed * rates_ref[states, :, lanes[i]]
        rows = pl.ds(pl.multiple_of(block * span * 8, span * 8), span * 8)
        for n in range(states):
            rate = [rates_ref[n, :, one] for one in lanes]
            hidden = [passed_ref[n, i] for i in range(len(lanes))]
            for i, one in enumerate(lanes):
                start_ref[block, n, :, one] = hidden[i]
            seen = []
            for j in range(span):
                t = block * span + j
                write = gate_of(spread_ref, t, n)
                read = gate_of(spread_ref, t, states + n)
                total = None
                for i in range(len(lanes)):
                    hidden[i] = jnp.exp2(pushed[j, i] * rate[i]) * hidden[i] + drives[j, i] * write
                    outs[j, i] = outs[j, i] + hidden[i] * read
                    one = grads[j, i] * hidden[i]
                    total = one if total is None else total + one
                seen.append(total)
            product_ref[rows, n * 128 : (n + 1) * 128] = jnp.concatenate(seen, axis=0).astype(bf16)
            for i in range(len(lanes)):
                passed_ref[n, i] = hidden[i]
        for j, i in spots:
            out_ref[block * span + j, :, lanes[i]] = outs[j, i]
        return inner_carry

    lax.fori_loop(0, steps // span, forward, 0)
    summed = dot(product_ref[...], unpick_ref[...])
    read_sum_ref[...] = summed.reshape(steps, 8, 128)


def backward_kernel(
    gates_ref, small_ref, step_ref, slope_ref, filter_ref, grad_ref, read_sum_ref, start_ref, arrive_ref,
    direct_ref, rank_ref, chosen_ref, decay_ref, skip_ref, bias_ref,
    rates_ref, spread_ref, pick_ref, product_ref, unpick_ref, delta_ref, sums_acc_ref,
    passed_ref, total_ref,
):
    half = pl.program_id(0)
    steps, _, width = step_ref.shape
    chunks = delta_ref.shape[1]
    blocks, states = start_ref.shape[:2]
    span = steps // blocks

    @pl.when(half == 0)
    def _():
        fill_rates(small_ref, rates_ref)
        fill_picks(pick_ref)
        fill_unpicks(unpick_ref, 64)
        decay_ref[...] = jnp.zeros_like(decay_ref)
        skip_ref[...] = jnp.zeros_like(skip_ref)
        rank_ref[...] = jnp.zeros_like(rank_ref)
        bias_ref[...] = jnp.zeros_like(bias_ref)
        rates_ref[states] = jnp.broadcast_to(small_row(small_ref, 6), (8, width))

    lanes = lane_slices(width)
    spots = [(j, i) for j in range(span) for i in range(len(lanes))]

    fill_gates(gates_ref, pick_ref, spread_ref, slice(None))
    at = pl.ds(pl.multiple_of(half * 8, 8), 8)
    for n in range(states):
        for i, one in enumerate(lanes):
            passed_ref[n, i] = arrive_ref[n, :, one]
            total_ref[n, i] = jnp.zeros((8, 128), f32)

    def backward(k, skips):
        block = blocks - 1 - k
        skips = list(skips)
        raw, feeds, pushed, drives, grads, weighted, slopes = {}, {}, {}, {}, {}, {}, {}
        for j, i in spots:
            t = block * span + j
            step = step_ref[t, :, lanes[i]]
            feed = filter_ref[t, :, lanes[i]]
            grad = grad_ref[t, :, lanes[i]]
            raw[j, i] = step
            feeds[j, i] = feed
            pushed[j, i] = step + gates_ref[t, :, 96:97]
            drives[j, i] = step * feed
            grads[j, i] = grad
            weighted[j, i] = jnp.zeros((8, 128), f32)
            slopes[j, i] = jnp.zeros((8, 128), f32)
            skips[i] = skips[i] + grad * feed
        rows = pl.ds(pl.multiple_of(block * span * 8, span * 8), span * 8)
        for n in range(states):
            rate = [rates_ref[n, :, one] for one in lanes]
            gone = [passed_ref[n, i] for i in range(len(lanes))]
            turns = [total_ref[n, i] for i in range(len(lanes))]
            hidden = [[start_ref[block, n, :, one] for one in lanes]]
            decays = []
            for j in range(span):
                decays.append([jnp.exp2(pushed[j, i] * rate[i]) for i in range(len(lanes))])
                if j < span - 1:
                    write = gate_of(spread_ref, block * span + j, n)
                    last = hidden[-1]
                    hidden.append(
                        [decays[j][i] * last[i] + drives[j, i] * write for i in range(len(lanes))]
                    )
            seen = [None] * span
            for j in reversed(range(span)):
                t = block * span + j
                write = gate_of(spread_ref, t, n)
                read = gate_of(spread_ref, t, states + n)
                for i in range(len(lanes)):
                    adjoint = read * grads[j, i] + gone[i]
                    weighted[j, i] = weighted[j, i] + adjoint * write
                    one = adjoint * drives[j, i]
                    seen[j] = one if seen[j] is None else seen[j] + one
                    gone[i] = adjoint * decays[j][i]
                    turn = gone[i] * hidden[j][i]
                    slopes[j, i] = slopes[j, i] + turn * rate[i]
                    turns[i] = turns[i] + turn * raw[j, i]
            product_ref[rows, n * 128 : (n + 1) * 128] = jnp.concatenate(seen, axis=0).astype(bf16)
            for i in range(len(lanes)):
                passed_ref[n, i] = gone[i]
                total_ref[n, i] = turns[i]
        for j, i in spots:
            t = block * span + j
            grown = slopes[j, i] * log_2 + weighted[j, i] * feeds[j, i]
            delta_ref[t, at, lanes[i]] = grown * slope_ref[t, :, lanes[i]]
            direct = weighted[j, i] * raw[j, i] + grads[j, i] * rates_ref[states, :, lanes[i]]
            direct_ref[t, :, lanes[i]] = direct
        return tuple(skips)

    start = tuple(jnp.zeros((8, 128), f32) for _ in lanes)
    skips = lax.fori_loop(0, blocks, backward, start)
    for i, one in enumerate(lanes):
        skip_ref[0:1, one] += jnp.sum(skips[i], axis=0, keepdims=True)
        for n in range(states):
            part = jnp.sum(total_ref[n, i], axis=0, keepdims=True)
            decay_ref[n : n + 1, one] += part * rates_ref[n, 0:1, one] * log_2
    summed = dot(product_ref[...], unpick_ref[...])
    sums_acc_ref[:, at, :] = summed.reshape(steps, 8, 128) + read_sum_ref[...]

    grads = delta_ref[:, at, :].reshape(steps * 8, width)
    bias_ref[...] += jnp.sum(grads, axis=0, keepdims=True)
    low = gates_ref[...].reshape(steps * 8, 128)[:, 0:64].astype(bf16)
    rank_ref[...] += dot(low, grads.astype(bf16), ((0,), (0,)))

    @pl.when(half == 1)
    def _():
        rows = steps * chunks
        whole = delta_ref[...].reshape(rows, width).astype(bf16)
        back = dot(small_ref[0:64, :], whole, ((1,), (1,)))
        sums = sums_acc_ref[...].reshape(rows, 128).T
        chosen_ref[0:64, :] = back.astype(bf16)
        chosen_ref[64:96, :] = sums[64:96, :].astype(bf16)


def store_rows(keep_ref, send_ref, order, values, block):
    _, sequences, _, width = keep_ref.shape
    back = dot(order, values.astype(bf16), ((0,), (0,)))
    shaped = back.reshape(4, sequences, 8, width).astype(bf16)
    at = pl.ds(pl.multiple_of(block * 8, 8), 8)
    for k in range(4):
        target = send_ref if k % 2 else keep_ref
        target[k // 2, :, at, :] = shaped[k]


def store_blocks(keep_ref, send_ref, me, *parts):
    count = keep_ref.shape[0]
    below = 0
    for values_ref in parts:
        rows = values_ref.shape[0] // (2 * count)
        for k in range(2 * count):
            source = pl.ds(pl.multiple_of((me ^ k) * rows, 8), rows)
            target = send_ref if k % 2 else keep_ref
            target[k // 2, below : below + rows, :] = values_ref[source, :].astype(bf16)
        below += rows


def leave_kernel(
    place_ref, scan_ref, value_ref, slope_ref, rows_ref, normed_ref, exit_near_ref, exit_far_ref,
    gating_ref, out_keep_ref, out_send_ref, exit_grad_ref, keep_ref, send_ref,
    gated_ref, entry_grad_ref, exit_ref, out_ref,
):
    assemble(exit_ref, (exit_near_ref, exit_far_ref), place_ref[0])
    sequences, steps = out_keep_ref.shape[1:3]
    groups = 4
    block_rows = groups * sequences * 8
    order = ordering(groups, sequences, place_ref[1])

    def lap(block, carry):
        at = pl.ds(pl.multiple_of(block * block_rows, block_rows), block_rows)
        scan_out = scan_ref[at, :].astype(bf16).astype(f32)
        gated = (scan_out * value_ref[at, :]).astype(bf16)
        gated_ref[at, :] = gated
        gating_ref[at, :] = (scan_out * slope_ref[at, :]).astype(bf16)
        return carry

    lax.fori_loop(0, steps // 8, lap, 0)
    span = 256

    def column_lap(block, carry):
        at = pl.ds(pl.multiple_of(block * span, span), span)
        out_ref[:, at] = dot(gated_ref[...], exit_ref[:, at]).astype(bf16)
        return carry

    lax.fori_loop(0, out_ref.shape[1] // span, column_lap, 0)

    def store_lap(block, carry):
        at = pl.ds(pl.multiple_of(block * block_rows, block_rows), block_rows)
        store_rows(out_keep_ref, out_send_ref, order, out_ref[at, :], block)
        return carry

    lax.fori_loop(0, steps // 8, store_lap, 0)
    exit_grad_ref[...] = dot(gated_ref[...], rows_ref[...], ((0,), (0,))).astype(bf16)
    entry_grad_ref[...] = dot(normed_ref[...], gating_ref[...], ((0,), (0,)))
    store_blocks(keep_ref, send_ref, place_ref[0], entry_grad_ref)


def filter_kernel(
    place_ref, chosen_ref, other_ref, direct_ref, inner_ref, filter_ref, mask_ref, small_ref,
    rank_ref, decay_ref, bias_ref, skip_ref, gate_keep_ref, gate_came_ref,
    back_ref, tail_ref, first_ref, small_out_ref, total_ref, *refs,
):
    part_refs, (packed_ref, picked_ref, taps_ref, offset_ref, grads_ref, past_ref) = refs[:-6], refs[-6:]
    rows, width = grads_ref.shape
    chunks, sequences = tail_ref.shape[1], first_ref.shape[1]
    rim_rows = 3 * chunks
    for k in range(3):
        past_ref[k, rows : rows + rim_rows, :] = jnp.zeros((rim_rows, width), f32)
    block_rows = chunks * 8
    chosen = (chosen_ref[...].astype(f32) + other_ref[...].astype(f32)).astype(bf16)
    packed_ref[0:64, :] = rank_ref[...]
    packed_ref[64:160, :] = dot(chosen, filter_ref[...].astype(bf16))
    packed_ref[160:176, :] = decay_ref[...]
    picked_ref[...] = chosen.astype(f32).T.astype(bf16)
    taps = [small_row(small_ref, k) for k in range(4)]
    offset = small_row(small_ref, 4)
    offset_ref[...] = jnp.zeros_like(offset_ref)
    taps_ref[...] = jnp.zeros_like(taps_ref)

    def lap(block, carry):
        base = pl.multiple_of(block * block_rows, block_rows)
        at = pl.ds(base, block_rows)
        total = offset
        shifted = []
        for k in range(4):
            part = inner_ref[pl.ds(pl.multiple_of(base + k * chunks, 16), block_rows), :].astype(f32)
            if k < 3:
                part = part * mask_ref[at, k : k + 1]
            shifted.append(part)
            total = total + taps[k] * part
        gate = sigmoid(total)
        grad = direct_ref[at, :] + dot(picked_ref[at, :], small_ref[64:160, :])
        grad = grad * (gate * (1.0 + total * (1.0 - gate)))
        grads_ref[at, :] = grad
        for k in range(3):
            past_ref[k, at, :] = grad * taps[k] * mask_ref[at, k : k + 1]
        offset_ref[...] += jnp.sum(grad, axis=0, keepdims=True)
        for k in range(4):
            taps_ref[k : k + 1, :] += jnp.sum(grad * shifted[k], axis=0, keepdims=True)
        return carry

    lax.fori_loop(0, rows // block_rows, lap, 0)
    packed_ref[176:180, :] = taps_ref[...]
    packed_ref[180:181, :] = offset_ref[...]
    packed_ref[181:182, :] = bias_ref[...]
    packed_ref[182:183, :] = skip_ref[...]
    packed_ref[183:192, :] = jnp.zeros((9, width), f32)
    small_out_ref[...] = packed_ref[...]
    height = gate_keep_ref.shape[1]
    below = (total_ref.shape[0] - height) * 4
    for k, target in enumerate((total_ref,) + part_refs):
        target[0:height, :] = (gate_keep_ref[k].astype(f32) + gate_came_ref[k].astype(f32)).astype(target.dtype)
        if below:
            lanes = pl.ds(pl.multiple_of(((place_ref[0] >> 1) ^ k) * 128, 128), 128)
            for q in range(4):
                values = packed_ref[q * below // 4 : (q + 1) * below // 4, lanes]
                target[height:, q * 128 : (q + 1) * 128] = values.astype(target.dtype)
    spills = []
    for u in range(3):
        total = jnp.zeros((chunks, width), f32)
        for t in range(u + 1):
            total = total + past_ref[u - t, t * chunks : (t + 1) * chunks, :]
        first_ref[u] = total[0:sequences, :]
        spills.append(jnp.concatenate([total[sequences:, :], jnp.zeros((sequences, width), f32)], axis=0))

    def back_lap(block, carry):
        base = pl.multiple_of(block * block_rows, block_rows)
        at = pl.ds(base, block_rows)
        total = grads_ref[at, :] * taps[3]
        for k in range(3):
            later = pl.ds(pl.multiple_of(base + (3 - k) * chunks, 16), block_rows)
            total = total + past_ref[k, later, :]
        back_ref[at, :] = total.astype(bf16)

        @pl.when(block == rows // block_rows - 1)
        def _():
            for u in range(3):
                first = block_rows - rim_rows + u * chunks
                tail_ref[u] = total[first : first + chunks, :] + spills[u]

        return carry

    lax.fori_loop(0, rows // block_rows, back_lap, 0)


def inner_kernel(back_ref, tail_ref, after_ref, normed_ref, inner_ref, entry_grad_ref):
    rows, width = back_ref.shape
    chunks, sequences = tail_ref.shape[1], after_ref.shape[1]
    rim_rows = 3 * chunks
    inner_ref[0 : rows - rim_rows, :] = back_ref[0 : rows - rim_rows, :]
    later = jnp.concatenate([jnp.zeros((3, chunks - sequences, width), f32), after_ref[...]], axis=1)
    tail = (tail_ref[...] + later).reshape(rim_rows, width)
    inner_ref[rows - rim_rows :, :] = tail.astype(bf16)
    entry_grad_ref[...] = dot(normed_ref[...], inner_ref[...], ((0,), (0,))).astype(bf16)


def normed_kernel(
    place_ref, inner_ref, gating_ref, near_ref, far_ref, gate_near_ref, gate_far_ref,
    out_keep_ref, out_send_ref,
    weight_ref, gate_weight_ref, grad_ref,
):
    assemble(weight_ref, (near_ref, far_ref), place_ref[0])
    assemble(gate_weight_ref, (gate_near_ref, gate_far_ref), place_ref[0])
    sequences, steps = out_keep_ref.shape[1:3]
    groups = 4
    block_rows = groups * sequences * 8
    order = ordering(groups, sequences, place_ref[1])

    span = 256

    def column_lap(block, carry):
        at = pl.ds(pl.multiple_of(block * span, span), span)
        grad = dot(inner_ref[...], weight_ref[at, :], ((1,), (1,)))
        grad = grad + dot(gating_ref[...], gate_weight_ref[at, :], ((1,), (1,)))
        grad_ref[:, at] = grad.astype(bf16)
        return carry

    lax.fori_loop(0, grad_ref.shape[1] // span, column_lap, 0)

    def lap(block, carry):
        at = pl.ds(pl.multiple_of(block * block_rows, block_rows), block_rows)
        store_rows(out_keep_ref, out_send_ref, order, grad_ref[at, :], block)
        return carry

    lax.fori_loop(0, steps // 8, lap, 0)


def side_sum_kernel(place_ref, total_ref, *refs):
    part_refs, out_refs, small_ref = refs[:-5], refs[-5:-1], refs[-1]
    total = total_ref[...]
    for part_ref in part_refs:
        total = total + part_ref[...].astype(f32)
    rows = out_refs[0].shape[0]
    for k, out_ref in enumerate(out_refs):
        block = total[0:rows, :]
        for j in range(1, len(out_refs)):
            block = jnp.where((place_ref[1] ^ k) == j, total[j * rows : (j + 1) * rows, :], block)
        out_ref[...] = block.astype(bf16)
    height = rows * len(out_refs)
    below = total.shape[0] - height
    if below:
        for q in range(4):
            small_ref[q * below : (q + 1) * below, :] = total[height:, q * 128 : (q + 1) * 128]
    else:
        small_ref[...] = jnp.zeros_like(small_ref)


def input_kernel(keep_ref, came_ref, other_ref, tokens_ref, cotangent_ref, gain_ref, out_ref):
    grad_hat = keep_ref[0].astype(f32) + came_ref[0].astype(f32) + other_ref[...].astype(f32)
    grad_hat = grad_hat * gain_ref[...]
    rows = tokens_ref[...].astype(f32)
    root = lax.rsqrt(jnp.mean(rows * rows, axis=2, keepdims=True) + epsilon)
    hat = rows * root
    grad = root * (grad_hat - hat * jnp.mean(grad_hat * hat, axis=2, keepdims=True))
    out_ref[...] = (cotangent_ref[...].astype(f32) + grad).astype(bf16)


def interleave_kernel(place_ref, weight_ref, inner_ref, gate0_ref, gate1_ref, gate2_ref, gate3_ref, out_ref, gain_ref):
    gate_refs = (gate0_ref, gate1_ref, gate2_ref, gate3_ref)
    pieces, groups, rows, width = inner_ref.shape
    for k in range(groups):
        inner = inner_ref[0, k].astype(f32)
        for piece in range(1, pieces):
            inner = inner + inner_ref[piece, k].astype(f32)
        gate = gate_refs[0][...].astype(f32)
        for m in range(1, groups):
            gate = jnp.where((place_ref[1] ^ m) == k, gate_refs[m][...].astype(f32), gate)
        for half, values in enumerate((inner, gate)):
            for j in range(width // 64):
                column = half * groups * width + (j * groups + k) * 64
                out_ref[:, column : column + 64] = values[:, j * 64 : (j + 1) * 64]
    total = jnp.sum(out_ref[...] * weight_ref[...].astype(f32), axis=1, keepdims=True)
    gain_ref[...] = jnp.broadcast_to(total, gain_ref.shape)


def local(
    tokens,
    segments,
    cotangent,
    norm_gain,
    entry_weight,
    kernel_weight,
    kernel_offset,
    select_weight,
    delta_weight,
    timestep_bias,
    decay_log,
    skip_gain,
    exit_weight,
):
    sequences, steps, width = tokens.shape
    pieces, groups = lax.axis_size("blk"), lax.axis_size("grp")
    piece, group = lax.axis_index("blk"), lax.axis_index("grp")
    place = jnp.stack([piece, group]).astype(jnp.int32)
    chunks = groups * sequences
    rows = steps * chunks
    slice_rows, entry_width = entry_weight.shape
    own = kernel_offset.shape[0]
    inner_width = entry_width // 2
    group_width = inner_width // groups
    states = decay_log.shape[0]
    rank = delta_weight.shape[0]

    def flipped(value, axis, bits):
        return lax.ppermute(value, axis, [(i, i ^ bits) for i in range(lax.axis_size(axis))])

    def after(value, *others):
        return lax.optimization_barrier((value,) + others)[0]

    def rounds(*values):
        return lax.optimization_barrier(values)

    packed = jnp.concatenate(
        [
            delta_weight,
            select_weight.T,
            decay_log,
            kernel_weight,
            kernel_offset[None],
            timestep_bias[None],
            skip_gain[None],
            jnp.zeros((small_rows - 183, own), bf16),
        ],
        axis=0,
    )
    def side_blocks(block):
        return [block] + [flipped(block, "blk", 2 * k) for k in range(1, pieces // 2)]

    place_of_gain = (piece * groups + group) * slice_rows
    gain_line = lax.dynamic_update_slice_in_dim(jnp.zeros((width,), bf16), norm_gain, place_of_gain, 0)
    gain_line = jnp.pad(gain_line.reshape(1, -1, group_width), ((0, 0), (0, 8 - width // group_width), (0, 0)))
    halves = entry_weight.reshape(slice_rows, 2, pieces, groups, own).transpose(3, 1, 0, 2, 4)
    halves = halves.reshape(groups, 2 * slice_rows, group_width)
    halves = jnp.concatenate([halves, jnp.broadcast_to(gain_line, (groups,) + gain_line.shape[1:])], axis=1)
    exit_block = jnp.concatenate([exit_weight, jnp.pad(packed.reshape(-1), (0, -packed.size % (16 * width))).reshape(-1, width)])
    halves, exit_block, tokens = rounds(halves, exit_block, tokens)
    halves = lax.all_to_all(halves, "grp", split_axis=0, concat_axis=0, tiled=True)
    exit_side = side_blocks(exit_block)
    token_pair = flipped(tokens, "grp", 2)
    halves, token_pair, tokens, *exit_side = rounds(halves, token_pair, tokens, *exit_side)

    gain_rows = jnp.sum(halves[:, 2 * slice_rows :].astype(f32), axis=0).astype(bf16)
    inner_block = halves[:, :slice_rows].reshape(groups * slice_rows, group_width)
    inner_block = jnp.concatenate([inner_block, gain_rows])
    gate_block = halves[:, slice_rows : 2 * slice_rows].reshape(groups * slice_rows, group_width)
    inner_side = side_blocks(inner_block)
    exit_near = jnp.stack(exit_side)
    exit_far = flipped(exit_near, "blk", 1)
    token_slabs = (tokens, flipped(tokens, "grp", 1), token_pair, flipped(token_pair, "grp", 1))
    exit_near, exit_far, gate_block, cotangent, *rest = rounds(
        exit_near, exit_far, gate_block, cotangent, *inner_side, *token_slabs
    )
    inner_side, token_slabs = rest[: pieces // 2], rest[pieces // 2 :]
    small = jnp.stack([exit_near[:, own:], exit_far[:, own:]], axis=1).reshape(pieces, -1)[:, : packed.size]
    bits = pieces.bit_length() - 1
    small = small.reshape((2,) * bits + (small_rows, own))
    for k in range(bits):
        small = jnp.where((piece >> (bits - 1 - k)) & 1, jnp.flip(small, k), small)
    small = small.reshape(pieces, small_rows, own).transpose(1, 0, 2).reshape(small_rows, group_width)

    inner_near = jnp.stack(inner_side)
    ahead = [(i, i + 1) for i in range(pieces - 1)]
    behind = [(i + 1, i) for i in range(pieces - 1)]
    tails = jnp.stack([slab[:, steps - 3 :] for slab in token_slabs])
    tail = lax.dynamic_index_in_dim(tails, group ^ (groups - 1), 0, keepdims=False)
    rim_source = tail.transpose(1, 0, 2).reshape(3 * sequences, width)
    rim = lax.ppermute(rim_source, "blk", ahead)
    inner_far = flipped(inner_near, "blk", 1)
    gate_block, cotangent = rounds(gate_block, cotangent, inner_near, rim_source)[:2]
    gate_side = side_blocks(gate_block)
    cotangent_pair = flipped(cotangent, "grp", 2)
    label_tail = lax.ppermute(segments[:, -3:], "blk", ahead)
    labels = jnp.concatenate([label_tail, segments], axis=1)
    length = segments.shape[1]
    shifted = jnp.stack([labels[:, k : k + length] for k in range(3)], axis=-1)
    same = (shifted == segments[:, :, None]).astype(f32)
    columns = jnp.concatenate([same, 1.0 - same[:, :, 2:3]], axis=2)
    mask = columns.reshape(sequences, groups, steps, 4).transpose(2, 1, 0, 3).reshape(rows, 4)
    gain_all = jnp.sum(inner_near[:, -8:].astype(f32), axis=0) + jnp.sum(inner_far[:, -8:].astype(f32), axis=0)
    gain_all = gain_all[: width // group_width].reshape(1, width)

    gate_near = jnp.stack(gate_side)
    gate_far = flipped(gate_near, "blk", 1)
    cotangent_slabs = (
        cotangent,
        flipped(cotangent, "grp", 1),
        cotangent_pair,
        flipped(cotangent_pair, "grp", 1),
    )

    def group_sum(value):
        half = value.astype(f32) + flipped(value, "grp", 1).astype(f32)
        half = half.astype(bf16)
        return half, flipped(half, "grp", 2)

    normed, inner, filtered, chosen = kernel_call(
        entry_kernel,
        9,
        [
            ((rows, width), bf16),
            ((rows + 3 * chunks, group_width), bf16),
            ((rows, group_width), f32),
            ((96, rows), bf16),
        ],
        [pltpu.VMEM((width, group_width), bf16)],
        12,
        place, *token_slabs, rim, gain_all, mask, inner_near, inner_far, small,
    )
    chosen_pair = group_sum(chosen)
    cotangent_rows, gate_value, gate_slope, grad_scan = kernel_call(
        gate_kernel,
        8,
        [
            ((rows, width), bf16),
            ((rows, group_width), f32),
            ((rows, group_width), f32),
            ((rows, group_width), f32),
        ],
        [
            pltpu.VMEM((width, group_width), bf16),
            pltpu.VMEM((group_width, width), bf16),
            pltpu.VMEM((rows, group_width), f32),
            pltpu.VMEM((rows, group_width), f32),
        ],
        16,
        place, *cotangent_slabs, normed, gate_near, gate_far, exit_near, exit_far,
    )
    cube = (steps, chunks, group_width)
    bank = (states, chunks, group_width)
    load_rows = (states + 2) * sequences
    gates, step_sizes, step_slopes, ends, keeps, gives, loads = kernel_call(
        piece_kernel,
        23,
        [
            ((steps, chunks, 128), f32),
            (cube, f32),
            (cube, f32),
            (bank, f32),
            (bank, f32),
            (bank, f32),
            ((pieces, load_rows, group_width), bf16),
        ],
        [
            pltpu.VMEM((states, 8, group_width), f32),
            pltpu.VMEM((steps * 8, 2 * states * 128), f32),
            pltpu.VMEM((4 * states, 2 * states * 128), bf16),
            pltpu.VMEM((chunks, group_width), f32),
            pltpu.VMEM((load_rows, group_width), f32),
            pltpu.VMEM((load_rows, group_width), f32),
        ],
        16,
        place, *chosen_pair, mask, small, filtered.reshape(cube), grad_scan.reshape(cube),
    )
    came = lax.all_to_all(loads, "blk", split_axis=0, concat_axis=0, tiled=True)

    lanes = group_width // 128
    gate_scratch = [
        pltpu.VMEM((states + 1, 8, group_width), f32),
        pltpu.VMEM((steps * 8, 2 * states * 128), f32),
        pltpu.VMEM((4 * states, 2 * states * 128), bf16),
    ]
    product_scratch = [pltpu.VMEM((steps * 8, states * 128), bf16), pltpu.VMEM((states * 128, 128), bf16)]
    starts = (steps // 4, states, chunks, group_width)
    scan_out, read_sums, block_starts, arrive = kernel_call(
        forward_kernel,
        18,
        [(cube, f32), ((steps, chunks, 128), f32), (starts, f32), (bank, f32)],
        gate_scratch
        + product_scratch
        + [pltpu.VMEM((states, lanes, 8, 128), f32), pltpu.VMEM((2, states * sequences, group_width), f32), pltpu.VMEM(bank, f32)],
        36,
        place, came, gates, small, step_sizes, filtered.reshape(cube), grad_scan.reshape(cube), ends, keeps, gives,
        halves=(None, None, 1, None, 1, 1, 1) + (None,) * 3 + (1, 1, 2, None),
    )
    half_slabs = ((2, sequences, steps, width), bf16)
    block_height = groups * slice_rows
    entry_half = ((pieces // 2, block_height, group_width), bf16)
    grad_gating, out_keep, out_send, exit_grad, gate_keep, gate_send = kernel_call(
        leave_kernel,
        12,
        [((rows, group_width), bf16), half_slabs, half_slabs, ((group_width, width), bf16), entry_half, entry_half],
        [
            pltpu.VMEM((rows, group_width), bf16),
            pltpu.VMEM((width, group_width), f32),
            pltpu.VMEM((group_width, width), bf16),
            pltpu.VMEM((rows, width), bf16),
        ],
        14,
        place, scan_out.reshape(rows, group_width), gate_value, gate_slope, cotangent_rows, normed, exit_near, exit_far,
    )

    exit_parts = lax.all_to_all(
        exit_grad.reshape(pieces, own, width), "blk", split_axis=0, concat_axis=0, tiled=True
    )
    gate_came = flipped(gate_send, "blk", 1)
    out_came = flipped(out_send, "grp", 1)
    grad_direct, rank_grad, chosen_grad, decay_grad, skip_grad, bias_grad = kernel_call(
        backward_kernel,
        35,
        [
            (cube, f32),
            ((rank, group_width), f32),
            ((96, rows), bf16),
            ((states, group_width), f32),
            ((1, group_width), f32),
            ((1, group_width), f32),
        ],
        gate_scratch
        + product_scratch
        + [
            pltpu.VMEM(cube, f32),
            pltpu.VMEM((steps, chunks, 128), f32),
            pltpu.VMEM((states, lanes, 8, 128), f32),
            pltpu.VMEM((states, lanes, 8, 128), f32),
        ],
        50,
        gates, small, step_sizes, step_slopes, filtered.reshape(cube), after(grad_scan, out_send).reshape(cube),
        read_sums, block_starts, arrive,
        halves=(1, None, 1, 1, 1, 1, 1, 2, 1, 1) + (None,) * 5,
    )
    chosen_grad, exit_parts, gate_came, out_came = rounds(chosen_grad, exit_parts, gate_came, out_came)
    chosen_grads = group_sum(chosen_grad)

    def slab_part(keep, came):
        return (keep[1].astype(f32) + came[1].astype(f32)).astype(bf16)

    exit_out = jnp.sum(after(exit_parts, chosen_grads[0]).astype(f32), axis=0)
    grad_direct, exit_out = rounds(grad_direct, exit_out)
    out_part = after(slab_part(out_keep, out_came), chosen_grads[0])
    out_other = flipped(out_part, "grp", 2)

    paired = 2 * own == 128
    side_block = (block_height + (small_rows // 4 if paired else 0), group_width)
    grad_back, tail_back, first_spill, small_grads, side_total, *side_parts = kernel_call(
        filter_kernel,
        6,
        [
            ((rows, group_width), bf16),
            ((3, chunks, group_width), f32),
            ((3, sequences, group_width), f32),
            ((small_rows, group_width), f32),
            (side_block, f32),
        ]
        + [(side_block, bf16)] * (pieces // 2 - 1),
        [
            pltpu.VMEM((small_rows, group_width), f32),
            pltpu.VMEM((rows, 96), bf16),
            pltpu.VMEM((4, group_width), f32),
            pltpu.VMEM((1, group_width), f32),
            pltpu.VMEM((rows, group_width), f32),
            pltpu.VMEM((3, rows + 3 * chunks, group_width), f32),
        ],
        62,
        place, *chosen_grads, grad_direct.reshape(rows, group_width), inner, filtered, mask, small,
        rank_grad, decay_grad, bias_grad, skip_grad, gate_keep, gate_came,
        free=True,
    )
    spill_after = lax.ppermute(first_spill, "blk", behind)
    side_parts = [flipped(part, "blk", 2 * k + 2) for k, part in enumerate(side_parts)]
    grad_inner, inner_entry = kernel_call(
        inner_kernel,
        4,
        [((rows, group_width), bf16), ((width, group_width), bf16)],
        [],
        12,
        grad_back, tail_back, spill_after, normed,
    )
    grad_inner, inner_entry, out_other = rounds(grad_inner, inner_entry, out_other)
    inner_parts = lax.all_to_all(
        inner_entry.reshape(pieces * groups, slice_rows, group_width), both, split_axis=0, concat_axis=0, tiled=True
    )
    grad_keep, grad_send = kernel_call(
        normed_kernel,
        10,
        [half_slabs, half_slabs],
        [
            pltpu.VMEM((width, group_width), bf16),
            pltpu.VMEM((width, group_width), bf16),
            pltpu.VMEM((rows, width), bf16),
        ],
        14,
        place, grad_inner, grad_gating, inner_near, inner_far, gate_near, gate_far,
    )
    grad_send, *side_parts = rounds(grad_send, *side_parts)
    grad_came = flipped(grad_send, "grp", 1)
    grad_part = slab_part(grad_keep, grad_came)
    grad_other = flipped(grad_part, "grp", 2)
    *gate_blocks, small_sum = kernel_call(
        side_sum_kernel,
        2,
        [((slice_rows, group_width), bf16)] * groups + [((small_rows, 128), f32)],
        [],
        16,
        place, after(side_total, grad_part), *side_parts,
    )
    gate_blocks = [gate_blocks[0]] + [flipped(gate_blocks[k], "grp", k) for k in range(1, groups)]
    residual = tokens.astype(f32)
    out_other, gate_blocks[3], small_sum = rounds(out_other, gate_blocks[3], small_sum)
    block_out = residual + out_keep[0].astype(f32) + out_came[0].astype(f32) + out_other.astype(f32)
    block_out = block_out.astype(bf16)
    inner_parts = inner_parts.reshape(pieces, groups, slice_rows, group_width)
    if own == 64:
        entry_out, gain_out = kernel_call(
            interleave_kernel,
            3,
            [((slice_rows, entry_width), f32), ((slice_rows, 128), f32)],
            [],
            16,
            place, entry_weight, inner_parts, *gate_blocks,
        )
        gain_out = gain_out[:, 0]
    else:
        inner_sum = jnp.sum(inner_parts.astype(f32), axis=0)
        gate_parts = jnp.stack(gate_blocks).astype(f32)
        for k in range(2):
            pairs = gate_parts.reshape(2, 2, slice_rows, group_width)
            gate_parts = jnp.where((group >> (1 - k)) & 1, jnp.flip(pairs, k), pairs)
        entry_parts = jnp.stack([inner_sum, gate_parts.reshape(inner_sum.shape)], axis=0)
        entry_parts = entry_parts.reshape(2, groups, slice_rows, pieces, own)
        entry_out = entry_parts.transpose(2, 0, 3, 1, 4).reshape(slice_rows, entry_width)
        gain_out = jnp.sum(entry_out * entry_weight.astype(f32), axis=1)
    gain_out = gain_out / norm_gain.astype(f32)

    if paired:
        small_sum = small_sum + flipped(small_sum, "blk", 1)
        mine = lax.dynamic_slice_in_dim(small_sum, (piece & 1) * own, own, 1)
    else:
        split = small_grads.reshape(small_rows, pieces, own).transpose(1, 0, 2)
        came_small = lax.all_to_all(split, "blk", split_axis=0, concat_axis=0, tiled=True)
        mine = jnp.sum(came_small, axis=0)

    input_grad = kernel_call(
        input_kernel,
        2,
        [((sequences, steps, width), bf16)],
        [],
        16,
        grad_keep, grad_came, after(grad_other, entry_out), tokens, cotangent, gain_all,
    )[0]
    return (
        block_out,
        input_grad,
        gain_out,
        entry_out,
        mine[176:180],
        mine[180],
        mine[64:160].T,
        mine[0:64],
        mine[181],
        mine[160:176],
        mine[182],
        exit_out,
    )


def solution(mesh):
    placed = (
        P(None, both, None),
        P(None, "blk"),
        P(None, both, None),
        P(both),
        P(both, None),
        P(None, both),
        P(both),
        P(both, None),
        P(None, both),
        P(both),
        P(None, both),
        P(both),
        P(both, None),
    )
    return jax.shard_map(
        local,
        mesh=mesh,
        in_specs=placed,
        out_specs=(
            P(None, both, None),
            P(None, both, None),
            P(both),
            P(both, None),
            P(None, both),
            P(both),
            P(both, None),
            P(None, both),
            P(both),
            P(None, both),
            P(both),
            P(both, None),
        ),
        check_vma=False,
    )
```

```python
import jax
import jax.numpy as jnp
from jax import lax
from jax.experimental import pallas as pl
from jax.experimental.pallas import tpu as pltpu
from jax.sharding import PartitionSpec as P

epsilon = 1e-05
log2_e = 1.4426950408889634
log_2 = 0.6931471805599453
reset_push = 1e6
f32 = jnp.float32
bf16 = jnp.bfloat16
small_rows = 192
both = ("blk", "grp")


def dot(left, right, dims=((1,), (0,))):
    return lax.dot_general(left, right, (dims, ((), ())), preferred_element_type=f32)


def sigmoid(values):
    return 1.0 / (1.0 + jnp.exp(-values))


def spread(block, axis):
    count = lax.axis_size(axis)
    copies = jnp.broadcast_to(block[None], (count,) + block.shape)
    return lax.all_to_all(copies, axis, split_axis=0, concat_axis=0, tiled=True)


def ordering(groups, sequences, me):
    chunks = groups * sequences
    rows = chunks * 8
    out_row = lax.broadcasted_iota(jnp.int32, (rows, rows), 0)
    in_row = lax.broadcasted_iota(jnp.int32, (rows, rows), 1)
    chunk = out_row % chunks
    wanted = (((chunk // sequences) ^ me) * sequences + chunk % sequences) * 8 + out_row // chunks
    return jnp.where(in_row == wanted, 1.0, 0.0).astype(bf16)


def kernel_call(body, micros, outs, scratch, limit, *operands, halves=None, free=False):
    whole = pl.BlockSpec(memory_space=pltpu.VMEM)
    kinds = [(value.shape, value.dtype) for value in operands] + list(outs)

    def place(index):
        shape, kind = kinds[index]
        if kind == jnp.int32:
            return pl.BlockSpec(memory_space=pltpu.SMEM)
        axis = halves[index] if halves else None
        if axis is None and free:
            return pl.BlockSpec(shape, lambda *_: (0,) * len(shape))
        if axis is None:
            return whole
        block = tuple(size // 2 if k == axis else size for k, size in enumerate(shape))
        return pl.BlockSpec(block, lambda half: tuple(half if k == axis else 0 for k in range(len(block))))

    places = [place(k) for k in range(len(kinds))]
    return pl.pallas_call(
        body,
        out_shape=[jax.ShapeDtypeStruct(shape, kind) for shape, kind in outs],
        grid=(2,) if halves else (),
        in_specs=places[: len(operands)],
        out_specs=places[len(operands) :],
        scratch_shapes=scratch,
        compiler_params=pltpu.CompilerParams(vmem_limit_bytes=limit << 20),
        cost_estimate=pl.CostEstimate(
            flops=micros * 1_150_000_000, bytes_accessed=8_000_000, transcendentals=0
        ),
    )(*operands)


def read_rows(slab_refs, block):
    sequences, _, width = slab_refs[0].shape
    at = pl.ds(pl.multiple_of(block * 8, 8), 8)
    parts = [slab[:, at, :].astype(f32) for slab in slab_refs]
    return jnp.concatenate(parts, axis=0).reshape(len(slab_refs) * sequences * 8, width)


def small_row(small_ref, index):
    tail = small_ref[176:192, :].astype(f32)
    return tail[index : index + 1, :]


def assemble(whole_ref, stacks, me):
    for side, stack_ref in enumerate(stacks):
        count = stack_ref.shape[0]
        rows = whole_ref.shape[0] // (2 * count)
        for k in range(count):
            target = pl.ds(pl.multiple_of((me ^ (2 * k + side)) * rows, 8), rows)
            whole_ref[target, :] = stack_ref[k, 0:rows, :]


def entry_kernel(
    place_ref, slab0_ref, slab1_ref, slab2_ref, slab3_ref, rim_ref, gain_ref, mask_ref, near_ref, far_ref, small_ref,
    normed_ref, inner_ref, filter_ref, chosen_ref, weight_ref,
):
    slabs = (slab0_ref, slab1_ref, slab2_ref, slab3_ref)
    groups = len(slabs)
    sequences, steps, width = slab0_ref.shape
    chunks = groups * sequences
    block_rows = chunks * 8
    inner_width = inner_ref.shape[1]
    order = ordering(groups, sequences, place_ref[1])
    assemble(weight_ref, (near_ref, far_ref), place_ref[0])

    def scaled(rows):
        root = lax.rsqrt(jnp.mean(rows * rows, axis=1, keepdims=True) + epsilon)
        return (rows * root * gain_ref[...]).astype(bf16)

    taps = [small_row(small_ref, k) for k in range(4)]
    offset = small_row(small_ref, 4)

    def norm_lap(block, carry):
        base = pl.multiple_of(block * block_rows, block_rows)
        normed = dot(order, scaled(read_rows(slabs, block))).astype(bf16)
        normed_ref[pl.ds(base, block_rows), :] = normed
        return carry

    lax.fori_loop(0, steps // 8, norm_lap, 0)
    inner_ref[3 * chunks :, :] = dot(normed_ref[...], weight_ref[...]).astype(bf16)
    last = inner_ref[steps * chunks :, :].astype(f32).reshape(3, chunks, inner_width)
    rim = dot(scaled(rim_ref[...].astype(f32)), weight_ref[...]).reshape(3, sequences, inner_width)
    rim = jnp.concatenate([rim, last[:, : chunks - sequences, :]], axis=1)
    inner_ref[0 : 3 * chunks, :] = rim.reshape(3 * chunks, inner_width).astype(bf16)

    def lap(block, carry):
        base = pl.multiple_of(block * block_rows, block_rows)
        total = offset
        for k in range(3):
            same = mask_ref[pl.ds(base, block_rows), k : k + 1]
            part = inner_ref[pl.ds(pl.multiple_of(base + k * chunks, 16), block_rows), :]
            total = total + taps[k] * part.astype(f32) * same
        inner = inner_ref[pl.ds(pl.multiple_of(base + 3 * chunks, 16), block_rows), :]
        total = total + taps[3] * inner.astype(f32)
        filtered = (total * sigmoid(total)).astype(bf16)
        filter_ref[pl.ds(base, block_rows), :] = filtered.astype(f32)
        chosen = dot(small_ref[64:160, :], filtered, ((1,), (1,)))
        chosen_ref[:, pl.ds(base, block_rows)] = chosen.astype(bf16)
        return carry

    lax.fori_loop(0, steps // 8, lap, 0)


def gate_kernel(
    place_ref, slab0_ref, slab1_ref, slab2_ref, slab3_ref, normed_ref, near_ref, far_ref, exit_near_ref, exit_far_ref,
    rows_ref, value_ref, slope_ref, grad_ref, weight_ref, exit_ref, gating_ref, gated_ref,
):
    slabs = (slab0_ref, slab1_ref, slab2_ref, slab3_ref)
    sequences, steps, width = slab0_ref.shape
    block_rows = len(slabs) * sequences * 8
    order = ordering(len(slabs), sequences, place_ref[1])
    assemble(weight_ref, (near_ref, far_ref), place_ref[0])
    assemble(exit_ref, (exit_near_ref, exit_far_ref), place_ref[0])

    def order_lap(block, carry):
        at = pl.ds(pl.multiple_of(block * block_rows, block_rows), block_rows)
        rows_ref[at, :] = dot(order, read_rows(slabs, block).astype(bf16)).astype(bf16)
        return carry

    lax.fori_loop(0, steps // 8, order_lap, 0)
    gating_ref[...] = dot(normed_ref[...], weight_ref[...])
    gated_ref[...] = dot(rows_ref[...], exit_ref[...], ((1,), (1,)))

    def lap(block, carry):
        at = pl.ds(pl.multiple_of(block * block_rows, block_rows), block_rows)
        gating = gating_ref[at, :]
        grad_gated = gated_ref[at, :]
        gate = sigmoid(gating)
        value = gating * gate
        value_ref[at, :] = value
        slope_ref[at, :] = grad_gated * (gate * (1.0 + gating * (1.0 - gate)))
        grad_ref[at, :] = (grad_gated * value).astype(bf16).astype(f32)
        return carry

    lax.fori_loop(0, steps // 8, lap, 0)


def fill_rates(small_ref, rates_ref):
    states = rates_ref.shape[0]
    rates = -jnp.exp(small_ref[160 : 160 + states, :].astype(f32)) * log2_e
    for n in range(states):
        rates_ref[n] = jnp.broadcast_to(rates[n : n + 1, :], rates_ref.shape[1:])


def fill_picks(pick_ref):
    depth, width = pick_ref.shape
    source = lax.broadcasted_iota(jnp.int32, (depth, width), 0) % (depth // 2)
    target = lax.broadcasted_iota(jnp.int32, (depth, width), 1) // 128
    pick_ref[...] = jnp.where(source == target, 1.0, 0.0).astype(bf16)


def fill_gates(gates_ref, pick_ref, spread_ref, at):
    steps = gates_ref.shape[0]
    values = gates_ref[:, at, :].reshape(steps * 8, 128)[:, 64:96]
    high = values.astype(bf16)
    rest = (values - high.astype(f32)).astype(bf16)
    pair = jnp.concatenate([high, rest], axis=1)
    span = 2048

    def lap(k, carry):
        columns = pl.ds(pl.multiple_of(k * span, span), span)
        spread_ref[:, columns] = dot(pair, pick_ref[:, columns])
        return carry

    lax.fori_loop(0, spread_ref.shape[1] // span, lap, 0)


def gate_of(spread_ref, t, n):
    return spread_ref[pl.ds(pl.multiple_of(t * 8, 8), 8), n * 128 : (n + 1) * 128]


def lane_slices(width):
    return [slice(k * 128, (k + 1) * 128) for k in range(width // 128)]


def piece_kernel(
    place_ref, chosen_ref, other_ref, mask_ref, small_ref, filter_ref, grad_ref,
    gates_ref, step_ref, slope_ref, end_ref, keep_ref, give_ref, load_ref,
    rates_ref, spread_ref, pick_ref, sum_ref, ahead_ref, back_ref,
):
    me = place_ref[0]
    steps, chunks, width = step_ref.shape
    states = end_ref.shape[0]
    chosen = chosen_ref[...].astype(f32) + other_ref[...].astype(f32)
    padded = jnp.concatenate([chosen, jnp.zeros((32, chosen.shape[1]), f32)], axis=0)
    gates_ref[...] = padded.T.reshape(steps, chunks, 128)
    fill_rates(small_ref, rates_ref)
    fill_picks(pick_ref)
    bias = small_row(small_ref, 5)
    delta = small_ref[0:64, :]

    def delta_lap(block, carry):
        at = pl.ds(pl.multiple_of(block * 8, 8), 8)
        low = gates_ref[at, :, :].reshape(8 * chunks, 128)[:, 0:64]
        high = low.astype(bf16)
        rest = (low - high.astype(f32)).astype(bf16)
        pre = dot(high, delta) + dot(rest, delta) + bias
        grown = jnp.exp(-jnp.abs(pre))
        step = jnp.maximum(pre, 0.0) + jnp.log1p(grown)
        step_ref[at, :, :] = step.reshape(8, chunks, width)
        slope_ref[at, :, :] = (jnp.where(pre >= 0, 1.0, grown) / (1.0 + grown)).reshape(8, chunks, width)
        return carry

    lax.fori_loop(0, steps // 8, delta_lap, 0)

    push = mask_ref[:, 3:4] * reset_push
    gates_ref[:, :, 96:97] = push.reshape(steps, chunks, 1)
    end_ref[...] = jnp.zeros_like(end_ref)
    give_ref[...] = jnp.zeros_like(give_ref)
    keep_ref[...] = jnp.ones_like(keep_ref)
    span = 4
    lanes = lane_slices(width)
    spots = [(j, i) for j in range(span) for i in range(len(lanes))]

    def half_lap(half, carry):
        at = pl.ds(pl.multiple_of(half * 8, 8), 8)
        fill_gates(gates_ref, pick_ref, spread_ref, at)

        def lap(block, totals):
            totals = list(totals)
            pushed, drives, grads = {}, {}, {}
            for j, i in spots:
                t = block * span + j
                step = step_ref[t, at, lanes[i]]
                push = step + gates_ref[t, at, 96:97]
                totals[i] = totals[i] + push
                pushed[j, i] = push
                drives[j, i] = step * filter_ref[t, at, lanes[i]]
                grads[j, i] = grad_ref[t, at, lanes[i]]
            for n in range(states):
                rate = [rates_ref[n, :, one] for one in lanes]
                end = [end_ref[n, at, one] for one in lanes]
                keep = [keep_ref[n, at, one] for one in lanes]
                give = [give_ref[n, at, one] for one in lanes]
                for j in range(span):
                    write = gate_of(spread_ref, block * span + j, n)
                    read = gate_of(spread_ref, block * span + j, states + n)
                    for i in range(len(lanes)):
                        decay = jnp.exp2(pushed[j, i] * rate[i])
                        end[i] = decay * end[i] + drives[j, i] * write
                        keep[i] = keep[i] * decay
                        give[i] = give[i] + keep[i] * (read * grads[j, i])
                for i, one in enumerate(lanes):
                    end_ref[n, at, one] = end[i]
                    keep_ref[n, at, one] = keep[i]
                    give_ref[n, at, one] = give[i]
            return tuple(totals)

        start = tuple(jnp.zeros((8, 128), f32) for _ in lanes)
        totals = lax.fori_loop(0, steps // span, lap, start)
        for i, one in enumerate(lanes):
            sum_ref[at, one] = totals[i]
        return carry

    lax.fori_loop(0, chunks // 8, half_lap, 0)

    sequences = ahead_ref.shape[0] // (states + 2)
    groups = chunks // sequences
    for n in range(states):
        rows = slice(n * sequences, (n + 1) * sequences)
        ahead = jnp.zeros((sequences, width), f32)
        back = jnp.zeros((sequences, width), f32)
        for k in range(groups):
            part = slice(k * sequences, (k + 1) * sequences)
            ahead = keep_ref[n, part, :] * ahead + end_ref[n, part, :]
            other = slice((groups - 1 - k) * sequences, (groups - k) * sequences)
            back = give_ref[n, other, :] + keep_ref[n, other, :] * back
        ahead_ref[rows, :] = ahead
        back_ref[rows, :] = back
    total = jnp.zeros((sequences, width), f32)
    for k in range(groups):
        total = total + sum_ref[k * sequences : (k + 1) * sequences, :]
    held = states * sequences
    for k in range(2):
        term = total.astype(bf16).astype(f32)
        ahead_ref[held + k * sequences : held + (k + 1) * sequences, :] = term
        total = total - term
    back_ref[held:, :] = ahead_ref[held:, :]

    def load_lap(piece, carry):
        load = jnp.where(piece > me, ahead_ref[...], back_ref[...])
        load_ref[piece] = load.astype(bf16)
        return carry

    lax.fori_loop(0, load_ref.shape[0], load_lap, 0)


def fill_unpicks(unpick_ref, first):
    spot = lax.broadcasted_iota(jnp.int32, unpick_ref.shape, 0) // 128
    column = lax.broadcasted_iota(jnp.int32, unpick_ref.shape, 1)
    unpick_ref[...] = jnp.where(column == spot + first, 1.0, 0.0).astype(bf16)


def forward_kernel(
    place_ref, came_ref, gates_ref, small_ref, step_ref, filter_ref, grad_ref, end_ref, keep_ref, give_ref,
    out_ref, read_sum_ref, start_ref, arrive_ref,
    rates_ref, spread_ref, pick_ref, product_ref, unpick_ref, passed_ref, whole_ref, enter_ref,
):
    me = place_ref[0]
    half = pl.program_id(0)
    steps, _, width = step_ref.shape
    states, chunks = end_ref.shape[:2]
    pieces = came_ref.shape[0]
    sequences = came_ref.shape[1] // (states + 2)
    groups = chunks // sequences
    @pl.when(half == 0)
    def _():
        fill_rates(small_ref, rates_ref)
        fill_picks(pick_ref)
        fill_unpicks(unpick_ref, 64 + states)
        rates_ref[states] = jnp.broadcast_to(small_row(small_ref, 6), (8, width))

        held = states * sequences
        rates = [jnp.broadcast_to(rates_ref[n, 0:1, :], (sequences, width)) for n in range(states)]
        rates = jnp.concatenate(rates, axis=0)

        def step_in(piece, state):
            values = came_ref[piece].astype(f32)
            total = values[held : held + sequences, :]
            total = total + values[held + sequences :, :]
            total = jnp.concatenate([total] * states, axis=0)
            return jnp.exp2(total * rates) * state + values[:held, :]

        def step_back(k, state):
            return step_in(pieces - 1 - k, state)

        zero = jnp.zeros((held, width), f32)
        whole_ref[0] = lax.fori_loop(0, me, step_in, zero)
        whole_ref[1] = lax.fori_loop(0, pieces - 1 - me, step_back, zero)
        for n in range(states):
            ahead = whole_ref[0, n * sequences : (n + 1) * sequences, :]
            back = whole_ref[1, n * sequences : (n + 1) * sequences, :]
            for k in range(groups):
                part = slice(k * sequences, (k + 1) * sequences)
                enter_ref[n, part, :] = ahead
                ahead = keep_ref[n, part, :] * ahead + end_ref[n, part, :]
                other = slice((groups - 1 - k) * sequences, (groups - k) * sequences)
                arrive_ref[n, other, :] = back
                back = give_ref[n, other, :] + keep_ref[n, other, :] * back

    span = 4
    lanes = lane_slices(width)
    spots = [(j, i) for j in range(span) for i in range(len(lanes))]

    fill_gates(gates_ref, pick_ref, spread_ref, slice(None))
    at = pl.ds(pl.multiple_of(half * 8, 8), 8)
    for n in range(states):
        for i, one in enumerate(lanes):
            passed_ref[n, i] = enter_ref[n, at, one]

    def forward(block, inner_carry):
        pushed, drives, grads, outs = {}, {}, {}, {}
        for j, i in spots:
            t = block * span + j
            step = step_ref[t, :, lanes[i]]
            feed = filter_ref[t, :, lanes[i]]
            pushed[j, i] = step + gates_ref[t, :, 96:97]
            drives[j, i] = step * feed
            grads[j, i] = grad_ref[t, :, lanes[i]]
            outs[j, i] = feed * rates_ref[states, :, lanes[i]]
        rows = pl.ds(pl.multiple_of(block * span * 8, span * 8), span * 8)
        for n in range(states):
            rate = [rates_ref[n, :, one] for one in lanes]
            hidden = [passed_ref[n, i] for i in range(len(lanes))]
            for i, one in enumerate(lanes):
                start_ref[block, n, :, one] = hidden[i]
            seen = []
            for j in range(span):
                t = block * span + j
                write = gate_of(spread_ref, t, n)
                read = gate_of(spread_ref, t, states + n)
                total = None
                for i in range(len(lanes)):
                    hidden[i] = jnp.exp2(pushed[j, i] * rate[i]) * hidden[i] + drives[j, i] * write
                    outs[j, i] = outs[j, i] + hidden[i] * read
                    one = grads[j, i] * hidden[i]
                    total = one if total is None else total + one
                seen.append(total)
            product_ref[rows, n * 128 : (n + 1) * 128] = jnp.concatenate(seen, axis=0).astype(bf16)
            for i in range(len(lanes)):
                passed_ref[n, i] = hidden[i]
        for j, i in spots:
            out_ref[block * span + j, :, lanes[i]] = outs[j, i]
        return inner_carry

    lax.fori_loop(0, steps // span, forward, 0)
    summed = dot(product_ref[...], unpick_ref[...])
    read_sum_ref[...] = summed.reshape(steps, 8, 128)


def backward_kernel(
    gates_ref, small_ref, step_ref, slope_ref, filter_ref, grad_ref, read_sum_ref, start_ref, arrive_ref,
    direct_ref, rank_ref, chosen_ref, decay_ref, skip_ref, bias_ref,
    rates_ref, spread_ref, pick_ref, product_ref, unpick_ref, delta_ref, sums_acc_ref,
    passed_ref, total_ref,
):
    half = pl.program_id(0)
    steps, _, width = step_ref.shape
    chunks = delta_ref.shape[1]
    blocks, states = start_ref.shape[:2]
    span = steps // blocks

    @pl.when(half == 0)
    def _():
        fill_rates(small_ref, rates_ref)
        fill_picks(pick_ref)
        fill_unpicks(unpick_ref, 64)
        decay_ref[...] = jnp.zeros_like(decay_ref)
        skip_ref[...] = jnp.zeros_like(skip_ref)
        rank_ref[...] = jnp.zeros_like(rank_ref)
        bias_ref[...] = jnp.zeros_like(bias_ref)
        rates_ref[states] = jnp.broadcast_to(small_row(small_ref, 6), (8, width))

    lanes = lane_slices(width)
    spots = [(j, i) for j in range(span) for i in range(len(lanes))]

    fill_gates(gates_ref, pick_ref, spread_ref, slice(None))
    at = pl.ds(pl.multiple_of(half * 8, 8), 8)
    for n in range(states):
        for i, one in enumerate(lanes):
            passed_ref[n, i] = arrive_ref[n, :, one]
            total_ref[n, i] = jnp.zeros((8, 128), f32)

    def backward(k, skips):
        block = blocks - 1 - k
        skips = list(skips)
        raw, feeds, pushed, drives, grads, weighted, slopes = {}, {}, {}, {}, {}, {}, {}
        for j, i in spots:
            t = block * span + j
            step = step_ref[t, :, lanes[i]]
            feed = filter_ref[t, :, lanes[i]]
            grad = grad_ref[t, :, lanes[i]]
            raw[j, i] = step
            feeds[j, i] = feed
            pushed[j, i] = step + gates_ref[t, :, 96:97]
            drives[j, i] = step * feed
            grads[j, i] = grad
            weighted[j, i] = jnp.zeros((8, 128), f32)
            slopes[j, i] = jnp.zeros((8, 128), f32)
            skips[i] = skips[i] + grad * feed
        rows = pl.ds(pl.multiple_of(block * span * 8, span * 8), span * 8)
        for n in range(states):
            rate = [rates_ref[n, :, one] for one in lanes]
            gone = [passed_ref[n, i] for i in range(len(lanes))]
            turns = [total_ref[n, i] for i in range(len(lanes))]
            hidden = [[start_ref[block, n, :, one] for one in lanes]]
            decays = []
            for j in range(span):
                decays.append([jnp.exp2(pushed[j, i] * rate[i]) for i in range(len(lanes))])
                if j < span - 1:
                    write = gate_of(spread_ref, block * span + j, n)
                    last = hidden[-1]
                    hidden.append(
                        [decays[j][i] * last[i] + drives[j, i] * write for i in range(len(lanes))]
                    )
            seen = [None] * span
            for j in reversed(range(span)):
                t = block * span + j
                write = gate_of(spread_ref, t, n)
                read = gate_of(spread_ref, t, states + n)
                for i in range(len(lanes)):
                    adjoint = read * grads[j, i] + gone[i]
                    weighted[j, i] = weighted[j, i] + adjoint * write
                    one = adjoint * drives[j, i]
                    seen[j] = one if seen[j] is None else seen[j] + one
                    gone[i] = adjoint * decays[j][i]
                    turn = gone[i] * hidden[j][i]
                    slopes[j, i] = slopes[j, i] + turn * rate[i]
                    turns[i] = turns[i] + turn * raw[j, i]
            product_ref[rows, n * 128 : (n + 1) * 128] = jnp.concatenate(seen, axis=0).astype(bf16)
            for i in range(len(lanes)):
                passed_ref[n, i] = gone[i]
                total_ref[n, i] = turns[i]
        for j, i in spots:
            t = block * span + j
            grown = slopes[j, i] * log_2 + weighted[j, i] * feeds[j, i]
            delta_ref[t, at, lanes[i]] = grown * slope_ref[t, :, lanes[i]]
            direct = weighted[j, i] * raw[j, i] + grads[j, i] * rates_ref[states, :, lanes[i]]
            direct_ref[t, :, lanes[i]] = direct
        return tuple(skips)

    start = tuple(jnp.zeros((8, 128), f32) for _ in lanes)
    skips = lax.fori_loop(0, blocks, backward, start)
    for i, one in enumerate(lanes):
        skip_ref[0:1, one] += jnp.sum(skips[i], axis=0, keepdims=True)
        for n in range(states):
            part = jnp.sum(total_ref[n, i], axis=0, keepdims=True)
            decay_ref[n : n + 1, one] += part * rates_ref[n, 0:1, one] * log_2
    summed = dot(product_ref[...], unpick_ref[...])
    sums_acc_ref[:, at, :] = summed.reshape(steps, 8, 128) + read_sum_ref[...]

    grads = delta_ref[:, at, :].reshape(steps * 8, width)
    bias_ref[...] += jnp.sum(grads, axis=0, keepdims=True)
    low = gates_ref[...].reshape(steps * 8, 128)[:, 0:64].astype(bf16)
    rank_ref[...] += dot(low, grads.astype(bf16), ((0,), (0,)))

    @pl.when(half == 1)
    def _():
        rows = steps * chunks
        whole = delta_ref[...].reshape(rows, width).astype(bf16)
        back = dot(small_ref[0:64, :], whole, ((1,), (1,)))
        sums = sums_acc_ref[...].reshape(rows, 128).T
        chosen_ref[0:64, :] = back.astype(bf16)
        chosen_ref[64:96, :] = sums[64:96, :].astype(bf16)


def store_rows(keep_ref, send_ref, order, values, block):
    _, sequences, _, width = keep_ref.shape
    back = dot(order, values.astype(bf16), ((0,), (0,)))
    shaped = back.reshape(4, sequences, 8, width).astype(bf16)
    at = pl.ds(pl.multiple_of(block * 8, 8), 8)
    for k in range(4):
        target = send_ref if k % 2 else keep_ref
        target[k // 2, :, at, :] = shaped[k]


def store_blocks(keep_ref, send_ref, me, *parts):
    count = keep_ref.shape[0]
    below = 0
    for values_ref in parts:
        rows = values_ref.shape[0] // (2 * count)
        for k in range(2 * count):
            source = pl.ds(pl.multiple_of((me ^ k) * rows, 8), rows)
            target = send_ref if k % 2 else keep_ref
            target[k // 2, below : below + rows, :] = values_ref[source, :].astype(bf16)
        below += rows


def leave_kernel(
    place_ref, scan_ref, value_ref, slope_ref, rows_ref, normed_ref, exit_near_ref, exit_far_ref,
    gating_ref, out_keep_ref, out_send_ref, exit_grad_ref, keep_ref, send_ref,
    gated_ref, entry_grad_ref, exit_ref, out_ref,
):
    assemble(exit_ref, (exit_near_ref, exit_far_ref), place_ref[0])
    sequences, steps = out_keep_ref.shape[1:3]
    groups = 4
    block_rows = groups * sequences * 8
    order = ordering(groups, sequences, place_ref[1])

    def lap(block, carry):
        at = pl.ds(pl.multiple_of(block * block_rows, block_rows), block_rows)
        scan_out = scan_ref[at, :].astype(bf16).astype(f32)
        gated = (scan_out * value_ref[at, :]).astype(bf16)
        gated_ref[at, :] = gated
        gating_ref[at, :] = (scan_out * slope_ref[at, :]).astype(bf16)
        return carry

    lax.fori_loop(0, steps // 8, lap, 0)
    span = 256

    def column_lap(block, carry):
        at = pl.ds(pl.multiple_of(block * span, span), span)
        out_ref[:, at] = dot(gated_ref[...], exit_ref[:, at]).astype(bf16)
        return carry

    lax.fori_loop(0, out_ref.shape[1] // span, column_lap, 0)

    def store_lap(block, carry):
        at = pl.ds(pl.multiple_of(block * block_rows, block_rows), block_rows)
        store_rows(out_keep_ref, out_send_ref, order, out_ref[at, :], block)
        return carry

    lax.fori_loop(0, steps // 8, store_lap, 0)
    exit_grad_ref[...] = dot(gated_ref[...], rows_ref[...], ((0,), (0,))).astype(bf16)
    entry_grad_ref[...] = dot(normed_ref[...], gating_ref[...], ((0,), (0,)))
    store_blocks(keep_ref, send_ref, place_ref[0], entry_grad_ref)


def filter_kernel(
    place_ref, chosen_ref, other_ref, direct_ref, inner_ref, filter_ref, mask_ref, small_ref,
    rank_ref, decay_ref, bias_ref, skip_ref, gate_keep_ref, gate_came_ref,
    back_ref, tail_ref, first_ref, small_out_ref, total_ref, *refs,
):
    part_refs, (packed_ref, picked_ref, taps_ref, offset_ref, grads_ref, past_ref) = refs[:-6], refs[-6:]
    rows, width = grads_ref.shape
    chunks, sequences = tail_ref.shape[1], first_ref.shape[1]
    rim_rows = 3 * chunks
    for k in range(3):
        past_ref[k, rows : rows + rim_rows, :] = jnp.zeros((rim_rows, width), f32)
    block_rows = chunks * 8
    chosen = (chosen_ref[...].astype(f32) + other_ref[...].astype(f32)).astype(bf16)
    packed_ref[0:64, :] = rank_ref[...]
    packed_ref[64:160, :] = dot(chosen, filter_ref[...].astype(bf16))
    packed_ref[160:176, :] = decay_ref[...]
    picked_ref[...] = chosen.astype(f32).T.astype(bf16)
    taps = [small_row(small_ref, k) for k in range(4)]
    offset = small_row(small_ref, 4)
    offset_ref[...] = jnp.zeros_like(offset_ref)
    taps_ref[...] = jnp.zeros_like(taps_ref)

    def lap(block, carry):
        base = pl.multiple_of(block * block_rows, block_rows)
        at = pl.ds(base, block_rows)
        total = offset
        shifted = []
        for k in range(4):
            part = inner_ref[pl.ds(pl.multiple_of(base + k * chunks, 16), block_rows), :].astype(f32)
            if k < 3:
                part = part * mask_ref[at, k : k + 1]
            shifted.append(part)
            total = total + taps[k] * part
        gate = sigmoid(total)
        grad = direct_ref[at, :] + dot(picked_ref[at, :], small_ref[64:160, :])
        grad = grad * (gate * (1.0 + total * (1.0 - gate)))
        grads_ref[at, :] = grad
        for k in range(3):
            past_ref[k, at, :] = grad * taps[k] * mask_ref[at, k : k + 1]
        offset_ref[...] += jnp.sum(grad, axis=0, keepdims=True)
        for k in range(4):
            taps_ref[k : k + 1, :] += jnp.sum(grad * shifted[k], axis=0, keepdims=True)
        return carry

    lax.fori_loop(0, rows // block_rows, lap, 0)
    packed_ref[176:180, :] = taps_ref[...]
    packed_ref[180:181, :] = offset_ref[...]
    packed_ref[181:182, :] = bias_ref[...]
    packed_ref[182:183, :] = skip_ref[...]
    packed_ref[183:192, :] = jnp.zeros((9, width), f32)
    small_out_ref[...] = packed_ref[...]
    height = gate_keep_ref.shape[1]
    below = (total_ref.shape[0] - height) * 4
    for k, target in enumerate((total_ref,) + part_refs):
        target[0:height, :] = (gate_keep_ref[k].astype(f32) + gate_came_ref[k].astype(f32)).astype(target.dtype)
        if below:
            lanes = pl.ds(pl.multiple_of(((place_ref[0] >> 1) ^ k) * 128, 128), 128)
            for q in range(4):
                values = packed_ref[q * below // 4 : (q + 1) * below // 4, lanes]
                target[height:, q * 128 : (q + 1) * 128] = values.astype(target.dtype)
    spills = []
    for u in range(3):
        total = jnp.zeros((chunks, width), f32)
        for t in range(u + 1):
            total = total + past_ref[u - t, t * chunks : (t + 1) * chunks, :]
        first_ref[u] = total[0:sequences, :]
        spills.append(jnp.concatenate([total[sequences:, :], jnp.zeros((sequences, width), f32)], axis=0))

    def back_lap(block, carry):
        base = pl.multiple_of(block * block_rows, block_rows)
        at = pl.ds(base, block_rows)
        total = grads_ref[at, :] * taps[3]
        for k in range(3):
            later = pl.ds(pl.multiple_of(base + (3 - k) * chunks, 16), block_rows)
            total = total + past_ref[k, later, :]
        back_ref[at, :] = total.astype(bf16)

        @pl.when(block == rows // block_rows - 1)
        def _():
            for u in range(3):
                first = block_rows - rim_rows + u * chunks
                tail_ref[u] = total[first : first + chunks, :] + spills[u]

        return carry

    lax.fori_loop(0, rows // block_rows, back_lap, 0)


def inner_kernel(back_ref, tail_ref, after_ref, normed_ref, inner_ref, entry_grad_ref):
    rows, width = back_ref.shape
    chunks, sequences = tail_ref.shape[1], after_ref.shape[1]
    rim_rows = 3 * chunks
    inner_ref[0 : rows - rim_rows, :] = back_ref[0 : rows - rim_rows, :]
    later = jnp.concatenate([jnp.zeros((3, chunks - sequences, width), f32), after_ref[...]], axis=1)
    tail = (tail_ref[...] + later).reshape(rim_rows, width)
    inner_ref[rows - rim_rows :, :] = tail.astype(bf16)
    entry_grad_ref[...] = dot(normed_ref[...], inner_ref[...], ((0,), (0,))).astype(bf16)


def normed_kernel(
    place_ref, inner_ref, gating_ref, near_ref, far_ref, gate_near_ref, gate_far_ref,
    out_keep_ref, out_send_ref,
    weight_ref, gate_weight_ref, grad_ref,
):
    assemble(weight_ref, (near_ref, far_ref), place_ref[0])
    assemble(gate_weight_ref, (gate_near_ref, gate_far_ref), place_ref[0])
    sequences, steps = out_keep_ref.shape[1:3]
    groups = 4
    block_rows = groups * sequences * 8
    order = ordering(groups, sequences, place_ref[1])

    span = 256

    def column_lap(block, carry):
        at = pl.ds(pl.multiple_of(block * span, span), span)
        grad = dot(inner_ref[...], weight_ref[at, :], ((1,), (1,)))
        grad = grad + dot(gating_ref[...], gate_weight_ref[at, :], ((1,), (1,)))
        grad_ref[:, at] = grad.astype(bf16)
        return carry

    lax.fori_loop(0, grad_ref.shape[1] // span, column_lap, 0)

    def lap(block, carry):
        at = pl.ds(pl.multiple_of(block * block_rows, block_rows), block_rows)
        store_rows(out_keep_ref, out_send_ref, order, grad_ref[at, :], block)
        return carry

    lax.fori_loop(0, steps // 8, lap, 0)


def side_sum_kernel(place_ref, total_ref, *refs):
    part_refs, out_refs, small_ref = refs[:-5], refs[-5:-1], refs[-1]
    total = total_ref[...]
    for part_ref in part_refs:
        total = total + part_ref[...].astype(f32)
    rows = out_refs[0].shape[0]
    for k, out_ref in enumerate(out_refs):
        block = total[0:rows, :]
        for j in range(1, len(out_refs)):
            block = jnp.where((place_ref[1] ^ k) == j, total[j * rows : (j + 1) * rows, :], block)
        out_ref[...] = block.astype(bf16)
    height = rows * len(out_refs)
    below = total.shape[0] - height
    if below:
        for q in range(4):
            small_ref[q * below : (q + 1) * below, :] = total[height:, q * 128 : (q + 1) * 128]
    else:
        small_ref[...] = jnp.zeros_like(small_ref)


def input_kernel(keep_ref, came_ref, other_ref, tokens_ref, cotangent_ref, gain_ref, out_ref):
    grad_hat = keep_ref[0].astype(f32) + came_ref[0].astype(f32) + other_ref[...].astype(f32)
    grad_hat = grad_hat * gain_ref[...]
    rows = tokens_ref[...].astype(f32)
    root = lax.rsqrt(jnp.mean(rows * rows, axis=2, keepdims=True) + epsilon)
    hat = rows * root
    grad = root * (grad_hat - hat * jnp.mean(grad_hat * hat, axis=2, keepdims=True))
    out_ref[...] = (cotangent_ref[...].astype(f32) + grad).astype(bf16)


def interleave_kernel(place_ref, weight_ref, inner_ref, gate0_ref, gate1_ref, gate2_ref, gate3_ref, out_ref, gain_ref):
    gate_refs = (gate0_ref, gate1_ref, gate2_ref, gate3_ref)
    pieces, groups, rows, width = inner_ref.shape
    for k in range(groups):
        inner = inner_ref[0, k].astype(f32)
        for piece in range(1, pieces):
            inner = inner + inner_ref[piece, k].astype(f32)
        gate = gate_refs[0][...].astype(f32)
        for m in range(1, groups):
            gate = jnp.where((place_ref[1] ^ m) == k, gate_refs[m][...].astype(f32), gate)
        for half, values in enumerate((inner, gate)):
            for j in range(width // 64):
                column = half * groups * width + (j * groups + k) * 64
                out_ref[:, column : column + 64] = values[:, j * 64 : (j + 1) * 64]
    total = jnp.sum(out_ref[...] * weight_ref[...].astype(f32), axis=1, keepdims=True)
    gain_ref[...] = jnp.broadcast_to(total, gain_ref.shape)


def local(
    tokens,
    segments,
    cotangent,
    norm_gain,
    entry_weight,
    kernel_weight,
    kernel_offset,
    select_weight,
    delta_weight,
    timestep_bias,
    decay_log,
    skip_gain,
    exit_weight,
):
    sequences, steps, width = tokens.shape
    pieces, groups = lax.axis_size("blk"), lax.axis_size("grp")
    piece, group = lax.axis_index("blk"), lax.axis_index("grp")
    place = jnp.stack([piece, group]).astype(jnp.int32)
    chunks = groups * sequences
    rows = steps * chunks
    slice_rows, entry_width = entry_weight.shape
    own = kernel_offset.shape[0]
    inner_width = entry_width // 2
    group_width = inner_width // groups
    states = decay_log.shape[0]
    rank = delta_weight.shape[0]

    def flipped(value, axis, bits):
        return lax.ppermute(value, axis, [(i, i ^ bits) for i in range(lax.axis_size(axis))])

    def after(value, *others):
        return lax.optimization_barrier((value,) + others)[0]

    def rounds(*values):
        return lax.optimization_barrier(values)

    packed = jnp.concatenate(
        [
            delta_weight,
            select_weight.T,
            decay_log,
            kernel_weight,
            jnp.concatenate([kernel_offset, timestep_bias, skip_gain]).reshape(3, own),
            jnp.zeros((small_rows - 183, own), bf16),
        ],
        axis=0,
    )
    def side_blocks(block):
        return [block] + [flipped(block, "blk", 2 * k) for k in range(1, pieces // 2)]

    place_of_gain = (piece * groups + group) * slice_rows
    gain_line = lax.dynamic_update_slice_in_dim(jnp.zeros((width,), bf16), norm_gain, place_of_gain, 0)
    gain_line = jnp.pad(gain_line.reshape(1, -1, group_width), ((0, 0), (0, 8 - width // group_width), (0, 0)))
    halves = entry_weight.reshape(slice_rows, 2, pieces, groups, own).transpose(3, 1, 0, 2, 4)
    halves = halves.reshape(groups, 2 * slice_rows, group_width)
    halves = jnp.concatenate([halves, jnp.broadcast_to(gain_line, (groups,) + gain_line.shape[1:])], axis=1)
    exit_block = jnp.concatenate([exit_weight, jnp.pad(packed.reshape(-1), (0, -packed.size % (16 * width))).reshape(-1, width)])
    halves, exit_block = rounds(halves, exit_block)
    halves = lax.all_to_all(halves, "grp", split_axis=0, concat_axis=0, tiled=True)
    exit_side = side_blocks(exit_block)
    token_pair = flipped(tokens, "grp", 2)
    halves, token_pair, tokens, *exit_side = rounds(halves, token_pair, tokens, *exit_side)

    gain_rows = jnp.sum(halves[:, 2 * slice_rows :].astype(f32), axis=0).astype(bf16)
    inner_block = halves[:, :slice_rows].reshape(groups * slice_rows, group_width)
    inner_block = jnp.concatenate([inner_block, gain_rows])
    gate_block = halves[:, slice_rows : 2 * slice_rows].reshape(groups * slice_rows, group_width)
    inner_side = side_blocks(inner_block)
    exit_near = jnp.stack(exit_side)
    exit_far = flipped(exit_near, "blk", 1)
    token_slabs = (tokens, flipped(tokens, "grp", 1), token_pair, flipped(token_pair, "grp", 1))
    exit_near, exit_far, gate_block, cotangent, *rest = rounds(
        exit_near, exit_far, gate_block, cotangent, *inner_side, *token_slabs
    )
    inner_side, token_slabs = rest[: pieces // 2], rest[pieces // 2 :]
    small = jnp.stack([exit_near[:, own:], exit_far[:, own:]], axis=1).reshape(pieces, -1)[:, : packed.size]
    bits = pieces.bit_length() - 1
    small = small.reshape((2,) * bits + (small_rows, own))
    for k in range(bits):
        small = jnp.where((piece >> (bits - 1 - k)) & 1, jnp.flip(small, k), small)
    small = small.reshape(pieces, small_rows, own).transpose(1, 0, 2).reshape(small_rows, group_width)

    inner_near = jnp.stack(inner_side)
    ahead = [(i, i + 1) for i in range(pieces - 1)]
    behind = [(i + 1, i) for i in range(pieces - 1)]
    tails = jnp.stack([slab[:, steps - 3 :] for slab in token_slabs])
    tail = lax.dynamic_index_in_dim(tails, group ^ (groups - 1), 0, keepdims=False)
    rim_source = tail.transpose(1, 0, 2).reshape(3 * sequences, width)
    rim = lax.ppermute(rim_source, "blk", ahead)
    inner_far = flipped(inner_near, "blk", 1)
    gate_block, cotangent = rounds(gate_block, cotangent, inner_near, rim_source)[:2]
    gate_side = side_blocks(gate_block)
    cotangent_pair = flipped(cotangent, "grp", 2)
    label_tail = lax.ppermute(segments[:, -3:], "blk", ahead)
    labels = jnp.concatenate([label_tail, segments], axis=1)
    length = segments.shape[1]
    shifted = jnp.stack([labels[:, k : k + length] for k in range(3)], axis=-1)
    same = (shifted == segments[:, :, None]).astype(f32)
    columns = jnp.concatenate([same, 1.0 - same[:, :, 2:3]], axis=2)
    mask = columns.reshape(sequences, groups, steps, 4).transpose(2, 1, 0, 3).reshape(rows, 4)
    gain_all = jnp.sum(inner_near[:, -8:].astype(f32), axis=0) + jnp.sum(inner_far[:, -8:].astype(f32), axis=0)
    gain_all = gain_all[: width // group_width].reshape(1, width)

    gate_near = jnp.stack(gate_side)
    gate_far = flipped(gate_near, "blk", 1)
    cotangent_slabs = (
        cotangent,
        flipped(cotangent, "grp", 1),
        cotangent_pair,
        flipped(cotangent_pair, "grp", 1),
    )

    def group_sum(value):
        half = value.astype(f32) + flipped(value, "grp", 1).astype(f32)
        half = half.astype(bf16)
        return half, flipped(half, "grp", 2)

    normed, inner, filtered, chosen = kernel_call(
        entry_kernel,
        9,
        [
            ((rows, width), bf16),
            ((rows + 3 * chunks, group_width), bf16),
            ((rows, group_width), f32),
            ((96, rows), bf16),
        ],
        [pltpu.VMEM((width, group_width), bf16)],
        12,
        place, *token_slabs, rim, gain_all, mask, inner_near, inner_far, small,
    )
    chosen_pair = group_sum(chosen)
    cotangent_rows, gate_value, gate_slope, grad_scan = kernel_call(
        gate_kernel,
        8,
        [
            ((rows, width), bf16),
            ((rows, group_width), f32),
            ((rows, group_width), f32),
            ((rows, group_width), f32),
        ],
        [
            pltpu.VMEM((width, group_width), bf16),
            pltpu.VMEM((group_width, width), bf16),
            pltpu.VMEM((rows, group_width), f32),
            pltpu.VMEM((rows, group_width), f32),
        ],
        16,
        place, *cotangent_slabs, normed, gate_near, gate_far, exit_near, exit_far,
    )
    cube = (steps, chunks, group_width)
    bank = (states, chunks, group_width)
    load_rows = (states + 2) * sequences
    gates, step_sizes, step_slopes, ends, keeps, gives, loads = kernel_call(
        piece_kernel,
        23,
        [
            ((steps, chunks, 128), f32),
            (cube, f32),
            (cube, f32),
            (bank, f32),
            (bank, f32),
            (bank, f32),
            ((pieces, load_rows, group_width), bf16),
        ],
        [
            pltpu.VMEM((states, 8, group_width), f32),
            pltpu.VMEM((steps * 8, 2 * states * 128), f32),
            pltpu.VMEM((4 * states, 2 * states * 128), bf16),
            pltpu.VMEM((chunks, group_width), f32),
            pltpu.VMEM((load_rows, group_width), f32),
            pltpu.VMEM((load_rows, group_width), f32),
        ],
        16,
        place, *chosen_pair, mask, small, filtered.reshape(cube), grad_scan.reshape(cube),
    )
    came = lax.all_to_all(loads, "blk", split_axis=0, concat_axis=0, tiled=True)

    lanes = group_width // 128
    gate_scratch = [
        pltpu.VMEM((states + 1, 8, group_width), f32),
        pltpu.VMEM((steps * 8, 2 * states * 128), f32),
        pltpu.VMEM((4 * states, 2 * states * 128), bf16),
    ]
    product_scratch = [pltpu.VMEM((steps * 8, states * 128), bf16), pltpu.VMEM((states * 128, 128), bf16)]
    starts = (steps // 4, states, chunks, group_width)
    scan_out, read_sums, block_starts, arrive = kernel_call(
        forward_kernel,
        18,
        [(cube, f32), ((steps, chunks, 128), f32), (starts, f32), (bank, f32)],
        gate_scratch
        + product_scratch
        + [pltpu.VMEM((states, lanes, 8, 128), f32), pltpu.VMEM((2, states * sequences, group_width), f32), pltpu.VMEM(bank, f32)],
        36,
        place, came, gates, small, step_sizes, filtered.reshape(cube), grad_scan.reshape(cube), ends, keeps, gives,
        halves=(None, None, 1, None, 1, 1, 1) + (None,) * 3 + (1, 1, 2, None),
    )
    half_slabs = ((2, sequences, steps, width), bf16)
    block_height = groups * slice_rows
    entry_half = ((pieces // 2, block_height, group_width), bf16)
    grad_gating, out_keep, out_send, exit_grad, gate_keep, gate_send = kernel_call(
        leave_kernel,
        12,
        [((rows, group_width), bf16), half_slabs, half_slabs, ((group_width, width), bf16), entry_half, entry_half],
        [
            pltpu.VMEM((rows, group_width), bf16),
            pltpu.VMEM((width, group_width), f32),
            pltpu.VMEM((group_width, width), bf16),
            pltpu.VMEM((rows, width), bf16),
        ],
        14,
        place, scan_out.reshape(rows, group_width), gate_value, gate_slope, cotangent_rows, normed, exit_near, exit_far,
    )

    exit_parts = lax.all_to_all(
        exit_grad.reshape(pieces, own, width), "blk", split_axis=0, concat_axis=0, tiled=True
    )
    gate_came = flipped(gate_send, "blk", 1)
    out_came = flipped(out_send, "grp", 1)
    grad_direct, rank_grad, chosen_grad, decay_grad, skip_grad, bias_grad = kernel_call(
        backward_kernel,
        35,
        [
            (cube, f32),
            ((rank, group_width), f32),
            ((96, rows), bf16),
            ((states, group_width), f32),
            ((1, group_width), f32),
            ((1, group_width), f32),
        ],
        gate_scratch
        + product_scratch
        + [
            pltpu.VMEM(cube, f32),
            pltpu.VMEM((steps, chunks, 128), f32),
            pltpu.VMEM((states, lanes, 8, 128), f32),
            pltpu.VMEM((states, lanes, 8, 128), f32),
        ],
        50,
        gates, small, step_sizes, step_slopes, filtered.reshape(cube), after(grad_scan, out_send).reshape(cube),
        read_sums, block_starts, arrive,
        halves=(1, None, 1, 1, 1, 1, 1, 2, 1, 1) + (None,) * 5,
    )
    chosen_grad, exit_parts, gate_came, out_came = rounds(chosen_grad, exit_parts, gate_came, out_came)
    chosen_grads = group_sum(chosen_grad)

    def slab_part(keep, came):
        return (keep[1].astype(f32) + came[1].astype(f32)).astype(bf16)

    exit_out = jnp.sum(after(exit_parts, chosen_grads[0]).astype(f32), axis=0)
    grad_direct, exit_out = rounds(grad_direct, exit_out)
    out_part = after(slab_part(out_keep, out_came), chosen_grads[0])
    out_other = flipped(out_part, "grp", 2)

    paired = 2 * own == 128
    side_block = (block_height + (small_rows // 4 if paired else 0), group_width)
    grad_back, tail_back, first_spill, small_grads, side_total, *side_parts = kernel_call(
        filter_kernel,
        6,
        [
            ((rows, group_width), bf16),
            ((3, chunks, group_width), f32),
            ((3, sequences, group_width), f32),
            ((small_rows, group_width), f32),
            (side_block, f32),
        ]
        + [(side_block, bf16)] * (pieces // 2 - 1),
        [
            pltpu.VMEM((small_rows, group_width), f32),
            pltpu.VMEM((rows, 96), bf16),
            pltpu.VMEM((4, group_width), f32),
            pltpu.VMEM((1, group_width), f32),
            pltpu.VMEM((rows, group_width), f32),
            pltpu.VMEM((3, rows + 3 * chunks, group_width), f32),
        ],
        62,
        place, *chosen_grads, grad_direct.reshape(rows, group_width), inner, filtered, mask, small,
        rank_grad, decay_grad, bias_grad, skip_grad, gate_keep, gate_came,
        free=True,
    )
    spill_after = lax.ppermute(first_spill, "blk", behind)
    side_parts = [flipped(part, "blk", 2 * k + 2) for k, part in enumerate(side_parts)]
    grad_inner, inner_entry = kernel_call(
        inner_kernel,
        4,
        [((rows, group_width), bf16), ((width, group_width), bf16)],
        [],
        12,
        grad_back, tail_back, spill_after, normed,
    )
    grad_inner, inner_entry, out_other = rounds(grad_inner, inner_entry, out_other)
    inner_parts = lax.all_to_all(
        inner_entry.reshape(pieces * groups, slice_rows, group_width), both, split_axis=0, concat_axis=0, tiled=True
    )
    grad_keep, grad_send = kernel_call(
        normed_kernel,
        10,
        [half_slabs, half_slabs],
        [
            pltpu.VMEM((width, group_width), bf16),
            pltpu.VMEM((width, group_width), bf16),
            pltpu.VMEM((rows, width), bf16),
        ],
        14,
        place, grad_inner, grad_gating, inner_near, inner_far, gate_near, gate_far,
    )
    grad_send, *side_parts = rounds(grad_send, *side_parts)
    grad_came = flipped(grad_send, "grp", 1)
    grad_part = slab_part(grad_keep, grad_came)
    grad_other = flipped(grad_part, "grp", 2)
    *gate_blocks, small_sum = kernel_call(
        side_sum_kernel,
        2,
        [((slice_rows, group_width), bf16)] * groups + [((small_rows, 128), f32)],
        [],
        16,
        place, after(side_total, grad_part), *side_parts,
    )
    gate_blocks = [gate_blocks[0]] + [flipped(gate_blocks[k], "grp", k) for k in range(1, groups)]
    residual = tokens.astype(f32)
    out_other, gate_blocks[3], small_sum = rounds(out_other, gate_blocks[3], small_sum)
    block_out = residual + out_keep[0].astype(f32) + out_came[0].astype(f32) + out_other.astype(f32)
    block_out = block_out.astype(bf16)
    inner_parts = inner_parts.reshape(pieces, groups, slice_rows, group_width)
    if own == 64:
        entry_out, gain_out = kernel_call(
            interleave_kernel,
            3,
            [((slice_rows, entry_width), f32), ((slice_rows, 128), f32)],
            [],
            16,
            place, entry_weight, inner_parts, *gate_blocks,
        )
        gain_out = gain_out[:, 0]
    else:
        inner_sum = jnp.sum(inner_parts.astype(f32), axis=0)
        gate_parts = jnp.stack(gate_blocks).astype(f32)
        for k in range(2):
            pairs = gate_parts.reshape(2, 2, slice_rows, group_width)
            gate_parts = jnp.where((group >> (1 - k)) & 1, jnp.flip(pairs, k), pairs)
        entry_parts = jnp.stack([inner_sum, gate_parts.reshape(inner_sum.shape)], axis=0)
        entry_parts = entry_parts.reshape(2, groups, slice_rows, pieces, own)
        entry_out = entry_parts.transpose(2, 0, 3, 1, 4).reshape(slice_rows, entry_width)
        gain_out = jnp.sum(entry_out * entry_weight.astype(f32), axis=1)
    gain_out = gain_out / norm_gain.astype(f32)

    if paired:
        small_sum = small_sum + flipped(small_sum, "blk", 1)
        mine = lax.dynamic_slice_in_dim(small_sum, (piece & 1) * own, own, 1)
    else:
        split = small_grads.reshape(small_rows, pieces, own).transpose(1, 0, 2)
        came_small = lax.all_to_all(split, "blk", split_axis=0, concat_axis=0, tiled=True)
        mine = jnp.sum(came_small, axis=0)

    input_grad = kernel_call(
        input_kernel,
        2,
        [((sequences, steps, width), bf16)],
        [],
        16,
        grad_keep, grad_came, after(grad_other, entry_out), tokens, cotangent, gain_all,
    )[0]
    return (
        block_out,
        input_grad,
        gain_out,
        entry_out,
        mine[176:180],
        mine[180],
        mine[64:160].T,
        mine[0:64],
        mine[181],
        mine[160:176],
        mine[182],
        exit_out,
    )


def solution(mesh):
    placed = (
        P(None, both, None),
        P(None, "blk"),
        P(None, both, None),
        P(both),
        P(both, None),
        P(None, both),
        P(both),
        P(both, None),
        P(None, both),
        P(both),
        P(None, both),
        P(both),
        P(both, None),
    )
    return jax.shard_map(
        local,
        mesh=mesh,
        in_specs=placed,
        out_specs=(
            P(None, both, None),
            P(None, both, None),
            P(both),
            P(both, None),
            P(None, both),
            P(both),
            P(both, None),
            P(None, both),
            P(both),
            P(None, both),
            P(both),
            P(both, None),
        ),
        check_vma=False,
    )
```

```python
import jax
import jax.numpy as jnp
from jax import lax
from jax.experimental import pallas as pl
from jax.experimental.pallas import tpu as pltpu
from jax.sharding import PartitionSpec as P

epsilon = 1e-05
log2_e = 1.4426950408889634
log_2 = 0.6931471805599453
reset_push = 1e6
f32 = jnp.float32
bf16 = jnp.bfloat16
small_rows = 192
both = ("blk", "grp")


def dot(left, right, dims=((1,), (0,))):
    return lax.dot_general(left, right, (dims, ((), ())), preferred_element_type=f32)


def sigmoid(values):
    return 1.0 / (1.0 + jnp.exp(-values))


def spread(block, axis):
    count = lax.axis_size(axis)
    copies = jnp.broadcast_to(block[None], (count,) + block.shape)
    return lax.all_to_all(copies, axis, split_axis=0, concat_axis=0, tiled=True)


def ordering(groups, sequences, me):
    chunks = groups * sequences
    rows = chunks * 8
    out_row = lax.broadcasted_iota(jnp.int32, (rows, rows), 0)
    in_row = lax.broadcasted_iota(jnp.int32, (rows, rows), 1)
    chunk = out_row % chunks
    wanted = (((chunk // sequences) ^ me) * sequences + chunk % sequences) * 8 + out_row // chunks
    return jnp.where(in_row == wanted, 1.0, 0.0).astype(bf16)


def kernel_call(body, micros, outs, scratch, limit, *operands, halves=None, free=False):
    whole = pl.BlockSpec(memory_space=pltpu.VMEM)
    kinds = [(value.shape, value.dtype) for value in operands] + list(outs)

    def place(index):
        shape, kind = kinds[index]
        if kind == jnp.int32:
            return pl.BlockSpec(memory_space=pltpu.SMEM)
        axis = halves[index] if halves else None
        if axis is None and free:
            return pl.BlockSpec(shape, lambda *_: (0,) * len(shape))
        if axis is None:
            return whole
        block = tuple(size // 2 if k == axis else size for k, size in enumerate(shape))
        return pl.BlockSpec(block, lambda half: tuple(half if k == axis else 0 for k in range(len(block))))

    places = [place(k) for k in range(len(kinds))]
    return pl.pallas_call(
        body,
        out_shape=[jax.ShapeDtypeStruct(shape, kind) for shape, kind in outs],
        grid=(2,) if halves else (),
        in_specs=places[: len(operands)],
        out_specs=places[len(operands) :],
        scratch_shapes=scratch,
        compiler_params=pltpu.CompilerParams(vmem_limit_bytes=limit << 20),
        cost_estimate=pl.CostEstimate(
            flops=micros * 1_150_000_000, bytes_accessed=8_000_000, transcendentals=0
        ),
    )(*operands)


def read_rows(slab_refs, block):
    sequences, _, width = slab_refs[0].shape
    at = pl.ds(pl.multiple_of(block * 8, 8), 8)
    parts = [slab[:, at, :].astype(f32) for slab in slab_refs]
    return jnp.concatenate(parts, axis=0).reshape(len(slab_refs) * sequences * 8, width)


def small_row(small_ref, index):
    tail = small_ref[176:192, :].astype(f32)
    return tail[index : index + 1, :]


def assemble(whole_ref, stacks, me):
    for side, stack_ref in enumerate(stacks):
        count = stack_ref.shape[0]
        rows = whole_ref.shape[0] // (2 * count)
        for k in range(count):
            target = pl.ds(pl.multiple_of((me ^ (2 * k + side)) * rows, 8), rows)
            whole_ref[target, :] = stack_ref[k, 0:rows, :]


def entry_kernel(
    place_ref, slab0_ref, slab1_ref, slab2_ref, slab3_ref, rim_ref, gain_ref, mask_ref, near_ref, far_ref, small_ref,
    normed_ref, inner_ref, filter_ref, chosen_ref, weight_ref,
):
    slabs = (slab0_ref, slab1_ref, slab2_ref, slab3_ref)
    groups = len(slabs)
    sequences, steps, width = slab0_ref.shape
    chunks = groups * sequences
    block_rows = chunks * 8
    inner_width = inner_ref.shape[1]
    order = ordering(groups, sequences, place_ref[1])
    assemble(weight_ref, (near_ref, far_ref), place_ref[0])

    def scaled(rows):
        root = lax.rsqrt(jnp.mean(rows * rows, axis=1, keepdims=True) + epsilon)
        return (rows * root * gain_ref[...]).astype(bf16)

    taps = [small_row(small_ref, k) for k in range(4)]
    offset = small_row(small_ref, 4)

    def norm_lap(block, carry):
        base = pl.multiple_of(block * block_rows, block_rows)
        normed = dot(order, scaled(read_rows(slabs, block))).astype(bf16)
        normed_ref[pl.ds(base, block_rows), :] = normed
        return carry

    lax.fori_loop(0, steps // 8, norm_lap, 0)
    inner_ref[3 * chunks :, :] = dot(normed_ref[...], weight_ref[...]).astype(bf16)
    last = inner_ref[steps * chunks :, :].astype(f32).reshape(3, chunks, inner_width)
    rim = dot(scaled(rim_ref[...].astype(f32)), weight_ref[...]).reshape(3, sequences, inner_width)
    rim = jnp.concatenate([rim, last[:, : chunks - sequences, :]], axis=1)
    inner_ref[0 : 3 * chunks, :] = rim.reshape(3 * chunks, inner_width).astype(bf16)

    def lap(block, carry):
        base = pl.multiple_of(block * block_rows, block_rows)
        total = offset
        for k in range(3):
            same = mask_ref[pl.ds(base, block_rows), k : k + 1]
            part = inner_ref[pl.ds(pl.multiple_of(base + k * chunks, 16), block_rows), :]
            total = total + taps[k] * part.astype(f32) * same
        inner = inner_ref[pl.ds(pl.multiple_of(base + 3 * chunks, 16), block_rows), :]
        total = total + taps[3] * inner.astype(f32)
        filtered = (total * sigmoid(total)).astype(bf16)
        filter_ref[pl.ds(base, block_rows), :] = filtered.astype(f32)
        chosen = dot(small_ref[64:160, :], filtered, ((1,), (1,)))
        chosen_ref[:, pl.ds(base, block_rows)] = chosen.astype(bf16)
        return carry

    lax.fori_loop(0, steps // 8, lap, 0)


def gate_kernel(
    place_ref, slab0_ref, slab1_ref, slab2_ref, slab3_ref, normed_ref, near_ref, far_ref, exit_near_ref, exit_far_ref,
    rows_ref, value_ref, slope_ref, grad_ref, weight_ref, exit_ref, gating_ref, gated_ref,
):
    slabs = (slab0_ref, slab1_ref, slab2_ref, slab3_ref)
    sequences, steps, width = slab0_ref.shape
    block_rows = len(slabs) * sequences * 8
    order = ordering(len(slabs), sequences, place_ref[1])
    assemble(weight_ref, (near_ref, far_ref), place_ref[0])
    assemble(exit_ref, (exit_near_ref, exit_far_ref), place_ref[0])

    def order_lap(block, carry):
        at = pl.ds(pl.multiple_of(block * block_rows, block_rows), block_rows)
        rows_ref[at, :] = dot(order, read_rows(slabs, block).astype(bf16)).astype(bf16)
        return carry

    lax.fori_loop(0, steps // 8, order_lap, 0)
    gating_ref[...] = dot(normed_ref[...], weight_ref[...])
    gated_ref[...] = dot(rows_ref[...], exit_ref[...], ((1,), (1,)))

    def lap(block, carry):
        at = pl.ds(pl.multiple_of(block * block_rows, block_rows), block_rows)
        gating = gating_ref[at, :]
        grad_gated = gated_ref[at, :]
        gate = sigmoid(gating)
        value = gating * gate
        value_ref[at, :] = value
        slope_ref[at, :] = grad_gated * (gate * (1.0 + gating * (1.0 - gate)))
        grad_ref[at, :] = (grad_gated * value).astype(bf16).astype(f32)
        return carry

    lax.fori_loop(0, steps // 8, lap, 0)


def fill_rates(small_ref, rates_ref):
    states = rates_ref.shape[0]
    rates = -jnp.exp(small_ref[160 : 160 + states, :].astype(f32)) * log2_e
    for n in range(states):
        rates_ref[n] = jnp.broadcast_to(rates[n : n + 1, :], rates_ref.shape[1:])


def fill_picks(pick_ref):
    depth, width = pick_ref.shape
    source = lax.broadcasted_iota(jnp.int32, (depth, width), 0) % (depth // 2)
    target = lax.broadcasted_iota(jnp.int32, (depth, width), 1) // 128
    pick_ref[...] = jnp.where(source == target, 1.0, 0.0).astype(bf16)


def fill_gates(gates_ref, pick_ref, spread_ref, at):
    steps = gates_ref.shape[0]
    values = gates_ref[:, at, :].reshape(steps * 8, 128)[:, 64:96]
    high = values.astype(bf16)
    rest = (values - high.astype(f32)).astype(bf16)
    pair = jnp.concatenate([high, rest], axis=1)
    span = 2048

    def lap(k, carry):
        columns = pl.ds(pl.multiple_of(k * span, span), span)
        spread_ref[:, columns] = dot(pair, pick_ref[:, columns])
        return carry

    lax.fori_loop(0, spread_ref.shape[1] // span, lap, 0)


def gate_of(spread_ref, t, n):
    return spread_ref[pl.ds(pl.multiple_of(t * 8, 8), 8), n * 128 : (n + 1) * 128]


def lane_slices(width):
    return [slice(k * 128, (k + 1) * 128) for k in range(width // 128)]


def piece_kernel(
    place_ref, chosen_ref, other_ref, mask_ref, small_ref, filter_ref, grad_ref,
    gates_ref, step_ref, slope_ref, end_ref, keep_ref, give_ref, load_ref,
    rates_ref, spread_ref, pick_ref, sum_ref, ahead_ref, back_ref,
):
    me = place_ref[0]
    steps, chunks, width = step_ref.shape
    states = end_ref.shape[0]
    chosen = chosen_ref[...].astype(f32) + other_ref[...].astype(f32)
    padded = jnp.concatenate([chosen, jnp.zeros((32, chosen.shape[1]), f32)], axis=0)
    gates_ref[...] = padded.T.reshape(steps, chunks, 128)
    fill_rates(small_ref, rates_ref)
    fill_picks(pick_ref)
    bias = small_row(small_ref, 5)
    delta = small_ref[0:64, :]

    def delta_lap(block, carry):
        at = pl.ds(pl.multiple_of(block * 8, 8), 8)
        low = gates_ref[at, :, :].reshape(8 * chunks, 128)[:, 0:64]
        high = low.astype(bf16)
        rest = (low - high.astype(f32)).astype(bf16)
        pre = dot(high, delta) + dot(rest, delta) + bias
        grown = jnp.exp(-jnp.abs(pre))
        step = jnp.maximum(pre, 0.0) + jnp.log1p(grown)
        step_ref[at, :, :] = step.reshape(8, chunks, width)
        slope_ref[at, :, :] = (jnp.where(pre >= 0, 1.0, grown) / (1.0 + grown)).reshape(8, chunks, width)
        return carry

    lax.fori_loop(0, steps // 8, delta_lap, 0)

    push = mask_ref[:, 3:4] * reset_push
    gates_ref[:, :, 96:97] = push.reshape(steps, chunks, 1)
    end_ref[...] = jnp.zeros_like(end_ref)
    give_ref[...] = jnp.zeros_like(give_ref)
    keep_ref[...] = jnp.ones_like(keep_ref)
    span = 8
    lanes = lane_slices(width)
    spots = [(j, i) for j in range(span) for i in range(len(lanes))]

    def half_lap(half, carry):
        at = pl.ds(pl.multiple_of(half * 8, 8), 8)
        fill_gates(gates_ref, pick_ref, spread_ref, at)

        def lap(block, totals):
            totals = list(totals)
            pushed, drives, grads = {}, {}, {}
            for j, i in spots:
                t = block * span + j
                step = step_ref[t, at, lanes[i]]
                push = step + gates_ref[t, at, 96:97]
                totals[i] = totals[i] + push
                pushed[j, i] = push
                drives[j, i] = step * filter_ref[t, at, lanes[i]]
                grads[j, i] = grad_ref[t, at, lanes[i]]
            for n in range(states):
                rate = [rates_ref[n, :, one] for one in lanes]
                end = [end_ref[n, at, one] for one in lanes]
                keep = [keep_ref[n, at, one] for one in lanes]
                give = [give_ref[n, at, one] for one in lanes]
                for j in range(span):
                    write = gate_of(spread_ref, block * span + j, n)
                    read = gate_of(spread_ref, block * span + j, states + n)
                    for i in range(len(lanes)):
                        decay = jnp.exp2(pushed[j, i] * rate[i])
                        end[i] = decay * end[i] + drives[j, i] * write
                        keep[i] = keep[i] * decay
                        give[i] = give[i] + keep[i] * (read * grads[j, i])
                for i, one in enumerate(lanes):
                    end_ref[n, at, one] = end[i]
                    keep_ref[n, at, one] = keep[i]
                    give_ref[n, at, one] = give[i]
            return tuple(totals)

        start = tuple(jnp.zeros((8, 128), f32) for _ in lanes)
        totals = lax.fori_loop(0, steps // span, lap, start)
        for i, one in enumerate(lanes):
            sum_ref[at, one] = totals[i]
        return carry

    lax.fori_loop(0, chunks // 8, half_lap, 0)

    sequences = ahead_ref.shape[0] // (states + 2)
    groups = chunks // sequences
    for n in range(states):
        rows = slice(n * sequences, (n + 1) * sequences)
        ahead = jnp.zeros((sequences, width), f32)
        back = jnp.zeros((sequences, width), f32)
        for k in range(groups):
            part = slice(k * sequences, (k + 1) * sequences)
            ahead = keep_ref[n, part, :] * ahead + end_ref[n, part, :]
            other = slice((groups - 1 - k) * sequences, (groups - k) * sequences)
            back = give_ref[n, other, :] + keep_ref[n, other, :] * back
        ahead_ref[rows, :] = ahead
        back_ref[rows, :] = back
    total = jnp.zeros((sequences, width), f32)
    for k in range(groups):
        total = total + sum_ref[k * sequences : (k + 1) * sequences, :]
    held = states * sequences
    for k in range(2):
        term = total.astype(bf16).astype(f32)
        ahead_ref[held + k * sequences : held + (k + 1) * sequences, :] = term
        total = total - term
    back_ref[held:, :] = ahead_ref[held:, :]

    def load_lap(piece, carry):
        load = jnp.where(piece > me, ahead_ref[...], back_ref[...])
        load_ref[piece] = load.astype(bf16)
        return carry

    lax.fori_loop(0, load_ref.shape[0], load_lap, 0)


def fill_unpicks(unpick_ref, first):
    spot = lax.broadcasted_iota(jnp.int32, unpick_ref.shape, 0) // 128
    column = lax.broadcasted_iota(jnp.int32, unpick_ref.shape, 1)
    unpick_ref[...] = jnp.where(column == spot + first, 1.0, 0.0).astype(bf16)


def forward_kernel(
    place_ref, came_ref, gates_ref, small_ref, step_ref, filter_ref, grad_ref, end_ref, keep_ref, give_ref,
    out_ref, read_sum_ref, start_ref, arrive_ref,
    rates_ref, spread_ref, pick_ref, product_ref, unpick_ref, passed_ref, whole_ref, enter_ref,
):
    me = place_ref[0]
    half = pl.program_id(0)
    steps, _, width = step_ref.shape
    states, chunks = end_ref.shape[:2]
    pieces = came_ref.shape[0]
    sequences = came_ref.shape[1] // (states + 2)
    groups = chunks // sequences
    @pl.when(half == 0)
    def _():
        fill_rates(small_ref, rates_ref)
        fill_picks(pick_ref)
        fill_unpicks(unpick_ref, 64 + states)
        rates_ref[states] = jnp.broadcast_to(small_row(small_ref, 6), (8, width))

        held = states * sequences
        rates = [jnp.broadcast_to(rates_ref[n, 0:1, :], (sequences, width)) for n in range(states)]
        rates = jnp.concatenate(rates, axis=0)

        def step_in(piece, state):
            values = came_ref[piece].astype(f32)
            total = values[held : held + sequences, :]
            total = total + values[held + sequences :, :]
            total = jnp.concatenate([total] * states, axis=0)
            return jnp.exp2(total * rates) * state + values[:held, :]

        def step_back(k, state):
            return step_in(pieces - 1 - k, state)

        zero = jnp.zeros((held, width), f32)
        whole_ref[0] = lax.fori_loop(0, me, step_in, zero)
        whole_ref[1] = lax.fori_loop(0, pieces - 1 - me, step_back, zero)
        for n in range(states):
            ahead = whole_ref[0, n * sequences : (n + 1) * sequences, :]
            back = whole_ref[1, n * sequences : (n + 1) * sequences, :]
            for k in range(groups):
                part = slice(k * sequences, (k + 1) * sequences)
                enter_ref[n, part, :] = ahead
                ahead = keep_ref[n, part, :] * ahead + end_ref[n, part, :]
                other = slice((groups - 1 - k) * sequences, (groups - k) * sequences)
                arrive_ref[n, other, :] = back
                back = give_ref[n, other, :] + keep_ref[n, other, :] * back

    span = 4
    lanes = lane_slices(width)
    spots = [(j, i) for j in range(span) for i in range(len(lanes))]

    fill_gates(gates_ref, pick_ref, spread_ref, slice(None))
    at = pl.ds(pl.multiple_of(half * 8, 8), 8)
    for n in range(states):
        for i, one in enumerate(lanes):
            passed_ref[n, i] = enter_ref[n, at, one]

    def forward(block, inner_carry):
        pushed, drives, grads, outs = {}, {}, {}, {}
        for j, i in spots:
            t = block * span + j
            step = step_ref[t, :, lanes[i]]
            feed = filter_ref[t, :, lanes[i]]
            pushed[j, i] = step + gates_ref[t, :, 96:97]
            drives[j, i] = step * feed
            grads[j, i] = grad_ref[t, :, lanes[i]]
            outs[j, i] = feed * rates_ref[states, :, lanes[i]]
        rows = pl.ds(pl.multiple_of(block * span * 8, span * 8), span * 8)
        for n in range(states):
            rate = [rates_ref[n, :, one] for one in lanes]
            hidden = [passed_ref[n, i] for i in range(len(lanes))]
            for i, one in enumerate(lanes):
                start_ref[block, n, :, one] = hidden[i]
            seen = []
            for j in range(span):
                t = block * span + j
                write = gate_of(spread_ref, t, n)
                read = gate_of(spread_ref, t, states + n)
                total = None
                for i in range(len(lanes)):
                    hidden[i] = jnp.exp2(pushed[j, i] * rate[i]) * hidden[i] + drives[j, i] * write
                    outs[j, i] = outs[j, i] + hidden[i] * read
                    one = grads[j, i] * hidden[i]
                    total = one if total is None else total + one
                seen.append(total)
            product_ref[rows, n * 128 : (n + 1) * 128] = jnp.concatenate(seen, axis=0).astype(bf16)
            for i in range(len(lanes)):
                passed_ref[n, i] = hidden[i]
        for j, i in spots:
            out_ref[block * span + j, :, lanes[i]] = outs[j, i]
        return inner_carry

    lax.fori_loop(0, steps // span, forward, 0)
    summed = dot(product_ref[...], unpick_ref[...])
    read_sum_ref[...] = summed.reshape(steps, 8, 128)


def backward_kernel(
    gates_ref, small_ref, step_ref, slope_ref, filter_ref, grad_ref, read_sum_ref, start_ref, arrive_ref,
    direct_ref, rank_ref, chosen_ref, decay_ref, skip_ref, bias_ref,
    rates_ref, spread_ref, pick_ref, product_ref, unpick_ref, delta_ref, sums_acc_ref,
    passed_ref, total_ref,
):
    half = pl.program_id(0)
    steps, _, width = step_ref.shape
    chunks = delta_ref.shape[1]
    blocks, states = start_ref.shape[:2]
    span = steps // blocks

    @pl.when(half == 0)
    def _():
        fill_rates(small_ref, rates_ref)
        fill_picks(pick_ref)
        fill_unpicks(unpick_ref, 64)
        decay_ref[...] = jnp.zeros_like(decay_ref)
        skip_ref[...] = jnp.zeros_like(skip_ref)
        rank_ref[...] = jnp.zeros_like(rank_ref)
        bias_ref[...] = jnp.zeros_like(bias_ref)
        rates_ref[states] = jnp.broadcast_to(small_row(small_ref, 6), (8, width))

    lanes = lane_slices(width)
    spots = [(j, i) for j in range(span) for i in range(len(lanes))]

    fill_gates(gates_ref, pick_ref, spread_ref, slice(None))
    at = pl.ds(pl.multiple_of(half * 8, 8), 8)
    for n in range(states):
        for i, one in enumerate(lanes):
            passed_ref[n, i] = arrive_ref[n, :, one]
            total_ref[n, i] = jnp.zeros((8, 128), f32)

    def backward(k, skips):
        block = blocks - 1 - k
        skips = list(skips)
        raw, feeds, pushed, drives, grads, weighted, slopes = {}, {}, {}, {}, {}, {}, {}
        for j, i in spots:
            t = block * span + j
            step = step_ref[t, :, lanes[i]]
            feed = filter_ref[t, :, lanes[i]]
            grad = grad_ref[t, :, lanes[i]]
            raw[j, i] = step
            feeds[j, i] = feed
            pushed[j, i] = step + gates_ref[t, :, 96:97]
            drives[j, i] = step * feed
            grads[j, i] = grad
            weighted[j, i] = jnp.zeros((8, 128), f32)
            slopes[j, i] = jnp.zeros((8, 128), f32)
            skips[i] = skips[i] + grad * feed
        rows = pl.ds(pl.multiple_of(block * span * 8, span * 8), span * 8)
        for n in range(states):
            rate = [rates_ref[n, :, one] for one in lanes]
            gone = [passed_ref[n, i] for i in range(len(lanes))]
            turns = [total_ref[n, i] for i in range(len(lanes))]
            hidden = [[start_ref[block, n, :, one] for one in lanes]]
            decays = []
            for j in range(span):
                decays.append([jnp.exp2(pushed[j, i] * rate[i]) for i in range(len(lanes))])
                if j < span - 1:
                    write = gate_of(spread_ref, block * span + j, n)
                    last = hidden[-1]
                    hidden.append(
                        [decays[j][i] * last[i] + drives[j, i] * write for i in range(len(lanes))]
                    )
            seen = [None] * span
            for j in reversed(range(span)):
                t = block * span + j
                write = gate_of(spread_ref, t, n)
                read = gate_of(spread_ref, t, states + n)
                for i in range(len(lanes)):
                    adjoint = read * grads[j, i] + gone[i]
                    weighted[j, i] = weighted[j, i] + adjoint * write
                    one = adjoint * drives[j, i]
                    seen[j] = one if seen[j] is None else seen[j] + one
                    gone[i] = adjoint * decays[j][i]
                    turn = gone[i] * hidden[j][i]
                    slopes[j, i] = slopes[j, i] + turn * rate[i]
                    turns[i] = turns[i] + turn * raw[j, i]
            product_ref[rows, n * 128 : (n + 1) * 128] = jnp.concatenate(seen, axis=0).astype(bf16)
            for i in range(len(lanes)):
                passed_ref[n, i] = gone[i]
                total_ref[n, i] = turns[i]
        for j, i in spots:
            t = block * span + j
            grown = slopes[j, i] * log_2 + weighted[j, i] * feeds[j, i]
            delta_ref[t, at, lanes[i]] = grown * slope_ref[t, :, lanes[i]]
            direct = weighted[j, i] * raw[j, i] + grads[j, i] * rates_ref[states, :, lanes[i]]
            direct_ref[t, :, lanes[i]] = direct
        return tuple(skips)

    start = tuple(jnp.zeros((8, 128), f32) for _ in lanes)
    skips = lax.fori_loop(0, blocks, backward, start)
    for i, one in enumerate(lanes):
        skip_ref[0:1, one] += jnp.sum(skips[i], axis=0, keepdims=True)
        for n in range(states):
            part = jnp.sum(total_ref[n, i], axis=0, keepdims=True)
            decay_ref[n : n + 1, one] += part * rates_ref[n, 0:1, one] * log_2
    summed = dot(product_ref[...], unpick_ref[...])
    sums_acc_ref[:, at, :] = summed.reshape(steps, 8, 128) + read_sum_ref[...]

    grads = delta_ref[:, at, :].reshape(steps * 8, width)
    bias_ref[...] += jnp.sum(grads, axis=0, keepdims=True)
    low = gates_ref[...].reshape(steps * 8, 128)[:, 0:64].astype(bf16)
    rank_ref[...] += dot(low, grads.astype(bf16), ((0,), (0,)))

    @pl.when(half == 1)
    def _():
        rows = steps * chunks
        whole = delta_ref[...].reshape(rows, width).astype(bf16)
        back = dot(small_ref[0:64, :], whole, ((1,), (1,)))
        sums = sums_acc_ref[...].reshape(rows, 128).T
        chosen_ref[0:64, :] = back.astype(bf16)
        chosen_ref[64:96, :] = sums[64:96, :].astype(bf16)


def store_rows(keep_ref, send_ref, order, values, block):
    _, sequences, _, width = keep_ref.shape
    back = dot(order, values.astype(bf16), ((0,), (0,)))
    shaped = back.reshape(4, sequences, 8, width).astype(bf16)
    at = pl.ds(pl.multiple_of(block * 8, 8), 8)
    for k in range(4):
        target = send_ref if k % 2 else keep_ref
        target[k // 2, :, at, :] = shaped[k]


def store_blocks(keep_ref, send_ref, me, *parts):
    count = keep_ref.shape[0]
    below = 0
    for values_ref in parts:
        rows = values_ref.shape[0] // (2 * count)
        for k in range(2 * count):
            source = pl.ds(pl.multiple_of((me ^ k) * rows, 8), rows)
            target = send_ref if k % 2 else keep_ref
            target[k // 2, below : below + rows, :] = values_ref[source, :].astype(bf16)
        below += rows


def leave_kernel(
    place_ref, scan_ref, value_ref, slope_ref, rows_ref, normed_ref, exit_near_ref, exit_far_ref,
    gating_ref, out_keep_ref, out_send_ref, exit_grad_ref, keep_ref, send_ref,
    gated_ref, entry_grad_ref, exit_ref, out_ref,
):
    assemble(exit_ref, (exit_near_ref, exit_far_ref), place_ref[0])
    sequences, steps = out_keep_ref.shape[1:3]
    groups = 4
    block_rows = groups * sequences * 8
    order = ordering(groups, sequences, place_ref[1])

    def lap(block, carry):
        at = pl.ds(pl.multiple_of(block * block_rows, block_rows), block_rows)
        scan_out = scan_ref[at, :].astype(bf16).astype(f32)
        gated = (scan_out * value_ref[at, :]).astype(bf16)
        gated_ref[at, :] = gated
        gating_ref[at, :] = (scan_out * slope_ref[at, :]).astype(bf16)
        return carry

    lax.fori_loop(0, steps // 8, lap, 0)
    span = 256

    def column_lap(block, carry):
        at = pl.ds(pl.multiple_of(block * span, span), span)
        out_ref[:, at] = dot(gated_ref[...], exit_ref[:, at]).astype(bf16)
        return carry

    lax.fori_loop(0, out_ref.shape[1] // span, column_lap, 0)

    def store_lap(block, carry):
        at = pl.ds(pl.multiple_of(block * block_rows, block_rows), block_rows)
        store_rows(out_keep_ref, out_send_ref, order, out_ref[at, :], block)
        return carry

    lax.fori_loop(0, steps // 8, store_lap, 0)
    exit_grad_ref[...] = dot(gated_ref[...], rows_ref[...], ((0,), (0,))).astype(bf16)
    entry_grad_ref[...] = dot(normed_ref[...], gating_ref[...], ((0,), (0,)))
    store_blocks(keep_ref, send_ref, place_ref[0], entry_grad_ref)


def filter_kernel(
    place_ref, chosen_ref, other_ref, direct_ref, inner_ref, filter_ref, mask_ref, small_ref,
    rank_ref, decay_ref, bias_ref, skip_ref, gate_keep_ref, gate_came_ref,
    back_ref, tail_ref, first_ref, small_out_ref, total_ref, *refs,
):
    part_refs, (packed_ref, picked_ref, taps_ref, offset_ref, grads_ref, past_ref) = refs[:-6], refs[-6:]
    rows, width = grads_ref.shape
    chunks, sequences = tail_ref.shape[1], first_ref.shape[1]
    rim_rows = 3 * chunks
    for k in range(3):
        past_ref[k, rows : rows + rim_rows, :] = jnp.zeros((rim_rows, width), f32)
    block_rows = chunks * 8
    chosen = (chosen_ref[...].astype(f32) + other_ref[...].astype(f32)).astype(bf16)
    packed_ref[0:64, :] = rank_ref[...]
    packed_ref[64:160, :] = dot(chosen, filter_ref[...].astype(bf16))
    packed_ref[160:176, :] = decay_ref[...]
    picked_ref[...] = chosen.astype(f32).T.astype(bf16)
    taps = [small_row(small_ref, k) for k in range(4)]
    offset = small_row(small_ref, 4)
    offset_ref[...] = jnp.zeros_like(offset_ref)
    taps_ref[...] = jnp.zeros_like(taps_ref)

    def lap(block, carry):
        base = pl.multiple_of(block * block_rows, block_rows)
        at = pl.ds(base, block_rows)
        total = offset
        shifted = []
        for k in range(4):
            part = inner_ref[pl.ds(pl.multiple_of(base + k * chunks, 16), block_rows), :].astype(f32)
            if k < 3:
                part = part * mask_ref[at, k : k + 1]
            shifted.append(part)
            total = total + taps[k] * part
        gate = sigmoid(total)
        grad = direct_ref[at, :] + dot(picked_ref[at, :], small_ref[64:160, :])
        grad = grad * (gate * (1.0 + total * (1.0 - gate)))
        grads_ref[at, :] = grad
        for k in range(3):
            past_ref[k, at, :] = grad * taps[k] * mask_ref[at, k : k + 1]
        offset_ref[...] += jnp.sum(grad, axis=0, keepdims=True)
        for k in range(4):
            taps_ref[k : k + 1, :] += jnp.sum(grad * shifted[k], axis=0, keepdims=True)
        return carry

    lax.fori_loop(0, rows // block_rows, lap, 0)
    packed_ref[176:180, :] = taps_ref[...]
    packed_ref[180:181, :] = offset_ref[...]
    packed_ref[181:182, :] = bias_ref[...]
    packed_ref[182:183, :] = skip_ref[...]
    packed_ref[183:192, :] = jnp.zeros((9, width), f32)
    small_out_ref[...] = packed_ref[...]
    height = gate_keep_ref.shape[1]
    below = (total_ref.shape[0] - height) * 4
    for k, target in enumerate((total_ref,) + part_refs):
        target[0:height, :] = (gate_keep_ref[k].astype(f32) + gate_came_ref[k].astype(f32)).astype(target.dtype)
        if below:
            lanes = pl.ds(pl.multiple_of(((place_ref[0] >> 1) ^ k) * 128, 128), 128)
            for q in range(4):
                values = packed_ref[q * below // 4 : (q + 1) * below // 4, lanes]
                target[height:, q * 128 : (q + 1) * 128] = values.astype(target.dtype)
    spills = []
    for u in range(3):
        total = jnp.zeros((chunks, width), f32)
        for t in range(u + 1):
            total = total + past_ref[u - t, t * chunks : (t + 1) * chunks, :]
        first_ref[u] = total[0:sequences, :]
        spills.append(jnp.concatenate([total[sequences:, :], jnp.zeros((sequences, width), f32)], axis=0))

    def back_lap(block, carry):
        base = pl.multiple_of(block * block_rows, block_rows)
        at = pl.ds(base, block_rows)
        total = grads_ref[at, :] * taps[3]
        for k in range(3):
            later = pl.ds(pl.multiple_of(base + (3 - k) * chunks, 16), block_rows)
            total = total + past_ref[k, later, :]
        back_ref[at, :] = total.astype(bf16)

        @pl.when(block == rows // block_rows - 1)
        def _():
            for u in range(3):
                first = block_rows - rim_rows + u * chunks
                tail_ref[u] = total[first : first + chunks, :] + spills[u]

        return carry

    lax.fori_loop(0, rows // block_rows, back_lap, 0)


def inner_kernel(back_ref, tail_ref, after_ref, normed_ref, inner_ref, entry_grad_ref):
    rows, width = back_ref.shape
    chunks, sequences = tail_ref.shape[1], after_ref.shape[1]
    rim_rows = 3 * chunks
    inner_ref[0 : rows - rim_rows, :] = back_ref[0 : rows - rim_rows, :]
    later = jnp.concatenate([jnp.zeros((3, chunks - sequences, width), f32), after_ref[...]], axis=1)
    tail = (tail_ref[...] + later).reshape(rim_rows, width)
    inner_ref[rows - rim_rows :, :] = tail.astype(bf16)
    entry_grad_ref[...] = dot(normed_ref[...], inner_ref[...], ((0,), (0,))).astype(bf16)


def normed_kernel(
    place_ref, inner_ref, gating_ref, near_ref, far_ref, gate_near_ref, gate_far_ref,
    out_keep_ref, out_send_ref,
    weight_ref, gate_weight_ref, grad_ref,
):
    assemble(weight_ref, (near_ref, far_ref), place_ref[0])
    assemble(gate_weight_ref, (gate_near_ref, gate_far_ref), place_ref[0])
    sequences, steps = out_keep_ref.shape[1:3]
    groups = 4
    block_rows = groups * sequences * 8
    order = ordering(groups, sequences, place_ref[1])

    span = 256

    def column_lap(block, carry):
        at = pl.ds(pl.multiple_of(block * span, span), span)
        grad = dot(inner_ref[...], weight_ref[at, :], ((1,), (1,)))
        grad = grad + dot(gating_ref[...], gate_weight_ref[at, :], ((1,), (1,)))
        grad_ref[:, at] = grad.astype(bf16)
        return carry

    lax.fori_loop(0, grad_ref.shape[1] // span, column_lap, 0)

    def lap(block, carry):
        at = pl.ds(pl.multiple_of(block * block_rows, block_rows), block_rows)
        store_rows(out_keep_ref, out_send_ref, order, grad_ref[at, :], block)
        return carry

    lax.fori_loop(0, steps // 8, lap, 0)


def side_sum_kernel(place_ref, total_ref, *refs):
    part_refs, out_refs, small_ref = refs[:-5], refs[-5:-1], refs[-1]
    total = total_ref[...]
    for part_ref in part_refs:
        total = total + part_ref[...].astype(f32)
    rows = out_refs[0].shape[0]
    for k, out_ref in enumerate(out_refs):
        block = total[0:rows, :]
        for j in range(1, len(out_refs)):
            block = jnp.where((place_ref[1] ^ k) == j, total[j * rows : (j + 1) * rows, :], block)
        out_ref[...] = block.astype(bf16)
    height = rows * len(out_refs)
    below = total.shape[0] - height
    if below:
        for q in range(4):
            small_ref[q * below : (q + 1) * below, :] = total[height:, q * 128 : (q + 1) * 128]
    else:
        small_ref[...] = jnp.zeros_like(small_ref)


def input_kernel(keep_ref, came_ref, other_ref, tokens_ref, cotangent_ref, gain_ref, out_ref):
    grad_hat = keep_ref[0].astype(f32) + came_ref[0].astype(f32) + other_ref[...].astype(f32)
    grad_hat = grad_hat * gain_ref[...]
    rows = tokens_ref[...].astype(f32)
    root = lax.rsqrt(jnp.mean(rows * rows, axis=2, keepdims=True) + epsilon)
    hat = rows * root
    grad = root * (grad_hat - hat * jnp.mean(grad_hat * hat, axis=2, keepdims=True))
    out_ref[...] = (cotangent_ref[...].astype(f32) + grad).astype(bf16)


def interleave_kernel(place_ref, weight_ref, inner_ref, gate0_ref, gate1_ref, gate2_ref, gate3_ref, out_ref, gain_ref):
    gate_refs = (gate0_ref, gate1_ref, gate2_ref, gate3_ref)
    pieces, groups, rows, width = inner_ref.shape
    for k in range(groups):
        inner = inner_ref[0, k].astype(f32)
        for piece in range(1, pieces):
            inner = inner + inner_ref[piece, k].astype(f32)
        gate = gate_refs[0][...].astype(f32)
        for m in range(1, groups):
            gate = jnp.where((place_ref[1] ^ m) == k, gate_refs[m][...].astype(f32), gate)
        for half, values in enumerate((inner, gate)):
            for j in range(width // 64):
                column = half * groups * width + (j * groups + k) * 64
                out_ref[:, column : column + 64] = values[:, j * 64 : (j + 1) * 64]
    total = jnp.sum(out_ref[...] * weight_ref[...].astype(f32), axis=1, keepdims=True)
    gain_ref[...] = jnp.broadcast_to(total, gain_ref.shape)


def local(
    tokens,
    segments,
    cotangent,
    norm_gain,
    entry_weight,
    kernel_weight,
    kernel_offset,
    select_weight,
    delta_weight,
    timestep_bias,
    decay_log,
    skip_gain,
    exit_weight,
):
    sequences, steps, width = tokens.shape
    pieces, groups = lax.axis_size("blk"), lax.axis_size("grp")
    piece, group = lax.axis_index("blk"), lax.axis_index("grp")
    place = jnp.stack([piece, group]).astype(jnp.int32)
    chunks = groups * sequences
    rows = steps * chunks
    slice_rows, entry_width = entry_weight.shape
    own = kernel_offset.shape[0]
    inner_width = entry_width // 2
    group_width = inner_width // groups
    states = decay_log.shape[0]
    rank = delta_weight.shape[0]

    def flipped(value, axis, bits):
        return lax.ppermute(value, axis, [(i, i ^ bits) for i in range(lax.axis_size(axis))])

    def after(value, *others):
        return lax.optimization_barrier((value,) + others)[0]

    def rounds(*values):
        return lax.optimization_barrier(values)

    packed = jnp.concatenate(
        [
            delta_weight,
            select_weight.T,
            decay_log,
            kernel_weight,
            jnp.concatenate([kernel_offset, timestep_bias, skip_gain]).reshape(3, own),
            jnp.zeros((small_rows - 183, own), bf16),
        ],
        axis=0,
    )
    def side_blocks(block):
        return [block] + [flipped(block, "blk", 2 * k) for k in range(1, pieces // 2)]

    place_of_gain = (piece * groups + group) * slice_rows
    gain_line = lax.dynamic_update_slice_in_dim(jnp.zeros((width,), bf16), norm_gain, place_of_gain, 0)
    gain_line = jnp.pad(gain_line.reshape(1, -1, group_width), ((0, 0), (0, 8 - width // group_width), (0, 0)))
    halves = entry_weight.reshape(slice_rows, 2, pieces, groups, own).transpose(3, 1, 0, 2, 4)
    halves = halves.reshape(groups, 2 * slice_rows, group_width)
    halves = jnp.concatenate([halves, jnp.broadcast_to(gain_line, (groups,) + gain_line.shape[1:])], axis=1)
    exit_block = jnp.concatenate([exit_weight, jnp.pad(packed.reshape(-1), (0, -packed.size % (16 * width))).reshape(-1, width)])
    halves, exit_block = rounds(halves, exit_block)
    halves = lax.all_to_all(halves, "grp", split_axis=0, concat_axis=0, tiled=True)
    exit_side = side_blocks(exit_block)
    token_pair = flipped(tokens, "grp", 2)
    halves, token_pair, tokens, *exit_side = rounds(halves, token_pair, tokens, *exit_side)

    gain_rows = jnp.sum(halves[:, 2 * slice_rows :].astype(f32), axis=0).astype(bf16)
    inner_block = halves[:, :slice_rows].reshape(groups * slice_rows, group_width)
    inner_block = jnp.concatenate([inner_block, gain_rows])
    gate_block = halves[:, slice_rows : 2 * slice_rows].reshape(groups * slice_rows, group_width)
    inner_side = side_blocks(inner_block)
    exit_near = jnp.stack(exit_side)
    exit_far = flipped(exit_near, "blk", 1)
    token_slabs = (tokens, flipped(tokens, "grp", 1), token_pair, flipped(token_pair, "grp", 1))
    exit_near, exit_far, gate_block, cotangent, *rest = rounds(
        exit_near, exit_far, gate_block, cotangent, *inner_side, *token_slabs
    )
    inner_side, token_slabs = rest[: pieces // 2], rest[pieces // 2 :]
    small = jnp.stack([exit_near[:, own:], exit_far[:, own:]], axis=1).reshape(pieces, -1)[:, : packed.size]
    bits = pieces.bit_length() - 1
    small = small.reshape((2,) * bits + (small_rows, own))
    for k in range(bits):
        small = jnp.where((piece >> (bits - 1 - k)) & 1, jnp.flip(small, k), small)
    small = small.reshape(pieces, small_rows, own).transpose(1, 0, 2).reshape(small_rows, group_width)

    inner_near = jnp.stack(inner_side)
    ahead = [(i, i + 1) for i in range(pieces - 1)]
    behind = [(i + 1, i) for i in range(pieces - 1)]
    tails = jnp.stack([slab[:, steps - 3 :] for slab in token_slabs])
    tail = lax.dynamic_index_in_dim(tails, group ^ (groups - 1), 0, keepdims=False)
    rim_source = tail.transpose(1, 0, 2).reshape(3 * sequences, width)
    rim = lax.ppermute(rim_source, "blk", ahead)
    inner_far = flipped(inner_near, "blk", 1)
    gate_block, cotangent = rounds(gate_block, cotangent, inner_near, rim_source)[:2]
    gate_side = side_blocks(gate_block)
    cotangent_pair = flipped(cotangent, "grp", 2)
    label_tail = lax.ppermute(segments[:, -3:], "blk", ahead)
    labels = jnp.concatenate([label_tail, segments], axis=1)
    length = segments.shape[1]
    shifted = jnp.stack([labels[:, k : k + length] for k in range(3)], axis=-1)
    same = (shifted == segments[:, :, None]).astype(f32)
    columns = jnp.concatenate([same, 1.0 - same[:, :, 2:3]], axis=2)
    mask = columns.reshape(sequences, groups, steps, 4).transpose(2, 1, 0, 3).reshape(rows, 4)
    gain_all = jnp.sum(inner_near[:, -8:].astype(f32), axis=0) + jnp.sum(inner_far[:, -8:].astype(f32), axis=0)
    gain_all = gain_all[: width // group_width].reshape(1, width)

    gate_near = jnp.stack(gate_side)
    gate_far = flipped(gate_near, "blk", 1)
    cotangent_slabs = (
        cotangent,
        flipped(cotangent, "grp", 1),
        cotangent_pair,
        flipped(cotangent_pair, "grp", 1),
    )

    def group_sum(value):
        half = value.astype(f32) + flipped(value, "grp", 1).astype(f32)
        half = half.astype(bf16)
        return half, flipped(half, "grp", 2)

    normed, inner, filtered, chosen = kernel_call(
        entry_kernel,
        9,
        [
            ((rows, width), bf16),
            ((rows + 3 * chunks, group_width), bf16),
            ((rows, group_width), f32),
            ((96, rows), bf16),
        ],
        [pltpu.VMEM((width, group_width), bf16)],
        12,
        place, *token_slabs, rim, gain_all, mask, inner_near, inner_far, small,
    )
    chosen_pair = group_sum(chosen)
    cotangent_rows, gate_value, gate_slope, grad_scan = kernel_call(
        gate_kernel,
        8,
        [
            ((rows, width), bf16),
            ((rows, group_width), f32),
            ((rows, group_width), f32),
            ((rows, group_width), f32),
        ],
        [
            pltpu.VMEM((width, group_width), bf16),
            pltpu.VMEM((group_width, width), bf16),
            pltpu.VMEM((rows, group_width), f32),
            pltpu.VMEM((rows, group_width), f32),
        ],
        16,
        place, *cotangent_slabs, normed, gate_near, gate_far, exit_near, exit_far,
    )
    cube = (steps, chunks, group_width)
    bank = (states, chunks, group_width)
    load_rows = (states + 2) * sequences
    gates, step_sizes, step_slopes, ends, keeps, gives, loads = kernel_call(
        piece_kernel,
        23,
        [
            ((steps, chunks, 128), f32),
            (cube, f32),
            (cube, f32),
            (bank, f32),
            (bank, f32),
            (bank, f32),
            ((pieces, load_rows, group_width), bf16),
        ],
        [
            pltpu.VMEM((states, 8, group_width), f32),
            pltpu.VMEM((steps * 8, 2 * states * 128), f32),
            pltpu.VMEM((4 * states, 2 * states * 128), bf16),
            pltpu.VMEM((chunks, group_width), f32),
            pltpu.VMEM((load_rows, group_width), f32),
            pltpu.VMEM((load_rows, group_width), f32),
        ],
        16,
        place, *chosen_pair, mask, small, filtered.reshape(cube), grad_scan.reshape(cube),
    )
    came = lax.all_to_all(loads, "blk", split_axis=0, concat_axis=0, tiled=True)

    lanes = group_width // 128
    gate_scratch = [
        pltpu.VMEM((states + 1, 8, group_width), f32),
        pltpu.VMEM((steps * 8, 2 * states * 128), f32),
        pltpu.VMEM((4 * states, 2 * states * 128), bf16),
    ]
    product_scratch = [pltpu.VMEM((steps * 8, states * 128), bf16), pltpu.VMEM((states * 128, 128), bf16)]
    starts = (steps // 4, states, chunks, group_width)
    scan_out, read_sums, block_starts, arrive = kernel_call(
        forward_kernel,
        18,
        [(cube, f32), ((steps, chunks, 128), f32), (starts, f32), (bank, f32)],
        gate_scratch
        + product_scratch
        + [pltpu.VMEM((states, lanes, 8, 128), f32), pltpu.VMEM((2, states * sequences, group_width), f32), pltpu.VMEM(bank, f32)],
        36,
        place, came, gates, small, step_sizes, filtered.reshape(cube), grad_scan.reshape(cube), ends, keeps, gives,
        halves=(None, None, 1, None, 1, 1, 1) + (None,) * 3 + (1, 1, 2, None),
    )
    half_slabs = ((2, sequences, steps, width), bf16)
    block_height = groups * slice_rows
    entry_half = ((pieces // 2, block_height, group_width), bf16)
    grad_gating, out_keep, out_send, exit_grad, gate_keep, gate_send = kernel_call(
        leave_kernel,
        12,
        [((rows, group_width), bf16), half_slabs, half_slabs, ((group_width, width), bf16), entry_half, entry_half],
        [
            pltpu.VMEM((rows, group_width), bf16),
            pltpu.VMEM((width, group_width), f32),
            pltpu.VMEM((group_width, width), bf16),
            pltpu.VMEM((rows, width), bf16),
        ],
        14,
        place, scan_out.reshape(rows, group_width), gate_value, gate_slope, cotangent_rows, normed, exit_near, exit_far,
    )

    exit_parts = lax.all_to_all(
        exit_grad.reshape(pieces, own, width), "blk", split_axis=0, concat_axis=0, tiled=True
    )
    gate_came = flipped(gate_send, "blk", 1)
    out_came = flipped(out_send, "grp", 1)
    grad_direct, rank_grad, chosen_grad, decay_grad, skip_grad, bias_grad = kernel_call(
        backward_kernel,
        35,
        [
            (cube, f32),
            ((rank, group_width), f32),
            ((96, rows), bf16),
            ((states, group_width), f32),
            ((1, group_width), f32),
            ((1, group_width), f32),
        ],
        gate_scratch
        + product_scratch
        + [
            pltpu.VMEM(cube, f32),
            pltpu.VMEM((steps, chunks, 128), f32),
            pltpu.VMEM((states, lanes, 8, 128), f32),
            pltpu.VMEM((states, lanes, 8, 128), f32),
        ],
        50,
        gates, small, step_sizes, step_slopes, filtered.reshape(cube), after(grad_scan, out_send).reshape(cube),
        read_sums, block_starts, arrive,
        halves=(1, None, 1, 1, 1, 1, 1, 2, 1, 1) + (None,) * 5,
    )
    chosen_grad, exit_parts, gate_came, out_came = rounds(chosen_grad, exit_parts, gate_came, out_came)
    chosen_grads = group_sum(chosen_grad)

    def slab_part(keep, came):
        return (keep[1].astype(f32) + came[1].astype(f32)).astype(bf16)

    exit_out = jnp.sum(after(exit_parts, chosen_grads[0]).astype(f32), axis=0)
    grad_direct, exit_out = rounds(grad_direct, exit_out)
    out_part = after(slab_part(out_keep, out_came), chosen_grads[0])
    out_other = flipped(out_part, "grp", 2)

    paired = 2 * own == 128
    side_block = (block_height + (small_rows // 4 if paired else 0), group_width)
    grad_back, tail_back, first_spill, small_grads, side_total, *side_parts = kernel_call(
        filter_kernel,
        6,
        [
            ((rows, group_width), bf16),
            ((3, chunks, group_width), f32),
            ((3, sequences, group_width), f32),
            ((small_rows, group_width), f32),
            (side_block, f32),
        ]
        + [(side_block, bf16)] * (pieces // 2 - 1),
        [
            pltpu.VMEM((small_rows, group_width), f32),
            pltpu.VMEM((rows, 96), bf16),
            pltpu.VMEM((4, group_width), f32),
            pltpu.VMEM((1, group_width), f32),
            pltpu.VMEM((rows, group_width), f32),
            pltpu.VMEM((3, rows + 3 * chunks, group_width), f32),
        ],
        62,
        place, *chosen_grads, grad_direct.reshape(rows, group_width), inner, filtered, mask, small,
        rank_grad, decay_grad, bias_grad, skip_grad, gate_keep, gate_came,
        free=True,
    )
    spill_after = lax.ppermute(first_spill, "blk", behind)
    side_parts = [flipped(part, "blk", 2 * k + 2) for k, part in enumerate(side_parts)]
    grad_inner, inner_entry = kernel_call(
        inner_kernel,
        4,
        [((rows, group_width), bf16), ((width, group_width), bf16)],
        [],
        12,
        grad_back, tail_back, spill_after, normed,
    )
    grad_inner, inner_entry, out_other = rounds(grad_inner, inner_entry, out_other)
    inner_parts = lax.all_to_all(
        inner_entry.reshape(pieces * groups, slice_rows, group_width), both, split_axis=0, concat_axis=0, tiled=True
    )
    grad_keep, grad_send = kernel_call(
        normed_kernel,
        10,
        [half_slabs, half_slabs],
        [
            pltpu.VMEM((width, group_width), bf16),
            pltpu.VMEM((width, group_width), bf16),
            pltpu.VMEM((rows, width), bf16),
        ],
        14,
        place, grad_inner, grad_gating, inner_near, inner_far, gate_near, gate_far,
    )
    grad_send, *side_parts = rounds(grad_send, *side_parts)
    grad_came = flipped(grad_send, "grp", 1)
    grad_part = slab_part(grad_keep, grad_came)
    grad_other = flipped(grad_part, "grp", 2)
    *gate_blocks, small_sum = kernel_call(
        side_sum_kernel,
        2,
        [((slice_rows, group_width), bf16)] * groups + [((small_rows, 128), f32)],
        [],
        16,
        place, after(side_total, grad_part), *side_parts,
    )
    gate_blocks = [gate_blocks[0]] + [flipped(gate_blocks[k], "grp", k) for k in range(1, groups)]
    residual = tokens.astype(f32)
    out_other, gate_blocks[3], small_sum = rounds(out_other, gate_blocks[3], small_sum)
    block_out = residual + out_keep[0].astype(f32) + out_came[0].astype(f32) + out_other.astype(f32)
    block_out = block_out.astype(bf16)
    inner_parts = inner_parts.reshape(pieces, groups, slice_rows, group_width)
    if own == 64:
        entry_out, gain_out = kernel_call(
            interleave_kernel,
            3,
            [((slice_rows, entry_width), f32), ((slice_rows, 128), f32)],
            [],
            16,
            place, entry_weight, inner_parts, *gate_blocks,
        )
        gain_out = gain_out[:, 0]
    else:
        inner_sum = jnp.sum(inner_parts.astype(f32), axis=0)
        gate_parts = jnp.stack(gate_blocks).astype(f32)
        for k in range(2):
            pairs = gate_parts.reshape(2, 2, slice_rows, group_width)
            gate_parts = jnp.where((group >> (1 - k)) & 1, jnp.flip(pairs, k), pairs)
        entry_parts = jnp.stack([inner_sum, gate_parts.reshape(inner_sum.shape)], axis=0)
        entry_parts = entry_parts.reshape(2, groups, slice_rows, pieces, own)
        entry_out = entry_parts.transpose(2, 0, 3, 1, 4).reshape(slice_rows, entry_width)
        gain_out = jnp.sum(entry_out * entry_weight.astype(f32), axis=1)
    gain_out = gain_out / norm_gain.astype(f32)

    if paired:
        small_sum = small_sum + flipped(small_sum, "blk", 1)
        mine = lax.dynamic_slice_in_dim(small_sum, (piece & 1) * own, own, 1)
    else:
        split = small_grads.reshape(small_rows, pieces, own).transpose(1, 0, 2)
        came_small = lax.all_to_all(split, "blk", split_axis=0, concat_axis=0, tiled=True)
        mine = jnp.sum(came_small, axis=0)

    input_grad = kernel_call(
        input_kernel,
        2,
        [((sequences, steps, width), bf16)],
        [],
        16,
        grad_keep, grad_came, after(grad_other, entry_out), tokens, cotangent, gain_all,
    )[0]
    return (
        block_out,
        input_grad,
        gain_out,
        entry_out,
        mine[176:180],
        mine[180],
        mine[64:160].T,
        mine[0:64],
        mine[181],
        mine[160:176],
        mine[182],
        exit_out,
    )


def solution(mesh):
    placed = (
        P(None, both, None),
        P(None, "blk"),
        P(None, both, None),
        P(both),
        P(both, None),
        P(None, both),
        P(both),
        P(both, None),
        P(None, both),
        P(both),
        P(None, both),
        P(both),
        P(both, None),
    )
    return jax.shard_map(
        local,
        mesh=mesh,
        in_specs=placed,
        out_specs=(
            P(None, both, None),
            P(None, both, None),
            P(both),
            P(both, None),
            P(None, both),
            P(both),
            P(both, None),
            P(None, both),
            P(both),
            P(None, both),
            P(both),
            P(both, None),
        ),
        check_vma=False,
    )
```

```python
import jax
import jax.numpy as jnp
from jax import lax
from jax.experimental import pallas as pl
from jax.experimental.pallas import tpu as pltpu
from jax.sharding import PartitionSpec as P

epsilon = 1e-05
log2_e = 1.4426950408889634
log_2 = 0.6931471805599453
reset_push = 1e6
f32 = jnp.float32
bf16 = jnp.bfloat16
small_rows = 192
both = ("blk", "grp")


def dot(left, right, dims=((1,), (0,))):
    return lax.dot_general(left, right, (dims, ((), ())), preferred_element_type=f32)


def sigmoid(values):
    return 1.0 / (1.0 + jnp.exp(-values))


def spread(block, axis):
    count = lax.axis_size(axis)
    copies = jnp.broadcast_to(block[None], (count,) + block.shape)
    return lax.all_to_all(copies, axis, split_axis=0, concat_axis=0, tiled=True)


def ordering(groups, sequences, me):
    chunks = groups * sequences
    rows = chunks * 8
    out_row = lax.broadcasted_iota(jnp.int32, (rows, rows), 0)
    in_row = lax.broadcasted_iota(jnp.int32, (rows, rows), 1)
    chunk = out_row % chunks
    wanted = (((chunk // sequences) ^ me) * sequences + chunk % sequences) * 8 + out_row // chunks
    return jnp.where(in_row == wanted, 1.0, 0.0).astype(bf16)


def kernel_call(body, micros, outs, scratch, limit, *operands, halves=None, free=False):
    whole = pl.BlockSpec(memory_space=pltpu.VMEM)
    kinds = [(value.shape, value.dtype) for value in operands] + list(outs)

    def place(index):
        shape, kind = kinds[index]
        if kind == jnp.int32:
            return pl.BlockSpec(memory_space=pltpu.SMEM)
        axis = halves[index] if halves else None
        if axis is None and free:
            return pl.BlockSpec(shape, lambda *_: (0,) * len(shape))
        if axis is None:
            return whole
        block = tuple(size // 2 if k == axis else size for k, size in enumerate(shape))
        return pl.BlockSpec(block, lambda half: tuple(half if k == axis else 0 for k in range(len(block))))

    places = [place(k) for k in range(len(kinds))]
    return pl.pallas_call(
        body,
        out_shape=[jax.ShapeDtypeStruct(shape, kind) for shape, kind in outs],
        grid=(2,) if halves else (),
        in_specs=places[: len(operands)],
        out_specs=places[len(operands) :],
        scratch_shapes=scratch,
        compiler_params=pltpu.CompilerParams(vmem_limit_bytes=limit << 20),
        cost_estimate=pl.CostEstimate(
            flops=micros * 1_150_000_000, bytes_accessed=8_000_000, transcendentals=0
        ),
    )(*operands)


def read_rows(slab_refs, block):
    sequences, _, width = slab_refs[0].shape
    at = pl.ds(pl.multiple_of(block * 8, 8), 8)
    parts = [slab[:, at, :].astype(f32) for slab in slab_refs]
    return jnp.concatenate(parts, axis=0).reshape(len(slab_refs) * sequences * 8, width)


def small_row(small_ref, index):
    tail = small_ref[176:192, :].astype(f32)
    return tail[index : index + 1, :]


def assemble(whole_ref, stacks, me):
    for side, stack_ref in enumerate(stacks):
        count = stack_ref.shape[0]
        rows = whole_ref.shape[0] // (2 * count)
        for k in range(count):
            target = pl.ds(pl.multiple_of((me ^ (2 * k + side)) * rows, 8), rows)
            whole_ref[target, :] = stack_ref[k, 0:rows, :]


def entry_kernel(
    place_ref, slab0_ref, slab1_ref, slab2_ref, slab3_ref, rim_ref, gain_ref, mask_ref, near_ref, far_ref, small_ref,
    normed_ref, inner_ref, filter_ref, chosen_ref, weight_ref,
):
    slabs = (slab0_ref, slab1_ref, slab2_ref, slab3_ref)
    groups = len(slabs)
    sequences, steps, width = slab0_ref.shape
    chunks = groups * sequences
    block_rows = chunks * 8
    inner_width = inner_ref.shape[1]
    order = ordering(groups, sequences, place_ref[1])
    assemble(weight_ref, (near_ref, far_ref), place_ref[0])

    def scaled(rows):
        root = lax.rsqrt(jnp.mean(rows * rows, axis=1, keepdims=True) + epsilon)
        return (rows * root * gain_ref[...]).astype(bf16)

    taps = [small_row(small_ref, k) for k in range(4)]
    offset = small_row(small_ref, 4)

    def norm_lap(block, carry):
        base = pl.multiple_of(block * block_rows, block_rows)
        normed = dot(order, scaled(read_rows(slabs, block))).astype(bf16)
        normed_ref[pl.ds(base, block_rows), :] = normed
        return carry

    lax.fori_loop(0, steps // 8, norm_lap, 0)
    inner_ref[3 * chunks :, :] = dot(normed_ref[...], weight_ref[...]).astype(bf16)
    last = inner_ref[steps * chunks :, :].astype(f32).reshape(3, chunks, inner_width)
    rim = dot(scaled(rim_ref[...].astype(f32)), weight_ref[...]).reshape(3, sequences, inner_width)
    rim = jnp.concatenate([rim, last[:, : chunks - sequences, :]], axis=1)
    inner_ref[0 : 3 * chunks, :] = rim.reshape(3 * chunks, inner_width).astype(bf16)

    def lap(block, carry):
        base = pl.multiple_of(block * block_rows, block_rows)
        total = offset
        for k in range(3):
            same = mask_ref[pl.ds(base, block_rows), k : k + 1]
            part = inner_ref[pl.ds(pl.multiple_of(base + k * chunks, 16), block_rows), :]
            total = total + taps[k] * part.astype(f32) * same
        inner = inner_ref[pl.ds(pl.multiple_of(base + 3 * chunks, 16), block_rows), :]
        total = total + taps[3] * inner.astype(f32)
        filtered = (total * sigmoid(total)).astype(bf16)
        filter_ref[pl.ds(base, block_rows), :] = filtered.astype(f32)
        chosen = dot(small_ref[64:160, :], filtered, ((1,), (1,)))
        chosen_ref[:, pl.ds(base, block_rows)] = chosen.astype(bf16)
        return carry

    lax.fori_loop(0, steps // 8, lap, 0)


def gate_kernel(
    place_ref, slab0_ref, slab1_ref, slab2_ref, slab3_ref, normed_ref, near_ref, far_ref, exit_near_ref, exit_far_ref,
    rows_ref, value_ref, slope_ref, grad_ref, weight_ref, exit_ref, gating_ref, gated_ref,
):
    slabs = (slab0_ref, slab1_ref, slab2_ref, slab3_ref)
    sequences, steps, width = slab0_ref.shape
    block_rows = len(slabs) * sequences * 8
    order = ordering(len(slabs), sequences, place_ref[1])
    assemble(weight_ref, (near_ref, far_ref), place_ref[0])
    assemble(exit_ref, (exit_near_ref, exit_far_ref), place_ref[0])

    def order_lap(block, carry):
        at = pl.ds(pl.multiple_of(block * block_rows, block_rows), block_rows)
        rows_ref[at, :] = dot(order, read_rows(slabs, block).astype(bf16)).astype(bf16)
        return carry

    lax.fori_loop(0, steps // 8, order_lap, 0)
    gating_ref[...] = dot(normed_ref[...], weight_ref[...])
    gated_ref[...] = dot(rows_ref[...], exit_ref[...], ((1,), (1,)))

    def lap(block, carry):
        at = pl.ds(pl.multiple_of(block * block_rows, block_rows), block_rows)
        gating = gating_ref[at, :]
        grad_gated = gated_ref[at, :]
        gate = sigmoid(gating)
        value = gating * gate
        value_ref[at, :] = value
        slope_ref[at, :] = grad_gated * (gate * (1.0 + gating * (1.0 - gate)))
        grad_ref[at, :] = (grad_gated * value).astype(bf16).astype(f32)
        return carry

    lax.fori_loop(0, steps // 8, lap, 0)


def fill_rates(small_ref, rates_ref):
    states = rates_ref.shape[0]
    rates = -jnp.exp(small_ref[160 : 160 + states, :].astype(f32)) * log2_e
    for n in range(states):
        rates_ref[n] = jnp.broadcast_to(rates[n : n + 1, :], rates_ref.shape[1:])


def fill_picks(pick_ref):
    depth, width = pick_ref.shape
    source = lax.broadcasted_iota(jnp.int32, (depth, width), 0) % (depth // 2)
    target = lax.broadcasted_iota(jnp.int32, (depth, width), 1) // 128
    pick_ref[...] = jnp.where(source == target, 1.0, 0.0).astype(bf16)


def fill_gates(gates_ref, pick_ref, spread_ref, at):
    steps = gates_ref.shape[0]
    values = gates_ref[:, at, :].reshape(steps * 8, 128)[:, 64:96]
    high = values.astype(bf16)
    rest = (values - high.astype(f32)).astype(bf16)
    pair = jnp.concatenate([high, rest], axis=1)
    span = 2048

    def lap(k, carry):
        columns = pl.ds(pl.multiple_of(k * span, span), span)
        spread_ref[:, columns] = dot(pair, pick_ref[:, columns])
        return carry

    lax.fori_loop(0, spread_ref.shape[1] // span, lap, 0)


def gate_of(spread_ref, t, n):
    return spread_ref[pl.ds(pl.multiple_of(t * 8, 8), 8), n * 128 : (n + 1) * 128]


def lane_slices(width):
    return [slice(k * 128, (k + 1) * 128) for k in range(width // 128)]


def piece_kernel(
    place_ref, chosen_ref, other_ref, mask_ref, small_ref, filter_ref, grad_ref,
    gates_ref, step_ref, slope_ref, end_ref, keep_ref, give_ref, load_ref,
    rates_ref, spread_ref, pick_ref, sum_ref, ahead_ref, back_ref,
):
    me = place_ref[0]
    steps, chunks, width = step_ref.shape
    states = end_ref.shape[0]
    chosen = chosen_ref[...].astype(f32) + other_ref[...].astype(f32)
    padded = jnp.concatenate([chosen, jnp.zeros((32, chosen.shape[1]), f32)], axis=0)
    gates_ref[...] = padded.T.reshape(steps, chunks, 128)
    fill_rates(small_ref, rates_ref)
    fill_picks(pick_ref)
    bias = small_row(small_ref, 5)
    delta = small_ref[0:64, :]

    def delta_lap(block, carry):
        at = pl.ds(pl.multiple_of(block * 8, 8), 8)
        low = gates_ref[at, :, :].reshape(8 * chunks, 128)[:, 0:64]
        high = low.astype(bf16)
        rest = (low - high.astype(f32)).astype(bf16)
        pre = dot(high, delta) + dot(rest, delta) + bias
        grown = jnp.exp(-jnp.abs(pre))
        step = jnp.maximum(pre, 0.0) + jnp.log1p(grown)
        step_ref[at, :, :] = step.reshape(8, chunks, width)
        slope_ref[at, :, :] = (jnp.where(pre >= 0, 1.0, grown) / (1.0 + grown)).reshape(8, chunks, width)
        return carry

    lax.fori_loop(0, steps // 8, delta_lap, 0)

    push = mask_ref[:, 3:4] * reset_push
    gates_ref[:, :, 96:97] = push.reshape(steps, chunks, 1)
    end_ref[...] = jnp.zeros_like(end_ref)
    give_ref[...] = jnp.zeros_like(give_ref)
    keep_ref[...] = jnp.ones_like(keep_ref)
    span = 8
    lanes = lane_slices(width)
    spots = [(j, i) for j in range(span) for i in range(len(lanes))]

    def half_lap(half, carry):
        at = pl.ds(pl.multiple_of(half * 8, 8), 8)
        fill_gates(gates_ref, pick_ref, spread_ref, at)

        def lap(block, totals):
            totals = list(totals)
            pushed, drives, grads = {}, {}, {}
            for j, i in spots:
                t = block * span + j
                step = step_ref[t, at, lanes[i]]
                push = step + gates_ref[t, at, 96:97]
                totals[i] = totals[i] + push
                pushed[j, i] = push
                drives[j, i] = step * filter_ref[t, at, lanes[i]]
                grads[j, i] = grad_ref[t, at, lanes[i]]
            for n in range(states):
                rate = [rates_ref[n, :, one] for one in lanes]
                end = [end_ref[n, at, one] for one in lanes]
                keep = [keep_ref[n, at, one] for one in lanes]
                give = [give_ref[n, at, one] for one in lanes]
                for j in range(span):
                    write = gate_of(spread_ref, block * span + j, n)
                    read = gate_of(spread_ref, block * span + j, states + n)
                    for i in range(len(lanes)):
                        decay = jnp.exp2(pushed[j, i] * rate[i])
                        end[i] = decay * end[i] + drives[j, i] * write
                        keep[i] = keep[i] * decay
                        give[i] = give[i] + keep[i] * (read * grads[j, i])
                for i, one in enumerate(lanes):
                    end_ref[n, at, one] = end[i]
                    keep_ref[n, at, one] = keep[i]
                    give_ref[n, at, one] = give[i]
            return tuple(totals)

        start = tuple(jnp.zeros((8, 128), f32) for _ in lanes)
        totals = lax.fori_loop(0, steps // span, lap, start)
        for i, one in enumerate(lanes):
            sum_ref[at, one] = totals[i]
        return carry

    lax.fori_loop(0, chunks // 8, half_lap, 0)

    sequences = ahead_ref.shape[0] // (states + 2)
    groups = chunks // sequences
    for n in range(states):
        rows = slice(n * sequences, (n + 1) * sequences)
        ahead = jnp.zeros((sequences, width), f32)
        back = jnp.zeros((sequences, width), f32)
        for k in range(groups):
            part = slice(k * sequences, (k + 1) * sequences)
            ahead = keep_ref[n, part, :] * ahead + end_ref[n, part, :]
            other = slice((groups - 1 - k) * sequences, (groups - k) * sequences)
            back = give_ref[n, other, :] + keep_ref[n, other, :] * back
        ahead_ref[rows, :] = ahead
        back_ref[rows, :] = back
    total = jnp.zeros((sequences, width), f32)
    for k in range(groups):
        total = total + sum_ref[k * sequences : (k + 1) * sequences, :]
    held = states * sequences
    for k in range(2):
        term = total.astype(bf16).astype(f32)
        ahead_ref[held + k * sequences : held + (k + 1) * sequences, :] = term
        total = total - term
    back_ref[held:, :] = ahead_ref[held:, :]

    def load_lap(piece, carry):
        load = jnp.where(piece > me, ahead_ref[...], back_ref[...])
        load_ref[piece] = load.astype(bf16)
        return carry

    lax.fori_loop(0, load_ref.shape[0], load_lap, 0)


def fill_unpicks(unpick_ref, first):
    spot = lax.broadcasted_iota(jnp.int32, unpick_ref.shape, 0) // 128
    column = lax.broadcasted_iota(jnp.int32, unpick_ref.shape, 1)
    unpick_ref[...] = jnp.where(column == spot + first, 1.0, 0.0).astype(bf16)


def forward_kernel(
    place_ref, came_ref, gates_ref, small_ref, step_ref, filter_ref, grad_ref, end_ref, keep_ref, give_ref,
    out_ref, read_sum_ref, start_ref, arrive_ref,
    rates_ref, spread_ref, pick_ref, product_ref, unpick_ref, passed_ref, whole_ref, enter_ref,
):
    me = place_ref[0]
    half = pl.program_id(0)
    steps, _, width = step_ref.shape
    states, chunks = end_ref.shape[:2]
    pieces = came_ref.shape[0]
    sequences = came_ref.shape[1] // (states + 2)
    groups = chunks // sequences
    @pl.when(half == 0)
    def _():
        fill_rates(small_ref, rates_ref)
        fill_picks(pick_ref)
        fill_unpicks(unpick_ref, 64 + states)
        rates_ref[states] = jnp.broadcast_to(small_row(small_ref, 6), (8, width))

        held = states * sequences
        rates = [jnp.broadcast_to(rates_ref[n, 0:1, :], (sequences, width)) for n in range(states)]
        rates = jnp.concatenate(rates, axis=0)

        def step_in(piece, state):
            values = came_ref[piece].astype(f32)
            total = values[held : held + sequences, :]
            total = total + values[held + sequences :, :]
            total = jnp.concatenate([total] * states, axis=0)
            return jnp.exp2(total * rates) * state + values[:held, :]

        def step_back(k, state):
            return step_in(pieces - 1 - k, state)

        zero = jnp.zeros((held, width), f32)
        whole_ref[0] = lax.fori_loop(0, me, step_in, zero)
        whole_ref[1] = lax.fori_loop(0, pieces - 1 - me, step_back, zero)
        for n in range(states):
            ahead = whole_ref[0, n * sequences : (n + 1) * sequences, :]
            back = whole_ref[1, n * sequences : (n + 1) * sequences, :]
            for k in range(groups):
                part = slice(k * sequences, (k + 1) * sequences)
                enter_ref[n, part, :] = ahead
                ahead = keep_ref[n, part, :] * ahead + end_ref[n, part, :]
                other = slice((groups - 1 - k) * sequences, (groups - k) * sequences)
                arrive_ref[n, other, :] = back
                back = give_ref[n, other, :] + keep_ref[n, other, :] * back

    span = 8
    lanes = lane_slices(width)
    spots = [(j, i) for j in range(span) for i in range(len(lanes))]

    fill_gates(gates_ref, pick_ref, spread_ref, slice(None))
    at = pl.ds(pl.multiple_of(half * 8, 8), 8)
    for n in range(states):
        for i, one in enumerate(lanes):
            passed_ref[n, i] = enter_ref[n, at, one]

    def forward(block, inner_carry):
        pushed, drives, grads, outs = {}, {}, {}, {}
        for j, i in spots:
            t = block * span + j
            step = step_ref[t, :, lanes[i]]
            feed = filter_ref[t, :, lanes[i]]
            pushed[j, i] = step + gates_ref[t, :, 96:97]
            drives[j, i] = step * feed
            grads[j, i] = grad_ref[t, :, lanes[i]]
            outs[j, i] = feed * rates_ref[states, :, lanes[i]]
        rows = pl.ds(pl.multiple_of(block * span * 8, span * 8), span * 8)
        for n in range(states):
            rate = [rates_ref[n, :, one] for one in lanes]
            hidden = [passed_ref[n, i] for i in range(len(lanes))]
            for i, one in enumerate(lanes):
                start_ref[block, n, :, one] = hidden[i]
            seen = []
            for j in range(span):
                t = block * span + j
                write = gate_of(spread_ref, t, n)
                read = gate_of(spread_ref, t, states + n)
                total = None
                for i in range(len(lanes)):
                    hidden[i] = jnp.exp2(pushed[j, i] * rate[i]) * hidden[i] + drives[j, i] * write
                    outs[j, i] = outs[j, i] + hidden[i] * read
                    one = grads[j, i] * hidden[i]
                    total = one if total is None else total + one
                seen.append(total)
            product_ref[rows, n * 128 : (n + 1) * 128] = jnp.concatenate(seen, axis=0).astype(bf16)
            for i in range(len(lanes)):
                passed_ref[n, i] = hidden[i]
        for j, i in spots:
            out_ref[block * span + j, :, lanes[i]] = outs[j, i]
        return inner_carry

    lax.fori_loop(0, steps // span, forward, 0)
    summed = dot(product_ref[...], unpick_ref[...])
    read_sum_ref[...] = summed.reshape(steps, 8, 128)


def backward_kernel(
    gates_ref, small_ref, step_ref, slope_ref, filter_ref, grad_ref, read_sum_ref, start_ref, arrive_ref,
    direct_ref, rank_ref, chosen_ref, decay_ref, skip_ref, bias_ref,
    rates_ref, spread_ref, pick_ref, product_ref, unpick_ref, delta_ref, sums_acc_ref,
    passed_ref, total_ref,
):
    half = pl.program_id(0)
    steps, _, width = step_ref.shape
    chunks = delta_ref.shape[1]
    blocks, states = start_ref.shape[:2]
    span = steps // blocks

    @pl.when(half == 0)
    def _():
        fill_rates(small_ref, rates_ref)
        fill_picks(pick_ref)
        fill_unpicks(unpick_ref, 64)
        decay_ref[...] = jnp.zeros_like(decay_ref)
        skip_ref[...] = jnp.zeros_like(skip_ref)
        rank_ref[...] = jnp.zeros_like(rank_ref)
        bias_ref[...] = jnp.zeros_like(bias_ref)
        rates_ref[states] = jnp.broadcast_to(small_row(small_ref, 6), (8, width))

    lanes = lane_slices(width)
    spots = [(j, i) for j in range(span) for i in range(len(lanes))]

    fill_gates(gates_ref, pick_ref, spread_ref, slice(None))
    at = pl.ds(pl.multiple_of(half * 8, 8), 8)
    for n in range(states):
        for i, one in enumerate(lanes):
            passed_ref[n, i] = arrive_ref[n, :, one]
            total_ref[n, i] = jnp.zeros((8, 128), f32)

    def backward(k, skips):
        block = blocks - 1 - k
        skips = list(skips)
        raw, feeds, pushed, drives, grads, weighted, slopes = {}, {}, {}, {}, {}, {}, {}
        for j, i in spots:
            t = block * span + j
            step = step_ref[t, :, lanes[i]]
            feed = filter_ref[t, :, lanes[i]]
            grad = grad_ref[t, :, lanes[i]]
            raw[j, i] = step
            feeds[j, i] = feed
            pushed[j, i] = step + gates_ref[t, :, 96:97]
            drives[j, i] = step * feed
            grads[j, i] = grad
            weighted[j, i] = jnp.zeros((8, 128), f32)
            slopes[j, i] = jnp.zeros((8, 128), f32)
            skips[i] = skips[i] + grad * feed
        rows = pl.ds(pl.multiple_of(block * span * 8, span * 8), span * 8)
        for n in range(states):
            rate = [rates_ref[n, :, one] for one in lanes]
            gone = [passed_ref[n, i] for i in range(len(lanes))]
            turns = [total_ref[n, i] for i in range(len(lanes))]
            hidden = [[start_ref[block, n, :, one] for one in lanes]]
            decays = []
            for j in range(span):
                decays.append([jnp.exp2(pushed[j, i] * rate[i]) for i in range(len(lanes))])
                if j < span - 1:
                    write = gate_of(spread_ref, block * span + j, n)
                    last = hidden[-1]
                    hidden.append(
                        [decays[j][i] * last[i] + drives[j, i] * write for i in range(len(lanes))]
                    )
            seen = [None] * span
            for j in reversed(range(span)):
                t = block * span + j
                write = gate_of(spread_ref, t, n)
                read = gate_of(spread_ref, t, states + n)
                for i in range(len(lanes)):
                    adjoint = read * grads[j, i] + gone[i]
                    weighted[j, i] = weighted[j, i] + adjoint * write
                    one = adjoint * drives[j, i]
                    seen[j] = one if seen[j] is None else seen[j] + one
                    gone[i] = adjoint * decays[j][i]
                    turn = gone[i] * hidden[j][i]
                    slopes[j, i] = slopes[j, i] + turn * rate[i]
                    turns[i] = turns[i] + turn * raw[j, i]
            product_ref[rows, n * 128 : (n + 1) * 128] = jnp.concatenate(seen, axis=0).astype(bf16)
            for i in range(len(lanes)):
                passed_ref[n, i] = gone[i]
                total_ref[n, i] = turns[i]
        for j, i in spots:
            t = block * span + j
            grown = slopes[j, i] * log_2 + weighted[j, i] * feeds[j, i]
            delta_ref[t, at, lanes[i]] = grown * slope_ref[t, :, lanes[i]]
            direct = weighted[j, i] * raw[j, i] + grads[j, i] * rates_ref[states, :, lanes[i]]
            direct_ref[t, :, lanes[i]] = direct
        return tuple(skips)

    start = tuple(jnp.zeros((8, 128), f32) for _ in lanes)
    skips = lax.fori_loop(0, blocks, backward, start)
    for i, one in enumerate(lanes):
        skip_ref[0:1, one] += jnp.sum(skips[i], axis=0, keepdims=True)
        for n in range(states):
            part = jnp.sum(total_ref[n, i], axis=0, keepdims=True)
            decay_ref[n : n + 1, one] += part * rates_ref[n, 0:1, one] * log_2
    summed = dot(product_ref[...], unpick_ref[...])
    sums_acc_ref[:, at, :] = summed.reshape(steps, 8, 128) + read_sum_ref[...]

    grads = delta_ref[:, at, :].reshape(steps * 8, width)
    bias_ref[...] += jnp.sum(grads, axis=0, keepdims=True)
    low = gates_ref[...].reshape(steps * 8, 128)[:, 0:64].astype(bf16)
    rank_ref[...] += dot(low, grads.astype(bf16), ((0,), (0,)))

    @pl.when(half == 1)
    def _():
        rows = steps * chunks
        whole = delta_ref[...].reshape(rows, width).astype(bf16)
        back = dot(small_ref[0:64, :], whole, ((1,), (1,)))
        sums = sums_acc_ref[...].reshape(rows, 128).T
        chosen_ref[0:64, :] = back.astype(bf16)
        chosen_ref[64:96, :] = sums[64:96, :].astype(bf16)


def store_rows(keep_ref, send_ref, order, values, block):
    _, sequences, _, width = keep_ref.shape
    back = dot(order, values.astype(bf16), ((0,), (0,)))
    shaped = back.reshape(4, sequences, 8, width).astype(bf16)
    at = pl.ds(pl.multiple_of(block * 8, 8), 8)
    for k in range(4):
        target = send_ref if k % 2 else keep_ref
        target[k // 2, :, at, :] = shaped[k]


def store_blocks(keep_ref, send_ref, me, *parts):
    count = keep_ref.shape[0]
    below = 0
    for values_ref in parts:
        rows = values_ref.shape[0] // (2 * count)
        for k in range(2 * count):
            source = pl.ds(pl.multiple_of((me ^ k) * rows, 8), rows)
            target = send_ref if k % 2 else keep_ref
            target[k // 2, below : below + rows, :] = values_ref[source, :].astype(bf16)
        below += rows


def leave_kernel(
    place_ref, scan_ref, value_ref, slope_ref, rows_ref, normed_ref, exit_near_ref, exit_far_ref,
    gating_ref, out_keep_ref, out_send_ref, exit_grad_ref, keep_ref, send_ref,
    gated_ref, entry_grad_ref, exit_ref, out_ref,
):
    assemble(exit_ref, (exit_near_ref, exit_far_ref), place_ref[0])
    sequences, steps = out_keep_ref.shape[1:3]
    groups = 4
    block_rows = groups * sequences * 8
    order = ordering(groups, sequences, place_ref[1])

    def lap(block, carry):
        at = pl.ds(pl.multiple_of(block * block_rows, block_rows), block_rows)
        scan_out = scan_ref[at, :].astype(bf16).astype(f32)
        gated = (scan_out * value_ref[at, :]).astype(bf16)
        gated_ref[at, :] = gated
        gating_ref[at, :] = (scan_out * slope_ref[at, :]).astype(bf16)
        return carry

    lax.fori_loop(0, steps // 8, lap, 0)
    span = 256

    def column_lap(block, carry):
        at = pl.ds(pl.multiple_of(block * span, span), span)
        out_ref[:, at] = dot(gated_ref[...], exit_ref[:, at]).astype(bf16)
        return carry

    lax.fori_loop(0, out_ref.shape[1] // span, column_lap, 0)

    def store_lap(block, carry):
        at = pl.ds(pl.multiple_of(block * block_rows, block_rows), block_rows)
        store_rows(out_keep_ref, out_send_ref, order, out_ref[at, :], block)
        return carry

    lax.fori_loop(0, steps // 8, store_lap, 0)
    exit_grad_ref[...] = dot(gated_ref[...], rows_ref[...], ((0,), (0,))).astype(bf16)
    entry_grad_ref[...] = dot(normed_ref[...], gating_ref[...], ((0,), (0,)))
    store_blocks(keep_ref, send_ref, place_ref[0], entry_grad_ref)


def filter_kernel(
    place_ref, chosen_ref, other_ref, direct_ref, inner_ref, filter_ref, mask_ref, small_ref,
    rank_ref, decay_ref, bias_ref, skip_ref, gate_keep_ref, gate_came_ref,
    back_ref, tail_ref, first_ref, small_out_ref, total_ref, *refs,
):
    part_refs, (packed_ref, picked_ref, taps_ref, offset_ref, grads_ref, past_ref) = refs[:-6], refs[-6:]
    rows, width = grads_ref.shape
    chunks, sequences = tail_ref.shape[1], first_ref.shape[1]
    rim_rows = 3 * chunks
    for k in range(3):
        past_ref[k, rows : rows + rim_rows, :] = jnp.zeros((rim_rows, width), f32)
    block_rows = chunks * 8
    chosen = (chosen_ref[...].astype(f32) + other_ref[...].astype(f32)).astype(bf16)
    packed_ref[0:64, :] = rank_ref[...]
    packed_ref[64:160, :] = dot(chosen, filter_ref[...].astype(bf16))
    packed_ref[160:176, :] = decay_ref[...]
    picked_ref[...] = chosen.astype(f32).T.astype(bf16)
    taps = [small_row(small_ref, k) for k in range(4)]
    offset = small_row(small_ref, 4)
    offset_ref[...] = jnp.zeros_like(offset_ref)
    taps_ref[...] = jnp.zeros_like(taps_ref)

    def lap(block, carry):
        base = pl.multiple_of(block * block_rows, block_rows)
        at = pl.ds(base, block_rows)
        total = offset
        shifted = []
        for k in range(4):
            part = inner_ref[pl.ds(pl.multiple_of(base + k * chunks, 16), block_rows), :].astype(f32)
            if k < 3:
                part = part * mask_ref[at, k : k + 1]
            shifted.append(part)
            total = total + taps[k] * part
        gate = sigmoid(total)
        grad = direct_ref[at, :] + dot(picked_ref[at, :], small_ref[64:160, :])
        grad = grad * (gate * (1.0 + total * (1.0 - gate)))
        grads_ref[at, :] = grad
        for k in range(3):
            past_ref[k, at, :] = grad * taps[k] * mask_ref[at, k : k + 1]
        offset_ref[...] += jnp.sum(grad, axis=0, keepdims=True)
        for k in range(4):
            taps_ref[k : k + 1, :] += jnp.sum(grad * shifted[k], axis=0, keepdims=True)
        return carry

    lax.fori_loop(0, rows // block_rows, lap, 0)
    packed_ref[176:180, :] = taps_ref[...]
    packed_ref[180:181, :] = offset_ref[...]
    packed_ref[181:182, :] = bias_ref[...]
    packed_ref[182:183, :] = skip_ref[...]
    packed_ref[183:192, :] = jnp.zeros((9, width), f32)
    small_out_ref[...] = packed_ref[...]
    height = gate_keep_ref.shape[1]
    below = (total_ref.shape[0] - height) * 4
    for k, target in enumerate((total_ref,) + part_refs):
        target[0:height, :] = (gate_keep_ref[k].astype(f32) + gate_came_ref[k].astype(f32)).astype(target.dtype)
        if below:
            lanes = pl.ds(pl.multiple_of(((place_ref[0] >> 1) ^ k) * 128, 128), 128)
            for q in range(4):
                values = packed_ref[q * below // 4 : (q + 1) * below // 4, lanes]
                target[height:, q * 128 : (q + 1) * 128] = values.astype(target.dtype)
    spills = []
    for u in range(3):
        total = jnp.zeros((chunks, width), f32)
        for t in range(u + 1):
            total = total + past_ref[u - t, t * chunks : (t + 1) * chunks, :]
        first_ref[u] = total[0:sequences, :]
        spills.append(jnp.concatenate([total[sequences:, :], jnp.zeros((sequences, width), f32)], axis=0))

    def back_lap(block, carry):
        base = pl.multiple_of(block * block_rows, block_rows)
        at = pl.ds(base, block_rows)
        total = grads_ref[at, :] * taps[3]
        for k in range(3):
            later = pl.ds(pl.multiple_of(base + (3 - k) * chunks, 16), block_rows)
            total = total + past_ref[k, later, :]
        back_ref[at, :] = total.astype(bf16)

        @pl.when(block == rows // block_rows - 1)
        def _():
            for u in range(3):
                first = block_rows - rim_rows + u * chunks
                tail_ref[u] = total[first : first + chunks, :] + spills[u]

        return carry

    lax.fori_loop(0, rows // block_rows, back_lap, 0)


def inner_kernel(back_ref, tail_ref, after_ref, normed_ref, inner_ref, entry_grad_ref):
    rows, width = back_ref.shape
    chunks, sequences = tail_ref.shape[1], after_ref.shape[1]
    rim_rows = 3 * chunks
    inner_ref[0 : rows - rim_rows, :] = back_ref[0 : rows - rim_rows, :]
    later = jnp.concatenate([jnp.zeros((3, chunks - sequences, width), f32), after_ref[...]], axis=1)
    tail = (tail_ref[...] + later).reshape(rim_rows, width)
    inner_ref[rows - rim_rows :, :] = tail.astype(bf16)
    entry_grad_ref[...] = dot(normed_ref[...], inner_ref[...], ((0,), (0,))).astype(bf16)


def normed_kernel(
    place_ref, inner_ref, gating_ref, near_ref, far_ref, gate_near_ref, gate_far_ref,
    out_keep_ref, out_send_ref,
    weight_ref, gate_weight_ref, grad_ref,
):
    assemble(weight_ref, (near_ref, far_ref), place_ref[0])
    assemble(gate_weight_ref, (gate_near_ref, gate_far_ref), place_ref[0])
    sequences, steps = out_keep_ref.shape[1:3]
    groups = 4
    block_rows = groups * sequences * 8
    order = ordering(groups, sequences, place_ref[1])

    span = 256

    def column_lap(block, carry):
        at = pl.ds(pl.multiple_of(block * span, span), span)
        grad = dot(inner_ref[...], weight_ref[at, :], ((1,), (1,)))
        grad = grad + dot(gating_ref[...], gate_weight_ref[at, :], ((1,), (1,)))
        grad_ref[:, at] = grad.astype(bf16)
        return carry

    lax.fori_loop(0, grad_ref.shape[1] // span, column_lap, 0)

    def lap(block, carry):
        at = pl.ds(pl.multiple_of(block * block_rows, block_rows), block_rows)
        store_rows(out_keep_ref, out_send_ref, order, grad_ref[at, :], block)
        return carry

    lax.fori_loop(0, steps // 8, lap, 0)


def side_sum_kernel(place_ref, total_ref, *refs):
    part_refs, out_refs, small_ref = refs[:-5], refs[-5:-1], refs[-1]
    total = total_ref[...]
    for part_ref in part_refs:
        total = total + part_ref[...].astype(f32)
    rows = out_refs[0].shape[0]
    for k, out_ref in enumerate(out_refs):
        block = total[0:rows, :]
        for j in range(1, len(out_refs)):
            block = jnp.where((place_ref[1] ^ k) == j, total[j * rows : (j + 1) * rows, :], block)
        out_ref[...] = block.astype(bf16)
    height = rows * len(out_refs)
    below = total.shape[0] - height
    if below:
        for q in range(4):
            small_ref[q * below : (q + 1) * below, :] = total[height:, q * 128 : (q + 1) * 128]
    else:
        small_ref[...] = jnp.zeros_like(small_ref)


def input_kernel(keep_ref, came_ref, other_ref, tokens_ref, cotangent_ref, gain_ref, out_ref):
    grad_hat = keep_ref[0].astype(f32) + came_ref[0].astype(f32) + other_ref[...].astype(f32)
    grad_hat = grad_hat * gain_ref[...]
    rows = tokens_ref[...].astype(f32)
    root = lax.rsqrt(jnp.mean(rows * rows, axis=2, keepdims=True) + epsilon)
    hat = rows * root
    grad = root * (grad_hat - hat * jnp.mean(grad_hat * hat, axis=2, keepdims=True))
    out_ref[...] = (cotangent_ref[...].astype(f32) + grad).astype(bf16)


def interleave_kernel(place_ref, weight_ref, inner_ref, gate0_ref, gate1_ref, gate2_ref, gate3_ref, out_ref, gain_ref):
    gate_refs = (gate0_ref, gate1_ref, gate2_ref, gate3_ref)
    pieces, groups, rows, width = inner_ref.shape
    for k in range(groups):
        inner = inner_ref[0, k].astype(f32)
        for piece in range(1, pieces):
            inner = inner + inner_ref[piece, k].astype(f32)
        gate = gate_refs[0][...].astype(f32)
        for m in range(1, groups):
            gate = jnp.where((place_ref[1] ^ m) == k, gate_refs[m][...].astype(f32), gate)
        for half, values in enumerate((inner, gate)):
            for j in range(width // 64):
                column = half * groups * width + (j * groups + k) * 64
                out_ref[:, column : column + 64] = values[:, j * 64 : (j + 1) * 64]
    total = jnp.sum(out_ref[...] * weight_ref[...].astype(f32), axis=1, keepdims=True)
    gain_ref[...] = jnp.broadcast_to(total, gain_ref.shape)


def local(
    tokens,
    segments,
    cotangent,
    norm_gain,
    entry_weight,
    kernel_weight,
    kernel_offset,
    select_weight,
    delta_weight,
    timestep_bias,
    decay_log,
    skip_gain,
    exit_weight,
):
    sequences, steps, width = tokens.shape
    pieces, groups = lax.axis_size("blk"), lax.axis_size("grp")
    piece, group = lax.axis_index("blk"), lax.axis_index("grp")
    place = jnp.stack([piece, group]).astype(jnp.int32)
    chunks = groups * sequences
    rows = steps * chunks
    slice_rows, entry_width = entry_weight.shape
    own = kernel_offset.shape[0]
    inner_width = entry_width // 2
    group_width = inner_width // groups
    states = decay_log.shape[0]
    rank = delta_weight.shape[0]

    def flipped(value, axis, bits):
        return lax.ppermute(value, axis, [(i, i ^ bits) for i in range(lax.axis_size(axis))])

    def after(value, *others):
        return lax.optimization_barrier((value,) + others)[0]

    def rounds(*values):
        return lax.optimization_barrier(values)

    packed = jnp.concatenate(
        [
            delta_weight,
            select_weight.T,
            decay_log,
            kernel_weight,
            jnp.concatenate([kernel_offset, timestep_bias, skip_gain]).reshape(3, own),
            jnp.zeros((small_rows - 183, own), bf16),
        ],
        axis=0,
    )
    def side_blocks(block):
        return [block] + [flipped(block, "blk", 2 * k) for k in range(1, pieces // 2)]

    place_of_gain = (piece * groups + group) * slice_rows
    gain_line = lax.dynamic_update_slice_in_dim(jnp.zeros((width,), bf16), norm_gain, place_of_gain, 0)
    gain_line = jnp.pad(gain_line.reshape(1, -1, group_width), ((0, 0), (0, 8 - width // group_width), (0, 0)))
    halves = entry_weight.reshape(slice_rows, 2, pieces, groups, own).transpose(3, 1, 0, 2, 4)
    halves = halves.reshape(groups, 2 * slice_rows, group_width)
    halves = jnp.concatenate([halves, jnp.broadcast_to(gain_line, (groups,) + gain_line.shape[1:])], axis=1)
    exit_block = jnp.concatenate([exit_weight, jnp.pad(packed.reshape(-1), (0, -packed.size % (16 * width))).reshape(-1, width)])
    halves, exit_block = rounds(halves, exit_block)
    halves = lax.all_to_all(halves, "grp", split_axis=0, concat_axis=0, tiled=True)
    exit_side = side_blocks(exit_block)
    token_pair = flipped(tokens, "grp", 2)
    halves, token_pair, tokens, *exit_side = rounds(halves, token_pair, tokens, *exit_side)

    gain_rows = jnp.sum(halves[:, 2 * slice_rows :].astype(f32), axis=0).astype(bf16)
    inner_block = halves[:, :slice_rows].reshape(groups * slice_rows, group_width)
    inner_block = jnp.concatenate([inner_block, gain_rows])
    gate_block = halves[:, slice_rows : 2 * slice_rows].reshape(groups * slice_rows, group_width)
    inner_side = side_blocks(inner_block)
    exit_near = jnp.stack(exit_side)
    exit_far = flipped(exit_near, "blk", 1)
    token_slabs = (tokens, flipped(tokens, "grp", 1), token_pair, flipped(token_pair, "grp", 1))
    exit_near, exit_far, gate_block, cotangent, *rest = rounds(
        exit_near, exit_far, gate_block, cotangent, *inner_side, *token_slabs
    )
    inner_side, token_slabs = rest[: pieces // 2], rest[pieces // 2 :]
    small = jnp.stack([exit_near[:, own:], exit_far[:, own:]], axis=1).reshape(pieces, -1)[:, : packed.size]
    bits = pieces.bit_length() - 1
    small = small.reshape((2,) * bits + (small_rows, own))
    for k in range(bits):
        small = jnp.where((piece >> (bits - 1 - k)) & 1, jnp.flip(small, k), small)
    small = small.reshape(pieces, small_rows, own).transpose(1, 0, 2).reshape(small_rows, group_width)

    inner_near = jnp.stack(inner_side)
    ahead = [(i, i + 1) for i in range(pieces - 1)]
    behind = [(i + 1, i) for i in range(pieces - 1)]
    tails = jnp.stack([slab[:, steps - 3 :] for slab in token_slabs])
    tail = lax.dynamic_index_in_dim(tails, group ^ (groups - 1), 0, keepdims=False)
    rim_source = tail.transpose(1, 0, 2).reshape(3 * sequences, width)
    rim = lax.ppermute(rim_source, "blk", ahead)
    inner_far = flipped(inner_near, "blk", 1)
    gate_block, cotangent = rounds(gate_block, cotangent, inner_near, rim_source)[:2]
    gate_side = side_blocks(gate_block)
    cotangent_pair = flipped(cotangent, "grp", 2)
    label_tail = lax.ppermute(segments[:, -3:], "blk", ahead)
    labels = jnp.concatenate([label_tail, segments], axis=1)
    length = segments.shape[1]
    shifted = jnp.stack([labels[:, k : k + length] for k in range(3)], axis=-1)
    same = (shifted == segments[:, :, None]).astype(f32)
    columns = jnp.concatenate([same, 1.0 - same[:, :, 2:3]], axis=2)
    mask = columns.reshape(sequences, groups, steps, 4).transpose(2, 1, 0, 3).reshape(rows, 4)
    gain_all = jnp.sum(inner_near[:, -8:].astype(f32), axis=0) + jnp.sum(inner_far[:, -8:].astype(f32), axis=0)
    gain_all = gain_all[: width // group_width].reshape(1, width)

    gate_near = jnp.stack(gate_side)
    gate_far = flipped(gate_near, "blk", 1)
    cotangent_slabs = (
        cotangent,
        flipped(cotangent, "grp", 1),
        cotangent_pair,
        flipped(cotangent_pair, "grp", 1),
    )

    def group_sum(value):
        half = value.astype(f32) + flipped(value, "grp", 1).astype(f32)
        half = half.astype(bf16)
        return half, flipped(half, "grp", 2)

    normed, inner, filtered, chosen = kernel_call(
        entry_kernel,
        9,
        [
            ((rows, width), bf16),
            ((rows + 3 * chunks, group_width), bf16),
            ((rows, group_width), f32),
            ((96, rows), bf16),
        ],
        [pltpu.VMEM((width, group_width), bf16)],
        12,
        place, *token_slabs, rim, gain_all, mask, inner_near, inner_far, small,
    )
    chosen_pair = group_sum(chosen)
    cotangent_rows, gate_value, gate_slope, grad_scan = kernel_call(
        gate_kernel,
        8,
        [
            ((rows, width), bf16),
            ((rows, group_width), f32),
            ((rows, group_width), f32),
            ((rows, group_width), f32),
        ],
        [
            pltpu.VMEM((width, group_width), bf16),
            pltpu.VMEM((group_width, width), bf16),
            pltpu.VMEM((rows, group_width), f32),
            pltpu.VMEM((rows, group_width), f32),
        ],
        16,
        place, *cotangent_slabs, normed, gate_near, gate_far, exit_near, exit_far,
    )
    cube = (steps, chunks, group_width)
    bank = (states, chunks, group_width)
    load_rows = (states + 2) * sequences
    gates, step_sizes, step_slopes, ends, keeps, gives, loads = kernel_call(
        piece_kernel,
        23,
        [
            ((steps, chunks, 128), f32),
            (cube, f32),
            (cube, f32),
            (bank, f32),
            (bank, f32),
            (bank, f32),
            ((pieces, load_rows, group_width), bf16),
        ],
        [
            pltpu.VMEM((states, 8, group_width), f32),
            pltpu.VMEM((steps * 8, 2 * states * 128), f32),
            pltpu.VMEM((4 * states, 2 * states * 128), bf16),
            pltpu.VMEM((chunks, group_width), f32),
            pltpu.VMEM((load_rows, group_width), f32),
            pltpu.VMEM((load_rows, group_width), f32),
        ],
        16,
        place, *chosen_pair, mask, small, filtered.reshape(cube), grad_scan.reshape(cube),
    )
    came = lax.all_to_all(loads, "blk", split_axis=0, concat_axis=0, tiled=True)

    lanes = group_width // 128
    gate_scratch = [
        pltpu.VMEM((states + 1, 8, group_width), f32),
        pltpu.VMEM((steps * 8, 2 * states * 128), f32),
        pltpu.VMEM((4 * states, 2 * states * 128), bf16),
    ]
    product_scratch = [pltpu.VMEM((steps * 8, states * 128), bf16), pltpu.VMEM((states * 128, 128), bf16)]
    starts = (steps // 8, states, chunks, group_width)
    scan_out, read_sums, block_starts, arrive = kernel_call(
        forward_kernel,
        18,
        [(cube, f32), ((steps, chunks, 128), f32), (starts, f32), (bank, f32)],
        gate_scratch
        + product_scratch
        + [pltpu.VMEM((states, lanes, 8, 128), f32), pltpu.VMEM((2, states * sequences, group_width), f32), pltpu.VMEM(bank, f32)],
        36,
        place, came, gates, small, step_sizes, filtered.reshape(cube), grad_scan.reshape(cube), ends, keeps, gives,
        halves=(None, None, 1, None, 1, 1, 1) + (None,) * 3 + (1, 1, 2, None),
    )
    half_slabs = ((2, sequences, steps, width), bf16)
    block_height = groups * slice_rows
    entry_half = ((pieces // 2, block_height, group_width), bf16)
    grad_gating, out_keep, out_send, exit_grad, gate_keep, gate_send = kernel_call(
        leave_kernel,
        12,
        [((rows, group_width), bf16), half_slabs, half_slabs, ((group_width, width), bf16), entry_half, entry_half],
        [
            pltpu.VMEM((rows, group_width), bf16),
            pltpu.VMEM((width, group_width), f32),
            pltpu.VMEM((group_width, width), bf16),
            pltpu.VMEM((rows, width), bf16),
        ],
        14,
        place, scan_out.reshape(rows, group_width), gate_value, gate_slope, cotangent_rows, normed, exit_near, exit_far,
    )

    exit_parts = lax.all_to_all(
        exit_grad.reshape(pieces, own, width), "blk", split_axis=0, concat_axis=0, tiled=True
    )
    gate_came = flipped(gate_send, "blk", 1)
    out_came = flipped(out_send, "grp", 1)
    grad_direct, rank_grad, chosen_grad, decay_grad, skip_grad, bias_grad = kernel_call(
        backward_kernel,
        35,
        [
            (cube, f32),
            ((rank, group_width), f32),
            ((96, rows), bf16),
            ((states, group_width), f32),
            ((1, group_width), f32),
            ((1, group_width), f32),
        ],
        gate_scratch
        + product_scratch
        + [
            pltpu.VMEM(cube, f32),
            pltpu.VMEM((steps, chunks, 128), f32),
            pltpu.VMEM((states, lanes, 8, 128), f32),
            pltpu.VMEM((states, lanes, 8, 128), f32),
        ],
        50,
        gates, small, step_sizes, step_slopes, filtered.reshape(cube), after(grad_scan, out_send).reshape(cube),
        read_sums, block_starts, arrive,
        halves=(1, None, 1, 1, 1, 1, 1, 2, 1, 1) + (None,) * 5,
    )
    chosen_grad, exit_parts, gate_came, out_came = rounds(chosen_grad, exit_parts, gate_came, out_came)
    chosen_grads = group_sum(chosen_grad)

    def slab_part(keep, came):
        return (keep[1].astype(f32) + came[1].astype(f32)).astype(bf16)

    exit_out = jnp.sum(after(exit_parts, chosen_grads[0]).astype(f32), axis=0)
    grad_direct, exit_out = rounds(grad_direct, exit_out)
    out_part = after(slab_part(out_keep, out_came), chosen_grads[0])
    out_other = flipped(out_part, "grp", 2)

    paired = 2 * own == 128
    side_block = (block_height + (small_rows // 4 if paired else 0), group_width)
    grad_back, tail_back, first_spill, small_grads, side_total, *side_parts = kernel_call(
        filter_kernel,
        6,
        [
            ((rows, group_width), bf16),
            ((3, chunks, group_width), f32),
            ((3, sequences, group_width), f32),
            ((small_rows, group_width), f32),
            (side_block, f32),
        ]
        + [(side_block, bf16)] * (pieces // 2 - 1),
        [
            pltpu.VMEM((small_rows, group_width), f32),
            pltpu.VMEM((rows, 96), bf16),
            pltpu.VMEM((4, group_width), f32),
            pltpu.VMEM((1, group_width), f32),
            pltpu.VMEM((rows, group_width), f32),
            pltpu.VMEM((3, rows + 3 * chunks, group_width), f32),
        ],
        62,
        place, *chosen_grads, grad_direct.reshape(rows, group_width), inner, filtered, mask, small,
        rank_grad, decay_grad, bias_grad, skip_grad, gate_keep, gate_came,
        free=True,
    )
    spill_after = lax.ppermute(first_spill, "blk", behind)
    side_parts = [flipped(part, "blk", 2 * k + 2) for k, part in enumerate(side_parts)]
    grad_inner, inner_entry = kernel_call(
        inner_kernel,
        4,
        [((rows, group_width), bf16), ((width, group_width), bf16)],
        [],
        12,
        grad_back, tail_back, spill_after, normed,
    )
    grad_inner, inner_entry, out_other = rounds(grad_inner, inner_entry, out_other)
    inner_parts = lax.all_to_all(
        inner_entry.reshape(pieces * groups, slice_rows, group_width), both, split_axis=0, concat_axis=0, tiled=True
    )
    grad_keep, grad_send = kernel_call(
        normed_kernel,
        10,
        [half_slabs, half_slabs],
        [
            pltpu.VMEM((width, group_width), bf16),
            pltpu.VMEM((width, group_width), bf16),
            pltpu.VMEM((rows, width), bf16),
        ],
        14,
        place, grad_inner, grad_gating, inner_near, inner_far, gate_near, gate_far,
    )
    grad_send, *side_parts = rounds(grad_send, *side_parts)
    grad_came = flipped(grad_send, "grp", 1)
    grad_part = slab_part(grad_keep, grad_came)
    grad_other = flipped(grad_part, "grp", 2)
    *gate_blocks, small_sum = kernel_call(
        side_sum_kernel,
        2,
        [((slice_rows, group_width), bf16)] * groups + [((small_rows, 128), f32)],
        [],
        16,
        place, after(side_total, grad_part), *side_parts,
    )
    gate_blocks = [gate_blocks[0]] + [flipped(gate_blocks[k], "grp", k) for k in range(1, groups)]
    residual = tokens.astype(f32)
    out_other, gate_blocks[3], small_sum = rounds(out_other, gate_blocks[3], small_sum)
    block_out = residual + out_keep[0].astype(f32) + out_came[0].astype(f32) + out_other.astype(f32)
    block_out = block_out.astype(bf16)
    inner_parts = inner_parts.reshape(pieces, groups, slice_rows, group_width)
    if own == 64:
        entry_out, gain_out = kernel_call(
            interleave_kernel,
            3,
            [((slice_rows, entry_width), f32), ((slice_rows, 128), f32)],
            [],
            16,
            place, entry_weight, inner_parts, *gate_blocks,
        )
        gain_out = gain_out[:, 0]
    else:
        inner_sum = jnp.sum(inner_parts.astype(f32), axis=0)
        gate_parts = jnp.stack(gate_blocks).astype(f32)
        for k in range(2):
            pairs = gate_parts.reshape(2, 2, slice_rows, group_width)
            gate_parts = jnp.where((group >> (1 - k)) & 1, jnp.flip(pairs, k), pairs)
        entry_parts = jnp.stack([inner_sum, gate_parts.reshape(inner_sum.shape)], axis=0)
        entry_parts = entry_parts.reshape(2, groups, slice_rows, pieces, own)
        entry_out = entry_parts.transpose(2, 0, 3, 1, 4).reshape(slice_rows, entry_width)
        gain_out = jnp.sum(entry_out * entry_weight.astype(f32), axis=1)
    gain_out = gain_out / norm_gain.astype(f32)

    if paired:
        small_sum = small_sum + flipped(small_sum, "blk", 1)
        mine = lax.dynamic_slice_in_dim(small_sum, (piece & 1) * own, own, 1)
    else:
        split = small_grads.reshape(small_rows, pieces, own).transpose(1, 0, 2)
        came_small = lax.all_to_all(split, "blk", split_axis=0, concat_axis=0, tiled=True)
        mine = jnp.sum(came_small, axis=0)

    input_grad = kernel_call(
        input_kernel,
        2,
        [((sequences, steps, width), bf16)],
        [],
        16,
        grad_keep, grad_came, after(grad_other, entry_out), tokens, cotangent, gain_all,
    )[0]
    return (
        block_out,
        input_grad,
        gain_out,
        entry_out,
        mine[176:180],
        mine[180],
        mine[64:160].T,
        mine[0:64],
        mine[181],
        mine[160:176],
        mine[182],
        exit_out,
    )


def solution(mesh):
    placed = (
        P(None, both, None),
        P(None, "blk"),
        P(None, both, None),
        P(both),
        P(both, None),
        P(None, both),
        P(both),
        P(both, None),
        P(None, both),
        P(both),
        P(None, both),
        P(both),
        P(both, None),
    )
    return jax.shard_map(
        local,
        mesh=mesh,
        in_specs=placed,
        out_specs=(
            P(None, both, None),
            P(None, both, None),
            P(both),
            P(both, None),
            P(None, both),
            P(both),
            P(both, None),
            P(None, both),
            P(both),
            P(None, both),
            P(both),
            P(both, None),
        ),
        check_vma=False,
    )
```
